32 devices in a mesh: seq: 2 (over x), shard: 16 (over z, y, core).
Axes of the slice: x: 2, y: 2, z: 4, core: 2. Of those that a mesh axis runs over, the one named last changes fastest.
Arguments:
- tokens: bfloat16 [32, 512, 1024], P(('seq', 'shard')), may hold values from -6 to 6
- cotangent: bfloat16 [32, 512, 1024], P(('seq', 'shard')), may hold values from -6 to 6
- lengths: int32 [16], replicated, may hold values from 512 to 1024, as said below
- first_gain: bfloat16 [1024], P('shard'), may hold values from 0.25 to 1.75
- first_bias: bfloat16 [1024], P('shard'), may hold values from -1.5 to 1.5
- qkv_weight: bfloat16 [1024, 3072], P('shard'), may hold values from -0.1875 to 0.1875
- qv_bias: bfloat16 [2048], P('shard'), may hold values from -1.5 to 1.5
- dense_weight: bfloat16 [1024, 1024], P('shard'), may hold values from -0.5 to 0.5
- dense_bias: bfloat16 [1024], P('shard'), may hold values from -1.5 to 1.5
- second_gain: bfloat16 [1024], P('shard'), may hold values from 0.25 to 1.75
- second_bias: bfloat16 [1024], P('shard'), may hold values from -1.5 to 1.5
- fc1_weight: bfloat16 [1024, 4096], P('shard'), may hold values from -0.1875 to 0.1875
- fc1_bias: bfloat16 [4096], P('shard'), may hold values from -1.5 to 1.5
- fc2_weight: bfloat16 [4096, 1024], P('shard'), may hold values from -0.09375 to 0.09375
- fc2_bias: bfloat16 [1024], P('shard'), may hold values from -1.5 to 1.5
Outputs:
- block_out: bfloat16 [32, 512, 1024], P(('seq', 'shard'))
- tokens_grad: bfloat16 [32, 512, 1024], P(('seq', 'shard'))
- first_gain_grad: float32 [1024], P('shard')
- first_bias_grad: float32 [1024], P('shard')
- qkv_weight_grad: float32 [1024, 3072], P('shard')
- qv_bias_grad: float32 [2048], P('shard')
- dense_weight_grad: float32 [1024, 1024], P('shard')
- dense_bias_grad: float32 [1024], P('shard')
- second_gain_grad: float32 [1024], P('shard')
- second_bias_grad: float32 [1024], P('shard')
- fc1_weight_grad: float32 [1024, 4096], P('shard')
- fc1_bias_grad: float32 [4096], P('shard')
- fc2_weight_grad: float32 [4096, 1024], P('shard')
- fc2_bias_grad: float32 [1024], P('shard')
The draws below stay inside these ranges and needn't reach their ends.
Inputs may be any that keep to these rules, and one draw needn't show every extreme that they name: Every length is a multiple of 32; the lengths of each group's 1 sequence sum to at most 1024, and in some group to exactly 1024.
All inputs are finite; a program needn't handle non-finite values.
Results may differ from the reference program's by a relative error of at most 0.019.
Values may be sent and summed in bfloat16 or wider, within the bound.
A program may use at most 192 MiB of HBM per device.

```python
import jax
import jax.numpy as jnp
from jax import lax

D = 1024
HEADS = 16
HEAD = 64
FF = 4096
SLOTS_DEV = 512
LANES = 32
CAP = 1024
SEQ_GROUP = 1
LMIN = 512
NSEQ = 16
TOKENS = 16384
N_SHARD = 16


def draw_lengths(key, part):
    base_key = jax.random.fold_in(key, 7103)
    key_list = jax.random.split(base_key, 3)
    least_units = max(1, LMIN // LANES)
    most_units = CAP // LANES
    group_units = jax.random.randint(key_list[0], (N_SHARD,), SEQ_GROUP * least_units, most_units + 1)
    share_draw = jax.random.randint(key_list[1], (N_SHARD, SEQ_GROUP), 1, 1000)
    extra_units = group_units - SEQ_GROUP * least_units
    running_sum = extra_units[:, None] * jnp.cumsum(share_draw, axis=1) // jnp.sum(share_draw, axis=1)[:, None]
    previous = jnp.concatenate([jnp.zeros((N_SHARD, 1), jnp.int32), running_sum[:, :-1].astype(jnp.int32)], axis=1)
    seq_units = least_units + running_sum.astype(jnp.int32) - previous
    fullest = jax.random.randint(key_list[2], (), 0, N_SHARD)
    longest_row = jnp.concatenate([jnp.array([most_units - (SEQ_GROUP - 1) * least_units], jnp.int32), jnp.full((SEQ_GROUP - 1,), least_units, jnp.int32)])
    shortest_row = jnp.full((SEQ_GROUP,), least_units, jnp.int32)
    group_ids = jnp.arange(N_SHARD)
    seq_units = jnp.where((group_ids == fullest)[:, None], longest_row[None, :], seq_units)
    seq_units = jnp.where((group_ids == (fullest + 1) % N_SHARD)[:, None], shortest_row[None, :], seq_units)
    return (seq_units.reshape(-1) * LANES).astype(jnp.int32)


def shard_levels(own_key, extent, cuts, least, largest):
    def one(dim, shards_of):
        heights = jax.random.uniform(jax.random.fold_in(jax.random.fold_in(own_key, 6), dim), (shards_of,), jnp.float32, least / len(cuts), largest / len(cuts))
        return jnp.repeat(jnp.exp(heights), extent[dim] // shards_of).reshape((-1,) + (1,) * (len(extent) - dim - 1))

    loudness = one(*cuts[0])
    for cut in cuts[1:]:
        loudness = loudness * one(*cut)
    return loudness


def noise(rng, dims, width, bound, cuts=(), kind=jnp.bfloat16):
    values = jax.random.normal(rng, dims, jnp.float32) * width
    if len(cuts) > 0:
        values = shard_levels(rng, dims, cuts, -0.22, 0.18) * values
    return jnp.clip(values, min=-bound, max=bound).astype(kind)


def setup_inputs(seed: int = 0) -> dict:
    splits = jax.random.split(jax.random.key(seed), 16)
    tokens = noise(splits[0], (LANES, SLOTS_DEV, D), 1.0, 6.0, ((0, 32),))
    cotangent = noise(splits[1], (LANES, SLOTS_DEV, D), 1.0, 6.0, ((0, 32),))
    lengths = draw_lengths(jax.random.fold_in(splits[15], 71), 0)
    first_gain = jnp.clip(1.0 + 0.15 * jax.random.normal(splits[3], (D,), jnp.float32), 0.25, 1.75).astype(jnp.bfloat16)
    first_bias = noise(splits[4], (D,), 0.3, 1.5, ((0, 16),))
    qkv_weight = noise(splits[5], (D, 3 * D), D ** -0.5, 0.1875, ((0, 16),))
    qv_bias = noise(splits[6], (2 * D,), 0.3, 1.5, ((0, 16),))
    dense_weight = noise(splits[7], (D, D), (D // 8) ** -0.5, 0.5, ((0, 16),))
    dense_bias = noise(splits[8], (D,), 0.3, 1.5, ((0, 16),))
    second_gain = jnp.clip(1.0 + 0.15 * jax.random.normal(splits[9], (D,), jnp.float32), 0.25, 1.75).astype(jnp.bfloat16)
    second_bias = noise(splits[10], (D,), 0.3, 1.5, ((0, 16),))
    fc1_weight = noise(splits[11], (D, FF), D ** -0.5, 0.1875, ((0, 16),))
    fc1_bias = noise(splits[12], (FF,), 0.3, 1.5, ((0, 16),))
    fc2_weight = noise(splits[13], (FF, D), FF ** -0.5, 0.09375, ((0, 16),))
    fc2_bias = noise(splits[14], (D,), 0.3, 1.5, ((0, 16),))
    return dict(tokens=tokens, cotangent=cotangent, lengths=lengths, first_gain=first_gain, first_bias=first_bias, qkv_weight=qkv_weight, qv_bias=qv_bias, dense_weight=dense_weight, dense_bias=dense_bias, second_gain=second_gain, second_bias=second_bias, fc1_weight=fc1_weight, fc1_bias=fc1_bias, fc2_weight=fc2_weight, fc2_bias=fc2_bias)


@jax.custom_vjp
def low(v):
    return lax.optimization_barrier(v.astype(jnp.bfloat16)).astype(jnp.float32)

@jax.custom_vjp
def low_back(v):
    return v

def low_keep(v):
    return (low(v), None)

def low_pass(kept, grad):
    return (grad,)

def back_keep(v):
    return (v, None)

def back_low(kept, grad):
    return (low(grad),)
low.defvjp(low_keep, low_pass)
low_back.defvjp(back_keep, back_low)
epsilon = 1e-05
masked_score = -1e+30

def norm_rows(hidden, gain, shift):
    center = hidden - lax.optimization_barrier(jnp.mean(hidden, axis=-1, keepdims=True))
    spread = lax.optimization_barrier(jnp.mean(center * center, axis=-1, keepdims=True))
    return center * lax.rsqrt(spread + epsilon) * gain + shift

def gelu_tanh(values):
    return 0.5 * values * (1.0 + jnp.tanh(0.7978845608028654 * (values + 0.044715 * values * values * values)))

def layout_tables(lengths, dealing, lane_count, group_count, per_group):
    seq_rows = (lengths // lane_count).astype(jnp.int32)
    row_start = (jnp.cumsum(seq_rows) - seq_rows).astype(jnp.int32)
    picked = (dealing[:, None] == jnp.arange(dealing.shape[0], dtype=jnp.int32)[None, :]).astype(jnp.int32)
    slot_rows = lax.optimization_barrier(jnp.sum(picked * seq_rows[:, None], axis=0)).astype(jnp.int32).reshape(group_count, per_group)
    slot_start = lax.optimization_barrier(jnp.sum(picked * row_start[:, None], axis=0)).astype(jnp.int32).reshape(group_count, per_group)
    slot_before = (jnp.cumsum(slot_rows, axis=1) - slot_rows).astype(jnp.int32)
    seq_before = lax.optimization_barrier(jnp.sum(picked * slot_before.reshape(-1)[None, :], axis=1)).astype(jnp.int32)
    return (seq_rows, row_start, slot_rows, slot_start, slot_before, seq_before)

def group_maps(slot_rows, slot_start, slot_before):
    places = jnp.arange(CAP, dtype=jnp.int32)
    row_in = (places // LANES)[None, :, None]
    lane_of = (places % LANES)[None, :]
    inside = ((row_in >= slot_before[:, None, :]) & (row_in < (slot_before + slot_rows)[:, None, :])).astype(jnp.int32)
    live = lax.optimization_barrier(jnp.sum(inside, axis=2)).astype(jnp.int32)
    offset_in = lax.optimization_barrier(jnp.sum(inside * (row_in - slot_before[:, None, :]), axis=2)).astype(jnp.int32)
    source_row = lax.optimization_barrier(jnp.sum(inside * (slot_start[:, None, :] + row_in - slot_before[:, None, :]), axis=2)).astype(jnp.int32)
    member = lax.optimization_barrier(jnp.sum(inside * jnp.arange(SEQ_GROUP, dtype=jnp.int32)[None, None, :], axis=2)).astype(jnp.int32)
    segment = jnp.where(live > 0, member, -1).astype(jnp.int32)
    position = (offset_in * LANES + lane_of).astype(jnp.int32)
    source = (source_row * LANES + lane_of).astype(jnp.int32)
    return (source, live, segment, position)

def stream_maps(seq_rows, row_start, seq_before, dealing):
    places = jnp.arange(TOKENS, dtype=jnp.int32)
    row_of = (places // LANES)[:, None]
    lane_of = places % LANES
    inside = ((row_of >= row_start[None, :]) & (row_of < (row_start + seq_rows)[None, :])).astype(jnp.int32)
    home_group = dealing // SEQ_GROUP
    target_row = seq_before[None, :] + row_of - row_start[None, :]
    target = (lax.optimization_barrier(jnp.sum(inside * (home_group[None, :] * CAP + target_row * LANES), axis=1)) + lane_of).astype(jnp.int32)
    live = lax.optimization_barrier(jnp.sum(inside, axis=1)).astype(jnp.int32)
    return (target, live)

def block_forward(hidden, segment, position, params):
    gain_one, bias_one, full_qkv, bias_qv, full_dense, bias_dense, gain_two, bias_two, full_up, bias_up, full_down, bias_down = params
    highest = lax.Precision.HIGHEST
    normed = low(norm_rows(hidden, gain_one, bias_one))
    bias_all = jnp.concatenate([bias_qv[:D], jnp.zeros_like(bias_qv[:D]), bias_qv[D:]])
    projected = low_back(low(jnp.dot(normed, full_qkv, precision=highest) + bias_all))
    queries = projected[:, :D].reshape(CAP, HEADS, HEAD).transpose(1, 0, 2)
    keys_all = projected[:, D:2 * D].reshape(CAP, HEADS, HEAD).transpose(1, 0, 2)
    values_all = projected[:, 2 * D:].reshape(CAP, HEADS, HEAD).transpose(1, 0, 2)
    slopes = 2.0 ** (-8.0 * (jnp.arange(HEADS, dtype=jnp.float32) + 1.0) / HEADS)
    allowed = (segment[:, None] == segment[None, :]) & (segment[None, :] >= 0) & (position[None, :] <= position[:, None])
    distance = (position[:, None] - position[None, :]).astype(jnp.float32)
    scale_factor = HEAD ** (-0.5)

    def one_head(items):
        query_h, key_h, value_h, slope = items
        raw_dot = low_back(jnp.dot(query_h, key_h.T, precision=highest))
        scored = jnp.where(allowed, raw_dot * scale_factor - slope * distance, masked_score)
        row_top = lax.optimization_barrier(jnp.max(scored, axis=-1, keepdims=True))
        expd = jnp.exp(scored - row_top)
        probs = low(expd / lax.optimization_barrier(jnp.sum(expd, axis=-1, keepdims=True)))
        return jnp.dot(probs, value_h, precision=highest)
    mixed = lax.map(jax.checkpoint(one_head), (queries, keys_all, values_all, slopes))
    mixed = low_back(low(mixed.transpose(1, 0, 2).reshape(CAP, D)))
    branch = low_back(jnp.dot(mixed, full_dense, precision=highest) + bias_dense)
    resid = hidden + branch
    normed_two = low(norm_rows(resid, gain_two, bias_two))
    upper = low_back(jnp.dot(normed_two, full_up, precision=highest) + bias_up)
    activ = low(gelu_tanh(upper))
    down = low_back(jnp.dot(activ, full_down, precision=highest) + bias_down)
    return resid + down

def reference(tokens, cotangent, lengths, first_gain, first_bias, qkv_weight, qv_bias, dense_weight, dense_bias, second_gain, second_bias, fc1_weight, fc1_bias, fc2_weight, fc2_bias):
    dealing = jnp.arange(NSEQ, dtype=jnp.int32)
    seq_rows, row_start, slot_rows, slot_start, slot_before, seq_before = layout_tables(lengths, dealing, LANES, N_SHARD, SEQ_GROUP)
    source, live, segment, position = group_maps(slot_rows, slot_start, slot_before)
    target, stream_live = stream_maps(seq_rows, row_start, seq_before, dealing)
    flat_in = tokens.astype(jnp.float32).transpose(1, 0, 2).reshape(TOKENS, D)
    flat_cot = cotangent.astype(jnp.float32).transpose(1, 0, 2).reshape(TOKENS, D)
    weights = tuple((w.astype(jnp.float32) for w in (first_gain, first_bias, qkv_weight, qv_bias, dense_weight, dense_bias, second_gain, second_bias, fc1_weight, fc1_bias, fc2_weight, fc2_bias)))
    live_mask = live[:, :, None].astype(jnp.float32)
    stream_mask = stream_live[:, None].astype(jnp.float32)

    def forward(flat, *params):
        grouped = flat[source] * live_mask

        def one_group(items):
            return block_forward(items[0], items[1], items[2], params)
        outs = lax.map(jax.checkpoint(one_group), (grouped, segment, position))
        return outs.reshape(N_SHARD * CAP, D)[target] * stream_mask
    result, pull = jax.vjp(forward, flat_in, *weights)
    grads = pull(flat_cot)
    block_out = result.reshape(SLOTS_DEV, LANES, D).transpose(1, 0, 2).astype(jnp.bfloat16)
    tokens_grad = grads[0].reshape(SLOTS_DEV, LANES, D).transpose(1, 0, 2).astype(jnp.bfloat16)
    return (block_out, tokens_grad, grads[1], grads[2], grads[3], grads[4], grads[5], grads[6], grads[7], grads[8], grads[9], grads[10], grads[11], grads[12])
```

```python
import functools

import jax
import jax.numpy as jnp
from jax import lax
from jax.experimental import pallas as pl
from jax.experimental.pallas import tpu as pltpu
from jax.sharding import PartitionSpec as P

HEADS = 16
HEAD = 64
ROWS = 8

epsilon = 1e-05
masked_score = -1e30
f32 = jnp.float32
bf16 = jnp.bfloat16


def gelu_tanh(values):
    return (
        0.5
        * values
        * (1.0 + jnp.tanh(0.7978845608028654 * (values + 0.044715 * values * values * values)))
    )


def normalize(hidden):
    center = hidden - jnp.mean(hidden, axis=-1, keepdims=True)
    spread = jnp.mean(center * center, axis=-1, keepdims=True)
    root = lax.rsqrt(spread + epsilon)
    return center * root, root


def norm_pull(grad, gain, xhat, root):
    scaled = grad * gain
    return root * (
        scaled
        - jnp.mean(scaled, axis=-1, keepdims=True)
        - xhat * jnp.mean(scaled * xhat, axis=-1, keepdims=True)
    )


def slot_ids(first, count, lanes):
    place = first + lax.broadcasted_iota(jnp.int32, (count, 1), 0)
    block, inside = place // (ROWS * lanes), place % (ROWS * lanes)
    return (block * ROWS + inside % ROWS) * lanes + inside // ROWS


def attn_mask(scored, allowed):
    return jnp.where(allowed, scored, masked_score)


def attn_fwd_kernel(lanes, tile, one_seq, slope_ref, idc_ref, idr_ref, beginc_ref, q_ref, k_ref, v_ref, o_ref):
    tokens = q_ref.shape[0]
    block = ROWS * lanes
    lane_id = lax.broadcasted_iota(jnp.int32, (1, 2 * HEAD), 1)
    for b in range(tokens // block):
        end = (b + 1) * block

        def step(t, _):
            at = pl.ds(pl.multiple_of(b * block + t * tile, tile), tile)
            q = q_ref[at, :] * jnp.asarray(HEAD**-0.5, bf16)
            ids_q = idc_ref[at, :]
            both = None
            for j in range(2):
                mine = (lane_id // HEAD) == j
                qj = jnp.where(mine, q, jnp.zeros_like(q))
                s = lax.dot_general(
                    qj, k_ref[:end, :], (((1,), (1,)), ((), ())), preferred_element_type=f32
                )
                s = s + slope_ref[0, 0, j] * idr_ref[:, :end]
                if one_seq:
                    own = s[:, b * block :]
                    own = attn_mask(own, idr_ref[:, b * block : end] <= ids_q)
                    s = jnp.concatenate([s[:, : b * block], own], axis=1) if b else own
                else:
                    ids_k = idr_ref[:, :end]
                    s = attn_mask(s, (ids_k <= ids_q) & (ids_k >= beginc_ref[at, :]))
                top = jnp.max(s, axis=1, keepdims=True)
                e = jnp.exp(s - top)
                total = jnp.sum(e, axis=1, keepdims=True)
                o = jnp.dot(e.astype(bf16), v_ref[:end, :], preferred_element_type=f32) / total
                both = o if both is None else jnp.where(mine, o, both)
            o_ref[at, :] = both.astype(bf16)
            return 0

        lax.fori_loop(0, block // tile, step, 0)


def attn_bwd_kernel(
    lanes, tile, one_seq, slope_ref, idc_ref, idr_ref, beginr_ref, q_ref, k_ref, v_ref, do_ref,
    dq_ref, dk_ref, dv_ref, dk_acc, dv_acc, bias_acc,
):
    tokens = q_ref.shape[0]
    block = ROWS * lanes
    lane_id = lax.broadcasted_iota(jnp.int32, (1, 2 * HEAD), 1)
    dk_acc[...] = jnp.zeros_like(dk_acc)
    dv_acc[...] = jnp.zeros_like(dv_acc)
    for j in range(2):
        bias_acc[j] = jnp.broadcast_to(slope_ref[0, 0, j] * idc_ref[...], (tokens, tile))
    for b in range(tokens // block):
        end = (b + 1) * block

        def step(t, _):
            at = pl.ds(pl.multiple_of(b * block + t * tile, tile), tile)
            q = q_ref[at, :] * jnp.asarray(HEAD**-0.5, bf16)
            do = do_ref[at, :]
            ids_q = idr_ref[:, at]
            both = None
            for j in range(2):
                mine = (lane_id // HEAD) == j
                qj = jnp.where(mine, q, jnp.zeros_like(q))
                doj = jnp.where(mine, do, jnp.zeros_like(do))
                s = lax.dot_general(
                    k_ref[:end, :], qj, (((1,), (1,)), ((), ())), preferred_element_type=f32
                )
                s = s + bias_acc[j, :end, :]
                if one_seq:
                    own = s[b * block :, :]
                    own = attn_mask(own, idc_ref[b * block : end, :] <= ids_q)
                    s = jnp.concatenate([s[: b * block, :], own], axis=0) if b else own
                else:
                    ids_k = idc_ref[:end, :]
                    s = attn_mask(s, (ids_k <= ids_q) & (ids_k >= beginr_ref[:, at]))
                top = jnp.max(s, axis=0, keepdims=True)
                e = jnp.exp(s - top)
                probs = e * (1.0 / jnp.sum(e, axis=0, keepdims=True))
                dv_acc[:end, :] += jnp.dot(probs.astype(bf16), doj, preferred_element_type=f32)
                dp = lax.dot_general(
                    v_ref[:end, :], doj, (((1,), (1,)), ((), ())), preferred_element_type=f32
                )
                inner = jnp.sum(probs * dp, axis=0, keepdims=True)
                ds = (probs * (dp - inner)).astype(bf16)
                dk_acc[:end, :] += jnp.dot(ds, qj, preferred_element_type=f32)
                dq = lax.dot_general(
                    ds, k_ref[:end, :], (((0,), (0,)), ((), ())), preferred_element_type=f32
                )
                both = dq if both is None else jnp.where(mine, dq, both)
            dq_ref[at, :] = (both * (HEAD**-0.5)).astype(bf16)
            return 0

        lax.fori_loop(0, block // tile, step, 0)
    dk_ref[...] = dk_acc[...].astype(bf16)
    dv_ref[...] = dv_acc[...].astype(bf16)


def attn_shape(tokens, width, lanes):
    pairs = width // (2 * HEAD)
    tile = min(256, ROWS * lanes)
    return pairs, tile


def attention_forward(qkv, slopes, ids, begins, lanes, one_seq):
    tokens, width = qkv.shape[0], qkv.shape[1] // 3
    pairs, tile = attn_shape(tokens, width, lanes)
    column = lambda part: pl.BlockSpec((tokens, 2 * HEAD), lambda h, part=part: (0, part * pairs + h))
    whole = lambda a: pl.BlockSpec(a.shape, lambda h: (0, 0))
    idc, idr, beginc = ids[:, None], ids[None, :], begins[:, None]
    half = tokens * tokens * 5 // 8
    return pl.pallas_call(
        functools.partial(attn_fwd_kernel, lanes, tile, one_seq),
        grid=(pairs,),
        in_specs=[
            pl.BlockSpec((1, 1, 2), lambda h: (h, 0, 0), memory_space=pltpu.SMEM),
            whole(idc), whole(idr), whole(beginc), column(0), column(1), column(2),
        ],
        out_specs=pl.BlockSpec((tokens, 2 * HEAD), lambda h: (0, h)),
        out_shape=jax.ShapeDtypeStruct((tokens, width), bf16),
        compiler_params=pltpu.CompilerParams(vmem_limit_bytes=48 * 2**20),
        cost_estimate=pl.CostEstimate(
            flops=8 * pairs * half * HEAD * 2, transcendentals=2 * pairs * half, bytes_accessed=8 * tokens * width
        ),
        name="attention_forward",
    )(slopes.reshape(pairs, 1, 2), idc, idr, beginc, qkv, qkv, qkv)


def attention_backward(qkv, grad_out, slopes, ids, begins, lanes, one_seq):
    tokens, width = qkv.shape[0], qkv.shape[1] // 3
    pairs, tile = attn_shape(tokens, width, lanes)
    column = lambda part: pl.BlockSpec((tokens, 2 * HEAD), lambda h, part=part: (0, part * pairs + h))
    whole = lambda a: pl.BlockSpec(a.shape, lambda h: (0, 0))
    idc, idr, beginr = ids[:, None], ids[None, :], begins[None, :]
    out = jax.ShapeDtypeStruct((tokens, width), bf16)
    half = tokens * tokens * 5 // 8
    return pl.pallas_call(
        functools.partial(attn_bwd_kernel, lanes, tile, one_seq),
        grid=(pairs,),
        in_specs=[
            pl.BlockSpec((1, 1, 2), lambda h: (h, 0, 0), memory_space=pltpu.SMEM),
            whole(idc), whole(idr), whole(beginr), column(0), column(1), column(2), column(0),
        ],
        out_specs=[column(0)] * 3,
        out_shape=[out] * 3,
        scratch_shapes=[
            pltpu.VMEM((tokens, 2 * HEAD), f32), pltpu.VMEM((tokens, 2 * HEAD), f32), pltpu.VMEM((2, tokens, tile), f32),
        ],
        compiler_params=pltpu.CompilerParams(vmem_limit_bytes=56 * 2**20),
        cost_estimate=pl.CostEstimate(
            flops=20 * pairs * half * HEAD * 2, transcendentals=2 * pairs * half, bytes_accessed=14 * tokens * width
        ),
        name="attention_backward",
    )(slopes.reshape(pairs, 1, 2), idc, idr, beginr, qkv, qkv, qkv, grad_out)


def take(blocks, index, axis=0):
    return lax.dynamic_index_in_dim(blocks, index, axis, keepdims=False)


def seq_gather(block, axis):
    n, me = lax.axis_size("seq"), lax.axis_index("seq")
    shape = block.shape[:axis] + (n,) + block.shape[axis:]
    if n == 2:
        peer = lax.ppermute(block, "seq", [(0, 1), (1, 0)])
        return jnp.where(me == 0, jnp.stack([block, peer], axis), jnp.stack([peer, block], axis))
    whole = lax.dynamic_update_index_in_dim(jnp.zeros(shape, block.dtype), block, me, axis)
    for d in range(1, n):
        got = lax.ppermute(block, "seq", [(i, (i + d) % n) for i in range(n)])
        whole = lax.dynamic_update_index_in_dim(whole, got, (me - d) % n, axis)
    return whole


def seq_blocks(whole, axis, dtype):
    n, me = lax.axis_size("seq"), lax.axis_index("seq")
    got = [take(whole, me, axis)]
    for d in range(1, n):
        sent = take(whole, (me + d) % n, axis).astype(dtype)
        got.append(lax.ppermute(sent, "seq", [(i, (i + d) % n) for i in range(n)]))
    return got


def seq_sum(whole, axis, dtype=bf16):
    got = seq_blocks(whole, axis, dtype)
    return sum((g.astype(f32) for g in got[1:]), got[0].astype(f32))


def shard_factors(n):
    nc = 2 if n % 2 == 0 else 1
    nz = 4 if n % (4 * nc) == 0 else 1
    return nz, n // (nz * nc), nc


def shard_reduce(blocks, dtype):
    n, me = lax.axis_size("shard"), lax.axis_index("shard")
    sizes = shard_factors(n)
    blocks = blocks.reshape(sizes + blocks.shape[1:])
    place = (me // (sizes[1] * sizes[2]), me // sizes[2] % sizes[1], me % sizes[2])
    strides = (sizes[1] * sizes[2], sizes[2], 1)
    for axis in (2, 1, 0):
        size, mine, stride = sizes[axis], place[axis], strides[axis]
        total = take(blocks, mine, axis).astype(f32)
        for d in range(1, size):
            sent = take(blocks, (mine + d) % size, axis).astype(dtype)
            pairs = [
                (i, i - (i // stride % size) * stride + ((i // stride % size + d) % size) * stride)
                for i in range(n)
            ]
            total = total + lax.ppermute(sent, "shard", pairs).astype(f32)
        blocks = total if axis == 0 else total.astype(dtype)
    return blocks


def layout_tables(lengths, lane_count, group_count, per_group):
    seq_rows = lengths // lane_count
    row_start = jnp.cumsum(seq_rows) - seq_rows
    slot_rows = seq_rows.reshape(group_count, per_group)
    slot_start = row_start.reshape(group_count, per_group)
    slot_before = jnp.cumsum(slot_rows, axis=1) - slot_rows
    return seq_rows, row_start, slot_rows, slot_start, slot_before


def per_device(
    tokens, cotangent, lengths, first_gain, first_bias, qkv_weight, qv_bias, dense_weight, dense_bias,
    second_gain, second_bias, fc1_weight, fc1_bias, fc2_weight, fc2_bias,
):
    shards, seqs = lax.axis_size("shard"), lax.axis_size("seq")
    lanes = shards * seqs
    slots, width = tokens.shape[1], tokens.shape[2]
    rows = slots // shards
    cap = slots * seqs
    per_group = lengths.shape[0] // shards
    hidden_units = fc1_weight.shape[1]
    me, group = lax.axis_index("seq"), lax.axis_index("shard")
    blocks = rows // ROWS
    heads = width // HEAD // seqs
    part = heads * HEAD
    ff_part = hidden_units // shards // seqs

    qkv_half = take(qkv_weight.reshape(-1, 3, seqs, part), me, 2).reshape(-1, 3 * part)
    fc1_half = take(fc1_weight.reshape(-1, shards, seqs, ff_part), me, 2).reshape(-1, shards * ff_part)
    fc2_half = take(fc2_weight.reshape(seqs, ff_part, width), me, 0)
    small = jnp.concatenate(
        [first_gain, first_bias, qv_bias, dense_bias, second_gain, second_bias, fc1_bias, fc2_bias]
    )
    small_rows = -(-small.shape[0] // (3 * part))
    small_rows += -small_rows % 16
    small = jnp.pad(small, (0, small_rows * 3 * part - small.shape[0])).reshape(small_rows, 3 * part)
    gather = lambda a: lax.all_gather(a, "shard", axis=0, tiled=False)
    qkv_small = gather(jnp.concatenate([qkv_half, small], axis=0))
    own_rows = qkv_half.shape[0]
    full_qkv = qkv_small[:, :own_rows].reshape(width, 3 * part)
    smalls = qkv_small[:, own_rows:].reshape(shards, -1).astype(f32)
    full_dense = gather(dense_weight).reshape(width, width)
    full_up = gather(fc1_half).reshape(width, shards * ff_part)
    full_down = gather(fc2_half).reshape(shards * ff_part, width)
    cuts, at = [], 0
    for a in (first_gain, first_bias, qv_bias, dense_bias, second_gain, second_bias, fc1_bias, fc2_bias):
        cuts.append(smalls[:, at : at + a.shape[0]].reshape(-1))
        at += a.shape[0]
    gain_one, bias_one, bias_qv, bias_dense, gain_two, bias_two, bias_up, bias_down = cuts
    bias_q, bias_v = (take(bias_qv[i * width : (i + 1) * width].reshape(seqs, part), me) for i in (0, 1))
    bias_all = jnp.concatenate([bias_q, jnp.zeros_like(bias_q), bias_v])
    bias_up = take(bias_up.reshape(shards, seqs, ff_part), me, 1).reshape(-1)

    seq_rows, row_start, slot_rows, slot_start, slot_before = layout_tables(lengths, lanes, shards, per_group)
    row_in = jnp.arange(rows, dtype=jnp.int32)[None, :, None]
    inside = ((row_in >= slot_before[:, None]) & (row_in < (slot_before + slot_rows)[:, None])).astype(jnp.int32)
    send_live = jnp.sum(inside, axis=2) > 0
    send_row = jnp.sum(inside * (slot_start[:, None] + row_in - slot_before[:, None]), axis=2).reshape(-1)

    def to_groups(source):
        packed = jnp.take(source, send_row, axis=0).reshape(shards, rows, width)
        packed = jnp.where(send_live[:, :, None], packed, jnp.zeros_like(packed))
        got = lax.all_to_all(packed, "shard", split_axis=0, concat_axis=0, tiled=True)
        own = got.reshape(shards, blocks, ROWS, width).transpose(1, 0, 2, 3).reshape(blocks, -1, width)
        return own, seq_gather(own, 1).reshape(cap, width)

    x_own, x_low = to_groups(tokens[0])
    cot_own, cot_low = to_groups(cotangent[0])

    def own_part(whole):
        return take(whole.reshape(blocks, seqs, -1, whole.shape[-1]), me, 1)

    place = jnp.arange(cap, dtype=jnp.int32)
    block_of, in_block = place // (ROWS * lanes), place % (ROWS * lanes)
    row_of = block_of * ROWS + in_block % ROWS
    ids = row_of * lanes + in_block // ROWS
    own_before, own_count = take(slot_before, group), take(slot_rows, group)
    holds = (row_of[:, None] >= own_before[None]) & (row_of[:, None] < (own_before + own_count)[None])
    begin_row = jnp.sum(jnp.where(holds, own_before[None], 0), axis=1)
    begins = jnp.where(jnp.any(holds, axis=1), begin_row * lanes, ids)
    ids, begins = ids.astype(f32), begins.astype(f32)
    head_ids = me * heads + jnp.arange(heads, dtype=jnp.int32)
    slopes = 2.0 ** (-8.0 * (head_ids.astype(f32) + 1.0) / HEADS)
    one_seq = per_group == 1

    hidden = x_low.astype(f32)
    xhat_one, _ = normalize(hidden)
    normed_one = (xhat_one * gain_one + bias_one).astype(bf16)
    qkv = (jnp.dot(normed_one, full_qkv, preferred_element_type=f32) + bias_all).astype(bf16)
    mixed = attention_forward(qkv, slopes, ids, begins, lanes, one_seq)
    mixed_all = seq_gather(mixed, 1).reshape(cap, width)
    branch = jnp.dot(mixed_all, full_dense, preferred_element_type=f32) + bias_dense
    resid = hidden + branch
    xhat_two, _ = normalize(resid)
    normed_two = (xhat_two * gain_two + bias_two).astype(bf16)
    upper = jnp.dot(normed_two, full_up, preferred_element_type=f32) + bias_up
    activ = gelu_tanh(upper).astype(bf16)
    down = jnp.dot(activ, full_down, preferred_element_type=f32)
    resid_own = own_part(resid)
    down_own = seq_sum(down.reshape(blocks, seqs, -1, width), 1)
    block_out = (resid_own + down_own + bias_down).astype(bf16)

    grad_down = jnp.dot(activ.T, cot_low, preferred_element_type=f32).astype(bf16)
    grad_activ = jnp.dot(cot_low, full_down.T, preferred_element_type=f32)
    grad_upper = jax.vjp(gelu_tanh, upper)[1](grad_activ)[0].astype(bf16)
    grad_up = jnp.dot(normed_two.T, grad_upper, preferred_element_type=f32).astype(bf16)
    grad_bup = jnp.sum(grad_upper.astype(f32), axis=0)
    grad_normed = jnp.dot(grad_upper, full_up.T, preferred_element_type=f32)
    grad_normed = seq_sum(grad_normed.reshape(blocks, seqs, -1, width), 1).reshape(slots, width)
    cot_full = cot_own.reshape(slots, width).astype(f32)
    grad_bdown = jnp.sum(cot_full, axis=0)
    xhat_two, root_two = normalize(resid_own.reshape(slots, width))
    grad_gain_two = jnp.sum(grad_normed * xhat_two, axis=0)
    grad_bias_two = jnp.sum(grad_normed, axis=0)
    grad_resid = cot_full + norm_pull(grad_normed, gain_two, xhat_two, root_two)

    grad_branch = grad_resid.astype(bf16)
    grad_dense = jnp.dot(own_part(mixed_all).reshape(slots, width).T, grad_branch, preferred_element_type=f32).astype(bf16)
    grad_bdense = jnp.sum(grad_branch.astype(f32), axis=0)
    grad_mixed = jnp.dot(grad_branch, full_dense.T, preferred_element_type=f32).astype(bf16)
    got = seq_blocks(grad_mixed.reshape(blocks, -1, seqs, part), 2, bf16)
    if seqs == 2:
        grad_mixed = jnp.where(me == 0, jnp.stack(got, 1), jnp.stack(got[::-1], 1))
    else:
        grad_mixed = jnp.zeros((blocks, seqs) + got[0].shape[1:], bf16)
        for d, g in enumerate(got):
            grad_mixed = lax.dynamic_update_index_in_dim(grad_mixed, g, (me - d) % seqs, 1)
    grad_mixed = grad_mixed.reshape(cap, part)
    grad_proj = jnp.concatenate(
        attention_backward(qkv, grad_mixed, slopes, ids, begins, lanes, one_seq), axis=1
    )
    grad_qkv = jnp.dot(normed_one.T, grad_proj, preferred_element_type=f32).astype(bf16)
    proj_sums = jnp.sum(grad_proj.astype(f32), axis=0)
    grad_one = jnp.dot(grad_proj, full_qkv.T, preferred_element_type=f32)
    grad_one = seq_sum(grad_one.reshape(blocks, seqs, -1, width), 1).reshape(slots, width)
    xhat_one, root_one = normalize(x_own.reshape(slots, width).astype(f32))
    grad_gain_one = jnp.sum(grad_one * xhat_one, axis=0)
    grad_bias_one = jnp.sum(grad_one, axis=0)
    tokens_grad = (grad_resid + norm_pull(grad_one, gain_one, xhat_one, root_one)).astype(bf16)

    row_here = jnp.arange(slots, dtype=jnp.int32)[:, None]
    seq_in = ((row_here >= row_start[None]) & (row_here < (row_start + seq_rows)[None])).astype(jnp.int32)
    home = jnp.arange(lengths.shape[0], dtype=jnp.int32) // per_group
    fetch = jnp.sum(seq_in * (home[None] * rows + slot_before.reshape(-1)[None] + row_here - row_start[None]), axis=1)
    fetch_live = jnp.sum(seq_in, axis=1) > 0

    def to_stream(own):
        sent = own.reshape(blocks, shards, ROWS, width).transpose(1, 0, 2, 3).reshape(shards, rows, width)
        got = lax.all_to_all(sent, "shard", split_axis=0, concat_axis=0, tiled=True)
        taken = jnp.take(got.reshape(-1, width), fetch, axis=0)
        return jnp.where(fetch_live[:, None], taken, jnp.zeros_like(taken))[None]

    down_block = shard_reduce(grad_down.reshape(shards, ff_part, width), bf16)
    up_block = shard_reduce(grad_up.reshape(shards, -1, shards * ff_part), bf16)
    dense_block = shard_reduce(grad_dense.reshape(shards, -1, width), bf16)
    qkv_block = shard_reduce(grad_qkv.reshape(shards, -1, 3 * part), bf16)

    def spread(vector, index_shape):
        zero = jnp.zeros(index_shape, f32)
        return lax.dynamic_update_index_in_dim(zero, vector, me, 1)

    sums = proj_sums.reshape(3, part)
    qv = spread(jnp.stack([sums[0], sums[2]]), (2, seqs, part)).reshape(shards, -1)
    bup = spread(grad_bup.reshape(shards, ff_part), (shards, seqs, ff_part)).reshape(shards, -1)
    rest = (grad_gain_one, grad_bias_one, grad_bdense, grad_gain_two, grad_bias_two, grad_bdown)
    packed = jnp.concatenate([a.reshape(shards, -1) for a in rest] + [qv, bup], axis=1)
    packed = shard_reduce(packed, f32)
    packed = jnp.sum(seq_gather(packed, 0), axis=0)
    cuts, at = [], 0
    for a in [a.reshape(shards, -1) for a in rest] + [qv, bup]:
        cuts.append(packed[at : at + a.shape[1]])
        at += a.shape[1]
    g_gain_one, g_bias_one, g_bdense, g_gain_two, g_bias_two, g_bdown, g_qv, g_bup = cuts

    g_dense = jnp.sum(seq_gather(dense_block.astype(bf16), 0).astype(f32), axis=0)
    g_qkv = seq_gather(qkv_block.astype(bf16).reshape(-1, 3, part), 2).reshape(-1, 3 * width).astype(f32)
    g_up = seq_gather(up_block.astype(bf16).reshape(-1, shards, ff_part), 2).reshape(-1, hidden_units).astype(f32)
    g_down = seq_gather(down_block.astype(bf16), 0).reshape(-1, width).astype(f32)
    return (
        to_stream(block_out), to_stream(tokens_grad.reshape(blocks, -1, width)),
        g_gain_one, g_bias_one, g_qkv, g_qv, g_dense, g_bdense, g_gain_two, g_bias_two, g_up, g_bup, g_down, g_bdown,
    )


def solution(mesh):
    rows, vector, stream = P("shard", None), P("shard"), P(("seq", "shard"), None, None)
    params = (vector, vector, rows, vector, rows, vector, vector, vector, rows, vector, rows, vector)
    return jax.shard_map(
        per_device, mesh=mesh, in_specs=(stream, stream, P()) + params, out_specs=(stream, stream) + params, check_vma=False
    )
```

```python
import functools

import jax
import jax.numpy as jnp
from jax import lax
from jax.experimental import pallas as pl
from jax.experimental.pallas import tpu as pltpu
from jax.sharding import PartitionSpec as P

HEADS = 16
HEAD = 64
ROWS = 8

epsilon = 1e-05
masked_score = -1e30
f32 = jnp.float32
bf16 = jnp.bfloat16


def gelu_tanh(values):
    return (
        0.5
        * values
        * (1.0 + jnp.tanh(0.7978845608028654 * (values + 0.044715 * values * values * values)))
    )


def normalize(hidden):
    center = hidden - jnp.mean(hidden, axis=-1, keepdims=True)
    spread = jnp.mean(center * center, axis=-1, keepdims=True)
    root = lax.rsqrt(spread + epsilon)
    return center * root, root


def norm_pull(grad, gain, xhat, root):
    scaled = grad * gain
    return root * (
        scaled
        - jnp.mean(scaled, axis=-1, keepdims=True)
        - xhat * jnp.mean(scaled * xhat, axis=-1, keepdims=True)
    )


def slot_ids(first, count, lanes):
    place = first + lax.broadcasted_iota(jnp.int32, (count, 1), 0)
    block, inside = place // (ROWS * lanes), place % (ROWS * lanes)
    return (block * ROWS + inside % ROWS) * lanes + inside // ROWS


def attn_mask(scored, allowed):
    return jnp.where(allowed, scored, masked_score)


def attn_fwd_kernel(lanes, tile, one_seq, slope_ref, idc_ref, idr_ref, beginc_ref, q_ref, k_ref, v_ref, o_ref):
    tokens = q_ref.shape[0]
    block = ROWS * lanes
    lane_id = lax.broadcasted_iota(jnp.int32, (1, 2 * HEAD), 1)
    for b in range(tokens // block):
        end = (b + 1) * block

        def step(t, _):
            at = pl.ds(pl.multiple_of(b * block + t * tile, tile), tile)
            q = q_ref[at, :] * jnp.asarray(HEAD**-0.5, bf16)
            ids_q = idc_ref[at, :]
            both = None
            for j in range(2):
                mine = (lane_id // HEAD) == j
                qj = jnp.where(mine, q, jnp.zeros_like(q))
                s = lax.dot_general(
                    qj, k_ref[:end, :], (((1,), (1,)), ((), ())), preferred_element_type=f32
                )
                s = s + slope_ref[0, 0, j] * idr_ref[:, :end]
                if one_seq:
                    own = s[:, b * block :]
                    own = attn_mask(own, idr_ref[:, b * block : end] <= ids_q)
                    s = jnp.concatenate([s[:, : b * block], own], axis=1) if b else own
                else:
                    ids_k = idr_ref[:, :end]
                    s = attn_mask(s, (ids_k <= ids_q) & (ids_k >= beginc_ref[at, :]))
                top = jnp.max(s, axis=1, keepdims=True)
                e = jnp.exp(s - top)
                total = jnp.sum(e, axis=1, keepdims=True)
                o = jnp.dot(e.astype(bf16), v_ref[:end, :], preferred_element_type=f32) / total
                both = o if both is None else jnp.where(mine, o, both)
            o_ref[at, :] = both.astype(bf16)
            return 0

        lax.fori_loop(0, block // tile, step, 0)


def attn_bwd_kernel(
    lanes, tile, one_seq, slope_ref, idc_ref, idr_ref, beginr_ref, q_ref, k_ref, v_ref, do_ref,
    dq_ref, dk_ref, dv_ref, dk_acc, dv_acc, bias_acc,
):
    tokens = q_ref.shape[0]
    block = ROWS * lanes
    lane_id = lax.broadcasted_iota(jnp.int32, (1, 2 * HEAD), 1)
    dk_acc[...] = jnp.zeros_like(dk_acc)
    dv_acc[...] = jnp.zeros_like(dv_acc)
    for j in range(2):
        bias_acc[j] = jnp.broadcast_to(slope_ref[0, 0, j] * idc_ref[...], (tokens, tile))
    for b in range(tokens // block):
        end = (b + 1) * block

        def step(t, _):
            at = pl.ds(pl.multiple_of(b * block + t * tile, tile), tile)
            q = q_ref[at, :] * jnp.asarray(HEAD**-0.5, bf16)
            do = do_ref[at, :]
            ids_q = idr_ref[:, at]
            both = None
            for j in range(2):
                mine = (lane_id // HEAD) == j
                qj = jnp.where(mine, q, jnp.zeros_like(q))
                doj = jnp.where(mine, do, jnp.zeros_like(do))
                s = lax.dot_general(
                    k_ref[:end, :], qj, (((1,), (1,)), ((), ())), preferred_element_type=f32
                )
                s = s + bias_acc[j, :end, :]
                if one_seq:
                    own = s[b * block :, :]
                    own = attn_mask(own, idc_ref[b * block : end, :] <= ids_q)
                    s = jnp.concatenate([s[: b * block, :], own], axis=0) if b else own
                else:
                    ids_k = idc_ref[:end, :]
                    s = attn_mask(s, (ids_k <= ids_q) & (ids_k >= beginr_ref[:, at]))
                top = jnp.max(s, axis=0, keepdims=True)
                e = jnp.exp(s - top)
                probs = e * (1.0 / jnp.sum(e, axis=0, keepdims=True))
                dv_acc[:end, :] += jnp.dot(probs.astype(bf16), doj, preferred_element_type=f32)
                dp = lax.dot_general(
                    v_ref[:end, :], doj, (((1,), (1,)), ((), ())), preferred_element_type=f32
                )
                inner = jnp.sum(probs * dp, axis=0, keepdims=True)
                ds = (probs * (dp - inner)).astype(bf16)
                dk_acc[:end, :] += jnp.dot(ds, qj, preferred_element_type=f32)
                dq = lax.dot_general(
                    ds, k_ref[:end, :], (((0,), (0,)), ((), ())), preferred_element_type=f32
                )
                both = dq if both is None else jnp.where(mine, dq, both)
            dq_ref[at, :] = (both * (HEAD**-0.5)).astype(bf16)
            return 0

        lax.fori_loop(0, block // tile, step, 0)
    dk_ref[...] = dk_acc[...].astype(bf16)
    dv_ref[...] = dv_acc[...].astype(bf16)


def attn_shape(tokens, width, lanes):
    pairs = width // (2 * HEAD)
    tile = min(256, ROWS * lanes)
    return pairs, tile


def attention_forward(qkv, slopes, ids, begins, lanes, one_seq):
    tokens, width = qkv.shape[0], qkv.shape[1] // 3
    pairs, tile = attn_shape(tokens, width, lanes)
    column = lambda part: pl.BlockSpec((tokens, 2 * HEAD), lambda h, part=part: (0, part * pairs + h))
    whole = lambda a: pl.BlockSpec(a.shape, lambda h: (0, 0))
    idc, idr, beginc = ids[:, None], ids[None, :], begins[:, None]
    half = tokens * tokens * 5 // 8
    return pl.pallas_call(
        functools.partial(attn_fwd_kernel, lanes, tile, one_seq),
        grid=(pairs,),
        in_specs=[
            pl.BlockSpec((1, 1, 2), lambda h: (h, 0, 0), memory_space=pltpu.SMEM),
            whole(idc), whole(idr), whole(beginc), column(0), column(1), column(2),
        ],
        out_specs=pl.BlockSpec((tokens, 2 * HEAD), lambda h: (0, h)),
        out_shape=jax.ShapeDtypeStruct((tokens, width), bf16),
        compiler_params=pltpu.CompilerParams(vmem_limit_bytes=48 * 2**20),
        cost_estimate=pl.CostEstimate(
            flops=8 * pairs * half * HEAD * 2, transcendentals=2 * pairs * half, bytes_accessed=8 * tokens * width
        ),
        name="attention_forward",
    )(slopes.reshape(pairs, 1, 2), idc, idr, beginc, qkv, qkv, qkv)


def attention_backward(qkv, grad_out, slopes, ids, begins, lanes, one_seq):
    tokens, width = grad_out.shape
    pairs, tile = attn_shape(tokens, width, lanes)
    column = lambda part: pl.BlockSpec((tokens, 2 * HEAD), lambda h, part=part: (0, part * pairs + h))
    whole = lambda a: pl.BlockSpec(a.shape, lambda h: (0, 0))
    idc, idr, beginr = ids[:, None], ids[None, :], begins[None, :]
    plane = lambda part: pl.BlockSpec((None, tokens, 2 * HEAD), lambda h, part=part: (part * pairs + h, 0, 0))
    out = jax.ShapeDtypeStruct((tokens, width), bf16)
    half = tokens * tokens * 5 // 8
    return pl.pallas_call(
        functools.partial(attn_bwd_kernel, lanes, tile, one_seq),
        grid=(pairs,),
        in_specs=[
            pl.BlockSpec((1, 1, 2), lambda h: (h, 0, 0), memory_space=pltpu.SMEM),
            whole(idc), whole(idr), whole(beginr), plane(0), plane(1), plane(2), column(0),
        ],
        out_specs=[column(0)] * 3,
        out_shape=[out] * 3,
        scratch_shapes=[
            pltpu.VMEM((tokens, 2 * HEAD), f32), pltpu.VMEM((tokens, 2 * HEAD), f32), pltpu.VMEM((2, tokens, tile), f32),
        ],
        compiler_params=pltpu.CompilerParams(vmem_limit_bytes=56 * 2**20),
        cost_estimate=pl.CostEstimate(
            flops=20 * pairs * half * HEAD * 2, transcendentals=2 * pairs * half, bytes_accessed=14 * tokens * width
        ),
        name="attention_backward",
    )(slopes.reshape(pairs, 1, 2), idc, idr, beginr, qkv, qkv, qkv, grad_out)


def take(blocks, index, axis=0):
    return lax.dynamic_index_in_dim(blocks, index, axis, keepdims=False)


def seq_gather(block, axis):
    n, me = lax.axis_size("seq"), lax.axis_index("seq")
    shape = block.shape[:axis] + (n,) + block.shape[axis:]
    if n == 2:
        peer = lax.ppermute(block, "seq", [(0, 1), (1, 0)])
        return jnp.where(me == 0, jnp.stack([block, peer], axis), jnp.stack([peer, block], axis))
    whole = lax.dynamic_update_index_in_dim(jnp.zeros(shape, block.dtype), block, me, axis)
    for d in range(1, n):
        got = lax.ppermute(block, "seq", [(i, (i + d) % n) for i in range(n)])
        whole = lax.dynamic_update_index_in_dim(whole, got, (me - d) % n, axis)
    return whole


def seq_blocks(whole, axis, dtype):
    n, me = lax.axis_size("seq"), lax.axis_index("seq")
    got = [take(whole, me, axis)]
    for d in range(1, n):
        sent = take(whole, (me + d) % n, axis).astype(dtype)
        got.append(lax.ppermute(sent, "seq", [(i, (i + d) % n) for i in range(n)]))
    return got


def seq_sum(whole, axis, dtype=bf16):
    got = seq_blocks(whole, axis, dtype)
    return sum((g.astype(f32) for g in got[1:]), got[0].astype(f32))


def shard_factors(n):
    nc = 2 if n % 2 == 0 else 1
    nz = 4 if n % (4 * nc) == 0 else 1
    return nz, n // (nz * nc), nc


def shard_reduce(blocks, dtype):
    n, me = lax.axis_size("shard"), lax.axis_index("shard")
    sizes = shard_factors(n)
    blocks = blocks.reshape(sizes + blocks.shape[1:])
    place = (me // (sizes[1] * sizes[2]), me // sizes[2] % sizes[1], me % sizes[2])
    strides = (sizes[1] * sizes[2], sizes[2], 1)
    for axis in (2, 1, 0):
        size, mine, stride = sizes[axis], place[axis], strides[axis]
        total = take(blocks, mine, axis).astype(f32)
        for d in range(1, size):
            sent = take(blocks, (mine + d) % size, axis).astype(dtype)
            pairs = [
                (i, i - (i // stride % size) * stride + ((i // stride % size + d) % size) * stride)
                for i in range(n)
            ]
            total = total + lax.ppermute(sent, "shard", pairs).astype(f32)
        blocks = total if axis == 0 else total.astype(dtype)
    return blocks


MESH = pl.DeviceIdType.MESH


class Geometry:
    def __init__(self, seqs, shards):
        self.seqs, self.shards = seqs, shards
        self.sizes = shard_factors(shards)
        self.s, self.k = lax.axis_index("seq"), lax.axis_index("shard")
        nz, ny, nc = self.sizes
        self.z, self.y, self.c = self.k // (ny * nc), self.k // nc % ny, self.k % nc
        self.inner = (self.z + 1) // 2 % 2
        high = self.z // 2
        self.line = (self.z, self.z + 1 - 2 * (self.z % 2), 2 - high, 3 - 3 * high)

    def slot(self, i, dy, dc):
        nz, ny, nc = self.sizes
        return (self.line[i] * ny + (self.y + dy) % ny) * nc + (self.c + dc) % nc


class Wires:
    def __init__(self, geometry, send_sems, recv_sems):
        self.g, self.send_sems, self.recv_sems = geometry, send_sems, recv_sems
        self.sends, self.used = [], 0

    def block(self, count):
        first = self.used
        self.used += count
        return first

    def copy(self, src, dst, sent, got, s, k):
        return pltpu.make_async_remote_copy(
            src_ref=src, dst_ref=dst, send_sem=self.send_sems.at[sent], recv_sem=self.recv_sems.at[got],
            device_id={"seq": s, "shard": k}, device_id_type=MESH,
        )

    def send_as(self, src, dst, sent, got, s, k, like):
        self.copy(src, dst, sent, got, s, k).start()
        self.sends.append((like, sent))

    def send(self, src, dst, index, s, k, like):
        self.send_as(src, dst, index, index, s, k, like)

    def arrived(self, dst, index):
        self.copy(dst, dst, index, index, 1 - self.g.s, self.g.k).wait_recv()

    def drain(self):
        for like, index in self.sends:
            self.copy(like, like, index, index, 1 - self.g.s, self.g.k).wait_send()
        self.sends = []


def enter(geometry):
    g = geometry
    barrier = pltpu.get_barrier_semaphore()
    for d in range(1, g.shards):
        pl.semaphore_signal(
            barrier, inc=1, device_id={"seq": g.s, "shard": (g.k + d) % g.shards}, device_id_type=MESH
        )
    pl.semaphore_signal(barrier, inc=1, device_id={"seq": 1 - g.s, "shard": g.k}, device_id_type=MESH)
    pl.semaphore_wait(barrier, g.shards)


class Gather:
    def __init__(self, wires, own, out):
        self.w, self.g, self.own, self.out = wires, wires.g, own, out
        nz, ny, nc = self.g.sizes
        self.z0 = wires.block(nz)
        self.on0 = wires.block(nz)
        self.y0 = wires.block(nz * ny)
        self.c0 = wires.block(nz * ny * nc)

    def on_y(self, i, src):
        g = self.g
        for dy in range(1, g.sizes[1]):
            self.w.send(src, self.out.at[g.slot(i, 0, 0)], self.y0 + i * g.sizes[1] + dy, g.s, g.slot(0, dy, 0), self.own)

    def on_core(self, i, dy, src):
        g = self.g
        for dc in range(1, g.sizes[2]):
            index = self.c0 + (i * g.sizes[1] + dy) * g.sizes[2] + dc
            self.w.send(src, self.out.at[g.slot(i, -dy, 0)], index, g.s, g.slot(0, 0, dc), self.own)

    def start(self):
        g = self.g
        here = self.out.at[g.k]
        self.w.send_as(self.own, here, self.z0 + 2, self.z0 + 3 - g.inner, g.s, g.slot(2, 0, 0), self.own)
        self.w.send(self.own, here, self.z0 + 1, g.s, g.slot(1, 0, 0), self.own)
        self.on_y(0, self.own)
        self.on_core(0, 0, self.own)

    def poll_z(self):
        g = self.g
        for i in (1, 2, 3):
            at = self.out.at[g.slot(i, 0, 0)]
            self.w.arrived(at, self.z0 + i)
            if i > 1:

                @pl.when(g.inner == 1)
                def _(at=at, i=i):
                    self.w.copy(at, at, self.on0 + i, self.z0 + i, g.s, g.slot(1, 0, 0)).start()

            self.on_y(i, at)
            self.on_core(i, 0, at)

    def poll_y(self):
        g = self.g
        for i in range(g.sizes[0]):
            for dy in range(1, g.sizes[1]):
                at = self.out.at[g.slot(i, -dy, 0)]
                self.w.arrived(at, self.y0 + i * g.sizes[1] + dy)
                self.on_core(i, dy, at)

    def finish(self):
        g = self.g
        for i in range(g.sizes[0]):
            for dy in range(g.sizes[1]):
                for dc in range(1, g.sizes[2]):
                    at = self.out.at[g.slot(i, -dy, -dc)]
                    self.w.arrived(at, self.c0 + (i * g.sizes[1] + dy) * g.sizes[2] + dc)

        @pl.when(g.inner == 1)
        def _():
            for i in (2, 3):
                self.w.copy(self.own, self.own, self.on0 + i, self.z0 + i, g.s, g.k).wait_send()


class Tokens:
    def __init__(self, wires, packed, out):
        self.w, self.g, self.packed, self.out = wires, wires.g, packed, out
        self.a0, self.f0 = wires.block(self.g.shards), wires.block(self.g.shards)

    def lane(self, s, k):
        return self.out.at[:, s * self.g.shards + k]

    def start(self):
        g = self.g
        for d in range(1, g.shards):
            to = (g.k + d) % g.shards
            self.w.send(self.packed.at[to], self.lane(g.s, g.k), self.a0 + d, g.s, to, self.packed.at[0])
        self.w.send(self.packed.at[g.k], self.lane(g.s, g.k), self.f0, 1 - g.s, g.k, self.packed.at[0])

    def poll(self):
        g = self.g
        for d in range(1, g.shards):
            at = self.lane(g.s, (g.k - d) % g.shards)
            self.w.arrived(at, self.a0 + d)
            self.w.send(at, at, self.f0 + d, 1 - g.s, g.k, self.packed.at[0])

    def finish(self):
        g = self.g
        for d in range(g.shards):
            self.w.arrived(self.lane(1 - g.s, (g.k - d) % g.shards), self.f0 + d)


def forward_kernel(
    seqs, shards, counts, one_seq,
    packed, packed_cot, qkv_w, small, dense_w, fc1_w, fc2_w, slopes, idc, idr, beginc,
    x_out, cot_out, n1_out, qkvw_out, small_out, dense_out, fc1_out, fc2_out, qkv_out, o_out,
    x_v, n1_v, qkvw_v, small_v, dense_v, fc1_v, fc2_v, cot_v, qkv_v, o_v, vec_v,
    send_sems, recv_sems, copy_sems,
):
    g = Geometry(seqs, shards)
    wires = Wires(g, send_sems, recv_sems)
    lanes = seqs * shards
    width = n1_v.shape[1]
    pairs = o_v.shape[0] // seqs
    part = pairs * 2 * HEAD
    ff_part = fc1_v.shape[1] // shards
    block = ROWS * lanes
    blocks = x_v.shape[0]

    local = []

    def bring(src, dst):
        made = pltpu.make_async_copy(src, dst, copy_sems.at[len(local)])
        made.start()
        local.append(made)
        return made

    tokens = Tokens(wires, packed, x_v)
    cots = Tokens(wires, packed_cot, cot_out)
    smalls_at = wires.block(shards)
    qkv_all = Gather(wires, qkvw_v.at[g.k], qkvw_v)
    dense_all = Gather(wires, dense_v, dense_out)
    up_all = Gather(wires, fc1_v, fc1_out)
    down_all = Gather(wires, fc2_v, fc2_out)
    heads_at = wires.block(pairs)

    staged_qkv = [
        bring(
            qkv_w.at[:, pl.ds(pl.multiple_of(p * width + g.s * part, 128), part)],
            qkvw_v.at[g.k, :, pl.ds(p * part, part)],
        )
        for p in range(3)
    ]
    staged_x = bring(packed.at[g.k], x_v.at[:, g.s * shards + g.k])
    staged_small = bring(small, small_v.at[g.k])
    staged_dense = bring(dense_w, dense_v)
    staged_down = bring(fc2_w.at[pl.ds(pl.multiple_of(g.s * ff_part, 8), ff_part), :], fc2_v)
    staged_cot = bring(packed_cot.at[g.k], cot_v)
    staged_up = [
        bring(
            fc1_w.at[:, pl.ds(pl.multiple_of((i * seqs + g.s) * ff_part, 128), ff_part)],
            fc1_v.at[:, pl.ds(i * ff_part, ff_part)],
        )
        for i in range(shards)
    ]
    enter(g)
    tokens.start()
    for made in staged_qkv:
        made.wait()
    qkv_all.start()
    staged_small.wait()
    for d in range(1, shards):
        wires.send(small_v.at[g.k], small_v.at[g.k], smalls_at + d, g.s, (g.k + d) % shards, small_v.at[0])
    tokens.poll()
    staged_dense.wait()
    for made in staged_up:
        made.wait()
    staged_down.wait()
    staged_cot.wait()
    kept = [
        bring(dense_v, dense_out.at[g.k]), bring(fc1_v, fc1_out.at[g.k]), bring(fc2_v, fc2_out.at[g.k]),
        bring(cot_v, cot_out.at[:, g.s * shards + g.k]),
    ]
    dense_all.start()
    up_all.start()
    qkv_all.poll_z()
    for d in range(1, shards):
        wires.arrived(small_v.at[(g.k - d) % shards], smalls_at + d)
    qkv_all.poll_y()

    own = width // shards
    for j in range(shards):
        for row in range(2):
            vec_v[row : row + 1, j * own : (j + 1) * own] = small_v[j, row : row + 1, :own]
    vec_v[2:3, :] = jnp.zeros((1, vec_v.shape[1]), f32)
    per = 2 * width // shards
    for i in range(part // per):
        for row, half in ((0, 0), (2, 1)):
            j = (half * width + g.s * part) // per + i
            vec_v[2:3, row * part + i * per : row * part + (i + 1) * per] = small_v[j, 2:3, :per]

    qkv_all.finish()
    down_all.start()
    cots.start()
    kept += [bring(qkvw_v, qkvw_out), bring(small_v, small_out)]
    staged_x.wait()
    tokens.finish()
    kept.append(bring(x_v, x_out))

    @pl.loop(0, blocks)
    def _(b):
        x = x_v[b].astype(f32).reshape(block, width)
        xhat, _ = normalize(x)
        n1 = (xhat * vec_v[0:1, :width] + vec_v[1:2, :width]).astype(bf16)
        at = pl.ds(pl.multiple_of(b * block, block), block)
        n1_v[at, :] = n1
        for p in range(3):
            weight = qkvw_v[:, :, p * part : (p + 1) * part].reshape(width, part)
            out = jnp.dot(n1, weight, preferred_element_type=f32) + vec_v[2:3, p * part : (p + 1) * part]
            out = out.astype(bf16)
            for h in range(pairs):
                qkv_v[p * pairs + h, at, :] = out[:, h * 2 * HEAD : (h + 1) * 2 * HEAD]

    kept += [bring(n1_v, n1_out), bring(qkv_v, qkv_out)]
    dense_all.poll_z()
    lane_id = lax.broadcasted_iota(jnp.int32, (1, 2 * HEAD), 1)

    tile = min(256, block)

    def attend(h):
        q_ref, k_ref, v_ref = qkv_v.at[h], qkv_v.at[pairs + h], qkv_v.at[2 * pairs + h]
        at_o = g.s * pairs + h
        for b in range(blocks):
            end = (b + 1) * block
            for t in range(block // tile):
                at = pl.ds(b * block + t * tile, tile)
                q = q_ref[at, :] * jnp.asarray(HEAD**-0.5, bf16)
                ids_q = idc[at, :]
                both = None
                for j in range(2):
                    mine = (lane_id // HEAD) == j
                    qj = jnp.where(mine, q, jnp.zeros_like(q))
                    s = lax.dot_general(
                        qj, k_ref[:end, :], (((1,), (1,)), ((), ())), preferred_element_type=f32
                    )
                    s = s + slopes[h, j] * idr[:, :end]
                    if one_seq:
                        tail = attn_mask(s[:, b * block :], idr[:, b * block : end] <= ids_q)
                        s = jnp.concatenate([s[:, : b * block], tail], axis=1) if b else tail
                    else:
                        ids_k = idr[:, :end]
                        s = attn_mask(s, (ids_k <= ids_q) & (ids_k >= beginc[at, :]))
                    top = jnp.max(s, axis=1, keepdims=True)
                    e = jnp.exp(s - top)
                    total = jnp.sum(e, axis=1, keepdims=True)
                    o = jnp.dot(e.astype(bf16), v_ref[:end, :], preferred_element_type=f32) / total
                    both = o if both is None else jnp.where(mine, o, both)
                o_v[at_o, at, :] = both.astype(bf16)

    @pl.loop(0, pairs)
    def _(h):
        attend(h)

        @pl.when(h == 0)
        def _():
            dense_all.poll_y()

        @pl.when(h == 1)
        def _():
            up_all.poll_z()

        mine = o_v.at[g.s * pairs + h]
        wires.copy(mine, mine, heads_at + h, heads_at + h, 1 - g.s, g.k).start()

    up_all.poll_y()
    down_all.poll_z()
    cots.poll()
    down_all.poll_y()
    dense_all.finish()
    up_all.finish()
    down_all.finish()
    cots.finish()
    for h in range(pairs):
        other = o_v.at[(1 - g.s) * pairs + h]
        wires.arrived(other, heads_at + h)
    for h in range(pairs):
        mine = o_v.at[g.s * pairs + h]
        wires.copy(mine, mine, heads_at + h, heads_at + h, 1 - g.s, g.k).wait_send()
    kept.append(bring(o_v, o_out))
    wires.drain()
    for made in kept:
        made.wait()
    assert wires.used <= counts[0] and len(local) <= counts[1]


def forward_exchange(packed, packed_cot, qkv_w, small, dense_w, fc1_w, fc2_w, slopes, ids, begins, seqs, shards, one_seq):
    width, own = qkv_w.shape[0] * shards, qkv_w.shape[0]
    lanes = seqs * shards
    blocks = packed.shape[1]
    cap = blocks * lanes * ROWS
    part = width // seqs
    pairs = part // (2 * HEAD)
    ff = fc1_w.shape[1] // seqs
    ff_part = ff // shards
    counts = (320, 48)
    any_ = pl.BlockSpec(memory_space=pl.ANY)
    vmem = pl.BlockSpec(memory_space=pltpu.VMEM)
    smem = pl.BlockSpec(memory_space=pltpu.SMEM)
    x_shape = (blocks, lanes, ROWS, width)
    outs = [
        (x_shape, bf16), (x_shape, bf16), ((cap, width), bf16), ((shards, own, 3 * part), bf16), ((shards,) + small.shape, f32),
        ((shards, own, width), bf16), ((shards, own, ff), bf16), ((shards, ff_part, width), bf16), ((3 * pairs, cap, 2 * HEAD), bf16),
        ((seqs * pairs, cap, 2 * HEAD), bf16),
    ]
    scratch = [
        (x_shape, bf16), ((cap, width), bf16), ((shards, own, 3 * part), bf16), ((shards,) + small.shape, f32),
        ((own, width), bf16), ((own, ff), bf16), ((ff_part, width), bf16), ((blocks, ROWS, width), bf16), ((3 * pairs, cap, 2 * HEAD), bf16),
        ((seqs * pairs, cap, 2 * HEAD), bf16), ((8, max(width, 3 * part)), f32),
    ]
    return pl.pallas_call(
        functools.partial(forward_kernel, seqs, shards, counts, one_seq),
        in_specs=[any_] * 7 + [smem, vmem, vmem, vmem],
        out_specs=[any_] * len(outs),
        out_shape=[jax.ShapeDtypeStruct(s, d) for s, d in outs],
        scratch_shapes=[pltpu.VMEM(s, d) for s, d in scratch]
        + [pltpu.SemaphoreType.DMA((counts[0],)), pltpu.SemaphoreType.DMA((counts[0],)), pltpu.SemaphoreType.DMA((counts[1],))],
        compiler_params=pltpu.CompilerParams(collective_id=1, has_side_effects=True, vmem_limit_bytes=56 * 2**20),
        name="forward_exchange",
    )(packed, packed_cot, qkv_w, small, dense_w, fc1_w, fc2_w, slopes.reshape(pairs, 2), ids[:, None], ids[None, :], begins[:, None])


def layout_tables(lengths, lane_count, group_count, per_group):
    seq_rows = lengths // lane_count
    row_start = jnp.cumsum(seq_rows) - seq_rows
    slot_rows = seq_rows.reshape(group_count, per_group)
    slot_start = row_start.reshape(group_count, per_group)
    slot_before = jnp.cumsum(slot_rows, axis=1) - slot_rows
    return seq_rows, row_start, slot_rows, slot_start, slot_before


def per_device(
    tokens, cotangent, lengths, first_gain, first_bias, qkv_weight, qv_bias, dense_weight, dense_bias,
    second_gain, second_bias, fc1_weight, fc1_bias, fc2_weight, fc2_bias,
):
    shards, seqs = lax.axis_size("shard"), lax.axis_size("seq")
    lanes = shards * seqs
    slots, width = tokens.shape[1], tokens.shape[2]
    rows = slots // shards
    cap = slots * seqs
    per_group = lengths.shape[0] // shards
    hidden_units = fc1_weight.shape[1]
    me, group = lax.axis_index("seq"), lax.axis_index("shard")
    blocks = rows // ROWS
    heads = width // HEAD // seqs
    part = heads * HEAD
    ff_part = hidden_units // shards // seqs

    smalls = (first_gain, first_bias, qv_bias, dense_bias, second_gain, second_bias, fc1_bias, fc2_bias)
    small_width = -(-max(a.shape[0] for a in smalls) // 128) * 128
    small = jnp.stack([jnp.pad(a.astype(f32), (0, small_width - a.shape[0])) for a in smalls])

    seq_rows, row_start, slot_rows, slot_start, slot_before = layout_tables(lengths, lanes, shards, per_group)
    row_in = jnp.arange(rows, dtype=jnp.int32)[None, :, None]
    inside = ((row_in >= slot_before[:, None]) & (row_in < (slot_before + slot_rows)[:, None])).astype(jnp.int32)
    send_live = jnp.sum(inside, axis=2) > 0
    send_row = jnp.sum(inside * (slot_start[:, None] + row_in - slot_before[:, None]), axis=2).reshape(-1)

    def pack(source):
        return jnp.take(source, send_row, axis=0).reshape(shards, rows, width)

    def own_part(whole):
        return take(whole.reshape(blocks, seqs, -1, whole.shape[-1]), me, 1)

    place = jnp.arange(cap, dtype=jnp.int32)
    block_of, in_block = place // (ROWS * lanes), place % (ROWS * lanes)
    row_of = block_of * ROWS + in_block % ROWS
    ids = row_of * lanes + in_block // ROWS
    own_before, own_count = take(slot_before, group), take(slot_rows, group)
    holds = (row_of[:, None] >= own_before[None]) & (row_of[:, None] < (own_before + own_count)[None])
    begin_row = jnp.sum(jnp.where(holds, own_before[None], 0), axis=1)
    begins = jnp.where(jnp.any(holds, axis=1), begin_row * lanes, ids)
    ids, begins = ids.astype(f32), begins.astype(f32)
    head_ids = me * heads + jnp.arange(heads, dtype=jnp.int32)
    slopes = 2.0 ** (-8.0 * (head_ids.astype(f32) + 1.0) / HEADS)
    one_seq = per_group == 1

    packed_cot = pack(cotangent[0])
    packed_cot = jnp.where(send_live[:, :, None], packed_cot, jnp.zeros_like(packed_cot))
    blocked = (shards, blocks, ROWS, width)
    x_all, cot_all, normed_one, full_qkv, smalls, full_dense, full_up, full_down, qkv, mixed_all = forward_exchange(
        pack(tokens[0]).reshape(blocked), packed_cot.reshape(blocked),
        qkv_weight, small, dense_weight, fc1_weight, fc2_weight,
        slopes, ids, begins, seqs, shards, one_seq,
    )
    full_qkv = full_qkv.reshape(width, 3 * part)
    full_dense = full_dense.reshape(width, width)
    full_up = full_up.reshape(width, shards * ff_part)
    full_down = full_down.reshape(shards * ff_part, width)
    cot_low = cot_all.reshape(cap, width)
    cot_own = own_part(cot_low)
    unpack = lambda i, count: smalls[:, i, :count].reshape(-1)
    own_rows = width // shards
    gain_one, bias_dense, gain_two, bias_two, bias_down = (unpack(i, own_rows) for i in (0, 3, 4, 5, 7))
    bias_up = take(unpack(6, seqs * ff_part).reshape(shards, seqs, ff_part), me, 1).reshape(-1)
    x_own = own_part(x_all.reshape(cap, width))
    hidden = x_all.reshape(cap, width).astype(f32)
    mixed_all = mixed_all.transpose(1, 0, 2).reshape(cap, width)
    branch = jnp.dot(mixed_all, full_dense, preferred_element_type=f32) + bias_dense
    resid = hidden + branch
    xhat_two, _ = normalize(resid)
    normed_two = (xhat_two * gain_two + bias_two).astype(bf16)
    upper = jnp.dot(normed_two, full_up, preferred_element_type=f32) + bias_up
    activ = gelu_tanh(upper).astype(bf16)
    down = jnp.dot(activ, full_down, preferred_element_type=f32)
    resid_own = own_part(resid)
    down_own = seq_sum(down.reshape(blocks, seqs, -1, width), 1)
    block_out = (resid_own + down_own + bias_down).astype(bf16)

    grad_down = jnp.dot(activ.T, cot_low, preferred_element_type=f32).astype(bf16)
    grad_activ = jnp.dot(cot_low, full_down.T, preferred_element_type=f32)
    grad_upper = jax.vjp(gelu_tanh, upper)[1](grad_activ)[0].astype(bf16)
    grad_up = jnp.dot(normed_two.T, grad_upper, preferred_element_type=f32).astype(bf16)
    grad_bup = jnp.sum(grad_upper.astype(f32), axis=0)
    grad_normed = jnp.dot(grad_upper, full_up.T, preferred_element_type=f32)
    grad_normed = seq_sum(grad_normed.reshape(blocks, seqs, -1, width), 1).reshape(slots, width)
    cot_full = cot_own.reshape(slots, width).astype(f32)
    grad_bdown = jnp.sum(cot_full, axis=0)
    xhat_two, root_two = normalize(resid_own.reshape(slots, width))
    grad_gain_two = jnp.sum(grad_normed * xhat_two, axis=0)
    grad_bias_two = jnp.sum(grad_normed, axis=0)
    grad_resid = cot_full + norm_pull(grad_normed, gain_two, xhat_two, root_two)

    grad_branch = grad_resid.astype(bf16)
    grad_dense = jnp.dot(own_part(mixed_all).reshape(slots, width).T, grad_branch, preferred_element_type=f32).astype(bf16)
    grad_bdense = jnp.sum(grad_branch.astype(f32), axis=0)
    grad_mixed = jnp.dot(grad_branch, full_dense.T, preferred_element_type=f32).astype(bf16)
    got = seq_blocks(grad_mixed.reshape(blocks, -1, seqs, part), 2, bf16)
    if seqs == 2:
        grad_mixed = jnp.where(me == 0, jnp.stack(got, 1), jnp.stack(got[::-1], 1))
    else:
        grad_mixed = jnp.zeros((blocks, seqs) + got[0].shape[1:], bf16)
        for d, g in enumerate(got):
            grad_mixed = lax.dynamic_update_index_in_dim(grad_mixed, g, (me - d) % seqs, 1)
    grad_mixed = grad_mixed.reshape(cap, part)
    grad_proj = jnp.concatenate(
        attention_backward(qkv, grad_mixed, slopes, ids, begins, lanes, one_seq), axis=1
    )
    grad_qkv = jnp.dot(normed_one.T, grad_proj, preferred_element_type=f32).astype(bf16)
    proj_sums = jnp.sum(grad_proj.astype(f32), axis=0)
    grad_one = jnp.dot(grad_proj, full_qkv.T, preferred_element_type=f32)
    grad_one = seq_sum(grad_one.reshape(blocks, seqs, -1, width), 1).reshape(slots, width)
    xhat_one, root_one = normalize(x_own.reshape(slots, width).astype(f32))
    grad_gain_one = jnp.sum(grad_one * xhat_one, axis=0)
    grad_bias_one = jnp.sum(grad_one, axis=0)
    tokens_grad = (grad_resid + norm_pull(grad_one, gain_one, xhat_one, root_one)).astype(bf16)

    row_here = jnp.arange(slots, dtype=jnp.int32)[:, None]
    seq_in = ((row_here >= row_start[None]) & (row_here < (row_start + seq_rows)[None])).astype(jnp.int32)
    home = jnp.arange(lengths.shape[0], dtype=jnp.int32) // per_group
    fetch = jnp.sum(seq_in * (home[None] * rows + slot_before.reshape(-1)[None] + row_here - row_start[None]), axis=1)
    fetch_live = jnp.sum(seq_in, axis=1) > 0

    def to_stream(own):
        sent = own.reshape(blocks, shards, ROWS, width).transpose(1, 0, 2, 3).reshape(shards, rows, width)
        got = lax.all_to_all(sent, "shard", split_axis=0, concat_axis=0, tiled=True)
        taken = jnp.take(got.reshape(-1, width), fetch, axis=0)
        return jnp.where(fetch_live[:, None], taken, jnp.zeros_like(taken))[None]

    down_block = shard_reduce(grad_down.reshape(shards, ff_part, width), bf16)
    up_block = shard_reduce(grad_up.reshape(shards, -1, shards * ff_part), bf16)
    dense_block = shard_reduce(grad_dense.reshape(shards, -1, width), bf16)
    qkv_block = shard_reduce(grad_qkv.reshape(shards, -1, 3 * part), bf16)

    def spread(vector, index_shape):
        zero = jnp.zeros(index_shape, f32)
        return lax.dynamic_update_index_in_dim(zero, vector, me, 1)

    sums = proj_sums.reshape(3, part)
    qv = spread(jnp.stack([sums[0], sums[2]]), (2, seqs, part)).reshape(shards, -1)
    bup = spread(grad_bup.reshape(shards, ff_part), (shards, seqs, ff_part)).reshape(shards, -1)
    rest = (grad_gain_one, grad_bias_one, grad_bdense, grad_gain_two, grad_bias_two, grad_bdown)
    packed = jnp.concatenate([a.reshape(shards, -1) for a in rest] + [qv, bup], axis=1)
    packed = shard_reduce(packed, f32)
    packed = jnp.sum(seq_gather(packed, 0), axis=0)
    cuts, at = [], 0
    for a in [a.reshape(shards, -1) for a in rest] + [qv, bup]:
        cuts.append(packed[at : at + a.shape[1]])
        at += a.shape[1]
    g_gain_one, g_bias_one, g_bdense, g_gain_two, g_bias_two, g_bdown, g_qv, g_bup = cuts

    g_dense = jnp.sum(seq_gather(dense_block.astype(bf16), 0).astype(f32), axis=0)
    g_qkv = seq_gather(qkv_block.astype(bf16).reshape(-1, 3, part), 2).reshape(-1, 3 * width).astype(f32)
    g_up = seq_gather(up_block.astype(bf16).reshape(-1, shards, ff_part), 2).reshape(-1, hidden_units).astype(f32)
    g_down = seq_gather(down_block.astype(bf16), 0).reshape(-1, width).astype(f32)
    return (
        to_stream(block_out), to_stream(tokens_grad.reshape(blocks, -1, width)),
        g_gain_one, g_bias_one, g_qkv, g_qv, g_dense, g_bdense, g_gain_two, g_bias_two, g_up, g_bup, g_down, g_bdown,
    )


def per_device_any(
    tokens, cotangent, lengths, first_gain, first_bias, qkv_weight, qv_bias, dense_weight, dense_bias,
    second_gain, second_bias, fc1_weight, fc1_bias, fc2_weight, fc2_bias,
):
    shards, seqs = lax.axis_size("shard"), lax.axis_size("seq")
    lanes = shards * seqs
    slots, width = tokens.shape[1], tokens.shape[2]
    rows = slots // shards
    cap = slots * seqs
    per_group = lengths.shape[0] // shards
    hidden_units = fc1_weight.shape[1]
    me, group = lax.axis_index("seq"), lax.axis_index("shard")
    blocks = rows // ROWS
    heads = width // HEAD // seqs
    part = heads * HEAD
    ff_part = hidden_units // shards // seqs

    qkv_half = take(qkv_weight.reshape(-1, 3, seqs, part), me, 2).reshape(-1, 3 * part)
    fc1_half = take(fc1_weight.reshape(-1, shards, seqs, ff_part), me, 2).reshape(-1, shards * ff_part)
    fc2_half = take(fc2_weight.reshape(seqs, ff_part, width), me, 0)
    small = jnp.concatenate(
        [first_gain, first_bias, qv_bias, dense_bias, second_gain, second_bias, fc1_bias, fc2_bias]
    )
    small_rows = -(-small.shape[0] // (3 * part))
    small_rows += -small_rows % 16
    small = jnp.pad(small, (0, small_rows * 3 * part - small.shape[0])).reshape(small_rows, 3 * part)
    gather = lambda a: lax.all_gather(a, "shard", axis=0, tiled=False)
    qkv_small = gather(jnp.concatenate([qkv_half, small], axis=0))
    own_rows = qkv_half.shape[0]
    full_qkv = qkv_small[:, :own_rows].reshape(width, 3 * part)
    smalls = qkv_small[:, own_rows:].reshape(shards, -1).astype(f32)
    full_dense = gather(dense_weight).reshape(width, width)
    full_up = gather(fc1_half).reshape(width, shards * ff_part)
    full_down = gather(fc2_half).reshape(shards * ff_part, width)
    cuts, at = [], 0
    for a in (first_gain, first_bias, qv_bias, dense_bias, second_gain, second_bias, fc1_bias, fc2_bias):
        cuts.append(smalls[:, at : at + a.shape[0]].reshape(-1))
        at += a.shape[0]
    gain_one, bias_one, bias_qv, bias_dense, gain_two, bias_two, bias_up, bias_down = cuts
    bias_q, bias_v = (take(bias_qv[i * width : (i + 1) * width].reshape(seqs, part), me) for i in (0, 1))
    bias_all = jnp.concatenate([bias_q, jnp.zeros_like(bias_q), bias_v])
    bias_up = take(bias_up.reshape(shards, seqs, ff_part), me, 1).reshape(-1)

    seq_rows, row_start, slot_rows, slot_start, slot_before = layout_tables(lengths, lanes, shards, per_group)
    row_in = jnp.arange(rows, dtype=jnp.int32)[None, :, None]
    inside = ((row_in >= slot_before[:, None]) & (row_in < (slot_before + slot_rows)[:, None])).astype(jnp.int32)
    send_live = jnp.sum(inside, axis=2) > 0
    send_row = jnp.sum(inside * (slot_start[:, None] + row_in - slot_before[:, None]), axis=2).reshape(-1)

    def to_groups(source):
        packed = jnp.take(source, send_row, axis=0).reshape(shards, rows, width)
        packed = jnp.where(send_live[:, :, None], packed, jnp.zeros_like(packed))
        got = lax.all_to_all(packed, "shard", split_axis=0, concat_axis=0, tiled=True)
        own = got.reshape(shards, blocks, ROWS, width).transpose(1, 0, 2, 3).reshape(blocks, -1, width)
        return own, seq_gather(own, 1).reshape(cap, width)

    x_own, x_low = to_groups(tokens[0])
    cot_own, cot_low = to_groups(cotangent[0])

    def own_part(whole):
        return take(whole.reshape(blocks, seqs, -1, whole.shape[-1]), me, 1)

    place = jnp.arange(cap, dtype=jnp.int32)
    block_of, in_block = place // (ROWS * lanes), place % (ROWS * lanes)
    row_of = block_of * ROWS + in_block % ROWS
    ids = row_of * lanes + in_block // ROWS
    own_before, own_count = take(slot_before, group), take(slot_rows, group)
    holds = (row_of[:, None] >= own_before[None]) & (row_of[:, None] < (own_before + own_count)[None])
    begin_row = jnp.sum(jnp.where(holds, own_before[None], 0), axis=1)
    begins = jnp.where(jnp.any(holds, axis=1), begin_row * lanes, ids)
    ids, begins = ids.astype(f32), begins.astype(f32)
    head_ids = me * heads + jnp.arange(heads, dtype=jnp.int32)
    slopes = 2.0 ** (-8.0 * (head_ids.astype(f32) + 1.0) / HEADS)
    one_seq = per_group == 1

    hidden = x_low.astype(f32)
    xhat_one, _ = normalize(hidden)
    normed_one = (xhat_one * gain_one + bias_one).astype(bf16)
    qkv = (jnp.dot(normed_one, full_qkv, preferred_element_type=f32) + bias_all).astype(bf16)
    mixed = attention_forward(qkv, slopes, ids, begins, lanes, one_seq)
    mixed_all = seq_gather(mixed, 1).reshape(cap, width)
    branch = jnp.dot(mixed_all, full_dense, preferred_element_type=f32) + bias_dense
    resid = hidden + branch
    xhat_two, _ = normalize(resid)
    normed_two = (xhat_two * gain_two + bias_two).astype(bf16)
    upper = jnp.dot(normed_two, full_up, preferred_element_type=f32) + bias_up
    activ = gelu_tanh(upper).astype(bf16)
    down = jnp.dot(activ, full_down, preferred_element_type=f32)
    resid_own = own_part(resid)
    down_own = seq_sum(down.reshape(blocks, seqs, -1, width), 1)
    block_out = (resid_own + down_own + bias_down).astype(bf16)

    grad_down = jnp.dot(activ.T, cot_low, preferred_element_type=f32).astype(bf16)
    grad_activ = jnp.dot(cot_low, full_down.T, preferred_element_type=f32)
    grad_upper = jax.vjp(gelu_tanh, upper)[1](grad_activ)[0].astype(bf16)
    grad_up = jnp.dot(normed_two.T, grad_upper, preferred_element_type=f32).astype(bf16)
    grad_bup = jnp.sum(grad_upper.astype(f32), axis=0)
    grad_normed = jnp.dot(grad_upper, full_up.T, preferred_element_type=f32)
    grad_normed = seq_sum(grad_normed.reshape(blocks, seqs, -1, width), 1).reshape(slots, width)
    cot_full = cot_own.reshape(slots, width).astype(f32)
    grad_bdown = jnp.sum(cot_full, axis=0)
    xhat_two, root_two = normalize(resid_own.reshape(slots, width))
    grad_gain_two = jnp.sum(grad_normed * xhat_two, axis=0)
    grad_bias_two = jnp.sum(grad_normed, axis=0)
    grad_resid = cot_full + norm_pull(grad_normed, gain_two, xhat_two, root_two)

    grad_branch = grad_resid.astype(bf16)
    grad_dense = jnp.dot(own_part(mixed_all).reshape(slots, width).T, grad_branch, preferred_element_type=f32).astype(bf16)
    grad_bdense = jnp.sum(grad_branch.astype(f32), axis=0)
    grad_mixed = jnp.dot(grad_branch, full_dense.T, preferred_element_type=f32).astype(bf16)
    got = seq_blocks(grad_mixed.reshape(blocks, -1, seqs, part), 2, bf16)
    if seqs == 2:
        grad_mixed = jnp.where(me == 0, jnp.stack(got, 1), jnp.stack(got[::-1], 1))
    else:
        grad_mixed = jnp.zeros((blocks, seqs) + got[0].shape[1:], bf16)
        for d, g in enumerate(got):
            grad_mixed = lax.dynamic_update_index_in_dim(grad_mixed, g, (me - d) % seqs, 1)
    grad_mixed = grad_mixed.reshape(cap, part)
    planes = qkv.reshape(cap, -1, 2 * HEAD).transpose(1, 0, 2)
    grad_proj = jnp.concatenate(
        attention_backward(planes, grad_mixed, slopes, ids, begins, lanes, one_seq), axis=1
    )
    grad_qkv = jnp.dot(normed_one.T, grad_proj, preferred_element_type=f32).astype(bf16)
    proj_sums = jnp.sum(grad_proj.astype(f32), axis=0)
    grad_one = jnp.dot(grad_proj, full_qkv.T, preferred_element_type=f32)
    grad_one = seq_sum(grad_one.reshape(blocks, seqs, -1, width), 1).reshape(slots, width)
    xhat_one, root_one = normalize(x_own.reshape(slots, width).astype(f32))
    grad_gain_one = jnp.sum(grad_one * xhat_one, axis=0)
    grad_bias_one = jnp.sum(grad_one, axis=0)
    tokens_grad = (grad_resid + norm_pull(grad_one, gain_one, xhat_one, root_one)).astype(bf16)

    row_here = jnp.arange(slots, dtype=jnp.int32)[:, None]
    seq_in = ((row_here >= row_start[None]) & (row_here < (row_start + seq_rows)[None])).astype(jnp.int32)
    home = jnp.arange(lengths.shape[0], dtype=jnp.int32) // per_group
    fetch = jnp.sum(seq_in * (home[None] * rows + slot_before.reshape(-1)[None] + row_here - row_start[None]), axis=1)
    fetch_live = jnp.sum(seq_in, axis=1) > 0

    def to_stream(own):
        sent = own.reshape(blocks, shards, ROWS, width).transpose(1, 0, 2, 3).reshape(shards, rows, width)
        got = lax.all_to_all(sent, "shard", split_axis=0, concat_axis=0, tiled=True)
        taken = jnp.take(got.reshape(-1, width), fetch, axis=0)
        return jnp.where(fetch_live[:, None], taken, jnp.zeros_like(taken))[None]

    down_block = shard_reduce(grad_down.reshape(shards, ff_part, width), bf16)
    up_block = shard_reduce(grad_up.reshape(shards, -1, shards * ff_part), bf16)
    dense_block = shard_reduce(grad_dense.reshape(shards, -1, width), bf16)
    qkv_block = shard_reduce(grad_qkv.reshape(shards, -1, 3 * part), bf16)

    def spread(vector, index_shape):
        zero = jnp.zeros(index_shape, f32)
        return lax.dynamic_update_index_in_dim(zero, vector, me, 1)

    sums = proj_sums.reshape(3, part)
    qv = spread(jnp.stack([sums[0], sums[2]]), (2, seqs, part)).reshape(shards, -1)
    bup = spread(grad_bup.reshape(shards, ff_part), (shards, seqs, ff_part)).reshape(shards, -1)
    rest = (grad_gain_one, grad_bias_one, grad_bdense, grad_gain_two, grad_bias_two, grad_bdown)
    packed = jnp.concatenate([a.reshape(shards, -1) for a in rest] + [qv, bup], axis=1)
    packed = shard_reduce(packed, f32)
    packed = jnp.sum(seq_gather(packed, 0), axis=0)
    cuts, at = [], 0
    for a in [a.reshape(shards, -1) for a in rest] + [qv, bup]:
        cuts.append(packed[at : at + a.shape[1]])
        at += a.shape[1]
    g_gain_one, g_bias_one, g_bdense, g_gain_two, g_bias_two, g_bdown, g_qv, g_bup = cuts

    g_dense = jnp.sum(seq_gather(dense_block.astype(bf16), 0).astype(f32), axis=0)
    g_qkv = seq_gather(qkv_block.astype(bf16).reshape(-1, 3, part), 2).reshape(-1, 3 * width).astype(f32)
    g_up = seq_gather(up_block.astype(bf16).reshape(-1, shards, ff_part), 2).reshape(-1, hidden_units).astype(f32)
    g_down = seq_gather(down_block.astype(bf16), 0).reshape(-1, width).astype(f32)
    return (
        to_stream(block_out), to_stream(tokens_grad.reshape(blocks, -1, width)),
        g_gain_one, g_bias_one, g_qkv, g_qv, g_dense, g_bdense, g_gain_two, g_bias_two, g_up, g_bup, g_down, g_bdown,
    )


def solution(mesh):
    rows, vector, stream = P("shard", None), P("shard"), P(("seq", "shard"), None, None)
    params = (vector, vector, rows, vector, rows, vector, vector, vector, rows, vector, rows, vector)
    fused = mesh.shape["seq"] == 2 and shard_factors(mesh.shape["shard"])[0] == 4
    return jax.shard_map(
        per_device if fused else per_device_any, mesh=mesh, in_specs=(stream, stream, P()) + params, out_specs=(stream, stream) + params, check_vma=False
    )
```

```python
import functools

import jax
import jax.numpy as jnp
from jax import lax
from jax.experimental import pallas as pl
from jax.experimental.pallas import tpu as pltpu
from jax.sharding import PartitionSpec as P

HEADS = 16
HEAD = 64
ROWS = 8

epsilon = 1e-05
masked_score = -1e30
f32 = jnp.float32
bf16 = jnp.bfloat16


def gelu_tanh(values):
    return (
        0.5
        * values
        * (1.0 + jnp.tanh(0.7978845608028654 * (values + 0.044715 * values * values * values)))
    )


def normalize(hidden):
    center = hidden - jnp.mean(hidden, axis=-1, keepdims=True)
    spread = jnp.mean(center * center, axis=-1, keepdims=True)
    root = lax.rsqrt(spread + epsilon)
    return center * root, root


def norm_pull(grad, gain, xhat, root):
    scaled = grad * gain
    return root * (
        scaled
        - jnp.mean(scaled, axis=-1, keepdims=True)
        - xhat * jnp.mean(scaled * xhat, axis=-1, keepdims=True)
    )


def slot_ids(first, count, lanes):
    place = first + lax.broadcasted_iota(jnp.int32, (count, 1), 0)
    block, inside = place // (ROWS * lanes), place % (ROWS * lanes)
    return (block * ROWS + inside % ROWS) * lanes + inside // ROWS


def attn_mask(scored, allowed):
    return jnp.where(allowed, scored, masked_score)


def attn_fwd_kernel(lanes, tile, one_seq, slope_ref, idc_ref, idr_ref, beginc_ref, q_ref, k_ref, v_ref, o_ref):
    tokens = q_ref.shape[0]
    block = ROWS * lanes
    lane_id = lax.broadcasted_iota(jnp.int32, (1, 2 * HEAD), 1)
    for b in range(tokens // block):
        end = (b + 1) * block

        def step(t, _):
            at = pl.ds(pl.multiple_of(b * block + t * tile, tile), tile)
            q = q_ref[at, :] * jnp.asarray(HEAD**-0.5, bf16)
            ids_q = idc_ref[at, :]
            both = None
            for j in range(2):
                mine = (lane_id // HEAD) == j
                qj = jnp.where(mine, q, jnp.zeros_like(q))
                s = lax.dot_general(
                    qj, k_ref[:end, :], (((1,), (1,)), ((), ())), preferred_element_type=f32
                )
                s = s + slope_ref[0, 0, j] * idr_ref[:, :end]
                if one_seq:
                    own = s[:, b * block :]
                    own = attn_mask(own, idr_ref[:, b * block : end] <= ids_q)
                    s = jnp.concatenate([s[:, : b * block], own], axis=1) if b else own
                else:
                    ids_k = idr_ref[:, :end]
                    s = attn_mask(s, (ids_k <= ids_q) & (ids_k >= beginc_ref[at, :]))
                top = jnp.max(s, axis=1, keepdims=True)
                e = jnp.exp(s - top)
                total = jnp.sum(e, axis=1, keepdims=True)
                o = jnp.dot(e.astype(bf16), v_ref[:end, :], preferred_element_type=f32) / total
                both = o if both is None else jnp.where(mine, o, both)
            o_ref[at, :] = both.astype(bf16)
            return 0

        lax.fori_loop(0, block // tile, step, 0)


def attn_bwd_kernel(
    lanes, tile, one_seq, slope_ref, idc_ref, idr_ref, beginr_ref, q_ref, k_ref, v_ref, do_ref,
    dq_ref, dk_ref, dv_ref, dk_acc, dv_acc, bias_acc,
):
    tokens = q_ref.shape[0]
    block = ROWS * lanes
    lane_id = lax.broadcasted_iota(jnp.int32, (1, 2 * HEAD), 1)
    dk_acc[...] = jnp.zeros_like(dk_acc)
    dv_acc[...] = jnp.zeros_like(dv_acc)
    for j in range(2):
        bias_acc[j] = jnp.broadcast_to(slope_ref[0, 0, j] * idc_ref[...], (tokens, tile))
    for b in range(tokens // block):
        end = (b + 1) * block

        def step(t, _):
            at = pl.ds(pl.multiple_of(b * block + t * tile, tile), tile)
            q = q_ref[at, :] * jnp.asarray(HEAD**-0.5, bf16)
            do = do_ref[at, :]
            ids_q = idr_ref[:, at]
            both = None
            for j in range(2):
                mine = (lane_id // HEAD) == j
                qj = jnp.where(mine, q, jnp.zeros_like(q))
                doj = jnp.where(mine, do, jnp.zeros_like(do))
                s = lax.dot_general(
                    k_ref[:end, :], qj, (((1,), (1,)), ((), ())), preferred_element_type=f32
                )
                s = s + bias_acc[j, :end, :]
                if one_seq:
                    own = s[b * block :, :]
                    own = attn_mask(own, idc_ref[b * block : end, :] <= ids_q)
                    s = jnp.concatenate([s[: b * block, :], own], axis=0) if b else own
                else:
                    ids_k = idc_ref[:end, :]
                    s = attn_mask(s, (ids_k <= ids_q) & (ids_k >= beginr_ref[:, at]))
                top = jnp.max(s, axis=0, keepdims=True)
                e = jnp.exp(s - top)
                probs = e * (1.0 / jnp.sum(e, axis=0, keepdims=True))
                dv_acc[:end, :] += jnp.dot(probs.astype(bf16), doj, preferred_element_type=f32)
                dp = lax.dot_general(
                    v_ref[:end, :], doj, (((1,), (1,)), ((), ())), preferred_element_type=f32
                )
                inner = jnp.sum(probs * dp, axis=0, keepdims=True)
                ds = (probs * (dp - inner)).astype(bf16)
                dk_acc[:end, :] += jnp.dot(ds, qj, preferred_element_type=f32)
                dq = lax.dot_general(
                    ds, k_ref[:end, :], (((0,), (0,)), ((), ())), preferred_element_type=f32
                )
                both = dq if both is None else jnp.where(mine, dq, both)
            dq_ref[at, :] = (both * (HEAD**-0.5)).astype(bf16)
            return 0

        lax.fori_loop(0, block // tile, step, 0)
    dk_ref[...] = dk_acc[...].astype(bf16)
    dv_ref[...] = dv_acc[...].astype(bf16)


def attn_shape(tokens, width, lanes):
    pairs = width // (2 * HEAD)
    tile = min(256, ROWS * lanes)
    return pairs, tile


def attention_forward(qkv, slopes, ids, begins, lanes, one_seq):
    tokens, width = qkv.shape[0], qkv.shape[1] // 3
    pairs, tile = attn_shape(tokens, width, lanes)
    column = lambda part: pl.BlockSpec((tokens, 2 * HEAD), lambda h, part=part: (0, part * pairs + h))
    whole = lambda a: pl.BlockSpec(a.shape, lambda h: (0, 0))
    idc, idr, beginc = ids[:, None], ids[None, :], begins[:, None]
    half = tokens * tokens * 5 // 8
    return pl.pallas_call(
        functools.partial(attn_fwd_kernel, lanes, tile, one_seq),
        grid=(pairs,),
        in_specs=[
            pl.BlockSpec((1, 1, 2), lambda h: (h, 0, 0), memory_space=pltpu.SMEM),
            whole(idc), whole(idr), whole(beginc), column(0), column(1), column(2),
        ],
        out_specs=pl.BlockSpec((tokens, 2 * HEAD), lambda h: (0, h)),
        out_shape=jax.ShapeDtypeStruct((tokens, width), bf16),
        compiler_params=pltpu.CompilerParams(vmem_limit_bytes=48 * 2**20),
        cost_estimate=pl.CostEstimate(
            flops=8 * pairs * half * HEAD * 2, transcendentals=2 * pairs * half, bytes_accessed=8 * tokens * width
        ),
        name="attention_forward",
    )(slopes.reshape(pairs, 1, 2), idc, idr, beginc, qkv, qkv, qkv)


def attention_backward(qkv, grad_out, slopes, ids, begins, lanes, one_seq):
    tokens, width = grad_out.shape
    pairs, tile = attn_shape(tokens, width, lanes)
    column = lambda part: pl.BlockSpec((tokens, 2 * HEAD), lambda h, part=part: (0, part * pairs + h))
    whole = lambda a: pl.BlockSpec(a.shape, lambda h: (0, 0))
    idc, idr, beginr = ids[:, None], ids[None, :], begins[None, :]
    plane = lambda part: pl.BlockSpec((None, tokens, 2 * HEAD), lambda h, part=part: (part * pairs + h, 0, 0))
    out = jax.ShapeDtypeStruct((tokens, width), bf16)
    half = tokens * tokens * 5 // 8
    return pl.pallas_call(
        functools.partial(attn_bwd_kernel, lanes, tile, one_seq),
        grid=(pairs,),
        in_specs=[
            pl.BlockSpec((1, 1, 2), lambda h: (h, 0, 0), memory_space=pltpu.SMEM),
            whole(idc), whole(idr), whole(beginr), plane(0), plane(1), plane(2), column(0),
        ],
        out_specs=[column(0)] * 3,
        out_shape=[out] * 3,
        scratch_shapes=[
            pltpu.VMEM((tokens, 2 * HEAD), f32), pltpu.VMEM((tokens, 2 * HEAD), f32), pltpu.VMEM((2, tokens, tile), f32),
        ],
        compiler_params=pltpu.CompilerParams(vmem_limit_bytes=56 * 2**20),
        cost_estimate=pl.CostEstimate(
            flops=20 * pairs * half * HEAD * 2, transcendentals=2 * pairs * half, bytes_accessed=14 * tokens * width
        ),
        name="attention_backward",
    )(slopes.reshape(pairs, 1, 2), idc, idr, beginr, qkv, qkv, qkv, grad_out)


def take(blocks, index, axis=0):
    return lax.dynamic_index_in_dim(blocks, index, axis, keepdims=False)


def seq_gather(block, axis):
    n, me = lax.axis_size("seq"), lax.axis_index("seq")
    shape = block.shape[:axis] + (n,) + block.shape[axis:]
    if n == 2:
        peer = lax.ppermute(block, "seq", [(0, 1), (1, 0)])
        return jnp.where(me == 0, jnp.stack([block, peer], axis), jnp.stack([peer, block], axis))
    whole = lax.dynamic_update_index_in_dim(jnp.zeros(shape, block.dtype), block, me, axis)
    for d in range(1, n):
        got = lax.ppermute(block, "seq", [(i, (i + d) % n) for i in range(n)])
        whole = lax.dynamic_update_index_in_dim(whole, got, (me - d) % n, axis)
    return whole


def seq_blocks(whole, axis, dtype):
    n, me = lax.axis_size("seq"), lax.axis_index("seq")
    got = [take(whole, me, axis)]
    for d in range(1, n):
        sent = take(whole, (me + d) % n, axis).astype(dtype)
        got.append(lax.ppermute(sent, "seq", [(i, (i + d) % n) for i in range(n)]))
    return got


def seq_sum(whole, axis, dtype=bf16):
    got = seq_blocks(whole, axis, dtype)
    return sum((g.astype(f32) for g in got[1:]), got[0].astype(f32))


def shard_factors(n):
    nc = 2 if n % 2 == 0 else 1
    nz = 4 if n % (4 * nc) == 0 else 1
    return nz, n // (nz * nc), nc


def shard_reduce(blocks, dtype):
    n, me = lax.axis_size("shard"), lax.axis_index("shard")
    sizes = shard_factors(n)
    blocks = blocks.reshape(sizes + blocks.shape[1:])
    place = (me // (sizes[1] * sizes[2]), me // sizes[2] % sizes[1], me % sizes[2])
    strides = (sizes[1] * sizes[2], sizes[2], 1)
    for axis in (2, 1, 0):
        size, mine, stride = sizes[axis], place[axis], strides[axis]
        total = take(blocks, mine, axis).astype(f32)
        for d in range(1, size):
            sent = take(blocks, (mine + d) % size, axis).astype(dtype)
            pairs = [
                (i, i - (i // stride % size) * stride + ((i // stride % size + d) % size) * stride)
                for i in range(n)
            ]
            total = total + lax.ppermute(sent, "shard", pairs).astype(f32)
        blocks = total if axis == 0 else total.astype(dtype)
    return blocks


MESH = pl.DeviceIdType.MESH


class Geometry:
    def __init__(self, seqs, shards):
        self.seqs, self.shards = seqs, shards
        self.sizes = shard_factors(shards)
        self.s, self.k = lax.axis_index("seq"), lax.axis_index("shard")
        nz, ny, nc = self.sizes
        self.z, self.y, self.c = self.k // (ny * nc), self.k // nc % ny, self.k % nc
        self.inner = (self.z + 1) // 2 % 2
        high = self.z // 2
        self.line = (self.z, self.z + 1 - 2 * (self.z % 2), 2 - high, 3 - 3 * high)

    def slot(self, i, dy, dc):
        nz, ny, nc = self.sizes
        return (self.line[i] * ny + (self.y + dy) % ny) * nc + (self.c + dc) % nc


class Wires:
    def __init__(self, geometry, send_sems, recv_sems):
        self.g, self.send_sems, self.recv_sems = geometry, send_sems, recv_sems
        self.sends, self.used = [], 0

    def block(self, count):
        first = self.used
        self.used += count
        return first

    def copy(self, src, dst, sent, got, s, k):
        return pltpu.make_async_remote_copy(
            src_ref=src, dst_ref=dst, send_sem=self.send_sems.at[sent], recv_sem=self.recv_sems.at[got],
            device_id={"seq": s, "shard": k}, device_id_type=MESH,
        )

    def send_as(self, src, dst, sent, got, s, k, like):
        self.copy(src, dst, sent, got, s, k).start()
        self.sends.append((like, sent))

    def send(self, src, dst, index, s, k, like):
        self.send_as(src, dst, index, index, s, k, like)

    def arrived(self, dst, index):
        self.copy(dst, dst, index, index, 1 - self.g.s, self.g.k).wait_recv()

    def drain(self):
        for like, index in self.sends:
            self.copy(like, like, index, index, 1 - self.g.s, self.g.k).wait_send()
        self.sends = []


def enter(geometry):
    g = geometry
    barrier = pltpu.get_barrier_semaphore()
    for d in range(1, g.shards):
        pl.semaphore_signal(
            barrier, inc=1, device_id={"seq": g.s, "shard": (g.k + d) % g.shards}, device_id_type=MESH
        )
    pl.semaphore_signal(barrier, inc=1, device_id={"seq": 1 - g.s, "shard": g.k}, device_id_type=MESH)
    pl.semaphore_wait(barrier, g.shards)


class Gather:
    def __init__(self, wires, own, out):
        self.w, self.g, self.own, self.out = wires, wires.g, own, out
        nz, ny, nc = self.g.sizes
        self.z0 = wires.block(nz)
        self.on0 = wires.block(nz)
        self.y0 = wires.block(nz * ny)
        self.c0 = wires.block(nz * ny * nc)

    def on_y(self, i, src):
        g = self.g
        for dy in range(1, g.sizes[1]):
            self.w.send(src, self.out.at[g.slot(i, 0, 0)], self.y0 + i * g.sizes[1] + dy, g.s, g.slot(0, dy, 0), self.own)

    def on_core(self, i, dy, src):
        g = self.g
        for dc in range(1, g.sizes[2]):
            index = self.c0 + (i * g.sizes[1] + dy) * g.sizes[2] + dc
            self.w.send(src, self.out.at[g.slot(i, -dy, 0)], index, g.s, g.slot(0, 0, dc), self.own)

    def start(self):
        g = self.g
        here = self.out.at[g.k]
        self.w.send_as(self.own, here, self.z0 + 2, self.z0 + 3 - g.inner, g.s, g.slot(2, 0, 0), self.own)
        self.w.send(self.own, here, self.z0 + 1, g.s, g.slot(1, 0, 0), self.own)
        self.on_y(0, self.own)
        self.on_core(0, 0, self.own)

    def poll_z(self):
        g = self.g
        for i in (1, 2, 3):
            at = self.out.at[g.slot(i, 0, 0)]
            self.w.arrived(at, self.z0 + i)
            if i > 1:

                @pl.when(g.inner == 1)
                def _(at=at, i=i):
                    self.w.copy(at, at, self.on0 + i, self.z0 + i, g.s, g.slot(1, 0, 0)).start()

            self.on_y(i, at)
            self.on_core(i, 0, at)

    def poll_y(self):
        g = self.g
        for i in range(g.sizes[0]):
            for dy in range(1, g.sizes[1]):
                at = self.out.at[g.slot(i, -dy, 0)]
                self.w.arrived(at, self.y0 + i * g.sizes[1] + dy)
                self.on_core(i, dy, at)

    def finish(self):
        g = self.g
        for i in range(g.sizes[0]):
            for dy in range(g.sizes[1]):
                for dc in range(1, g.sizes[2]):
                    at = self.out.at[g.slot(i, -dy, -dc)]
                    self.w.arrived(at, self.c0 + (i * g.sizes[1] + dy) * g.sizes[2] + dc)

        @pl.when(g.inner == 1)
        def _():
            for i in (2, 3):
                self.w.copy(self.own, self.own, self.on0 + i, self.z0 + i, g.s, g.k).wait_send()


class Tokens:
    def __init__(self, wires, packed, out):
        self.w, self.g, self.packed, self.out = wires, wires.g, packed, out
        self.a0, self.f0 = wires.block(self.g.shards), wires.block(self.g.shards)

    def lane(self, s, k):
        return self.out.at[:, s * self.g.shards + k]

    def start(self):
        g = self.g
        for d in range(1, g.shards):
            to = (g.k + d) % g.shards
            self.w.send(self.packed.at[to], self.lane(g.s, g.k), self.a0 + d, g.s, to, self.packed.at[0])
        self.w.send(self.packed.at[g.k], self.lane(g.s, g.k), self.f0, 1 - g.s, g.k, self.packed.at[0])

    def poll(self):
        g = self.g
        for d in range(1, g.shards):
            at = self.lane(g.s, (g.k - d) % g.shards)
            self.w.arrived(at, self.a0 + d)
            self.w.send(at, at, self.f0 + d, 1 - g.s, g.k, self.packed.at[0])

    def finish(self):
        g = self.g
        for d in range(g.shards):
            self.w.arrived(self.lane(1 - g.s, (g.k - d) % g.shards), self.f0 + d)


def forward_kernel(
    seqs, shards, counts, one_seq,
    packed, packed_cot, qkv_w, small, dense_w, fc1_w, fc2_w, slopes, idc, idr, beginc,
    x_out, cot_out, n1_out, qkvw_out, small_out, dense_out, fc1_out, fc2_out, qkv_out, o_out,
    x_v, n1_v, qkvw_v, small_v, dense_v, fc1_v, fc2_v, cot_v, qkv_v, o_v, vec_v,
    send_sems, recv_sems, copy_sems,
):
    g = Geometry(seqs, shards)
    wires = Wires(g, send_sems, recv_sems)
    lanes = seqs * shards
    width = n1_v.shape[1]
    pairs = o_v.shape[0] // seqs
    part = pairs * 2 * HEAD
    ff_part = fc1_v.shape[1] // shards
    block = ROWS * lanes
    blocks = x_v.shape[0]

    local = []

    def bring(src, dst):
        made = pltpu.make_async_copy(src, dst, copy_sems.at[len(local)])
        made.start()
        local.append(made)
        return made

    tokens = Tokens(wires, packed, x_v)
    cots = Tokens(wires, packed_cot, cot_out)
    smalls_at = wires.block(shards)
    qkv_all = Gather(wires, qkvw_v.at[g.k], qkvw_v)
    dense_all = Gather(wires, dense_v, dense_out)
    up_all = Gather(wires, fc1_v, fc1_out)
    down_all = Gather(wires, fc2_v, fc2_out)
    heads_at = wires.block(pairs)

    staged_qkv = [
        bring(
            qkv_w.at[:, pl.ds(pl.multiple_of(p * width + g.s * part, 128), part)],
            qkvw_v.at[g.k, :, pl.ds(p * part, part)],
        )
        for p in range(3)
    ]
    staged_x = bring(packed.at[g.k], x_v.at[:, g.s * shards + g.k])
    staged_small = bring(small, small_v.at[g.k])
    staged_dense = bring(dense_w, dense_v)
    staged_down = bring(fc2_w.at[pl.ds(pl.multiple_of(g.s * ff_part, 8), ff_part), :], fc2_v)
    staged_cot = bring(packed_cot.at[g.k], cot_v)
    staged_up = [
        bring(
            fc1_w.at[:, pl.ds(pl.multiple_of((i * seqs + g.s) * ff_part, 128), ff_part)],
            fc1_v.at[:, pl.ds(i * ff_part, ff_part)],
        )
        for i in range(shards)
    ]
    enter(g)
    tokens.start()
    for made in staged_qkv:
        made.wait()
    qkv_all.start()
    staged_small.wait()
    for d in range(1, shards):
        wires.send(small_v.at[g.k], small_v.at[g.k], smalls_at + d, g.s, (g.k + d) % shards, small_v.at[0])
    tokens.poll()
    staged_dense.wait()
    for made in staged_up:
        made.wait()
    staged_down.wait()
    staged_cot.wait()
    kept = [
        bring(dense_v, dense_out.at[g.k]), bring(fc1_v, fc1_out.at[g.k]), bring(fc2_v, fc2_out.at[g.k]),
        bring(cot_v, cot_out.at[:, g.s * shards + g.k]),
    ]
    dense_all.start()
    up_all.start()
    qkv_all.poll_z()
    for d in range(1, shards):
        wires.arrived(small_v.at[(g.k - d) % shards], smalls_at + d)
    qkv_all.poll_y()

    own = width // shards
    for j in range(shards):
        for row in range(2):
            vec_v[row : row + 1, j * own : (j + 1) * own] = small_v[j, row : row + 1, :own]
    vec_v[2:3, :] = jnp.zeros((1, vec_v.shape[1]), f32)
    per = 2 * width // shards
    for i in range(part // per):
        for row, half in ((0, 0), (2, 1)):
            j = (half * width + g.s * part) // per + i
            vec_v[2:3, row * part + i * per : row * part + (i + 1) * per] = small_v[j, 2:3, :per]

    qkv_all.finish()
    down_all.start()
    cots.start()
    kept += [bring(qkvw_v, qkvw_out), bring(small_v, small_out)]
    staged_x.wait()
    tokens.finish()
    kept.append(bring(x_v, x_out))

    @pl.loop(0, blocks)
    def _(b):
        x = x_v[b].astype(f32).reshape(block, width)
        xhat, _ = normalize(x)
        n1 = (xhat * vec_v[0:1, :width] + vec_v[1:2, :width]).astype(bf16)
        at = pl.ds(pl.multiple_of(b * block, block), block)
        n1_v[at, :] = n1
        for p in range(3):
            weight = qkvw_v[:, :, p * part : (p + 1) * part].reshape(width, part)
            out = jnp.dot(n1, weight, preferred_element_type=f32) + vec_v[2:3, p * part : (p + 1) * part]
            out = out.astype(bf16)
            for h in range(pairs):
                qkv_v[p * pairs + h, at, :] = out[:, h * 2 * HEAD : (h + 1) * 2 * HEAD]

    kept += [bring(n1_v, n1_out), bring(qkv_v, qkv_out)]
    dense_all.poll_z()
    lane_id = lax.broadcasted_iota(jnp.int32, (1, 2 * HEAD), 1)

    tile = min(256, block)

    def attend(h):
        q_ref, k_ref, v_ref = qkv_v.at[h], qkv_v.at[pairs + h], qkv_v.at[2 * pairs + h]
        at_o = g.s * pairs + h
        for b in range(blocks):
            end = (b + 1) * block
            for t in range(block // tile):
                at = pl.ds(b * block + t * tile, tile)
                q = q_ref[at, :] * jnp.asarray(HEAD**-0.5, bf16)
                ids_q = idc[at, :]
                both = None
                for j in range(2):
                    mine = (lane_id // HEAD) == j
                    qj = jnp.where(mine, q, jnp.zeros_like(q))
                    s = lax.dot_general(
                        qj, k_ref[:end, :], (((1,), (1,)), ((), ())), preferred_element_type=f32
                    )
                    s = s + slopes[h, j] * idr[:, :end]
                    if one_seq:
                        tail = attn_mask(s[:, b * block :], idr[:, b * block : end] <= ids_q)
                        s = jnp.concatenate([s[:, : b * block], tail], axis=1) if b else tail
                    else:
                        ids_k = idr[:, :end]
                        s = attn_mask(s, (ids_k <= ids_q) & (ids_k >= beginc[at, :]))
                    top = jnp.max(s, axis=1, keepdims=True)
                    e = jnp.exp(s - top)
                    total = jnp.sum(e, axis=1, keepdims=True)
                    o = jnp.dot(e.astype(bf16), v_ref[:end, :], preferred_element_type=f32) / total
                    both = o if both is None else jnp.where(mine, o, both)
                o_v[at_o, at, :] = both.astype(bf16)

    @pl.loop(0, pairs)
    def _(h):
        attend(h)

        @pl.when(h == 0)
        def _():
            dense_all.poll_y()

        @pl.when(h == 1)
        def _():
            up_all.poll_z()

        mine = o_v.at[g.s * pairs + h]
        wires.copy(mine, mine, heads_at + h, heads_at + h, 1 - g.s, g.k).start()

    up_all.poll_y()
    down_all.poll_z()
    cots.poll()
    down_all.poll_y()
    dense_all.finish()
    up_all.finish()
    down_all.finish()
    cots.finish()
    for h in range(pairs):
        other = o_v.at[(1 - g.s) * pairs + h]
        wires.arrived(other, heads_at + h)
    for h in range(pairs):
        mine = o_v.at[g.s * pairs + h]
        wires.copy(mine, mine, heads_at + h, heads_at + h, 1 - g.s, g.k).wait_send()
    kept.append(bring(o_v, o_out))
    wires.drain()
    for made in kept:
        made.wait()
    assert wires.used <= counts[0] and len(local) <= counts[1]


def forward_exchange(packed, packed_cot, qkv_w, small, dense_w, fc1_w, fc2_w, slopes, ids, begins, seqs, shards, one_seq):
    width, own = qkv_w.shape[0] * shards, qkv_w.shape[0]
    lanes = seqs * shards
    blocks = packed.shape[1]
    cap = blocks * lanes * ROWS
    part = width // seqs
    pairs = part // (2 * HEAD)
    ff = fc1_w.shape[1] // seqs
    ff_part = ff // shards
    counts = (320, 48)
    any_ = pl.BlockSpec(memory_space=pl.ANY)
    vmem = pl.BlockSpec(memory_space=pltpu.VMEM)
    smem = pl.BlockSpec(memory_space=pltpu.SMEM)
    x_shape = (blocks, lanes, ROWS, width)
    outs = [
        (x_shape, bf16), (x_shape, bf16), ((cap, width), bf16), ((shards, own, 3 * part), bf16), ((shards,) + small.shape, f32),
        ((shards, own, width), bf16), ((shards, own, ff), bf16), ((shards, ff_part, width), bf16), ((3 * pairs, cap, 2 * HEAD), bf16),
        ((seqs * pairs, cap, 2 * HEAD), bf16),
    ]
    scratch = [
        (x_shape, bf16), ((cap, width), bf16), ((shards, own, 3 * part), bf16), ((shards,) + small.shape, f32),
        ((own, width), bf16), ((own, ff), bf16), ((ff_part, width), bf16), ((blocks, ROWS, width), bf16), ((3 * pairs, cap, 2 * HEAD), bf16),
        ((seqs * pairs, cap, 2 * HEAD), bf16), ((8, max(width, 3 * part)), f32),
    ]
    return pl.pallas_call(
        functools.partial(forward_kernel, seqs, shards, counts, one_seq),
        in_specs=[any_] * 7 + [smem, vmem, vmem, vmem],
        out_specs=[any_] * len(outs),
        out_shape=[jax.ShapeDtypeStruct(s, d) for s, d in outs],
        scratch_shapes=[pltpu.VMEM(s, d) for s, d in scratch]
        + [pltpu.SemaphoreType.DMA((counts[0],)), pltpu.SemaphoreType.DMA((counts[0],)), pltpu.SemaphoreType.DMA((counts[1],))],
        compiler_params=pltpu.CompilerParams(collective_id=1, has_side_effects=True, vmem_limit_bytes=56 * 2**20),
        name="forward_exchange",
    )(packed, packed_cot, qkv_w, small, dense_w, fc1_w, fc2_w, slopes.reshape(pairs, 2), ids[:, None], ids[None, :], begins[:, None])


class Scatter:
    def __init__(self, wires, full, own, bufs):
        self.w, self.g, self.full, self.own = wires, wires.g, full, own
        self.rc, self.ry, self.rz, self.fin = bufs
        self.at = wires.block(8)

    def add(self, count, into, other):
        @pl.loop(0, count)
        def _(i):
            a, b = into(i), other(i)
            a[...] = (a[...].astype(f32) + b[...].astype(f32)).astype(bf16)

    def core_send(self):
        g = self.g
        self.w.send(self.full.at[:, :, 1 - g.c], self.rc, self.at, g.s, g.slot(0, 0, 1), self.rc)

    def core_done(self):
        g = self.g
        self.w.arrived(self.rc, self.at)
        self.add(8, lambda i: self.rc.at[i // 2, i % 2], lambda i: self.own(i // 2, i % 2))
        self.w.send(self.rc.at[:, 1 - g.y], self.ry, self.at + 1, g.s, g.slot(0, 1, 0), self.ry)

    def y_done(self):
        g = self.g
        self.w.arrived(self.ry, self.at + 1)
        self.add(4, lambda i: self.ry.at[i], lambda i: self.rc.at[i, g.y])
        partner = g.slot(1, 0, 0)
        self.w.send(self.ry.at[g.line[1]], self.rz.at[0], self.at + 2, g.s, partner, self.rz.at[0])

        @pl.when(g.inner == 0)
        def _():
            for i in (2, 3):
                self.w.copy(self.ry.at[g.line[i]], self.rz.at[i], self.at + 1 + i, self.at + 1 + i, g.s, partner).start()

    def z_done(self):
        g = self.g

        @pl.when(g.inner == 1)
        def _():
            for i in (2, 3):
                self.w.arrived(self.rz.at[i], self.at + 1 + i)
                a = self.rz.at[i]
                a[...] = (a[...].astype(f32) + self.ry[g.line[i]].astype(f32)).astype(bf16)
                self.w.copy(a, self.rz.at[1], self.at + 1 + i, self.at + 5, g.s, g.slot(i, 0, 0)).start()

    def final(self):
        g = self.g
        self.w.arrived(self.rz.at[0], self.at + 2)
        self.w.arrived(self.rz.at[1], self.at + 5)
        total = self.ry[g.z].astype(f32) + self.rz[0].astype(f32) + self.rz[1].astype(f32)
        self.fin[0] = total.astype(bf16)
        self.w.send(self.fin.at[0], self.fin.at[1], self.at + 6, 1 - g.s, g.k, self.fin.at[0])

    def done(self):
        self.w.arrived(self.fin.at[1], self.at + 6)
        for i in (2, 3):
            self.w.copy(self.fin.at[0], self.fin.at[0], self.at + 1 + i, self.at + 1 + i, self.g.s, self.g.k).wait_send()


class Back:
    def __init__(self, wires, src, dst, pieces):
        self.w, self.g, self.src, self.dst, self.pieces = wires, wires.g, src, dst, pieces
        self.at = wires.block(wires.g.shards * pieces)
        self.per = src.shape[0] // pieces

    def cut(self, ref, i):
        return ref.at[pl.ds(i * self.per, self.per)]

    def send(self, i):
        g = self.g
        for d in range(1, g.shards):
            to = (g.k + d) % g.shards
            src = self.src.at[pl.ds(i * self.per, self.per), to]
            self.w.send(src, self.cut(self.dst.at[g.k], i), self.at + i * g.shards + d, g.s, to, src)

    def finish(self):
        g = self.g
        for i in range(self.pieces):
            for d in range(1, g.shards):
                self.w.arrived(self.cut(self.dst.at[(g.k - d) % g.shards], i), self.at + i * g.shards + d)


def backward_kernel(
    seqs, shards, counts, one_seq,
    qkv, do, n1, qkvw, x_all, dh2, y_own, w2, w1, wd, smalls, gain, slopes, idc, idr, beginr,
    ret_y, ret_x, o_qkv, o_dense, o_up, o_down, o_small,
    qkv_v, do_v, dqkv_v, n1_v, qkvw_v, x_v, dh2_v, dk_acc, dv_acc, bias_acc, mine_v, sent_v, got_v, dx_v, gq_v,
    small_v, small_got, small_fin, small_last, f_qkv, f_dense, f_up, f_down, own_w2, own_w1, own_wd,
    *rest,
):
    bufs, (send_sems, recv_sems, copy_sems) = rest[:-3], rest[-3:]
    g = Geometry(seqs, shards)
    wires = Wires(g, send_sems, recv_sems)
    pairs, tokens = do_v.shape[0], do_v.shape[1]
    part = pairs * 2 * HEAD
    width = n1_v.shape[1]
    lanes = seqs * shards
    block = ROWS * lanes
    blocks = tokens // block
    half = block // seqs
    tile = bias_acc.shape[2]
    local = []

    def bring(src, dst):
        made = pltpu.make_async_copy(src, dst, copy_sems.at[len(local)])
        made.start()
        local.append(made)
        return made

    def held(ref):
        return lambda i, j: ref.at[i, j]

    down = Scatter(wires, w2, held(own_w2), bufs[0:4])
    up = Scatter(wires, w1, held(own_w1), bufs[4:8])
    dense = Scatter(wires, wd, held(own_wd), bufs[8:12])
    qkv_sum = Scatter(wires, gq_v, lambda i, j: gq_v.at[i, j, g.c], bufs[12:16])
    back_y = Back(wires, y_own, ret_y, 1)
    back_x = Back(wires, dx_v, ret_x, blocks)
    half_at = wires.block(blocks)
    small_at = wires.block(shards + 1)

    first = [bring(qkv, qkv_v)] + [bring(do.at[:, pl.ds(h * 2 * HEAD, 2 * HEAD)], do_v.at[h]) for h in range(pairs)]
    owns = [bring(a.at[:, :, g.c], b) for a, b in ((w2, own_w2), (w1, own_w1), (wd, own_wd))]
    later = [
        bring(n1, n1_v), bring(qkvw, qkvw_v), bring(x_all.at[:, pl.ds(g.s * shards, shards)], x_v), bring(dh2, dh2_v),
        bring(smalls, small_v),
    ]
    enter(g)
    down.core_send()
    up.core_send()
    dense.core_send()
    back_y.send(0)
    own_y = bring(y_own.at[:, g.k], dx_v.at[:, g.k])
    for made in first + owns:
        made.wait()

    lane_id = lax.broadcasted_iota(jnp.int32, (1, 2 * HEAD), 1)

    def attend(h):
        q_ref, k_ref, v_ref, do_ref = qkv_v.at[h], qkv_v.at[pairs + h], qkv_v.at[2 * pairs + h], do_v.at[h]
        dk_acc[...] = jnp.zeros_like(dk_acc)
        dv_acc[...] = jnp.zeros_like(dv_acc)
        for j in range(2):
            bias_acc[j] = jnp.broadcast_to(slopes[h, j] * idc[...], bias_acc.shape[1:])
        cols = pl.ds(pl.multiple_of(h * 2 * HEAD, 2 * HEAD), 2 * HEAD)
        for b in range(blocks):
            end = (b + 1) * block
            for t in range(block // tile):
                at = pl.ds(b * block + t * tile, tile)
                q = q_ref[at, :] * jnp.asarray(HEAD**-0.5, bf16)
                grad = do_ref[at, :]
                ids_q = idr[:, at]
                both = None
                for j in range(2):
                    mine = (lane_id // HEAD) == j
                    qj = jnp.where(mine, q, jnp.zeros_like(q))
                    doj = jnp.where(mine, grad, jnp.zeros_like(grad))
                    s = lax.dot_general(
                        k_ref[:end, :], qj, (((1,), (1,)), ((), ())), preferred_element_type=f32
                    )
                    s = s + bias_acc[j, :end, :]
                    if one_seq:
                        tail = attn_mask(s[b * block :, :], idc[b * block : end, :] <= ids_q)
                        s = jnp.concatenate([s[: b * block, :], tail], axis=0) if b else tail
                    else:
                        ids_k = idc[:end, :]
                        s = attn_mask(s, (ids_k <= ids_q) & (ids_k >= beginr[:, at]))
                    top = jnp.max(s, axis=0, keepdims=True)
                    e = jnp.exp(s - top)
                    probs = e * (1.0 / jnp.sum(e, axis=0, keepdims=True))
                    dv_acc[:end, :] += jnp.dot(probs.astype(bf16), doj, preferred_element_type=f32)
                    dp = lax.dot_general(
                        v_ref[:end, :], doj, (((1,), (1,)), ((), ())), preferred_element_type=f32
                    )
                    inner = jnp.sum(probs * dp, axis=0, keepdims=True)
                    ds = (probs * (dp - inner)).astype(bf16)
                    dk_acc[:end, :] += jnp.dot(ds, qj, preferred_element_type=f32)
                    dq = lax.dot_general(
                        ds, k_ref[:end, :], (((0,), (0,)), ((), ())), preferred_element_type=f32
                    )
                    both = dq if both is None else jnp.where(mine, dq, both)
                dqkv_v[0, at, cols] = (both * (HEAD**-0.5)).astype(bf16)
        dqkv_v[1, :, cols] = dk_acc[...].astype(bf16)
        dqkv_v[2, :, cols] = dv_acc[...].astype(bf16)

    @pl.loop(0, pairs)
    def _(h):
        attend(h)

        @pl.when(h == 0)
        def _():
            down.core_done()

        @pl.when(h == 1)
        def _():
            up.core_done()

        @pl.when(h == 2)
        def _():
            dense.core_done()

    for made in later:
        made.wait()

    for b in range(blocks):
        total = None
        for p in range(3):
            weight = qkvw_v[:, :, p * part : (p + 1) * part].reshape(width, part)
            term = lax.dot_general(
                dqkv_v[p, b * block : (b + 1) * block, :], weight, (((1,), (1,)), ((), ())), preferred_element_type=f32
            )
            total = term if total is None else total + term

        @pl.when(g.s == 0)
        def _(total=total, b=b):
            mine_v[b] = total[:half]
            sent_v[b] = total[half:].astype(bf16)

        @pl.when(g.s == 1)
        def _(total=total, b=b):
            mine_v[b] = total[half:]
            sent_v[b] = total[:half].astype(bf16)

        if b:
            wires.send(sent_v.at[b - 1], got_v.at[b - 1], half_at + b - 1, 1 - g.s, g.k, sent_v.at[b - 1])
    down.y_done()
    wires.send(sent_v.at[blocks - 1], got_v.at[blocks - 1], half_at + blocks - 1, 1 - g.s, g.k, sent_v.at[0])

    rows = width // shards

    @pl.loop(0, blocks)
    def _(m):
        cut = n1_v[:, pl.ds(pl.multiple_of(m * block, block), block)]
        for p in range(3):
            out = lax.dot_general(cut, dqkv_v[p], (((0,), (0,)), ((), ())), preferred_element_type=f32).astype(bf16)
            out = out.reshape(block // rows // 2, 2, rows, part)
            for i in range(block // rows // 2):
                at = m * (block // rows // 2) + i
                for j in range(2):
                    gq_v[at // 2, at % 2, j, :, p * part : (p + 1) * part] = out[i, j]

    sums = [jnp.sum(dqkv_v[p].astype(f32), axis=0, keepdims=True) for p in (0, 2)]
    per = 2 * width // shards
    for i in range(part // per):
        for half_no in range(2):
            small_v[(half_no * width + g.s * part) // per + i, 2:3, :per] = sums[half_no][:, i * per : (i + 1) * per]
    qkv_sum.core_send()
    own_y.wait()
    kept_y = bring(dx_v.at[:, g.k], ret_y.at[g.k])
    kept_y.wait()

    gains = biases = jnp.zeros((1, width), f32)
    for b in range(blocks):
        wires.arrived(got_v.at[b], half_at + b)
        grad = mine_v[b] + got_v[b].astype(f32)
        xhat, root = normalize(x_v[b].astype(f32).reshape(half, width))
        gains = gains + jnp.sum(grad * xhat, axis=0, keepdims=True)
        biases = biases + jnp.sum(grad, axis=0, keepdims=True)
        dx = dh2_v[b] + norm_pull(grad, gain[...], xhat, root)
        dx_v[b] = dx.reshape(shards, ROWS, width).astype(bf16)
        back_x.send(b)
        if b == 0:
            up.y_done()
        if b == 1:
            down.z_done()
    for j in range(shards):
        small_v[j, 0:1, :rows] = gains[:, j * rows : (j + 1) * rows]
        small_v[j, 1:2, :rows] = biases[:, j * rows : (j + 1) * rows]
    kept = [bring(dx_v.at[:, g.k], ret_x.at[g.k])]
    for d in range(1, shards):
        to = (g.k + d) % shards
        wires.send(small_v.at[to], small_got.at[g.k], small_at + d, g.s, to, small_v.at[0])
    small_got[g.k] = small_v[g.k]
    qkv_sum.core_done()
    dense.y_done()
    up.z_done()
    down.final()
    dense.z_done()
    qkv_sum.y_done()
    for d in range(1, shards):
        wires.arrived(small_got.at[(g.k - d) % shards], small_at + d)
    small_fin[0] = jnp.sum(small_got[...], axis=0)
    wires.send(small_fin.at[0], small_fin.at[1], small_at + shards, 1 - g.s, g.k, small_fin.at[0])
    up.final()
    dense.final()
    qkv_sum.z_done()

    down.done()
    ff_part = f_down.shape[0] // seqs
    for i, at in ((0, g.s), (1, 1 - g.s)):
        f_down[pl.ds(pl.multiple_of(at * ff_part, ff_part), ff_part), :] = down.fin[i].astype(f32)
    kept.append(bring(f_down, o_down))
    up.done()
    for i, at in ((0, g.s), (1, 1 - g.s)):
        for j in range(shards):
            f_up[:, pl.ds(pl.multiple_of((j * seqs + at) * ff_part, 128), ff_part)] = up.fin[
                i, :, j * ff_part : (j + 1) * ff_part
            ].astype(f32)
    kept.append(bring(f_up, o_up))
    dense.done()
    f_dense[...] = dense.fin[0].astype(f32) + dense.fin[1].astype(f32)
    kept.append(bring(f_dense, o_dense))
    wires.arrived(small_fin.at[1], small_at + shards)
    small_last[...] = small_fin[0] + small_fin[1]
    kept.append(bring(small_last, o_small))
    qkv_sum.final()
    qkv_sum.done()
    for i, at in ((0, g.s), (1, 1 - g.s)):
        for p in range(3):
            f_qkv[:, pl.ds(pl.multiple_of(p * width + at * part, 128), part)] = qkv_sum.fin[
                i, :, p * part : (p + 1) * part
            ].astype(f32)
    kept.append(bring(f_qkv, o_qkv))
    back_y.finish()
    back_x.finish()
    wires.drain()
    for made in kept:
        made.wait()
    assert wires.used <= counts[0] and len(local) <= counts[1]


def backward_exchange(
    qkv, do, n1, qkvw, x_all, dh2, y_own, w2, w1, wd, smalls, gain, slopes, ids, begins, seqs, shards, one_seq
):
    tokens, part = do.shape
    width = n1.shape[1]
    pairs = part // (2 * HEAD)
    lanes = seqs * shards
    block = ROWS * lanes
    blocks, half = tokens // block, block // seqs
    tile = min(256, block)
    rows, ff = width // shards, w1.shape[2]
    ff_part = ff // shards
    counts = (256, 48)
    cut = lambda a: a.reshape((4, 2, 2) + a.shape[1:])
    any_, vmem = pl.BlockSpec(memory_space=pl.ANY), pl.BlockSpec(memory_space=pltpu.VMEM)
    ret = (shards, blocks, ROWS, width)
    outs = [
        (ret, bf16), (ret, bf16), ((rows, 3 * width), f32), ((rows, width), f32), ((rows, seqs * ff), f32),
        ((seqs * ff_part, width), f32), (smalls.shape[1:], f32),
    ]
    blks = [(ff_part, width), (rows, ff), (rows, width), (rows, 3 * part)]
    scratch = [
        ((3 * pairs, tokens, 2 * HEAD), bf16), ((pairs, tokens, 2 * HEAD), bf16), ((3, tokens, part), bf16),
        ((tokens, width), bf16), ((shards, rows, 3 * part), bf16), ((blocks, shards, ROWS, width), bf16),
        ((blocks, half, width), f32), ((tokens, 2 * HEAD), f32), ((tokens, 2 * HEAD), f32), ((2, tokens, tile), f32),
        ((blocks, half, width), f32), ((blocks, half, width), bf16), ((blocks, half, width), bf16),
        ((blocks, shards, ROWS, width), bf16), ((4, 2, 2) + blks[3], bf16), (smalls.shape, f32), (smalls.shape, f32),
        ((2,) + smalls.shape[1:], f32), (smalls.shape[1:], f32), ((rows, 3 * width), f32), ((rows, width), f32), ((rows, seqs * ff), f32),
        ((seqs * ff_part, width), f32), ((4, 2) + blks[0], bf16), ((4, 2) + blks[1], bf16), ((4, 2) + blks[2], bf16),
    ]
    for blk in blks:
        scratch += [((4, 2) + blk, bf16), ((4,) + blk, bf16), ((4,) + blk, bf16), ((2,) + blk, bf16)]
    return pl.pallas_call(
        functools.partial(backward_kernel, seqs, shards, counts, one_seq),
        in_specs=[any_] * 11 + [vmem, pl.BlockSpec(memory_space=pltpu.SMEM)] + [vmem] * 3,
        out_specs=[any_] * len(outs),
        out_shape=[jax.ShapeDtypeStruct(s, d) for s, d in outs],
        scratch_shapes=[pltpu.VMEM(s, d) for s, d in scratch]
        + [pltpu.SemaphoreType.DMA((counts[0],)), pltpu.SemaphoreType.DMA((counts[0],)), pltpu.SemaphoreType.DMA((counts[1],))],
        compiler_params=pltpu.CompilerParams(collective_id=2, has_side_effects=True, vmem_limit_bytes=60 * 2**20),
        name="backward_exchange",
    )(
        qkv, do, n1, qkvw, x_all, dh2, y_own, cut(w2), cut(w1), cut(wd), smalls, gain, slopes.reshape(pairs, 2),
        ids[:, None], ids[None, :], begins[None, :],
    )


def layout_tables(lengths, lane_count, group_count, per_group):
    seq_rows = lengths // lane_count
    row_start = jnp.cumsum(seq_rows) - seq_rows
    slot_rows = seq_rows.reshape(group_count, per_group)
    slot_start = row_start.reshape(group_count, per_group)
    slot_before = jnp.cumsum(slot_rows, axis=1) - slot_rows
    return seq_rows, row_start, slot_rows, slot_start, slot_before


def per_device(
    tokens, cotangent, lengths, first_gain, first_bias, qkv_weight, qv_bias, dense_weight, dense_bias,
    second_gain, second_bias, fc1_weight, fc1_bias, fc2_weight, fc2_bias,
):
    shards, seqs = lax.axis_size("shard"), lax.axis_size("seq")
    lanes = shards * seqs
    slots, width = tokens.shape[1], tokens.shape[2]
    rows = slots // shards
    cap = slots * seqs
    per_group = lengths.shape[0] // shards
    hidden_units = fc1_weight.shape[1]
    me, group = lax.axis_index("seq"), lax.axis_index("shard")
    blocks = rows // ROWS
    heads = width // HEAD // seqs
    part = heads * HEAD
    ff_part = hidden_units // shards // seqs

    smalls_in = (first_gain, first_bias, qv_bias, dense_bias, second_gain, second_bias, fc1_bias, fc2_bias)
    small_width = -(-max(a.shape[0] for a in smalls_in) // 128) * 128
    small = jnp.stack([jnp.pad(a.astype(f32), (0, small_width - a.shape[0])) for a in smalls_in])

    seq_rows, row_start, slot_rows, slot_start, slot_before = layout_tables(lengths, lanes, shards, per_group)
    row_in = jnp.arange(rows, dtype=jnp.int32)[None, :, None]
    inside = ((row_in >= slot_before[:, None]) & (row_in < (slot_before + slot_rows)[:, None])).astype(jnp.int32)
    send_live = jnp.sum(inside, axis=2) > 0
    send_row = jnp.sum(inside * (slot_start[:, None] + row_in - slot_before[:, None]), axis=2).reshape(-1)

    def pack(source):
        return jnp.take(source, send_row, axis=0).reshape(shards, rows, width)

    def own_part(whole):
        return take(whole.reshape(blocks, seqs, -1, whole.shape[-1]), me, 1)

    place = jnp.arange(cap, dtype=jnp.int32)
    block_of, in_block = place // (ROWS * lanes), place % (ROWS * lanes)
    row_of = block_of * ROWS + in_block % ROWS
    ids = row_of * lanes + in_block // ROWS
    own_before, own_count = take(slot_before, group), take(slot_rows, group)
    holds = (row_of[:, None] >= own_before[None]) & (row_of[:, None] < (own_before + own_count)[None])
    begin_row = jnp.sum(jnp.where(holds, own_before[None], 0), axis=1)
    begins = jnp.where(jnp.any(holds, axis=1), begin_row * lanes, ids)
    ids, begins = ids.astype(f32), begins.astype(f32)
    head_ids = me * heads + jnp.arange(heads, dtype=jnp.int32)
    slopes = 2.0 ** (-8.0 * (head_ids.astype(f32) + 1.0) / HEADS)
    one_seq = per_group == 1

    packed_cot = pack(cotangent[0])
    packed_cot = jnp.where(send_live[:, :, None], packed_cot, jnp.zeros_like(packed_cot))
    blocked = (shards, blocks, ROWS, width)
    x_all, cot_all, normed_one, full_qkv, smalls, full_dense, full_up, full_down, qkv, mixed_all = forward_exchange(
        pack(tokens[0]).reshape(blocked), packed_cot.reshape(blocked),
        qkv_weight, small, dense_weight, fc1_weight, fc2_weight,
        slopes, ids, begins, seqs, shards, one_seq,
    )
    full_qkv = full_qkv.reshape(width, 3 * part)
    full_dense = full_dense.reshape(width, width)
    full_up = full_up.reshape(width, shards * ff_part)
    full_down = full_down.reshape(shards * ff_part, width)
    cot_low = cot_all.reshape(cap, width)
    cot_own = own_part(cot_low)
    unpack = lambda i, count: smalls[:, i, :count].reshape(-1)
    own_rows = width // shards
    gain_one, bias_dense, gain_two, bias_two, bias_down = (unpack(i, own_rows) for i in (0, 3, 4, 5, 7))
    bias_up = take(unpack(6, seqs * ff_part).reshape(shards, seqs, ff_part), me, 1).reshape(-1)
    x_own = own_part(x_all.reshape(cap, width))
    hidden = x_all.reshape(cap, width).astype(f32)
    mixed_all = mixed_all.transpose(1, 0, 2).reshape(cap, width)
    branch = jnp.dot(mixed_all, full_dense, preferred_element_type=f32) + bias_dense
    resid = hidden + branch
    xhat_two, _ = normalize(resid)
    normed_two = (xhat_two * gain_two + bias_two).astype(bf16)
    upper = jnp.dot(normed_two, full_up, preferred_element_type=f32) + bias_up
    activ = gelu_tanh(upper).astype(bf16)
    down = jnp.dot(activ, full_down, preferred_element_type=f32)
    resid_own = own_part(resid)
    down_own = seq_sum(down.reshape(blocks, seqs, -1, width), 1)
    block_out = (resid_own + down_own + bias_down).astype(bf16)

    grad_down = jnp.dot(activ.T, cot_low, preferred_element_type=f32).astype(bf16)
    grad_activ = jnp.dot(cot_low, full_down.T, preferred_element_type=f32)
    grad_upper = jax.vjp(gelu_tanh, upper)[1](grad_activ)[0].astype(bf16)
    grad_up = jnp.dot(normed_two.T, grad_upper, preferred_element_type=f32).astype(bf16)
    grad_bup = jnp.sum(grad_upper.astype(f32), axis=0)
    grad_normed = jnp.dot(grad_upper, full_up.T, preferred_element_type=f32)
    grad_normed = seq_sum(grad_normed.reshape(blocks, seqs, -1, width), 1).reshape(slots, width)
    cot_full = cot_own.reshape(slots, width).astype(f32)
    grad_bdown = jnp.sum(cot_full, axis=0)
    xhat_two, root_two = normalize(resid_own.reshape(slots, width))
    grad_gain_two = jnp.sum(grad_normed * xhat_two, axis=0)
    grad_bias_two = jnp.sum(grad_normed, axis=0)
    grad_resid = cot_full + norm_pull(grad_normed, gain_two, xhat_two, root_two)

    grad_branch = grad_resid.astype(bf16)
    grad_dense = jnp.dot(own_part(mixed_all).reshape(slots, width).T, grad_branch, preferred_element_type=f32).astype(bf16)
    grad_bdense = jnp.sum(grad_branch.astype(f32), axis=0)
    grad_mixed = jnp.dot(grad_branch, full_dense.T, preferred_element_type=f32).astype(bf16)
    got = seq_blocks(grad_mixed.reshape(blocks, -1, seqs, part), 2, bf16)
    if seqs == 2:
        grad_mixed = jnp.where(me == 0, jnp.stack(got, 1), jnp.stack(got[::-1], 1))
    else:
        grad_mixed = jnp.zeros((blocks, seqs) + got[0].shape[1:], bf16)
        for d, g in enumerate(got):
            grad_mixed = lax.dynamic_update_index_in_dim(grad_mixed, g, (me - d) % seqs, 1)
    grad_mixed = grad_mixed.reshape(cap, part)
    vectors = {3: grad_bdense, 4: grad_gain_two, 5: grad_bias_two, 7: grad_bdown}
    zero = jnp.zeros((shards, seqs, ff_part), f32)
    vectors[6] = lax.dynamic_update_index_in_dim(zero, grad_bup.reshape(shards, ff_part), me, 1)
    pieces = [vectors[i].reshape(shards, -1) if i in vectors else jnp.zeros((shards, 1), f32) for i in range(8)]
    small_grads = jnp.stack([jnp.pad(p, ((0, 0), (0, small_width - p.shape[1]))) for p in pieces], axis=1)
    ret_out, ret_grad, g_qkv, g_dense, g_up, g_down, g_small = backward_exchange(
        qkv, grad_mixed, normed_one, full_qkv.reshape(shards, -1, 3 * part), x_all,
        grad_resid.reshape(blocks, -1, width), block_out.reshape(blocks, shards, ROWS, width),
        grad_down.reshape(shards, ff_part, width), grad_up.reshape(shards, -1, shards * ff_part),
        grad_dense.reshape(shards, -1, width), small_grads, gain_one[None],
        slopes, ids, begins, seqs, shards, one_seq,
    )

    row_here = jnp.arange(slots, dtype=jnp.int32)[:, None]
    seq_in = ((row_here >= row_start[None]) & (row_here < (row_start + seq_rows)[None])).astype(jnp.int32)
    home = jnp.arange(lengths.shape[0], dtype=jnp.int32) // per_group
    fetch = jnp.sum(seq_in * (home[None] * rows + slot_before.reshape(-1)[None] + row_here - row_start[None]), axis=1)
    fetch_live = jnp.sum(seq_in, axis=1) > 0

    def to_stream(got):
        taken = jnp.take(got.reshape(-1, width), fetch, axis=0)
        return jnp.where(fetch_live[:, None], taken, jnp.zeros_like(taken))[None]

    g_gain_one, g_bias_one, g_qv, g_bdense, g_gain_two, g_bias_two, g_bup, g_bdown = (
        g_small[i, : a.shape[0]] for i, a in enumerate(smalls_in)
    )
    return (
        to_stream(ret_out), to_stream(ret_grad),
        g_gain_one, g_bias_one, g_qkv, g_qv, g_dense, g_bdense, g_gain_two, g_bias_two, g_up, g_bup, g_down, g_bdown,
    )


def per_device_any(
    tokens, cotangent, lengths, first_gain, first_bias, qkv_weight, qv_bias, dense_weight, dense_bias,
    second_gain, second_bias, fc1_weight, fc1_bias, fc2_weight, fc2_bias,
):
    shards, seqs = lax.axis_size("shard"), lax.axis_size("seq")
    lanes = shards * seqs
    slots, width = tokens.shape[1], tokens.shape[2]
    rows = slots // shards
    cap = slots * seqs
    per_group = lengths.shape[0] // shards
    hidden_units = fc1_weight.shape[1]
    me, group = lax.axis_index("seq"), lax.axis_index("shard")
    blocks = rows // ROWS
    heads = width // HEAD // seqs
    part = heads * HEAD
    ff_part = hidden_units // shards // seqs

    qkv_half = take(qkv_weight.reshape(-1, 3, seqs, part), me, 2).reshape(-1, 3 * part)
    fc1_half = take(fc1_weight.reshape(-1, shards, seqs, ff_part), me, 2).reshape(-1, shards * ff_part)
    fc2_half = take(fc2_weight.reshape(seqs, ff_part, width), me, 0)
    small = jnp.concatenate(
        [first_gain, first_bias, qv_bias, dense_bias, second_gain, second_bias, fc1_bias, fc2_bias]
    )
    small_rows = -(-small.shape[0] // (3 * part))
    small_rows += -small_rows % 16
    small = jnp.pad(small, (0, small_rows * 3 * part - small.shape[0])).reshape(small_rows, 3 * part)
    gather = lambda a: lax.all_gather(a, "shard", axis=0, tiled=False)
    qkv_small = gather(jnp.concatenate([qkv_half, small], axis=0))
    own_rows = qkv_half.shape[0]
    full_qkv = qkv_small[:, :own_rows].reshape(width, 3 * part)
    smalls = qkv_small[:, own_rows:].reshape(shards, -1).astype(f32)
    full_dense = gather(dense_weight).reshape(width, width)
    full_up = gather(fc1_half).reshape(width, shards * ff_part)
    full_down = gather(fc2_half).reshape(shards * ff_part, width)
    cuts, at = [], 0
    for a in (first_gain, first_bias, qv_bias, dense_bias, second_gain, second_bias, fc1_bias, fc2_bias):
        cuts.append(smalls[:, at : at + a.shape[0]].reshape(-1))
        at += a.shape[0]
    gain_one, bias_one, bias_qv, bias_dense, gain_two, bias_two, bias_up, bias_down = cuts
    bias_q, bias_v = (take(bias_qv[i * width : (i + 1) * width].reshape(seqs, part), me) for i in (0, 1))
    bias_all = jnp.concatenate([bias_q, jnp.zeros_like(bias_q), bias_v])
    bias_up = take(bias_up.reshape(shards, seqs, ff_part), me, 1).reshape(-1)

    seq_rows, row_start, slot_rows, slot_start, slot_before = layout_tables(lengths, lanes, shards, per_group)
    row_in = jnp.arange(rows, dtype=jnp.int32)[None, :, None]
    inside = ((row_in >= slot_before[:, None]) & (row_in < (slot_before + slot_rows)[:, None])).astype(jnp.int32)
    send_live = jnp.sum(inside, axis=2) > 0
    send_row = jnp.sum(inside * (slot_start[:, None] + row_in - slot_before[:, None]), axis=2).reshape(-1)

    def to_groups(source):
        packed = jnp.take(source, send_row, axis=0).reshape(shards, rows, width)
        packed = jnp.where(send_live[:, :, None], packed, jnp.zeros_like(packed))
        got = lax.all_to_all(packed, "shard", split_axis=0, concat_axis=0, tiled=True)
        own = got.reshape(shards, blocks, ROWS, width).transpose(1, 0, 2, 3).reshape(blocks, -1, width)
        return own, seq_gather(own, 1).reshape(cap, width)

    x_own, x_low = to_groups(tokens[0])
    cot_own, cot_low = to_groups(cotangent[0])

    def own_part(whole):
        return take(whole.reshape(blocks, seqs, -1, whole.shape[-1]), me, 1)

    place = jnp.arange(cap, dtype=jnp.int32)
    block_of, in_block = place // (ROWS * lanes), place % (ROWS * lanes)
    row_of = block_of * ROWS + in_block % ROWS
    ids = row_of * lanes + in_block // ROWS
    own_before, own_count = take(slot_before, group), take(slot_rows, group)
    holds = (row_of[:, None] >= own_before[None]) & (row_of[:, None] < (own_before + own_count)[None])
    begin_row = jnp.sum(jnp.where(holds, own_before[None], 0), axis=1)
    begins = jnp.where(jnp.any(holds, axis=1), begin_row * lanes, ids)
    ids, begins = ids.astype(f32), begins.astype(f32)
    head_ids = me * heads + jnp.arange(heads, dtype=jnp.int32)
    slopes = 2.0 ** (-8.0 * (head_ids.astype(f32) + 1.0) / HEADS)
    one_seq = per_group == 1

    hidden = x_low.astype(f32)
    xhat_one, _ = normalize(hidden)
    normed_one = (xhat_one * gain_one + bias_one).astype(bf16)
    qkv = (jnp.dot(normed_one, full_qkv, preferred_element_type=f32) + bias_all).astype(bf16)
    mixed = attention_forward(qkv, slopes, ids, begins, lanes, one_seq)
    mixed_all = seq_gather(mixed, 1).reshape(cap, width)
    branch = jnp.dot(mixed_all, full_dense, preferred_element_type=f32) + bias_dense
    resid = hidden + branch
    xhat_two, _ = normalize(resid)
    normed_two = (xhat_two * gain_two + bias_two).astype(bf16)
    upper = jnp.dot(normed_two, full_up, preferred_element_type=f32) + bias_up
    activ = gelu_tanh(upper).astype(bf16)
    down = jnp.dot(activ, full_down, preferred_element_type=f32)
    resid_own = own_part(resid)
    down_own = seq_sum(down.reshape(blocks, seqs, -1, width), 1)
    block_out = (resid_own + down_own + bias_down).astype(bf16)

    grad_down = jnp.dot(activ.T, cot_low, preferred_element_type=f32).astype(bf16)
    grad_activ = jnp.dot(cot_low, full_down.T, preferred_element_type=f32)
    grad_upper = jax.vjp(gelu_tanh, upper)[1](grad_activ)[0].astype(bf16)
    grad_up = jnp.dot(normed_two.T, grad_upper, preferred_element_type=f32).astype(bf16)
    grad_bup = jnp.sum(grad_upper.astype(f32), axis=0)
    grad_normed = jnp.dot(grad_upper, full_up.T, preferred_element_type=f32)
    grad_normed = seq_sum(grad_normed.reshape(blocks, seqs, -1, width), 1).reshape(slots, width)
    cot_full = cot_own.reshape(slots, width).astype(f32)
    grad_bdown = jnp.sum(cot_full, axis=0)
    xhat_two, root_two = normalize(resid_own.reshape(slots, width))
    grad_gain_two = jnp.sum(grad_normed * xhat_two, axis=0)
    grad_bias_two = jnp.sum(grad_normed, axis=0)
    grad_resid = cot_full + norm_pull(grad_normed, gain_two, xhat_two, root_two)

    grad_branch = grad_resid.astype(bf16)
    grad_dense = jnp.dot(own_part(mixed_all).reshape(slots, width).T, grad_branch, preferred_element_type=f32).astype(bf16)
    grad_bdense = jnp.sum(grad_branch.astype(f32), axis=0)
    grad_mixed = jnp.dot(grad_branch, full_dense.T, preferred_element_type=f32).astype(bf16)
    got = seq_blocks(grad_mixed.reshape(blocks, -1, seqs, part), 2, bf16)
    if seqs == 2:
        grad_mixed = jnp.where(me == 0, jnp.stack(got, 1), jnp.stack(got[::-1], 1))
    else:
        grad_mixed = jnp.zeros((blocks, seqs) + got[0].shape[1:], bf16)
        for d, g in enumerate(got):
            grad_mixed = lax.dynamic_update_index_in_dim(grad_mixed, g, (me - d) % seqs, 1)
    grad_mixed = grad_mixed.reshape(cap, part)
    planes = qkv.reshape(cap, -1, 2 * HEAD).transpose(1, 0, 2)
    grad_proj = jnp.concatenate(
        attention_backward(planes, grad_mixed, slopes, ids, begins, lanes, one_seq), axis=1
    )
    grad_qkv = jnp.dot(normed_one.T, grad_proj, preferred_element_type=f32).astype(bf16)
    proj_sums = jnp.sum(grad_proj.astype(f32), axis=0)
    grad_one = jnp.dot(grad_proj, full_qkv.T, preferred_element_type=f32)
    grad_one = seq_sum(grad_one.reshape(blocks, seqs, -1, width), 1).reshape(slots, width)
    xhat_one, root_one = normalize(x_own.reshape(slots, width).astype(f32))
    grad_gain_one = jnp.sum(grad_one * xhat_one, axis=0)
    grad_bias_one = jnp.sum(grad_one, axis=0)
    tokens_grad = (grad_resid + norm_pull(grad_one, gain_one, xhat_one, root_one)).astype(bf16)

    row_here = jnp.arange(slots, dtype=jnp.int32)[:, None]
    seq_in = ((row_here >= row_start[None]) & (row_here < (row_start + seq_rows)[None])).astype(jnp.int32)
    home = jnp.arange(lengths.shape[0], dtype=jnp.int32) // per_group
    fetch = jnp.sum(seq_in * (home[None] * rows + slot_before.reshape(-1)[None] + row_here - row_start[None]), axis=1)
    fetch_live = jnp.sum(seq_in, axis=1) > 0

    def to_stream(own):
        sent = own.reshape(blocks, shards, ROWS, width).transpose(1, 0, 2, 3).reshape(shards, rows, width)
        got = lax.all_to_all(sent, "shard", split_axis=0, concat_axis=0, tiled=True)
        taken = jnp.take(got.reshape(-1, width), fetch, axis=0)
        return jnp.where(fetch_live[:, None], taken, jnp.zeros_like(taken))[None]

    down_block = shard_reduce(grad_down.reshape(shards, ff_part, width), bf16)
    up_block = shard_reduce(grad_up.reshape(shards, -1, shards * ff_part), bf16)
    dense_block = shard_reduce(grad_dense.reshape(shards, -1, width), bf16)
    qkv_block = shard_reduce(grad_qkv.reshape(shards, -1, 3 * part), bf16)

    def spread(vector, index_shape):
        zero = jnp.zeros(index_shape, f32)
        return lax.dynamic_update_index_in_dim(zero, vector, me, 1)

    sums = proj_sums.reshape(3, part)
    qv = spread(jnp.stack([sums[0], sums[2]]), (2, seqs, part)).reshape(shards, -1)
    bup = spread(grad_bup.reshape(shards, ff_part), (shards, seqs, ff_part)).reshape(shards, -1)
    rest = (grad_gain_one, grad_bias_one, grad_bdense, grad_gain_two, grad_bias_two, grad_bdown)
    packed = jnp.concatenate([a.reshape(shards, -1) for a in rest] + [qv, bup], axis=1)
    packed = shard_reduce(packed, f32)
    packed = jnp.sum(seq_gather(packed, 0), axis=0)
    cuts, at = [], 0
    for a in [a.reshape(shards, -1) for a in rest] + [qv, bup]:
        cuts.append(packed[at : at + a.shape[1]])
        at += a.shape[1]
    g_gain_one, g_bias_one, g_bdense, g_gain_two, g_bias_two, g_bdown, g_qv, g_bup = cuts

    g_dense = jnp.sum(seq_gather(dense_block.astype(bf16), 0).astype(f32), axis=0)
    g_qkv = seq_gather(qkv_block.astype(bf16).reshape(-1, 3, part), 2).reshape(-1, 3 * width).astype(f32)
    g_up = seq_gather(up_block.astype(bf16).reshape(-1, shards, ff_part), 2).reshape(-1, hidden_units).astype(f32)
    g_down = seq_gather(down_block.astype(bf16), 0).reshape(-1, width).astype(f32)
    return (
        to_stream(block_out), to_stream(tokens_grad.reshape(blocks, -1, width)),
        g_gain_one, g_bias_one, g_qkv, g_qv, g_dense, g_bdense, g_gain_two, g_bias_two, g_up, g_bup, g_down, g_bdown,
    )


def solution(mesh):
    rows, vector, stream = P("shard", None), P("shard"), P(("seq", "shard"), None, None)
    params = (vector, vector, rows, vector, rows, vector, vector, vector, rows, vector, rows, vector)
    fused = mesh.shape["seq"] == 2 and shard_factors(mesh.shape["shard"])[0] == 4
    return jax.shard_map(
        per_device if fused else per_device_any, mesh=mesh, in_specs=(stream, stream, P()) + params, out_specs=(stream, stream) + params, check_vma=False
    )
```

```python
import functools

import jax
import jax.numpy as jnp
from jax import lax
from jax.experimental import pallas as pl
from jax.experimental.pallas import tpu as pltpu
from jax.sharding import PartitionSpec as P

HEADS = 16
HEAD = 64
ROWS = 8

epsilon = 1e-05
masked_score = -1e30
f32 = jnp.float32
bf16 = jnp.bfloat16


def gelu_tanh(values):
    return (
        0.5
        * values
        * (1.0 + jnp.tanh(0.7978845608028654 * (values + 0.044715 * values * values * values)))
    )


def normalize(hidden):
    center = hidden - jnp.mean(hidden, axis=-1, keepdims=True)
    spread = jnp.mean(center * center, axis=-1, keepdims=True)
    root = lax.rsqrt(spread + epsilon)
    return center * root, root


def norm_pull(grad, gain, xhat, root):
    scaled = grad * gain
    return root * (
        scaled
        - jnp.mean(scaled, axis=-1, keepdims=True)
        - xhat * jnp.mean(scaled * xhat, axis=-1, keepdims=True)
    )


def slot_ids(first, count, lanes):
    place = first + lax.broadcasted_iota(jnp.int32, (count, 1), 0)
    block, inside = place // (ROWS * lanes), place % (ROWS * lanes)
    return (block * ROWS + inside % ROWS) * lanes + inside // ROWS


def attn_mask(scored, allowed):
    return jnp.where(allowed, scored, masked_score)


def attn_fwd_kernel(lanes, tile, one_seq, slope_ref, idc_ref, idr_ref, beginc_ref, q_ref, k_ref, v_ref, o_ref):
    tokens = q_ref.shape[0]
    block = ROWS * lanes
    lane_id = lax.broadcasted_iota(jnp.int32, (1, 2 * HEAD), 1)
    for b in range(tokens // block):
        end = (b + 1) * block

        def step(t, _):
            at = pl.ds(pl.multiple_of(b * block + t * tile, tile), tile)
            q = q_ref[at, :] * jnp.asarray(HEAD**-0.5, bf16)
            ids_q = idc_ref[at, :]
            both = None
            for j in range(2):
                mine = (lane_id // HEAD) == j
                qj = jnp.where(mine, q, jnp.zeros_like(q))
                s = lax.dot_general(
                    qj, k_ref[:end, :], (((1,), (1,)), ((), ())), preferred_element_type=f32
                )
                s = s + slope_ref[0, 0, j] * idr_ref[:, :end]
                if one_seq:
                    own = s[:, b * block :]
                    own = attn_mask(own, idr_ref[:, b * block : end] <= ids_q)
                    s = jnp.concatenate([s[:, : b * block], own], axis=1) if b else own
                else:
                    ids_k = idr_ref[:, :end]
                    s = attn_mask(s, (ids_k <= ids_q) & (ids_k >= beginc_ref[at, :]))
                top = jnp.max(s, axis=1, keepdims=True)
                e = jnp.exp(s - top)
                total = jnp.sum(e, axis=1, keepdims=True)
                o = jnp.dot(e.astype(bf16), v_ref[:end, :], preferred_element_type=f32) / total
                both = o if both is None else jnp.where(mine, o, both)
            o_ref[at, :] = both.astype(bf16)
            return 0

        lax.fori_loop(0, block // tile, step, 0)


def attn_bwd_kernel(
    lanes, tile, one_seq, slope_ref, idc_ref, idr_ref, beginr_ref, q_ref, k_ref, v_ref, do_ref,
    dq_ref, dk_ref, dv_ref, dk_acc, dv_acc, bias_acc,
):
    tokens = q_ref.shape[0]
    block = ROWS * lanes
    lane_id = lax.broadcasted_iota(jnp.int32, (1, 2 * HEAD), 1)
    dk_acc[...] = jnp.zeros_like(dk_acc)
    dv_acc[...] = jnp.zeros_like(dv_acc)
    for j in range(2):
        bias_acc[j] = jnp.broadcast_to(slope_ref[0, 0, j] * idc_ref[...], (tokens, tile))
    for b in range(tokens // block):
        end = (b + 1) * block

        def step(t, _):
            at = pl.ds(pl.multiple_of(b * block + t * tile, tile), tile)
            q = q_ref[at, :] * jnp.asarray(HEAD**-0.5, bf16)
            do = do_ref[at, :]
            ids_q = idr_ref[:, at]
            both = None
            for j in range(2):
                mine = (lane_id // HEAD) == j
                qj = jnp.where(mine, q, jnp.zeros_like(q))
                doj = jnp.where(mine, do, jnp.zeros_like(do))
                s = lax.dot_general(
                    k_ref[:end, :], qj, (((1,), (1,)), ((), ())), preferred_element_type=f32
                )
                s = s + bias_acc[j, :end, :]
                if one_seq:
                    own = s[b * block :, :]
                    own = attn_mask(own, idc_ref[b * block : end, :] <= ids_q)
                    s = jnp.concatenate([s[: b * block, :], own], axis=0) if b else own
                else:
                    ids_k = idc_ref[:end, :]
                    s = attn_mask(s, (ids_k <= ids_q) & (ids_k >= beginr_ref[:, at]))
                top = jnp.max(s, axis=0, keepdims=True)
                e = jnp.exp(s - top)
                probs = e * (1.0 / jnp.sum(e, axis=0, keepdims=True))
                dv_acc[:end, :] += jnp.dot(probs.astype(bf16), doj, preferred_element_type=f32)
                dp = lax.dot_general(
                    v_ref[:end, :], doj, (((1,), (1,)), ((), ())), preferred_element_type=f32
                )
                inner = jnp.sum(probs * dp, axis=0, keepdims=True)
                ds = (probs * (dp - inner)).astype(bf16)
                dk_acc[:end, :] += jnp.dot(ds, qj, preferred_element_type=f32)
                dq = lax.dot_general(
                    ds, k_ref[:end, :], (((0,), (0,)), ((), ())), preferred_element_type=f32
                )
                both = dq if both is None else jnp.where(mine, dq, both)
            dq_ref[at, :] = (both * (HEAD**-0.5)).astype(bf16)
            return 0

        lax.fori_loop(0, block // tile, step, 0)
    dk_ref[...] = dk_acc[...].astype(bf16)
    dv_ref[...] = dv_acc[...].astype(bf16)


def attn_shape(tokens, width, lanes):
    pairs = width // (2 * HEAD)
    tile = min(256, ROWS * lanes)
    return pairs, tile


def attention_forward(qkv, slopes, ids, begins, lanes, one_seq):
    tokens, width = qkv.shape[0], qkv.shape[1] // 3
    pairs, tile = attn_shape(tokens, width, lanes)
    column = lambda part: pl.BlockSpec((tokens, 2 * HEAD), lambda h, part=part: (0, part * pairs + h))
    whole = lambda a: pl.BlockSpec(a.shape, lambda h: (0, 0))
    idc, idr, beginc = ids[:, None], ids[None, :], begins[:, None]
    half = tokens * tokens * 5 // 8
    return pl.pallas_call(
        functools.partial(attn_fwd_kernel, lanes, tile, one_seq),
        grid=(pairs,),
        in_specs=[
            pl.BlockSpec((1, 1, 2), lambda h: (h, 0, 0), memory_space=pltpu.SMEM),
            whole(idc), whole(idr), whole(beginc), column(0), column(1), column(2),
        ],
        out_specs=pl.BlockSpec((tokens, 2 * HEAD), lambda h: (0, h)),
        out_shape=jax.ShapeDtypeStruct((tokens, width), bf16),
        compiler_params=pltpu.CompilerParams(vmem_limit_bytes=48 * 2**20),
        cost_estimate=pl.CostEstimate(
            flops=8 * pairs * half * HEAD * 2, transcendentals=2 * pairs * half, bytes_accessed=8 * tokens * width
        ),
        name="attention_forward",
    )(slopes.reshape(pairs, 1, 2), idc, idr, beginc, qkv, qkv, qkv)


def attention_backward(qkv, grad_out, slopes, ids, begins, lanes, one_seq):
    tokens, width = grad_out.shape
    pairs, tile = attn_shape(tokens, width, lanes)
    column = lambda part: pl.BlockSpec((tokens, 2 * HEAD), lambda h, part=part: (0, part * pairs + h))
    whole = lambda a: pl.BlockSpec(a.shape, lambda h: (0, 0))
    idc, idr, beginr = ids[:, None], ids[None, :], begins[None, :]
    plane = lambda part: pl.BlockSpec((None, tokens, 2 * HEAD), lambda h, part=part: (part * pairs + h, 0, 0))
    out = jax.ShapeDtypeStruct((tokens, width), bf16)
    half = tokens * tokens * 5 // 8
    return pl.pallas_call(
        functools.partial(attn_bwd_kernel, lanes, tile, one_seq),
        grid=(pairs,),
        in_specs=[
            pl.BlockSpec((1, 1, 2), lambda h: (h, 0, 0), memory_space=pltpu.SMEM),
            whole(idc), whole(idr), whole(beginr), plane(0), plane(1), plane(2), column(0),
        ],
        out_specs=[column(0)] * 3,
        out_shape=[out] * 3,
        scratch_shapes=[
            pltpu.VMEM((tokens, 2 * HEAD), f32), pltpu.VMEM((tokens, 2 * HEAD), f32), pltpu.VMEM((2, tokens, tile), f32),
        ],
        compiler_params=pltpu.CompilerParams(vmem_limit_bytes=56 * 2**20),
        cost_estimate=pl.CostEstimate(
            flops=20 * pairs * half * HEAD * 2, transcendentals=2 * pairs * half, bytes_accessed=14 * tokens * width
        ),
        name="attention_backward",
    )(slopes.reshape(pairs, 1, 2), idc, idr, beginr, qkv, qkv, qkv, grad_out)


def take(blocks, index, axis=0):
    return lax.dynamic_index_in_dim(blocks, index, axis, keepdims=False)


def seq_gather(block, axis):
    n, me = lax.axis_size("seq"), lax.axis_index("seq")
    shape = block.shape[:axis] + (n,) + block.shape[axis:]
    if n == 2:
        peer = lax.ppermute(block, "seq", [(0, 1), (1, 0)])
        return jnp.where(me == 0, jnp.stack([block, peer], axis), jnp.stack([peer, block], axis))
    whole = lax.dynamic_update_index_in_dim(jnp.zeros(shape, block.dtype), block, me, axis)
    for d in range(1, n):
        got = lax.ppermute(block, "seq", [(i, (i + d) % n) for i in range(n)])
        whole = lax.dynamic_update_index_in_dim(whole, got, (me - d) % n, axis)
    return whole


def seq_blocks(whole, axis, dtype):
    n, me = lax.axis_size("seq"), lax.axis_index("seq")
    got = [take(whole, me, axis)]
    for d in range(1, n):
        sent = take(whole, (me + d) % n, axis).astype(dtype)
        got.append(lax.ppermute(sent, "seq", [(i, (i + d) % n) for i in range(n)]))
    return got


def seq_sum(whole, axis, dtype=bf16):
    got = seq_blocks(whole, axis, dtype)
    return sum((g.astype(f32) for g in got[1:]), got[0].astype(f32))


def shard_factors(n):
    nc = 2 if n % 2 == 0 else 1
    nz = 4 if n % (4 * nc) == 0 else 1
    return nz, n // (nz * nc), nc


def shard_reduce(blocks, dtype):
    n, me = lax.axis_size("shard"), lax.axis_index("shard")
    sizes = shard_factors(n)
    blocks = blocks.reshape(sizes + blocks.shape[1:])
    place = (me // (sizes[1] * sizes[2]), me // sizes[2] % sizes[1], me % sizes[2])
    strides = (sizes[1] * sizes[2], sizes[2], 1)
    for axis in (2, 1, 0):
        size, mine, stride = sizes[axis], place[axis], strides[axis]
        total = take(blocks, mine, axis).astype(f32)
        for d in range(1, size):
            sent = take(blocks, (mine + d) % size, axis).astype(dtype)
            pairs = [
                (i, i - (i // stride % size) * stride + ((i // stride % size + d) % size) * stride)
                for i in range(n)
            ]
            total = total + lax.ppermute(sent, "shard", pairs).astype(f32)
        blocks = total if axis == 0 else total.astype(dtype)
    return blocks


MESH = pl.DeviceIdType.MESH


class Geometry:
    def __init__(self, seqs, shards):
        self.seqs, self.shards = seqs, shards
        self.sizes = shard_factors(shards)
        self.s, self.k = lax.axis_index("seq"), lax.axis_index("shard")
        nz, ny, nc = self.sizes
        self.z, self.y, self.c = self.k // (ny * nc), self.k // nc % ny, self.k % nc
        self.inner = (self.z + 1) // 2 % 2
        high = self.z // 2
        self.line = (self.z, self.z + 1 - 2 * (self.z % 2), 2 - high, 3 - 3 * high)

    def slot(self, i, dy, dc):
        nz, ny, nc = self.sizes
        return (self.line[i] * ny + (self.y + dy) % ny) * nc + (self.c + dc) % nc


class Wires:
    def __init__(self, geometry, send_sems, recv_sems):
        self.g, self.send_sems, self.recv_sems = geometry, send_sems, recv_sems
        self.sends, self.used = [], 0

    def block(self, count):
        first = self.used
        self.used += count
        return first

    def copy(self, src, dst, sent, got, s, k):
        return pltpu.make_async_remote_copy(
            src_ref=src, dst_ref=dst, send_sem=self.send_sems.at[sent], recv_sem=self.recv_sems.at[got],
            device_id={"seq": s, "shard": k}, device_id_type=MESH,
        )

    def send_as(self, src, dst, sent, got, s, k, like):
        self.copy(src, dst, sent, got, s, k).start()
        self.sends.append((like, sent))

    def send(self, src, dst, index, s, k, like):
        self.send_as(src, dst, index, index, s, k, like)

    def arrived(self, dst, index):
        self.copy(dst, dst, index, index, 1 - self.g.s, self.g.k).wait_recv()

    def drain(self):
        for like, index in self.sends:
            self.copy(like, like, index, index, 1 - self.g.s, self.g.k).wait_send()
        self.sends = []


def enter(geometry):
    g = geometry
    barrier = pltpu.get_barrier_semaphore()
    for d in range(1, g.shards):
        pl.semaphore_signal(
            barrier, inc=1, device_id={"seq": g.s, "shard": (g.k + d) % g.shards}, device_id_type=MESH
        )
    pl.semaphore_signal(barrier, inc=1, device_id={"seq": 1 - g.s, "shard": g.k}, device_id_type=MESH)
    pl.semaphore_wait(barrier, g.shards)


class Gather:
    def __init__(self, wires, own, out):
        self.w, self.g, self.own, self.out = wires, wires.g, own, out
        nz, ny, nc = self.g.sizes
        self.z0 = wires.block(nz)
        self.on0 = wires.block(nz)
        self.y0 = wires.block(nz * ny)
        self.c0 = wires.block(nz * ny * nc)

    def on_y(self, i, src):
        g = self.g
        for dy in range(1, g.sizes[1]):
            self.w.send(src, self.out.at[g.slot(i, 0, 0)], self.y0 + i * g.sizes[1] + dy, g.s, g.slot(0, dy, 0), self.own)

    def on_core(self, i, dy, src):
        g = self.g
        for dc in range(1, g.sizes[2]):
            index = self.c0 + (i * g.sizes[1] + dy) * g.sizes[2] + dc
            self.w.send(src, self.out.at[g.slot(i, -dy, 0)], index, g.s, g.slot(0, 0, dc), self.own)

    def start(self):
        g = self.g
        here = self.out.at[g.k]
        self.w.send_as(self.own, here, self.z0 + 2, self.z0 + 3 - g.inner, g.s, g.slot(2, 0, 0), self.own)
        self.w.send(self.own, here, self.z0 + 1, g.s, g.slot(1, 0, 0), self.own)
        self.on_y(0, self.own)
        self.on_core(0, 0, self.own)

    def poll_z(self):
        g = self.g
        for i in (1, 2, 3):
            at = self.out.at[g.slot(i, 0, 0)]
            self.w.arrived(at, self.z0 + i)
            if i > 1:

                @pl.when(g.inner == 1)
                def _(at=at, i=i):
                    self.w.copy(at, at, self.on0 + i, self.z0 + i, g.s, g.slot(1, 0, 0)).start()

            self.on_y(i, at)
            self.on_core(i, 0, at)

    def poll_y(self):
        g = self.g
        for i in range(g.sizes[0]):
            for dy in range(1, g.sizes[1]):
                at = self.out.at[g.slot(i, -dy, 0)]
                self.w.arrived(at, self.y0 + i * g.sizes[1] + dy)
                self.on_core(i, dy, at)

    def finish(self):
        g = self.g
        for i in range(g.sizes[0]):
            for dy in range(g.sizes[1]):
                for dc in range(1, g.sizes[2]):
                    at = self.out.at[g.slot(i, -dy, -dc)]
                    self.w.arrived(at, self.c0 + (i * g.sizes[1] + dy) * g.sizes[2] + dc)

        @pl.when(g.inner == 1)
        def _():
            for i in (2, 3):
                self.w.copy(self.own, self.own, self.on0 + i, self.z0 + i, g.s, g.k).wait_send()


class Tokens:
    def __init__(self, wires, packed, out):
        self.w, self.g, self.packed, self.out = wires, wires.g, packed, out
        self.a0, self.f0 = wires.block(self.g.shards), wires.block(self.g.shards)

    def lane(self, s, k):
        return self.out.at[:, s * self.g.shards + k]

    def start(self):
        g = self.g
        for d in range(1, g.shards):
            to = (g.k + d) % g.shards
            self.w.send(self.packed.at[to], self.lane(g.s, g.k), self.a0 + d, g.s, to, self.packed.at[0])
        self.w.send(self.packed.at[g.k], self.lane(g.s, g.k), self.f0, 1 - g.s, g.k, self.packed.at[0])

    def poll(self):
        g = self.g
        for d in range(1, g.shards):
            at = self.lane(g.s, (g.k - d) % g.shards)
            self.w.arrived(at, self.a0 + d)
            self.w.send(at, at, self.f0 + d, 1 - g.s, g.k, self.packed.at[0])

    def finish(self):
        g = self.g
        for d in range(g.shards):
            self.w.arrived(self.lane(1 - g.s, (g.k - d) % g.shards), self.f0 + d)


def side_by_side(vec, small, row, to, count):
    for j in range(small.shape[0]):
        vec[to : to + 1, j * count : (j + 1) * count] = small[j, row : row + 1, :count]


def forward_kernel(
    seqs, shards, counts, one_seq,
    packed, packed_cot, qkv_w, small, dense_w, fc1_w, fc2_w, slopes, idc, idr, beginc, live,
    x_out, cot_out, n1_out, n2_out, qkvw_out, dense_out, fc1_out, fc2_out, qkv_out, o_out, h2_out, a_out, slope_out,
    w2_out, vec_out,
    x_v, n1_v, n2_v, qkvw_v, small_v, dense_v, fc1_v, fc2_v, blocks_v, cot_v, qkv_v, o_v, h2_v, a_v, slope_v, w2_v, vec_v,
    send_sems, recv_sems, copy_sems,
):
    g = Geometry(seqs, shards)
    wires = Wires(g, send_sems, recv_sems)
    lanes = seqs * shards
    width = n1_v.shape[1]
    part = o_v.shape[2]
    pairs = part // (2 * HEAD)
    ff = fc1_v.shape[2]
    ff_part = ff // shards
    block = ROWS * lanes
    blocks = x_v.shape[0]
    half = block // seqs
    rows = width // shards
    local = []

    def bring(src, dst):
        made = pltpu.make_async_copy(src, dst, copy_sems.at[len(local)])
        made.start()
        local.append(made)
        return made

    def at_block(b):
        return pl.ds(pl.multiple_of(b * block, block), block)

    tokens = Tokens(wires, packed, x_v)
    cots = Tokens(wires, packed_cot, blocks_v)
    smalls_at = wires.block(shards)
    qkv_all = Gather(wires, qkvw_v.at[g.k], qkvw_v)
    dense_all = Gather(wires, dense_v.at[g.k], dense_v)
    up_all = Gather(wires, fc1_v.at[g.k], fc1_v)
    down_all = Gather(wires, fc2_v, fc2_out)
    heads_at = wires.block(pairs)

    staged_qkv = [
        bring(
            qkv_w.at[:, pl.ds(pl.multiple_of(p * width + g.s * part, 128), part)],
            qkvw_v.at[g.k, :, pl.ds(p * part, part)],
        )
        for p in range(3)
    ]
    staged_small = bring(small, small_v.at[g.k])
    staged_dense = bring(dense_w, dense_v.at[g.k])
    staged_up = [
        bring(
            fc1_w.at[:, pl.ds(pl.multiple_of((i * seqs + g.s) * ff_part, 128), ff_part)],
            fc1_v.at[g.k, :, pl.ds(i * ff_part, ff_part)],
        )
        for i in range(shards)
    ]
    staged_x = bring(packed.at[g.k], x_v.at[:, g.s * shards + g.k])
    staged_down = bring(fc2_w.at[pl.ds(pl.multiple_of(g.s * ff_part, 8), ff_part), :], fc2_v)
    staged_cot = bring(packed_cot.at[g.k], blocks_v.at[:, g.s * shards + g.k])
    enter(g)
    tokens.start()
    for made in staged_qkv:
        made.wait()
    qkv_all.start()
    staged_small.wait()
    for d in range(1, shards):
        wires.send(small_v.at[g.k], small_v.at[g.k], smalls_at + d, g.s, (g.k + d) % shards, small_v.at[0])
    staged_dense.wait()
    dense_all.start()
    tokens.poll()
    for made in staged_up:
        made.wait()
    up_all.start()
    qkv_all.poll_z()
    for d in range(1, shards):
        wires.arrived(small_v.at[(g.k - d) % shards], smalls_at + d)
    qkv_all.poll_y()
    cots.start()

    for row in (0, 1, 3, 4, 5, 7):
        side_by_side(vec_v, small_v, row, row, rows)
    vec_v[2:3, :] = jnp.zeros((1, vec_v.shape[1]), f32)
    per = 2 * width // shards
    for i in range(part // per):
        for row, side in ((0, 0), (2, 1)):
            j = (side * width + g.s * part) // per + i
            vec_v[2:3, row * part + i * per : row * part + (i + 1) * per] = small_v[j, 2:3, :per]
    for j in range(shards):
        vec_v[6:7, j * ff_part : (j + 1) * ff_part] = small_v[j, 6:7, pl.ds(pl.multiple_of(g.s * ff_part, 128), ff_part)]

    dense_all.poll_z()
    qkv_all.finish()
    kept = [bring(qkvw_v, qkvw_out), bring(vec_v, vec_out)]
    staged_x.wait()
    tokens.finish()
    kept.append(bring(x_v, x_out))
    staged_down.wait()
    down_all.start()
    kept.append(bring(fc2_v, fc2_out.at[g.k]))

    @pl.loop(0, blocks)
    def _(b):
        x = x_v[b].astype(f32).reshape(block, width)
        xhat, _ = normalize(x)
        n1 = (xhat * vec_v[0:1, :width] + vec_v[1:2, :width]).astype(bf16)
        at = at_block(b)
        n1_v[at, :] = n1
        for p in range(3):
            weight = qkvw_v[:, :, p * part : (p + 1) * part].reshape(width, part)
            out = jnp.dot(n1, weight, preferred_element_type=f32) + vec_v[2:3, p * part : (p + 1) * part]
            out = out.astype(bf16)
            for h in range(pairs):
                qkv_v[p * pairs + h, at, :] = out[:, h * 2 * HEAD : (h + 1) * 2 * HEAD]

    kept += [bring(n1_v, n1_out), bring(qkv_v, qkv_out)]
    dense_all.poll_y()
    up_all.poll_z()
    lane_id = lax.broadcasted_iota(jnp.int32, (1, 2 * HEAD), 1)

    tile = min(256, block)

    def cols_of(h):
        return pl.ds(pl.multiple_of(h * 2 * HEAD, 2 * HEAD), 2 * HEAD)

    def attend(h):
        q_ref, k_ref, v_ref = qkv_v.at[h], qkv_v.at[pairs + h], qkv_v.at[2 * pairs + h]
        for b in range(blocks):
            end = (b + 1) * block
            for t in range(block // tile):
                at = pl.ds(b * block + t * tile, tile)
                q = q_ref[at, :] * jnp.asarray(HEAD**-0.5, bf16)
                ids_q = idc[at, :]
                both = None
                for j in range(2):
                    mine = (lane_id // HEAD) == j
                    qj = jnp.where(mine, q, jnp.zeros_like(q))
                    s = lax.dot_general(
                        qj, k_ref[:end, :], (((1,), (1,)), ((), ())), preferred_element_type=f32
                    )
                    s = s + slopes[h, j] * idr[:, :end]
                    if one_seq:
                        tail = attn_mask(s[:, b * block :], idr[:, b * block : end] <= ids_q)
                        s = jnp.concatenate([s[:, : b * block], tail], axis=1) if b else tail
                    else:
                        ids_k = idr[:, :end]
                        s = attn_mask(s, (ids_k <= ids_q) & (ids_k >= beginc[at, :]))
                    top = jnp.max(s, axis=1, keepdims=True)
                    e = jnp.exp(s - top)
                    total = jnp.sum(e, axis=1, keepdims=True)
                    o = jnp.dot(e.astype(bf16), v_ref[:end, :], preferred_element_type=f32) / total
                    both = o if both is None else jnp.where(mine, o, both)
                o_v[g.s, at, cols_of(h)] = both.astype(bf16)

    def head_copy(h):
        mine = o_v.at[g.s, :, cols_of(h)]
        return wires.copy(mine, mine, heads_at + h, heads_at + h, 1 - g.s, g.k)

    @pl.loop(0, pairs)
    def _(h):
        attend(h)

        @pl.when(h == 1)
        def _():
            up_all.poll_y()

        head_copy(h).start()

    dense_all.finish()
    kept.append(bring(dense_v, dense_out))
    cots.poll()
    for h in range(pairs):
        wires.arrived(o_v.at[1 - g.s, :, cols_of(h)], heads_at + h)
    up_all.finish()
    kept += [bring(fc1_v, fc1_out), bring(o_v, o_out)]

    @pl.loop(0, blocks)
    def _(b):
        at = at_block(b)
        branch = jnp.dot(
            o_v[0, at, :], dense_v[: shards // 2].reshape(part, width), preferred_element_type=f32
        ) + jnp.dot(o_v[1, at, :], dense_v[shards // 2 :].reshape(part, width), preferred_element_type=f32)
        resid = x_v[b].astype(f32).reshape(block, width) + branch + vec_v[3:4, :width]
        h2_v[b] = jnp.where(g.s == 0, resid[:half], resid[half:])
        xhat, _ = normalize(resid)
        n2 = (xhat * vec_v[4:5, :width] + vec_v[5:6, :width]).astype(bf16)
        n2_v[at, :] = n2
        step = min(512, ff)
        for n in range(ff // step):
            cut = slice(n * step, (n + 1) * step)
            u = jnp.dot(n2, fc1_v[:, :, cut].reshape(width, step), preferred_element_type=f32) + vec_v[6:7, cut]
            inside = 0.7978845608028654 * u * (1.0 + 0.044715 * u * u)
            t = jnp.tanh(inside)
            a_v[at, cut] = (0.5 * u * (1.0 + t)).astype(bf16)
            slope = 0.5 * (1.0 + t) + 0.5 * u * (1.0 - t * t) * (
                0.7978845608028654 + (0.7978845608028654 * 3.0 * 0.044715) * u * u
            )
            slope_v[at, cut] = slope.astype(bf16)

        @pl.when(b == 1)
        def _():
            down_all.poll_z()

    kept += [bring(n2_v, n2_out), bring(h2_v, h2_out), bring(a_v, a_out), bring(slope_v, slope_out)]
    staged_cot.wait()
    cots.finish()
    down_all.poll_y()

    @pl.loop(0, blocks)
    def _(b):
        at = at_block(b)
        grad = blocks_v[b].astype(f32).reshape(block, width)
        cot_v[at, :] = jnp.where(live[at, :] > 0, grad, 0.0).astype(bf16)

    kept.append(bring(cot_v, cot_out))

    @pl.loop(0, ff // (2 * ff_part))
    def _(m):
        cut = a_v[:, pl.ds(pl.multiple_of(m * 2 * ff_part, 128), 2 * ff_part)]
        out = lax.dot_general(cut, cot_v[...], (((0,), (0,)), ((), ())), preferred_element_type=f32).astype(bf16)
        w2_v[pl.ds(2 * m, 2)] = out.reshape(2, ff_part, width)

    kept.append(bring(w2_v, w2_out))
    down_all.finish()
    for h in range(pairs):
        head_copy(h).wait_send()
    wires.drain()
    for made in kept:
        made.wait()
    assert wires.used <= counts[0] and len(local) <= counts[1]


def forward_exchange(packed, packed_cot, qkv_w, small, dense_w, fc1_w, fc2_w, slopes, ids, begins, live, seqs, shards, one_seq):
    width, own = qkv_w.shape[0] * shards, qkv_w.shape[0]
    lanes = seqs * shards
    blocks = packed.shape[1]
    block = lanes * ROWS
    cap = blocks * block
    part = width // seqs
    pairs = part // (2 * HEAD)
    ff = fc1_w.shape[1] // seqs
    ff_part = ff // shards
    counts = (320, 64)
    any_ = pl.BlockSpec(memory_space=pl.ANY)
    vmem = pl.BlockSpec(memory_space=pltpu.VMEM)
    smem = pl.BlockSpec(memory_space=pltpu.SMEM)
    x_shape = ((blocks, lanes, ROWS, width), bf16)
    wide, long = ((cap, width), bf16), ((cap, ff), bf16)
    qkvw, dense, fc1, fc2 = (
        ((shards,) + tail, bf16) for tail in ((own, 3 * part), (own, width), (own, ff), (ff_part, width))
    )
    qkv, heads = ((3 * pairs, cap, 2 * HEAD), bf16), ((seqs, cap, part), bf16)
    h2, vec = ((blocks, block // seqs, width), f32), ((8, max(width, 3 * part, ff)), f32)
    outs = [x_shape, wide, wide, wide, qkvw, dense, fc1, fc2, qkv, heads, h2, long, long, fc2, vec]
    scratch = [
        x_shape, wide, wide, qkvw, ((shards,) + small.shape, f32), dense, fc1, ((ff_part, width), bf16), x_shape, wide,
        qkv, heads, h2, long, long, fc2, vec,
    ]
    return pl.pallas_call(
        functools.partial(forward_kernel, seqs, shards, counts, one_seq),
        in_specs=[any_] * 7 + [smem] + [vmem] * 4,
        out_specs=[any_] * len(outs),
        out_shape=[jax.ShapeDtypeStruct(s, d) for s, d in outs],
        scratch_shapes=[pltpu.VMEM(s, d) for s, d in scratch]
        + [pltpu.SemaphoreType.DMA((counts[0],)), pltpu.SemaphoreType.DMA((counts[0],)), pltpu.SemaphoreType.DMA((counts[1],))],
        compiler_params=pltpu.CompilerParams(collective_id=1, has_side_effects=True, vmem_limit_bytes=60 * 2**20),
        name="forward_exchange",
    )(
        packed, packed_cot, qkv_w, small, dense_w, fc1_w, fc2_w, slopes.reshape(pairs, 2),
        ids[:, None], ids[None, :], begins[:, None], live[:, None],
    )


class Scatter:
    def __init__(self, wires, full, own, bufs):
        self.w, self.g, self.full, self.own = wires, wires.g, full, own
        self.rc, self.ry, self.rz, self.fin = bufs
        self.at = wires.block(8)

    def add(self, count, into, other):
        @pl.loop(0, count)
        def _(i):
            a, b = into(i), other(i)
            a[...] = (a[...].astype(f32) + b[...].astype(f32)).astype(bf16)

    def core_send(self):
        g = self.g
        self.w.send(self.full.at[:, :, 1 - g.c], self.rc, self.at, g.s, g.slot(0, 0, 1), self.rc)

    def core_done(self):
        g = self.g
        self.w.arrived(self.rc, self.at)
        self.add(8, lambda i: self.rc.at[i // 2, i % 2], lambda i: self.own(i // 2, i % 2))
        self.w.send(self.rc.at[:, 1 - g.y], self.ry, self.at + 1, g.s, g.slot(0, 1, 0), self.ry)

    def y_done(self):
        g = self.g
        self.w.arrived(self.ry, self.at + 1)
        self.add(4, lambda i: self.ry.at[i], lambda i: self.rc.at[i, g.y])

    def z_send(self):
        g = self.g
        partner = g.slot(1, 0, 0)
        self.w.send(self.ry.at[g.line[1]], self.rz.at[0], self.at + 2, g.s, partner, self.rz.at[0])

        @pl.when(g.inner == 0)
        def _():
            for i in (2, 3):
                self.w.copy(self.ry.at[g.line[i]], self.rz.at[i], self.at + 1 + i, self.at + 1 + i, g.s, partner).start()

    def z_done(self):
        g = self.g

        @pl.when(g.inner == 1)
        def _():
            for i in (2, 3):
                self.w.arrived(self.rz.at[i], self.at + 1 + i)
                a = self.rz.at[i]
                a[...] = (a[...].astype(f32) + self.ry[g.line[i]].astype(f32)).astype(bf16)
                self.w.copy(a, self.rz.at[1], self.at + 1 + i, self.at + 5, g.s, g.slot(i, 0, 0)).start()

    def final(self):
        g = self.g
        self.w.arrived(self.rz.at[0], self.at + 2)
        self.w.arrived(self.rz.at[1], self.at + 5)
        total = self.ry[g.z].astype(f32) + self.rz[0].astype(f32) + self.rz[1].astype(f32)
        self.fin[0] = total.astype(bf16)
        self.w.send(self.fin.at[0], self.fin.at[1], self.at + 6, 1 - g.s, g.k, self.fin.at[0])

    def done(self):
        self.w.arrived(self.fin.at[1], self.at + 6)
        for i in (2, 3):
            self.w.copy(self.fin.at[0], self.fin.at[0], self.at + 1 + i, self.at + 1 + i, self.g.s, self.g.k).wait_send()


class Back:
    def __init__(self, wires, src, dst, pieces):
        self.w, self.g, self.src, self.dst, self.pieces = wires, wires.g, src, dst, pieces
        self.at = wires.block(wires.g.shards * pieces)
        self.per = src.shape[0] // pieces

    def cut(self, ref, i):
        return ref.at[pl.ds(i * self.per, self.per)]

    def send(self, i):
        g = self.g
        for d in range(1, g.shards):
            to = (g.k + d) % g.shards
            src = self.src.at[pl.ds(i * self.per, self.per), to]
            self.w.send(src, self.cut(self.dst.at[g.k], i), self.at + i * g.shards + d, g.s, to, src)

    def finish(self):
        g = self.g
        for i in range(self.pieces):
            for d in range(1, g.shards):
                self.w.arrived(self.cut(self.dst.at[(g.k - d) % g.shards], i), self.at + i * g.shards + d)


def middle_kernel(
    seqs, shards, counts,
    a, slope, n2, fc1, fc2, dense, cot, h2, heads, w2, vec,
    dh2_out, do_out, w1_out, wd_out, keep_out, give_out, ry_out, small_out,
    a_v, du_v, n2_v, fc1_v, fc2_v, dense_v, cot_v, h2_v, heads_v, own_w2, w1_v, wd_v, mine_v, sent_v, got_v,
    da_v, do_v, do_sent, small_v, rc, ry,
    send_sems, recv_sems, copy_sems,
):
    g = Geometry(seqs, shards)
    wires = Wires(g, send_sems, recv_sems)
    blocks, half, width = h2_v.shape
    block = half * seqs
    ff = a_v.shape[1]
    ff_part = ff // shards
    rows = width // shards
    part = width // seqs
    local = []

    def bring(src, dst):
        made = pltpu.make_async_copy(src, dst, copy_sems.at[len(local)])
        made.start()
        local.append(made)
        return made

    def at_block(b):
        return pl.ds(pl.multiple_of(b * block, block), block)

    def own_rows(b):
        return pl.ds(pl.multiple_of(b * block + g.s * half, half), half)

    down = Scatter(wires, w2, lambda i, j: own_w2.at[i, j], (rc, ry, None, None))
    half_at, do_at = wires.block(blocks), wires.block(blocks)
    first = [bring(cot, cot_v), bring(fc2, fc2_v), bring(slope, du_v), bring(fc1, fc1_v)]
    own = bring(w2.at[:, :, g.c], own_w2)
    later = [bring(n2, n2_v), bring(a, a_v), bring(h2, h2_v), bring(dense, dense_v)]
    later += [bring(heads.at[i, own_rows(b), :], heads_v.at[i, pl.ds(b * half, half)]) for i in range(seqs) for b in range(blocks)]
    enter(g)
    down.core_send()
    for made in first:
        made.wait()
    step = min(512, ff)
    per = step // ff_part

    def half_copy(b):
        return wires.copy(sent_v.at[b], got_v.at[b], half_at + b, half_at + b, 1 - g.s, g.k)

    def do_copy(b):
        return wires.copy(do_sent.at[b], do_v.at[b, g.s], do_at + b, do_at + b, 1 - g.s, g.k)

    small_v[...] = jnp.zeros_like(small_v)

    def split(b, total, keep, give):
        @pl.when(g.s == 0)
        def _():
            keep(total[:half])
            give[b] = total[half:].astype(bf16)

        @pl.when(g.s == 1)
        def _():
            keep(total[half:])
            give[b] = total[:half].astype(bf16)

    def du_step(b, sums):
        at = at_block(b)
        grad = cot_v[at, :]
        total, new = None, []
        for n in range(ff // step):
            cut = slice(n * step, (n + 1) * step)
            weight = fc2_v[n * per : (n + 1) * per].reshape(step, width)
            da = lax.dot_general(grad, weight, (((1,), (1,)), ((), ())), preferred_element_type=f32)
            du = (da * du_v[at, cut].astype(f32)).astype(bf16)
            du_v[at, cut] = du
            new.append(sums[n] + jnp.sum(du.astype(f32), axis=0, keepdims=True))
            weight = fc1_v[:, :, cut].reshape(width, step)
            term = lax.dot_general(du, weight, (((1,), (1,)), ((), ())), preferred_element_type=f32)
            total = term if total is None else total + term

        def keep(value):
            mine_v[b] = value

        split(b, total, keep, sent_v)

        @pl.when(b > 0)
        def _():
            half_copy(b - 1).start()

        @pl.when(b == 0)
        def _():
            own.wait()
            down.core_done()

        return tuple(new)

    zero = jnp.zeros((1, step), f32)
    sums = lax.fori_loop(0, blocks, du_step, (zero,) * (ff // step))
    for made in later:
        made.wait()

    @pl.loop(0, width // (4 * rows))
    def _(m):
        @pl.when(m == 0)
        def _():
            half_copy(blocks - 1).start()

        left = n2_v[:, pl.ds(pl.multiple_of(m * 4 * rows, 128), 4 * rows)]
        for n in range(ff // step):
            cut = slice(n * step, (n + 1) * step)
            out = lax.dot_general(left, du_v[:, cut], (((0,), (0,)), ((), ())), preferred_element_type=f32)
            w1_v[pl.ds(4 * m, 4), :, cut] = out.astype(bf16).reshape(4, rows, step)

    kept = [bring(w1_v, w1_out)]
    for n in range(ff // step):
        for i in range(per):
            small_v[n * per + i, 6:7, pl.ds(pl.multiple_of(g.s * ff_part, 128), ff_part)] = sums[n][
                :, i * ff_part : (i + 1) * ff_part
            ]

    def norm_step(b, sums):
        gains, biases, branch, cots = sums
        wires.arrived(got_v.at[b], half_at + b)
        grad = mine_v[b] + got_v[b].astype(f32)
        xhat, root = normalize(h2_v[b])
        gains = gains + jnp.sum(grad * xhat, axis=0, keepdims=True)
        biases = biases + jnp.sum(grad, axis=0, keepdims=True)
        cot_b = cot_v[own_rows(b), :].astype(f32)
        cots = cots + jnp.sum(cot_b, axis=0, keepdims=True)
        dh2 = cot_b + norm_pull(grad, vec[4:5, :width], xhat, root)
        mine_v[b] = dh2
        da = dh2.astype(bf16)
        branch = branch + jnp.sum(da.astype(f32), axis=0, keepdims=True)
        da_v[pl.ds(pl.multiple_of(b * half, half), half), :] = da
        grads = [
            lax.dot_general(
                da, dense_v[i * (shards // seqs) : (i + 1) * (shards // seqs)].reshape(part, width),
                (((1,), (1,)), ((), ())), preferred_element_type=f32,
            ).astype(bf16)
            for i in range(seqs)
        ]
        do_v[b, g.s] = jnp.where(g.s == 0, grads[0], grads[1])
        do_sent[b] = jnp.where(g.s == 0, grads[1], grads[0])

        @pl.when(b > 0)
        def _():
            do_copy(b - 1).start()

        return gains, biases, branch, cots

    zero = jnp.zeros((1, width), f32)
    sums = lax.fori_loop(0, blocks, norm_step, (zero,) * 4)
    kept.append(bring(mine_v, dh2_out))
    for row, vector in ((4, sums[0]), (5, sums[1]), (3, sums[2]), (7, sums[3])):
        for j in range(shards):
            small_v[j, row : row + 1, :rows] = vector[:, j * rows : (j + 1) * rows]
    do_copy(blocks - 1).start()
    kept.append(bring(small_v, small_out))

    for i in range(seqs):
        out = lax.dot_general(heads_v[i], da_v[...], (((0,), (0,)), ((), ())), preferred_element_type=f32).astype(bf16)
        wd_v[i * (shards // seqs) : (i + 1) * (shards // seqs)] = out.reshape(shards // seqs, rows, width)
    kept.append(bring(wd_v, wd_out))

    @pl.loop(0, blocks)
    def _(b):
        at = at_block(b)
        total = None
        for n in range(ff // step):
            weight = fc2_v[n * per : (n + 1) * per].reshape(step, width)
            term = jnp.dot(a_v[at, n * step : (n + 1) * step], weight, preferred_element_type=f32)
            total = term if total is None else total + term

        def keep(value):
            h2_v[b] = h2_v[b] + value + vec[7:8, :width]

        split(b, total, keep, got_v)

    kept += [bring(h2_v, keep_out), bring(got_v, give_out)]
    down.y_done()
    kept.append(bring(ry, ry_out))
    for b in range(blocks):
        wires.arrived(do_v.at[b, 1 - g.s], do_at + b)
    kept.append(bring(do_v, do_out))
    for b in range(blocks):
        half_copy(b).wait_send()
        do_copy(b).wait_send()
    wires.drain()
    for made in kept:
        made.wait()
    assert wires.used <= counts[0] and len(local) <= counts[1]


def middle_exchange(a, slope, n2, fc1, fc2, dense, cot, h2, heads, w2, vec, seqs, shards):
    blocks, half, width = h2.shape
    tokens, ff = a.shape
    part = width // seqs
    rows, ff_part = width // shards, ff // shards
    counts = (32, 40)
    any_, vmem = pl.BlockSpec(memory_space=pl.ANY), pl.BlockSpec(memory_space=pltpu.VMEM)
    own32, own16 = ((blocks, half, width), f32), ((blocks, half, width), bf16)
    do, smalls = ((blocks, seqs, half, part), bf16), ((shards, 8, 256), f32)
    w1, wd, ry = ((shards, rows, ff), bf16), ((shards, rows, width), bf16), ((4, ff_part, width), bf16)
    outs = [own32, do, w1, wd, own32, own16, ry, smalls]
    rc = ((4, 2, ff_part, width), bf16)
    scratch = [(v.shape, bf16) for v in (a, slope, n2, fc1, fc2, dense, cot)] + [
        own32, ((seqs, blocks * half, part), bf16), rc, w1, wd, own32, own16, own16, ((blocks * half, width), bf16), do,
        ((blocks, half, part), bf16), smalls, rc, ry,
    ]
    return pl.pallas_call(
        functools.partial(middle_kernel, seqs, shards, counts),
        in_specs=[any_] * 10 + [vmem],
        out_specs=[any_] * len(outs),
        out_shape=[jax.ShapeDtypeStruct(s, d) for s, d in outs],
        scratch_shapes=[pltpu.VMEM(s, d) for s, d in scratch]
        + [pltpu.SemaphoreType.DMA((counts[0],)), pltpu.SemaphoreType.DMA((counts[0],)), pltpu.SemaphoreType.DMA((counts[1],))],
        compiler_params=pltpu.CompilerParams(collective_id=3, has_side_effects=True, vmem_limit_bytes=62 * 2**20),
        name="middle_exchange",
    )(a, slope, n2, fc1, fc2, dense, cot, h2, heads, w2.reshape((4, 2, 2) + w2.shape[1:]), vec)


def backward_kernel(
    seqs, shards, counts, one_seq,
    qkv, do, n1, qkvw, x_all, dh2, keep, give, ry2, w1, wd, smalls, vec, slopes, idc, idr, beginr,
    ret_y, ret_x, o_qkv, o_dense, o_up, o_down, o_small,
    qkv_v, do_v, dqkv_v, n1_v, qkvw_v, x_v, dh2_v, dk_acc, dv_acc, bias_acc, mine_v, sent_v, got_v, dx_v, gq_v,
    small_v, small_got, small_fin, small_last, f_qkv, f_dense, f_up, f_down, keep_v, give_v, y_v, own_w1, own_wd,
    *rest,
):
    bufs, (send_sems, recv_sems, copy_sems) = rest[:-3], rest[-3:]
    g = Geometry(seqs, shards)
    wires = Wires(g, send_sems, recv_sems)
    pairs, tokens = do_v.shape[0], do_v.shape[1]
    part = pairs * 2 * HEAD
    width = n1_v.shape[1]
    lanes = seqs * shards
    block = ROWS * lanes
    blocks = tokens // block
    half = block // seqs
    tile = bias_acc.shape[2]
    local = []

    def bring(src, dst):
        made = pltpu.make_async_copy(src, dst, copy_sems.at[len(local)])
        made.start()
        local.append(made)
        return made

    def held(ref):
        return lambda i, j: ref.at[i, j]

    down = Scatter(wires, None, None, (None,) + bufs[0:3])
    up = Scatter(wires, w1, held(own_w1), bufs[3:7])
    dense = Scatter(wires, wd, held(own_wd), bufs[7:11])
    qkv_sum = Scatter(wires, gq_v, lambda i, j: gq_v.at[i, j, g.c], bufs[11:15])
    back_y = Back(wires, y_v, ret_y, 1)
    give_at = wires.block(1)
    back_x = Back(wires, dx_v, ret_x, blocks)
    half_at = wires.block(blocks)
    small_at = wires.block(shards + 1)

    ry_in = bring(ry2, down.ry)
    first = [bring(qkv, qkv_v)] + [bring(do.at[:, pl.ds(h * 2 * HEAD, 2 * HEAD)], do_v.at[h]) for h in range(pairs)]
    owns = [bring(a.at[:, :, g.c], b) for a, b in ((w1, own_w1), (wd, own_wd))] + [bring(keep, keep_v)]
    later = [
        bring(n1, n1_v), bring(qkvw, qkvw_v), bring(x_all.at[:, pl.ds(g.s * shards, shards)], x_v), bring(dh2, dh2_v),
        bring(smalls, small_v),
    ]
    enter(g)
    up.core_send()
    dense.core_send()
    ry_in.wait()
    down.z_send()
    wires.send(give, give_v, give_at, 1 - g.s, g.k, give)
    for made in first + owns:
        made.wait()

    lane_id = lax.broadcasted_iota(jnp.int32, (1, 2 * HEAD), 1)

    def attend(h):
        q_ref, k_ref, v_ref, do_ref = qkv_v.at[h], qkv_v.at[pairs + h], qkv_v.at[2 * pairs + h], do_v.at[h]
        dk_acc[...] = jnp.zeros_like(dk_acc)
        dv_acc[...] = jnp.zeros_like(dv_acc)
        for j in range(2):
            bias_acc[j] = jnp.broadcast_to(slopes[h, j] * idc[...], bias_acc.shape[1:])
        cols = pl.ds(pl.multiple_of(h * 2 * HEAD, 2 * HEAD), 2 * HEAD)
        for b in range(blocks):
            end = (b + 1) * block
            for t in range(block // tile):
                at = pl.ds(b * block + t * tile, tile)
                q = q_ref[at, :] * jnp.asarray(HEAD**-0.5, bf16)
                grad = do_ref[at, :]
                ids_q = idr[:, at]
                both = None
                for j in range(2):
                    mine = (lane_id // HEAD) == j
                    qj = jnp.where(mine, q, jnp.zeros_like(q))
                    doj = jnp.where(mine, grad, jnp.zeros_like(grad))
                    s = lax.dot_general(
                        k_ref[:end, :], qj, (((1,), (1,)), ((), ())), preferred_element_type=f32
                    )
                    s = s + bias_acc[j, :end, :]
                    if one_seq:
                        tail = attn_mask(s[b * block :, :], idc[b * block : end, :] <= ids_q)
                        s = jnp.concatenate([s[: b * block, :], tail], axis=0) if b else tail
                    else:
                        ids_k = idc[:end, :]
                        s = attn_mask(s, (ids_k <= ids_q) & (ids_k >= beginr[:, at]))
                    top = jnp.max(s, axis=0, keepdims=True)
                    e = jnp.exp(s - top)
                    probs = e * (1.0 / jnp.sum(e, axis=0, keepdims=True))
                    dv_acc[:end, :] += jnp.dot(probs.astype(bf16), doj, preferred_element_type=f32)
                    dp = lax.dot_general(
                        v_ref[:end, :], doj, (((1,), (1,)), ((), ())), preferred_element_type=f32
                    )
                    inner = jnp.sum(probs * dp, axis=0, keepdims=True)
                    ds = (probs * (dp - inner)).astype(bf16)
                    dk_acc[:end, :] += jnp.dot(ds, qj, preferred_element_type=f32)
                    dq = lax.dot_general(
                        ds, k_ref[:end, :], (((0,), (0,)), ((), ())), preferred_element_type=f32
                    )
                    both = dq if both is None else jnp.where(mine, dq, both)
                dqkv_v[0, at, cols] = (both * (HEAD**-0.5)).astype(bf16)
        dqkv_v[1, :, cols] = dk_acc[...].astype(bf16)
        dqkv_v[2, :, cols] = dv_acc[...].astype(bf16)

    @pl.loop(0, pairs)
    def _(h):
        attend(h)

        @pl.when(h == 0)
        def _():
            up.core_done()

        @pl.when(h == 1)
        def _():
            dense.core_done()

        @pl.when(h == 2)
        def _():
            down.z_done()

    wires.arrived(give_v, give_at)

    @pl.loop(0, blocks)
    def _(b):
        y_v[b] = (keep_v[b] + give_v[b].astype(f32)).reshape(shards, ROWS, width).astype(bf16)

    for made in later:
        made.wait()

    for b in range(blocks):
        total = None
        for p in range(3):
            weight = qkvw_v[:, :, p * part : (p + 1) * part].reshape(width, part)
            term = lax.dot_general(
                dqkv_v[p, b * block : (b + 1) * block, :], weight, (((1,), (1,)), ((), ())), preferred_element_type=f32
            )
            total = term if total is None else total + term

        @pl.when(g.s == 0)
        def _(total=total, b=b):
            mine_v[b] = total[:half]
            sent_v[b] = total[half:].astype(bf16)

        @pl.when(g.s == 1)
        def _(total=total, b=b):
            mine_v[b] = total[half:]
            sent_v[b] = total[:half].astype(bf16)

        if b:
            wires.send(sent_v.at[b - 1], got_v.at[b - 1], half_at + b - 1, 1 - g.s, g.k, sent_v.at[b - 1])
    back_y.send(0)
    own_y = bring(y_v.at[:, g.k], ret_y.at[g.k])
    wires.send(sent_v.at[blocks - 1], got_v.at[blocks - 1], half_at + blocks - 1, 1 - g.s, g.k, sent_v.at[0])

    rows = width // shards

    @pl.loop(0, blocks)
    def _(m):
        cut = n1_v[:, pl.ds(pl.multiple_of(m * block, block), block)]
        for p in range(3):
            out = lax.dot_general(cut, dqkv_v[p], (((0,), (0,)), ((), ())), preferred_element_type=f32).astype(bf16)
            out = out.reshape(block // rows // 2, 2, rows, part)
            for i in range(block // rows // 2):
                at = m * (block // rows // 2) + i
                for j in range(2):
                    gq_v[at // 2, at % 2, j, :, p * part : (p + 1) * part] = out[i, j]

    sums = [jnp.sum(dqkv_v[p].astype(f32), axis=0, keepdims=True) for p in (0, 2)]
    per = 2 * width // shards
    for i in range(part // per):
        for half_no in range(2):
            small_v[(half_no * width + g.s * part) // per + i, 2:3, :per] = sums[half_no][:, i * per : (i + 1) * per]
    qkv_sum.core_send()
    up.y_done()
    up.z_send()

    gains = biases = jnp.zeros((1, width), f32)
    for b in range(blocks):
        wires.arrived(got_v.at[b], half_at + b)
        grad = mine_v[b] + got_v[b].astype(f32)
        xhat, root = normalize(x_v[b].astype(f32).reshape(half, width))
        gains = gains + jnp.sum(grad * xhat, axis=0, keepdims=True)
        biases = biases + jnp.sum(grad, axis=0, keepdims=True)
        dx = dh2_v[b] + norm_pull(grad, vec[0:1, :width], xhat, root)
        dx_v[b] = dx.reshape(shards, ROWS, width).astype(bf16)
        back_x.send(b)
        if b == 1:
            qkv_sum.core_done()
    for j in range(shards):
        small_v[j, 0:1, :rows] = gains[:, j * rows : (j + 1) * rows]
        small_v[j, 1:2, :rows] = biases[:, j * rows : (j + 1) * rows]
    kept = [own_y, bring(dx_v.at[:, g.k], ret_x.at[g.k])]
    for d in range(1, shards):
        to = (g.k + d) % shards
        wires.send(small_v.at[to], small_got.at[g.k], small_at + d, g.s, to, small_v.at[0])
    small_got[g.k] = small_v[g.k]
    dense.y_done()
    dense.z_send()
    up.z_done()
    down.final()
    qkv_sum.y_done()
    qkv_sum.z_send()
    dense.z_done()
    for d in range(1, shards):
        wires.arrived(small_got.at[(g.k - d) % shards], small_at + d)
    small_fin[0] = jnp.sum(small_got[...], axis=0)
    wires.send(small_fin.at[0], small_fin.at[1], small_at + shards, 1 - g.s, g.k, small_fin.at[0])
    up.final()
    dense.final()
    qkv_sum.z_done()

    down.done()
    ff_part = f_down.shape[0] // seqs
    for i, at in ((0, g.s), (1, 1 - g.s)):
        f_down[pl.ds(pl.multiple_of(at * ff_part, ff_part), ff_part), :] = down.fin[i].astype(f32)
    kept.append(bring(f_down, o_down))
    up.done()
    for i, at in ((0, g.s), (1, 1 - g.s)):
        for j in range(shards):
            f_up[:, pl.ds(pl.multiple_of((j * seqs + at) * ff_part, 128), ff_part)] = up.fin[
                i, :, j * ff_part : (j + 1) * ff_part
            ].astype(f32)
    kept.append(bring(f_up, o_up))
    dense.done()
    f_dense[...] = dense.fin[0].astype(f32) + dense.fin[1].astype(f32)
    kept.append(bring(f_dense, o_dense))
    wires.arrived(small_fin.at[1], small_at + shards)
    small_last[...] = small_fin[0] + small_fin[1]
    kept.append(bring(small_last, o_small))
    qkv_sum.final()
    qkv_sum.done()
    for i, at in ((0, g.s), (1, 1 - g.s)):
        for p in range(3):
            f_qkv[:, pl.ds(pl.multiple_of(p * width + at * part, 128), part)] = qkv_sum.fin[
                i, :, p * part : (p + 1) * part
            ].astype(f32)
    kept.append(bring(f_qkv, o_qkv))
    back_y.finish()
    back_x.finish()
    wires.drain()
    for made in kept:
        made.wait()
    assert wires.used <= counts[0] and len(local) <= counts[1]


def backward_exchange(
    qkv, do, n1, qkvw, x_all, dh2, keep, give, ry2, w1, wd, smalls, vec, slopes, ids, begins, seqs, shards, one_seq
):
    tokens, part = do.shape
    width = n1.shape[1]
    pairs = part // (2 * HEAD)
    lanes = seqs * shards
    block = ROWS * lanes
    blocks, half = tokens // block, block // seqs
    tile = min(256, block)
    rows, ff = width // shards, w1.shape[2]
    ff_part = ff // shards
    counts = (256, 48)
    cut = lambda a: a.reshape((4, 2, 2) + a.shape[1:])
    any_, vmem = pl.BlockSpec(memory_space=pl.ANY), pl.BlockSpec(memory_space=pltpu.VMEM)
    ret = (shards, blocks, ROWS, width)
    outs = [
        (ret, bf16), (ret, bf16), ((rows, 3 * width), f32), ((rows, width), f32), ((rows, seqs * ff), f32),
        ((seqs * ff_part, width), f32), (smalls.shape[1:], f32),
    ]
    blks = [(ff_part, width), (rows, ff), (rows, width), (rows, 3 * part)]
    scratch = [
        ((3 * pairs, tokens, 2 * HEAD), bf16), ((pairs, tokens, 2 * HEAD), bf16), ((3, tokens, part), bf16),
        ((tokens, width), bf16), ((shards, rows, 3 * part), bf16), ((blocks, shards, ROWS, width), bf16),
        ((blocks, half, width), f32), ((tokens, 2 * HEAD), f32), ((tokens, 2 * HEAD), f32), ((2, tokens, tile), f32),
        ((blocks, half, width), f32), ((blocks, half, width), bf16), ((blocks, half, width), bf16),
        ((blocks, shards, ROWS, width), bf16), ((4, 2, 2) + blks[3], bf16), (smalls.shape, f32), (smalls.shape, f32),
        ((2,) + smalls.shape[1:], f32), (smalls.shape[1:], f32), ((rows, 3 * width), f32), ((rows, width), f32), ((rows, seqs * ff), f32),
        ((seqs * ff_part, width), f32), ((blocks, half, width), f32), ((blocks, half, width), bf16),
        ((blocks, shards, ROWS, width), bf16), ((4, 2) + blks[1], bf16), ((4, 2) + blks[2], bf16),
    ]
    for blk in blks:
        scratch += [((4, 2) + blk, bf16)] * (blk is not blks[0])
        scratch += [((4,) + blk, bf16), ((4,) + blk, bf16), ((2,) + blk, bf16)]
    return pl.pallas_call(
        functools.partial(backward_kernel, seqs, shards, counts, one_seq),
        in_specs=[any_] * 12 + [vmem, pl.BlockSpec(memory_space=pltpu.SMEM)] + [vmem] * 3,
        out_specs=[any_] * len(outs),
        out_shape=[jax.ShapeDtypeStruct(s, d) for s, d in outs],
        scratch_shapes=[pltpu.VMEM(s, d) for s, d in scratch]
        + [pltpu.SemaphoreType.DMA((counts[0],)), pltpu.SemaphoreType.DMA((counts[0],)), pltpu.SemaphoreType.DMA((counts[1],))],
        compiler_params=pltpu.CompilerParams(collective_id=2, has_side_effects=True, vmem_limit_bytes=60 * 2**20),
        name="backward_exchange",
    )(
        qkv, do, n1, qkvw, x_all, dh2, keep, give, ry2, cut(w1), cut(wd), smalls, vec, slopes.reshape(pairs, 2),
        ids[:, None], ids[None, :], begins[None, :],
    )


def layout_tables(lengths, lane_count, group_count, per_group):
    seq_rows = lengths // lane_count
    row_start = jnp.cumsum(seq_rows) - seq_rows
    slot_rows = seq_rows.reshape(group_count, per_group)
    slot_start = row_start.reshape(group_count, per_group)
    slot_before = jnp.cumsum(slot_rows, axis=1) - slot_rows
    return seq_rows, row_start, slot_rows, slot_start, slot_before


def per_device(
    tokens, cotangent, lengths, first_gain, first_bias, qkv_weight, qv_bias, dense_weight, dense_bias,
    second_gain, second_bias, fc1_weight, fc1_bias, fc2_weight, fc2_bias,
):
    shards, seqs = lax.axis_size("shard"), lax.axis_size("seq")
    lanes = shards * seqs
    slots, width = tokens.shape[1], tokens.shape[2]
    rows = slots // shards
    cap = slots * seqs
    per_group = lengths.shape[0] // shards
    hidden_units = fc1_weight.shape[1]
    me, group = lax.axis_index("seq"), lax.axis_index("shard")
    blocks = rows // ROWS
    heads = width // HEAD // seqs
    part = heads * HEAD
    ff_part = hidden_units // shards // seqs

    smalls_in = (first_gain, first_bias, qv_bias, dense_bias, second_gain, second_bias, fc1_bias, fc2_bias)
    small_width = -(-max(a.shape[0] for a in smalls_in) // 128) * 128
    small = jnp.stack([jnp.pad(a.astype(f32), (0, small_width - a.shape[0])) for a in smalls_in])

    seq_rows, row_start, slot_rows, slot_start, slot_before = layout_tables(lengths, lanes, shards, per_group)
    row_in = jnp.arange(rows, dtype=jnp.int32)[None, :, None]
    inside = ((row_in >= slot_before[:, None]) & (row_in < (slot_before + slot_rows)[:, None])).astype(jnp.int32)
    send_live = jnp.sum(inside, axis=2) > 0
    send_row = jnp.sum(inside * (slot_start[:, None] + row_in - slot_before[:, None]), axis=2).reshape(-1)

    def pack(source):
        return jnp.take(source, send_row, axis=0).reshape(shards, rows, width)

    place = jnp.arange(cap, dtype=jnp.int32)
    block_of, in_block = place // (ROWS * lanes), place % (ROWS * lanes)
    row_of = block_of * ROWS + in_block % ROWS
    ids = row_of * lanes + in_block // ROWS
    own_before, own_count = take(slot_before, group), take(slot_rows, group)
    holds = (row_of[:, None] >= own_before[None]) & (row_of[:, None] < (own_before + own_count)[None])
    begin_row = jnp.sum(jnp.where(holds, own_before[None], 0), axis=1)
    begins = jnp.where(jnp.any(holds, axis=1), begin_row * lanes, ids)
    ids, begins = ids.astype(f32), begins.astype(f32)
    head_ids = me * heads + jnp.arange(heads, dtype=jnp.int32)
    slopes = 2.0 ** (-8.0 * (head_ids.astype(f32) + 1.0) / HEADS)
    one_seq = per_group == 1

    blocked = (shards, blocks, ROWS, width)
    live = jnp.any(holds, axis=1).astype(f32)
    (
        x_all, cot_all, normed_one, normed_two, full_qkv, full_dense, full_up, full_down, qkv, mixed, resid, activ, slope,
        grad_down, vectors,
    ) = forward_exchange(
        pack(tokens[0]).reshape(blocked), pack(cotangent[0]).reshape(blocked),
        qkv_weight, small, dense_weight, fc1_weight, fc2_weight,
        slopes, ids, begins, live, seqs, shards, one_seq,
    )
    grad_resid, grad_mixed, grad_up, grad_dense, keep, give, half_sums, small_grads = middle_exchange(
        activ, slope, normed_two, full_up, full_down, full_dense, cot_all, resid, mixed, grad_down, vectors, seqs, shards
    )
    ret_out, ret_grad, g_qkv, g_dense, g_up, g_down, g_small = backward_exchange(
        qkv, grad_mixed.reshape(cap, part), normed_one, full_qkv, x_all, grad_resid, keep, give, half_sums,
        grad_up, grad_dense, small_grads, vectors, slopes, ids, begins, seqs, shards, one_seq,
    )

    row_here = jnp.arange(slots, dtype=jnp.int32)[:, None]
    seq_in = ((row_here >= row_start[None]) & (row_here < (row_start + seq_rows)[None])).astype(jnp.int32)
    home = jnp.arange(lengths.shape[0], dtype=jnp.int32) // per_group
    fetch = jnp.sum(seq_in * (home[None] * rows + slot_before.reshape(-1)[None] + row_here - row_start[None]), axis=1)
    fetch_live = jnp.sum(seq_in, axis=1) > 0

    def to_stream(got):
        taken = jnp.take(got.reshape(-1, width), fetch, axis=0)
        return jnp.where(fetch_live[:, None], taken, jnp.zeros_like(taken))[None]

    g_gain_one, g_bias_one, g_qv, g_bdense, g_gain_two, g_bias_two, g_bup, g_bdown = (
        g_small[i, : a.shape[0]] for i, a in enumerate(smalls_in)
    )
    return (
        to_stream(ret_out), to_stream(ret_grad),
        g_gain_one, g_bias_one, g_qkv, g_qv, g_dense, g_bdense, g_gain_two, g_bias_two, g_up, g_bup, g_down, g_bdown,
    )


def per_device_any(
    tokens, cotangent, lengths, first_gain, first_bias, qkv_weight, qv_bias, dense_weight, dense_bias,
    second_gain, second_bias, fc1_weight, fc1_bias, fc2_weight, fc2_bias,
):
    shards, seqs = lax.axis_size("shard"), lax.axis_size("seq")
    lanes = shards * seqs
    slots, width = tokens.shape[1], tokens.shape[2]
    rows = slots // shards
    cap = slots * seqs
    per_group = lengths.shape[0] // shards
    hidden_units = fc1_weight.shape[1]
    me, group = lax.axis_index("seq"), lax.axis_index("shard")
    blocks = rows // ROWS
    heads = width // HEAD // seqs
    part = heads * HEAD
    ff_part = hidden_units // shards // seqs

    qkv_half = take(qkv_weight.reshape(-1, 3, seqs, part), me, 2).reshape(-1, 3 * part)
    fc1_half = take(fc1_weight.reshape(-1, shards, seqs, ff_part), me, 2).reshape(-1, shards * ff_part)
    fc2_half = take(fc2_weight.reshape(seqs, ff_part, width), me, 0)
    small = jnp.concatenate(
        [first_gain, first_bias, qv_bias, dense_bias, second_gain, second_bias, fc1_bias, fc2_bias]
    )
    small_rows = -(-small.shape[0] // (3 * part))
    small_rows += -small_rows % 16
    small = jnp.pad(small, (0, small_rows * 3 * part - small.shape[0])).reshape(small_rows, 3 * part)
    gather = lambda a: lax.all_gather(a, "shard", axis=0, tiled=False)
    qkv_small = gather(jnp.concatenate([qkv_half, small], axis=0))
    own_rows = qkv_half.shape[0]
    full_qkv = qkv_small[:, :own_rows].reshape(width, 3 * part)
    smalls = qkv_small[:, own_rows:].reshape(shards, -1).astype(f32)
    full_dense = gather(dense_weight).reshape(width, width)
    full_up = gather(fc1_half).reshape(width, shards * ff_part)
    full_down = gather(fc2_half).reshape(shards * ff_part, width)
    cuts, at = [], 0
    for a in (first_gain, first_bias, qv_bias, dense_bias, second_gain, second_bias, fc1_bias, fc2_bias):
        cuts.append(smalls[:, at : at + a.shape[0]].reshape(-1))
        at += a.shape[0]
    gain_one, bias_one, bias_qv, bias_dense, gain_two, bias_two, bias_up, bias_down = cuts
    bias_q, bias_v = (take(bias_qv[i * width : (i + 1) * width].reshape(seqs, part), me) for i in (0, 1))
    bias_all = jnp.concatenate([bias_q, jnp.zeros_like(bias_q), bias_v])
    bias_up = take(bias_up.reshape(shards, seqs, ff_part), me, 1).reshape(-1)

    seq_rows, row_start, slot_rows, slot_start, slot_before = layout_tables(lengths, lanes, shards, per_group)
    row_in = jnp.arange(rows, dtype=jnp.int32)[None, :, None]
    inside = ((row_in >= slot_before[:, None]) & (row_in < (slot_before + slot_rows)[:, None])).astype(jnp.int32)
    send_live = jnp.sum(inside, axis=2) > 0
    send_row = jnp.sum(inside * (slot_start[:, None] + row_in - slot_before[:, None]), axis=2).reshape(-1)

    def to_groups(source):
        packed = jnp.take(source, send_row, axis=0).reshape(shards, rows, width)
        packed = jnp.where(send_live[:, :, None], packed, jnp.zeros_like(packed))
        got = lax.all_to_all(packed, "shard", split_axis=0, concat_axis=0, tiled=True)
        own = got.reshape(shards, blocks, ROWS, width).transpose(1, 0, 2, 3).reshape(blocks, -1, width)
        return own, seq_gather(own, 1).reshape(cap, width)

    x_own, x_low = to_groups(tokens[0])
    cot_own, cot_low = to_groups(cotangent[0])

    def own_part(whole):
        return take(whole.reshape(blocks, seqs, -1, whole.shape[-1]), me, 1)

    place = jnp.arange(cap, dtype=jnp.int32)
    block_of, in_block = place // (ROWS * lanes), place % (ROWS * lanes)
    row_of = block_of * ROWS + in_block % ROWS
    ids = row_of * lanes + in_block // ROWS
    own_before, own_count = take(slot_before, group), take(slot_rows, group)
    holds = (row_of[:, None] >= own_before[None]) & (row_of[:, None] < (own_before + own_count)[None])
    begin_row = jnp.sum(jnp.where(holds, own_before[None], 0), axis=1)
    begins = jnp.where(jnp.any(holds, axis=1), begin_row * lanes, ids)
    ids, begins = ids.astype(f32), begins.astype(f32)
    head_ids = me * heads + jnp.arange(heads, dtype=jnp.int32)
    slopes = 2.0 ** (-8.0 * (head_ids.astype(f32) + 1.0) / HEADS)
    one_seq = per_group == 1

    hidden = x_low.astype(f32)
    xhat_one, _ = normalize(hidden)
    normed_one = (xhat_one * gain_one + bias_one).astype(bf16)
    qkv = (jnp.dot(normed_one, full_qkv, preferred_element_type=f32) + bias_all).astype(bf16)
    mixed = attention_forward(qkv, slopes, ids, begins, lanes, one_seq)
    mixed_all = seq_gather(mixed, 1).reshape(cap, width)
    branch = jnp.dot(mixed_all, full_dense, preferred_element_type=f32) + bias_dense
    resid = hidden + branch
    xhat_two, _ = normalize(resid)
    normed_two = (xhat_two * gain_two + bias_two).astype(bf16)
    upper = jnp.dot(normed_two, full_up, preferred_element_type=f32) + bias_up
    activ = gelu_tanh(upper).astype(bf16)
    down = jnp.dot(activ, full_down, preferred_element_type=f32)
    resid_own = own_part(resid)
    down_own = seq_sum(down.reshape(blocks, seqs, -1, width), 1)
    block_out = (resid_own + down_own + bias_down).astype(bf16)

    grad_down = jnp.dot(activ.T, cot_low, preferred_element_type=f32).astype(bf16)
    grad_activ = jnp.dot(cot_low, full_down.T, preferred_element_type=f32)
    grad_upper = jax.vjp(gelu_tanh, upper)[1](grad_activ)[0].astype(bf16)
    grad_up = jnp.dot(normed_two.T, grad_upper, preferred_element_type=f32).astype(bf16)
    grad_bup = jnp.sum(grad_upper.astype(f32), axis=0)
    grad_normed = jnp.dot(grad_upper, full_up.T, preferred_element_type=f32)
    grad_normed = seq_sum(grad_normed.reshape(blocks, seqs, -1, width), 1).reshape(slots, width)
    cot_full = cot_own.reshape(slots, width).astype(f32)
    grad_bdown = jnp.sum(cot_full, axis=0)
    xhat_two, root_two = normalize(resid_own.reshape(slots, width))
    grad_gain_two = jnp.sum(grad_normed * xhat_two, axis=0)
    grad_bias_two = jnp.sum(grad_normed, axis=0)
    grad_resid = cot_full + norm_pull(grad_normed, gain_two, xhat_two, root_two)

    grad_branch = grad_resid.astype(bf16)
    grad_dense = jnp.dot(own_part(mixed_all).reshape(slots, width).T, grad_branch, preferred_element_type=f32).astype(bf16)
    grad_bdense = jnp.sum(grad_branch.astype(f32), axis=0)
    grad_mixed = jnp.dot(grad_branch, full_dense.T, preferred_element_type=f32).astype(bf16)
    got = seq_blocks(grad_mixed.reshape(blocks, -1, seqs, part), 2, bf16)
    if seqs == 2:
        grad_mixed = jnp.where(me == 0, jnp.stack(got, 1), jnp.stack(got[::-1], 1))
    else:
        grad_mixed = jnp.zeros((blocks, seqs) + got[0].shape[1:], bf16)
        for d, g in enumerate(got):
            grad_mixed = lax.dynamic_update_index_in_dim(grad_mixed, g, (me - d) % seqs, 1)
    grad_mixed = grad_mixed.reshape(cap, part)
    planes = qkv.reshape(cap, -1, 2 * HEAD).transpose(1, 0, 2)
    grad_proj = jnp.concatenate(
        attention_backward(planes, grad_mixed, slopes, ids, begins, lanes, one_seq), axis=1
    )
    grad_qkv = jnp.dot(normed_one.T, grad_proj, preferred_element_type=f32).astype(bf16)
    proj_sums = jnp.sum(grad_proj.astype(f32), axis=0)
    grad_one = jnp.dot(grad_proj, full_qkv.T, preferred_element_type=f32)
    grad_one = seq_sum(grad_one.reshape(blocks, seqs, -1, width), 1).reshape(slots, width)
    xhat_one, root_one = normalize(x_own.reshape(slots, width).astype(f32))
    grad_gain_one = jnp.sum(grad_one * xhat_one, axis=0)
    grad_bias_one = jnp.sum(grad_one, axis=0)
    tokens_grad = (grad_resid + norm_pull(grad_one, gain_one, xhat_one, root_one)).astype(bf16)

    row_here = jnp.arange(slots, dtype=jnp.int32)[:, None]
    seq_in = ((row_here >= row_start[None]) & (row_here < (row_start + seq_rows)[None])).astype(jnp.int32)
    home = jnp.arange(lengths.shape[0], dtype=jnp.int32) // per_group
    fetch = jnp.sum(seq_in * (home[None] * rows + slot_before.reshape(-1)[None] + row_here - row_start[None]), axis=1)
    fetch_live = jnp.sum(seq_in, axis=1) > 0

    def to_stream(own):
        sent = own.reshape(blocks, shards, ROWS, width).transpose(1, 0, 2, 3).reshape(shards, rows, width)
        got = lax.all_to_all(sent, "shard", split_axis=0, concat_axis=0, tiled=True)
        taken = jnp.take(got.reshape(-1, width), fetch, axis=0)
        return jnp.where(fetch_live[:, None], taken, jnp.zeros_like(taken))[None]

    down_block = shard_reduce(grad_down.reshape(shards, ff_part, width), bf16)
    up_block = shard_reduce(grad_up.reshape(shards, -1, shards * ff_part), bf16)
    dense_block = shard_reduce(grad_dense.reshape(shards, -1, width), bf16)
    qkv_block = shard_reduce(grad_qkv.reshape(shards, -1, 3 * part), bf16)

    def spread(vector, index_shape):
        zero = jnp.zeros(index_shape, f32)
        return lax.dynamic_update_index_in_dim(zero, vector, me, 1)

    sums = proj_sums.reshape(3, part)
    qv = spread(jnp.stack([sums[0], sums[2]]), (2, seqs, part)).reshape(shards, -1)
    bup = spread(grad_bup.reshape(shards, ff_part), (shards, seqs, ff_part)).reshape(shards, -1)
    rest = (grad_gain_one, grad_bias_one, grad_bdense, grad_gain_two, grad_bias_two, grad_bdown)
    packed = jnp.concatenate([a.reshape(shards, -1) for a in rest] + [qv, bup], axis=1)
    packed = shard_reduce(packed, f32)
    packed = jnp.sum(seq_gather(packed, 0), axis=0)
    cuts, at = [], 0
    for a in [a.reshape(shards, -1) for a in rest] + [qv, bup]:
        cuts.append(packed[at : at + a.shape[1]])
        at += a.shape[1]
    g_gain_one, g_bias_one, g_bdense, g_gain_two, g_bias_two, g_bdown, g_qv, g_bup = cuts

    g_dense = jnp.sum(seq_gather(dense_block.astype(bf16), 0).astype(f32), axis=0)
    g_qkv = seq_gather(qkv_block.astype(bf16).reshape(-1, 3, part), 2).reshape(-1, 3 * width).astype(f32)
    g_up = seq_gather(up_block.astype(bf16).reshape(-1, shards, ff_part), 2).reshape(-1, hidden_units).astype(f32)
    g_down = seq_gather(down_block.astype(bf16), 0).reshape(-1, width).astype(f32)
    return (
        to_stream(block_out), to_stream(tokens_grad.reshape(blocks, -1, width)),
        g_gain_one, g_bias_one, g_qkv, g_qv, g_dense, g_bdense, g_gain_two, g_bias_two, g_up, g_bup, g_down, g_bdown,
    )


def solution(mesh):
    rows, vector, stream = P("shard", None), P("shard"), P(("seq", "shard"), None, None)
    params = (vector, vector, rows, vector, rows, vector, vector, vector, rows, vector, rows, vector)
    fused = mesh.shape["seq"] == 2 and shard_factors(mesh.shape["shard"])[0] == 4
    return jax.shard_map(
        per_device if fused else per_device_any, mesh=mesh, in_specs=(stream, stream, P()) + params, out_specs=(stream, stream) + params, check_vma=False
    )
```

```python
import functools

import jax
import jax.numpy as jnp
from jax import lax
from jax.experimental import pallas as pl
from jax.experimental.pallas import tpu as pltpu
from jax.sharding import PartitionSpec as P

HEADS = 16
HEAD = 64
ROWS = 8

epsilon = 1e-05
masked_score = -1e30
f32 = jnp.float32
bf16 = jnp.bfloat16


def gelu_tanh(values):
    return (
        0.5
        * values
        * (1.0 + jnp.tanh(0.7978845608028654 * (values + 0.044715 * values * values * values)))
    )


def normalize(hidden):
    center = hidden - jnp.mean(hidden, axis=-1, keepdims=True)
    spread = jnp.mean(center * center, axis=-1, keepdims=True)
    root = lax.rsqrt(spread + epsilon)
    return center * root, root


def norm_pull(grad, gain, xhat, root):
    scaled = grad * gain
    return root * (
        scaled
        - jnp.mean(scaled, axis=-1, keepdims=True)
        - xhat * jnp.mean(scaled * xhat, axis=-1, keepdims=True)
    )


def slot_ids(first, count, lanes):
    place = first + lax.broadcasted_iota(jnp.int32, (count, 1), 0)
    block, inside = place // (ROWS * lanes), place % (ROWS * lanes)
    return (block * ROWS + inside % ROWS) * lanes + inside // ROWS


def attn_mask(scored, allowed):
    return jnp.where(allowed, scored, masked_score)


def attn_fwd_kernel(lanes, tile, one_seq, slope_ref, idc_ref, idr_ref, beginc_ref, q_ref, k_ref, v_ref, o_ref):
    tokens = q_ref.shape[0]
    block = ROWS * lanes
    lane_id = lax.broadcasted_iota(jnp.int32, (1, 2 * HEAD), 1)
    for b in range(tokens // block):
        end = (b + 1) * block

        def step(t, _):
            at = pl.ds(pl.multiple_of(b * block + t * tile, tile), tile)
            q = q_ref[at, :] * jnp.asarray(HEAD**-0.5, bf16)
            ids_q = idc_ref[at, :]
            both = None
            for j in range(2):
                mine = (lane_id // HEAD) == j
                qj = jnp.where(mine, q, jnp.zeros_like(q))
                s = lax.dot_general(
                    qj, k_ref[:end, :], (((1,), (1,)), ((), ())), preferred_element_type=f32
                )
                s = s + slope_ref[0, 0, j] * idr_ref[:, :end]
                if one_seq:
                    own = s[:, b * block :]
                    own = attn_mask(own, idr_ref[:, b * block : end] <= ids_q)
                    s = jnp.concatenate([s[:, : b * block], own], axis=1) if b else own
                else:
                    ids_k = idr_ref[:, :end]
                    s = attn_mask(s, (ids_k <= ids_q) & (ids_k >= beginc_ref[at, :]))
                top = jnp.max(s, axis=1, keepdims=True)
                e = jnp.exp(s - top)
                total = jnp.sum(e, axis=1, keepdims=True)
                o = jnp.dot(e.astype(bf16), v_ref[:end, :], preferred_element_type=f32) / total
                both = o if both is None else jnp.where(mine, o, both)
            o_ref[at, :] = both.astype(bf16)
            return 0

        lax.fori_loop(0, block // tile, step, 0)


def attn_bwd_kernel(
    lanes, tile, one_seq, slope_ref, idc_ref, idr_ref, beginr_ref, q_ref, k_ref, v_ref, do_ref,
    dq_ref, dk_ref, dv_ref, dk_acc, dv_acc, bias_acc,
):
    tokens = q_ref.shape[0]
    block = ROWS * lanes
    lane_id = lax.broadcasted_iota(jnp.int32, (1, 2 * HEAD), 1)
    dk_acc[...] = jnp.zeros_like(dk_acc)
    dv_acc[...] = jnp.zeros_like(dv_acc)
    for j in range(2):
        bias_acc[j] = jnp.broadcast_to(slope_ref[0, 0, j] * idc_ref[...], (tokens, tile))
    for b in range(tokens // block):
        end = (b + 1) * block

        def step(t, _):
            at = pl.ds(pl.multiple_of(b * block + t * tile, tile), tile)
            q = q_ref[at, :] * jnp.asarray(HEAD**-0.5, bf16)
            do = do_ref[at, :]
            ids_q = idr_ref[:, at]
            both = None
            for j in range(2):
                mine = (lane_id // HEAD) == j
                qj = jnp.where(mine, q, jnp.zeros_like(q))
                doj = jnp.where(mine, do, jnp.zeros_like(do))
                s = lax.dot_general(
                    k_ref[:end, :], qj, (((1,), (1,)), ((), ())), preferred_element_type=f32
                )
                s = s + bias_acc[j, :end, :]
                if one_seq:
                    own = s[b * block :, :]
                    own = attn_mask(own, idc_ref[b * block : end, :] <= ids_q)
                    s = jnp.concatenate([s[: b * block, :], own], axis=0) if b else own
                else:
                    ids_k = idc_ref[:end, :]
                    s = attn_mask(s, (ids_k <= ids_q) & (ids_k >= beginr_ref[:, at]))
                top = jnp.max(s, axis=0, keepdims=True)
                e = jnp.exp(s - top)
                probs = e * (1.0 / jnp.sum(e, axis=0, keepdims=True))
                dv_acc[:end, :] += jnp.dot(probs.astype(bf16), doj, preferred_element_type=f32)
                dp = lax.dot_general(
                    v_ref[:end, :], doj, (((1,), (1,)), ((), ())), preferred_element_type=f32
                )
                inner = jnp.sum(probs * dp, axis=0, keepdims=True)
                ds = (probs * (dp - inner)).astype(bf16)
                dk_acc[:end, :] += jnp.dot(ds, qj, preferred_element_type=f32)
                dq = lax.dot_general(
                    ds, k_ref[:end, :], (((0,), (0,)), ((), ())), preferred_element_type=f32
                )
                both = dq if both is None else jnp.where(mine, dq, both)
            dq_ref[at, :] = (both * (HEAD**-0.5)).astype(bf16)
            return 0

        lax.fori_loop(0, block // tile, step, 0)
    dk_ref[...] = dk_acc[...].astype(bf16)
    dv_ref[...] = dv_acc[...].astype(bf16)


def attn_shape(tokens, width, lanes):
    pairs = width // (2 * HEAD)
    tile = min(256, ROWS * lanes)
    return pairs, tile


def attention_forward(qkv, slopes, ids, begins, lanes, one_seq):
    tokens, width = qkv.shape[0], qkv.shape[1] // 3
    pairs, tile = attn_shape(tokens, width, lanes)
    column = lambda part: pl.BlockSpec((tokens, 2 * HEAD), lambda h, part=part: (0, part * pairs + h))
    whole = lambda a: pl.BlockSpec(a.shape, lambda h: (0, 0))
    idc, idr, beginc = ids[:, None], ids[None, :], begins[:, None]
    half = tokens * tokens * 5 // 8
    return pl.pallas_call(
        functools.partial(attn_fwd_kernel, lanes, tile, one_seq),
        grid=(pairs,),
        in_specs=[
            pl.BlockSpec((1, 1, 2), lambda h: (h, 0, 0), memory_space=pltpu.SMEM),
            whole(idc), whole(idr), whole(beginc), column(0), column(1), column(2),
        ],
        out_specs=pl.BlockSpec((tokens, 2 * HEAD), lambda h: (0, h)),
        out_shape=jax.ShapeDtypeStruct((tokens, width), bf16),
        compiler_params=pltpu.CompilerParams(vmem_limit_bytes=48 * 2**20),
        cost_estimate=pl.CostEstimate(
            flops=8 * pairs * half * HEAD * 2, transcendentals=2 * pairs * half, bytes_accessed=8 * tokens * width
        ),
        name="attention_forward",
    )(slopes.reshape(pairs, 1, 2), idc, idr, beginc, qkv, qkv, qkv)


def attention_backward(qkv, grad_out, slopes, ids, begins, lanes, one_seq):
    tokens, width = grad_out.shape
    pairs, tile = attn_shape(tokens, width, lanes)
    column = lambda part: pl.BlockSpec((tokens, 2 * HEAD), lambda h, part=part: (0, part * pairs + h))
    whole = lambda a: pl.BlockSpec(a.shape, lambda h: (0, 0))
    idc, idr, beginr = ids[:, None], ids[None, :], begins[None, :]
    plane = lambda part: pl.BlockSpec((None, tokens, 2 * HEAD), lambda h, part=part: (part * pairs + h, 0, 0))
    out = jax.ShapeDtypeStruct((tokens, width), bf16)
    half = tokens * tokens * 5 // 8
    return pl.pallas_call(
        functools.partial(attn_bwd_kernel, lanes, tile, one_seq),
        grid=(pairs,),
        in_specs=[
            pl.BlockSpec((1, 1, 2), lambda h: (h, 0, 0), memory_space=pltpu.SMEM),
            whole(idc), whole(idr), whole(beginr), plane(0), plane(1), plane(2), column(0),
        ],
        out_specs=[column(0)] * 3,
        out_shape=[out] * 3,
        scratch_shapes=[
            pltpu.VMEM((tokens, 2 * HEAD), f32), pltpu.VMEM((tokens, 2 * HEAD), f32), pltpu.VMEM((2, tokens, tile), f32),
        ],
        compiler_params=pltpu.CompilerParams(vmem_limit_bytes=56 * 2**20),
        cost_estimate=pl.CostEstimate(
            flops=20 * pairs * half * HEAD * 2, transcendentals=2 * pairs * half, bytes_accessed=14 * tokens * width
        ),
        name="attention_backward",
    )(slopes.reshape(pairs, 1, 2), idc, idr, beginr, qkv, qkv, qkv, grad_out)


def take(blocks, index, axis=0):
    return lax.dynamic_index_in_dim(blocks, index, axis, keepdims=False)


def seq_gather(block, axis):
    n, me = lax.axis_size("seq"), lax.axis_index("seq")
    shape = block.shape[:axis] + (n,) + block.shape[axis:]
    if n == 2:
        peer = lax.ppermute(block, "seq", [(0, 1), (1, 0)])
        return jnp.where(me == 0, jnp.stack([block, peer], axis), jnp.stack([peer, block], axis))
    whole = lax.dynamic_update_index_in_dim(jnp.zeros(shape, block.dtype), block, me, axis)
    for d in range(1, n):
        got = lax.ppermute(block, "seq", [(i, (i + d) % n) for i in range(n)])
        whole = lax.dynamic_update_index_in_dim(whole, got, (me - d) % n, axis)
    return whole


def seq_blocks(whole, axis, dtype):
    n, me = lax.axis_size("seq"), lax.axis_index("seq")
    got = [take(whole, me, axis)]
    for d in range(1, n):
        sent = take(whole, (me + d) % n, axis).astype(dtype)
        got.append(lax.ppermute(sent, "seq", [(i, (i + d) % n) for i in range(n)]))
    return got


def seq_sum(whole, axis, dtype=bf16):
    got = seq_blocks(whole, axis, dtype)
    return sum((g.astype(f32) for g in got[1:]), got[0].astype(f32))


def shard_factors(n):
    nc = 2 if n % 2 == 0 else 1
    nz = 4 if n % (4 * nc) == 0 else 1
    return nz, n // (nz * nc), nc


def shard_reduce(blocks, dtype):
    n, me = lax.axis_size("shard"), lax.axis_index("shard")
    sizes = shard_factors(n)
    blocks = blocks.reshape(sizes + blocks.shape[1:])
    place = (me // (sizes[1] * sizes[2]), me // sizes[2] % sizes[1], me % sizes[2])
    strides = (sizes[1] * sizes[2], sizes[2], 1)
    for axis in (2, 1, 0):
        size, mine, stride = sizes[axis], place[axis], strides[axis]
        total = take(blocks, mine, axis).astype(f32)
        for d in range(1, size):
            sent = take(blocks, (mine + d) % size, axis).astype(dtype)
            pairs = [
                (i, i - (i // stride % size) * stride + ((i // stride % size + d) % size) * stride)
                for i in range(n)
            ]
            total = total + lax.ppermute(sent, "shard", pairs).astype(f32)
        blocks = total if axis == 0 else total.astype(dtype)
    return blocks


MESH = pl.DeviceIdType.MESH


class Geometry:
    def __init__(self, seqs, shards):
        self.seqs, self.shards = seqs, shards
        self.sizes = shard_factors(shards)
        self.s, self.k = lax.axis_index("seq"), lax.axis_index("shard")
        nz, ny, nc = self.sizes
        self.z, self.y, self.c = self.k // (ny * nc), self.k // nc % ny, self.k % nc
        self.inner = (self.z + 1) // 2 % 2
        high = self.z // 2
        self.line = (self.z, self.z + 1 - 2 * (self.z % 2), 2 - high, 3 - 3 * high)

    def slot(self, i, dy, dc):
        nz, ny, nc = self.sizes
        return (self.line[i] * ny + (self.y + dy) % ny) * nc + (self.c + dc) % nc


class Wires:
    def __init__(self, geometry, send_sems, recv_sems):
        self.g, self.send_sems, self.recv_sems = geometry, send_sems, recv_sems
        self.sends, self.used = [], 0

    def block(self, count):
        first = self.used
        self.used += count
        return first

    def copy(self, src, dst, sent, got, s, k):
        return pltpu.make_async_remote_copy(
            src_ref=src, dst_ref=dst, send_sem=self.send_sems.at[sent], recv_sem=self.recv_sems.at[got],
            device_id={"seq": s, "shard": k}, device_id_type=MESH,
        )

    def send_as(self, src, dst, sent, got, s, k, like):
        self.copy(src, dst, sent, got, s, k).start()
        self.sends.append((like, sent))

    def send(self, src, dst, index, s, k, like):
        self.send_as(src, dst, index, index, s, k, like)

    def arrived(self, dst, index):
        self.copy(dst, dst, index, index, 1 - self.g.s, self.g.k).wait_recv()

    def drain(self):
        for like, index in self.sends:
            self.copy(like, like, index, index, 1 - self.g.s, self.g.k).wait_send()
        self.sends = []


def enter(geometry):
    g = geometry
    barrier = pltpu.get_barrier_semaphore()
    for d in range(1, g.shards):
        pl.semaphore_signal(
            barrier, inc=1, device_id={"seq": g.s, "shard": (g.k + d) % g.shards}, device_id_type=MESH
        )
    pl.semaphore_signal(barrier, inc=1, device_id={"seq": 1 - g.s, "shard": g.k}, device_id_type=MESH)
    pl.semaphore_wait(barrier, g.shards)


class Gather:
    def __init__(self, wires, own, out):
        self.w, self.g, self.own, self.out = wires, wires.g, own, out
        nz, ny, nc = self.g.sizes
        self.z0 = wires.block(nz)
        self.on0 = wires.block(nz)
        self.y0 = wires.block(nz * ny)
        self.c0 = wires.block(nz * ny * nc)

    def on_y(self, i, src):
        g = self.g
        for dy in range(1, g.sizes[1]):
            self.w.send(src, self.out.at[g.slot(i, 0, 0)], self.y0 + i * g.sizes[1] + dy, g.s, g.slot(0, dy, 0), self.own)

    def on_core(self, i, dy, src):
        g = self.g
        for dc in range(1, g.sizes[2]):
            index = self.c0 + (i * g.sizes[1] + dy) * g.sizes[2] + dc
            self.w.send(src, self.out.at[g.slot(i, -dy, 0)], index, g.s, g.slot(0, 0, dc), self.own)

    def start(self):
        g = self.g
        here = self.out.at[g.k]
        self.w.send_as(self.own, here, self.z0 + 2, self.z0 + 3 - g.inner, g.s, g.slot(2, 0, 0), self.own)
        self.w.send(self.own, here, self.z0 + 1, g.s, g.slot(1, 0, 0), self.own)

    def start_near(self):
        self.on_y(0, self.own)
        self.on_core(0, 0, self.own)

    def poll_z(self):
        g = self.g
        for i in (1, 2, 3):
            at = self.out.at[g.slot(i, 0, 0)]
            self.w.arrived(at, self.z0 + i)
            if i > 1:

                @pl.when(g.inner == 1)
                def _(at=at, i=i):
                    self.w.copy(at, at, self.on0 + i, self.z0 + i, g.s, g.slot(1, 0, 0)).start()

            self.on_y(i, at)
            self.on_core(i, 0, at)

    def poll_y(self):
        g = self.g
        for i in range(g.sizes[0]):
            for dy in range(1, g.sizes[1]):
                at = self.out.at[g.slot(i, -dy, 0)]
                self.w.arrived(at, self.y0 + i * g.sizes[1] + dy)
                self.on_core(i, dy, at)

    def finish(self):
        g = self.g
        for i in range(g.sizes[0]):
            for dy in range(g.sizes[1]):
                for dc in range(1, g.sizes[2]):
                    at = self.out.at[g.slot(i, -dy, -dc)]
                    self.w.arrived(at, self.c0 + (i * g.sizes[1] + dy) * g.sizes[2] + dc)

        @pl.when(g.inner == 1)
        def _():
            for i in (2, 3):
                self.w.copy(self.own, self.own, self.on0 + i, self.z0 + i, g.s, g.k).wait_send()


class Tokens:
    def __init__(self, wires, packed, out):
        self.w, self.g, self.packed, self.out = wires, wires.g, packed, out
        self.blocks = out.shape[0]
        self.at = wires.block((self.g.shards + 1) * self.blocks)
        self.like, self.row = packed.at[0, 0], packed.at[:, 0]

    def index(self, b, d):
        return self.at + b * (self.g.shards + 1) + d

    def mine(self, b, s):
        return self.out.at[b, pl.ds(pl.multiple_of(s * self.g.shards, self.g.shards), self.g.shards)]

    def start(self, b):
        g = self.g
        for d in range(1, g.shards):
            to = (g.k + d) % g.shards
            lane = self.out.at[b, g.s * g.shards + g.k]
            self.w.send(self.packed.at[to, b], lane, self.index(b, d), g.s, to, self.like)

    def poll(self, b):
        g = self.g
        for d in range(1, g.shards):
            self.w.arrived(self.out.at[b, g.s * g.shards + (g.k - d) % g.shards], self.index(b, d))
        self.w.send(self.mine(b, g.s), self.mine(b, g.s), self.index(b, g.shards), 1 - g.s, g.k, self.row)

    def finish(self, b):
        self.w.arrived(self.mine(b, 1 - self.g.s), self.index(b, self.g.shards))


class Smalls:
    def __init__(self, wires, held, at):
        self.w, self.g, self.held, self.at = wires, wires.g, held, at

    def start(self):
        g = self.g
        mine = self.held.at[g.k]
        for d in range(1, g.shards):
            self.w.send(mine, mine, self.at + d, g.s, (g.k + d) % g.shards, mine)

    def finish(self):
        g = self.g
        for d in range(1, g.shards):
            self.w.arrived(self.held.at[(g.k - d) % g.shards], self.at + d)


def side_by_side(vec, small, row, to, count):
    for j in range(small.shape[0]):
        vec[to : to + 1, j * count : (j + 1) * count] = small[j, row : row + 1, :count]


def forward_kernel(
    seqs, shards, counts, one_seq,
    packed, packed_cot, qkv_w, small, dense_w, fc1_w, fc2_w, slopes, idc, idr, beginc, live,
    x_out, cot_out, n1_out, n2_out, qkvw_out, dense_out, fc1_out, fc2_out, qkv_out, o_out, h2_out, a_out, slope_out,
    w2_out, vec_out,
    x_v, n1_v, n2_v, qkvw_v, small_v, dense_v, fc1_v, fc2_v, blocks_v, cot_v, qkv_v, o_v, h2_v, a_v, slope_v, w2_v, vec_v,
    send_sems, recv_sems, copy_sems,
):
    g = Geometry(seqs, shards)
    wires = Wires(g, send_sems, recv_sems)
    lanes = seqs * shards
    width = n1_v.shape[1]
    part = o_v.shape[2]
    pairs = part // (2 * HEAD)
    ff = fc1_v.shape[2]
    ff_part = ff // shards
    block = ROWS * lanes
    blocks = x_v.shape[0]
    half = block // seqs
    rows = width // shards
    local = []

    def bring(src, dst):
        made = pltpu.make_async_copy(src, dst, copy_sems.at[len(local)])
        made.start()
        local.append(made)
        return made

    def at_block(b):
        return pl.ds(pl.multiple_of(b * block, block), block)

    tokens = Tokens(wires, packed, x_v)
    cots = Tokens(wires, packed_cot, blocks_v)
    smalls_at = wires.block(shards)
    qkv_all = Gather(wires, qkvw_v.at[g.k], qkvw_v)
    dense_all = Gather(wires, dense_v.at[g.k], dense_v)
    up_all = Gather(wires, fc1_v.at[g.k], fc1_v)
    down_all = Gather(wires, fc2_v, fc2_out)
    heads_at = wires.block(blocks)

    staged_qkv = [
        bring(
            qkv_w.at[:, pl.ds(pl.multiple_of(p * width + g.s * part, 128), part)],
            qkvw_v.at[g.k, :, pl.ds(p * part, part)],
        )
        for p in range(3)
    ]
    staged_small = bring(small, small_v.at[g.k])
    staged_dense = bring(dense_w, dense_v.at[g.k])
    staged_up = [
        bring(
            fc1_w.at[:, pl.ds(pl.multiple_of((i * seqs + g.s) * ff_part, 128), ff_part)],
            fc1_v.at[g.k, :, pl.ds(i * ff_part, ff_part)],
        )
        for i in range(shards)
    ]
    staged_x = bring(packed.at[g.k], x_v.at[:, g.s * shards + g.k])
    staged_down = bring(fc2_w.at[pl.ds(pl.multiple_of(g.s * ff_part, 8), ff_part), :], fc2_v)
    staged_cot = bring(packed_cot.at[g.k], blocks_v.at[:, g.s * shards + g.k])
    enter(g)
    for made in staged_qkv:
        made.wait()
    staged_small.wait()
    staged_dense.wait()
    for made in staged_up:
        made.wait()
    staged_down.wait()
    staged_x.wait()
    staged_cot.wait()
    kept = [bring(fc2_v, fc2_out.at[g.k])]
    smalls = Smalls(wires, small_v, smalls_at)
    qkv_all.start()
    qkv_all.start_near()
    tokens.start(0)
    tokens.start(1)
    smalls.start()
    dense_all.start_near()
    up_all.start_near()
    down_all.start_near()
    tokens.poll(0)
    tokens.start(2)
    qkv_all.poll_z()
    tokens.poll(1)
    tokens.start(3)
    dense_all.start()
    up_all.start()
    smalls.finish()

    for row in (0, 1, 3, 4, 5, 7):
        side_by_side(vec_v, small_v, row, row, rows)
    vec_v[2:3, :] = jnp.zeros((1, vec_v.shape[1]), f32)
    per = 2 * width // shards
    for i in range(part // per):
        for row, side in ((0, 0), (2, 1)):
            j = (side * width + g.s * part) // per + i
            vec_v[2:3, row * part + i * per : row * part + (i + 1) * per] = small_v[j, 2:3, :per]
    for j in range(shards):
        vec_v[6:7, j * ff_part : (j + 1) * ff_part] = small_v[j, 6:7, pl.ds(pl.multiple_of(g.s * ff_part, 128), ff_part)]

    qkv_all.poll_y()
    tokens.poll(2)
    tokens.poll(3)
    down_all.start()
    qkv_all.finish()
    kept += [bring(qkvw_v, qkvw_out), bring(vec_v, vec_out)]

    lane_id = lax.broadcasted_iota(jnp.int32, (1, 2 * HEAD), 1)
    tile = min(256, block)

    def project(b):
        x = x_v[b].astype(f32).reshape(block, width)
        xhat, _ = normalize(x)
        n1 = (xhat * vec_v[0:1, :width] + vec_v[1:2, :width]).astype(bf16)
        at = at_block(b)
        n1_v[at, :] = n1
        for p in range(3):
            weight = qkvw_v[:, :, p * part : (p + 1) * part].reshape(width, part)
            out = jnp.dot(n1, weight, preferred_element_type=f32) + vec_v[2:3, p * part : (p + 1) * part]
            out = out.astype(bf16)
            for h in range(pairs):
                qkv_v[p * pairs + h, at, :] = out[:, h * 2 * HEAD : (h + 1) * 2 * HEAD]

    def attend(b):
        end = (b + 1) * block

        @pl.loop(0, pairs)
        def _(h):
            q_ref, k_ref, v_ref = qkv_v.at[h], qkv_v.at[pairs + h], qkv_v.at[2 * pairs + h]
            for t in range(block // tile):
                at = pl.ds(b * block + t * tile, tile)
                q = q_ref[at, :] * jnp.asarray(HEAD**-0.5, bf16)
                ids_q = idc[at, :]
                both = None
                for j in range(2):
                    mine = (lane_id // HEAD) == j
                    qj = jnp.where(mine, q, jnp.zeros_like(q))
                    s = lax.dot_general(
                        qj, k_ref[:end, :], (((1,), (1,)), ((), ())), preferred_element_type=f32
                    )
                    s = s + slopes[h, j] * idr[:, :end]
                    if one_seq:
                        tail = attn_mask(s[:, b * block :], idr[:, b * block : end] <= ids_q)
                        s = jnp.concatenate([s[:, : b * block], tail], axis=1) if b else tail
                    else:
                        ids_k = idr[:, :end]
                        s = attn_mask(s, (ids_k <= ids_q) & (ids_k >= beginc[at, :]))
                    top = jnp.max(s, axis=1, keepdims=True)
                    e = jnp.exp(s - top)
                    total = jnp.sum(e, axis=1, keepdims=True)
                    o = jnp.dot(e.astype(bf16), v_ref[:end, :], preferred_element_type=f32) / total
                    both = o if both is None else jnp.where(mine, o, both)
                o_v[g.s, at, pl.ds(pl.multiple_of(h * 2 * HEAD, 2 * HEAD), 2 * HEAD)] = both.astype(bf16)

    def head_copy(b):
        mine = o_v.at[g.s, at_block(b)]
        return wires.copy(mine, mine, heads_at + b, heads_at + b, 1 - g.s, g.k)

    for b in range(blocks):
        tokens.finish(b)
        project(b)
        attend(b)
        head_copy(b).start()
        if b == 0:
            dense_all.poll_z()
        if b == 1:
            up_all.poll_z()
        if b == 2:
            dense_all.poll_y()
            cots.start(0)
            cots.start(1)
        if b == 3:
            up_all.poll_y()
    kept += [bring(x_v, x_out), bring(n1_v, n1_out), bring(qkv_v, qkv_out)]
    down_all.poll_z()
    dense_all.finish()
    kept.append(bring(dense_v, dense_out))
    up_all.finish()
    kept.append(bring(fc1_v, fc1_out))

    @pl.loop(0, blocks)
    def _(b):
        at = at_block(b)
        wires.arrived(o_v.at[1 - g.s, at], heads_at + b)
        branch = jnp.dot(
            o_v[0, at, :], dense_v[: shards // 2].reshape(part, width), preferred_element_type=f32
        ) + jnp.dot(o_v[1, at, :], dense_v[shards // 2 :].reshape(part, width), preferred_element_type=f32)
        resid = x_v[b].astype(f32).reshape(block, width) + branch + vec_v[3:4, :width]
        h2_v[b] = jnp.where(g.s == 0, resid[:half], resid[half:])
        xhat, _ = normalize(resid)
        n2 = (xhat * vec_v[4:5, :width] + vec_v[5:6, :width]).astype(bf16)
        n2_v[at, :] = n2
        step = min(512, ff)
        for n in range(ff // step):
            cut = slice(n * step, (n + 1) * step)
            u = jnp.dot(n2, fc1_v[:, :, cut].reshape(width, step), preferred_element_type=f32) + vec_v[6:7, cut]
            inside = 0.7978845608028654 * u * (1.0 + 0.044715 * u * u)
            t = jnp.tanh(inside)
            a_v[at, cut] = (0.5 * u * (1.0 + t)).astype(bf16)
            slope = 0.5 * (1.0 + t) + 0.5 * u * (1.0 - t * t) * (
                0.7978845608028654 + (0.7978845608028654 * 3.0 * 0.044715) * u * u
            )
            slope_v[at, cut] = slope.astype(bf16)

        @pl.when(b == 0)
        def _():
            cots.poll(0)
            cots.start(2)

        @pl.when(b == 1)
        def _():
            cots.poll(1)
            cots.start(3)

        @pl.when(b == 2)
        def _():
            cots.poll(2)


    cots.poll(3)
    kept.append(bring(o_v, o_out))
    kept += [bring(n2_v, n2_out), bring(h2_v, h2_out), bring(a_v, a_out), bring(slope_v, slope_out)]
    down_all.poll_y()
    for b in range(blocks):
        cots.finish(b)

    @pl.loop(0, blocks)
    def _(b):
        at = at_block(b)
        grad = blocks_v[b].astype(f32).reshape(block, width)
        cot_v[at, :] = jnp.where(live[at, :] > 0, grad, 0.0).astype(bf16)

    kept.append(bring(cot_v, cot_out))

    @pl.loop(0, ff // (2 * ff_part))
    def _(m):
        cut = a_v[:, pl.ds(pl.multiple_of(m * 2 * ff_part, 128), 2 * ff_part)]
        out = lax.dot_general(cut, cot_v[...], (((0,), (0,)), ((), ())), preferred_element_type=f32).astype(bf16)
        w2_v[pl.ds(2 * m, 2)] = out.reshape(2, ff_part, width)

    kept.append(bring(w2_v, w2_out))
    down_all.finish()
    for b in range(blocks):
        head_copy(b).wait_send()
    wires.drain()
    for made in kept:
        made.wait()
    assert wires.used <= counts[0] and len(local) <= counts[1]


def forward_exchange(packed, packed_cot, qkv_w, small, dense_w, fc1_w, fc2_w, slopes, ids, begins, live, seqs, shards, one_seq):
    width, own = qkv_w.shape[0] * shards, qkv_w.shape[0]
    lanes = seqs * shards
    blocks = packed.shape[1]
    block = lanes * ROWS
    cap = blocks * block
    part = width // seqs
    pairs = part // (2 * HEAD)
    ff = fc1_w.shape[1] // seqs
    ff_part = ff // shards
    counts = (384, 64)
    any_ = pl.BlockSpec(memory_space=pl.ANY)
    vmem = pl.BlockSpec(memory_space=pltpu.VMEM)
    smem = pl.BlockSpec(memory_space=pltpu.SMEM)
    x_shape = ((blocks, lanes, ROWS, width), bf16)
    wide, long = ((cap, width), bf16), ((cap, ff), bf16)
    qkvw, dense, fc1, fc2 = (
        ((shards,) + tail, bf16) for tail in ((own, 3 * part), (own, width), (own, ff), (ff_part, width))
    )
    qkv, heads = ((3 * pairs, cap, 2 * HEAD), bf16), ((seqs, cap, part), bf16)
    h2, vec = ((blocks, block // seqs, width), f32), ((8, max(width, 3 * part, ff)), f32)
    outs = [x_shape, wide, wide, wide, qkvw, dense, fc1, fc2, qkv, heads, h2, long, long, fc2, vec]
    scratch = [
        x_shape, wide, wide, qkvw, ((shards,) + small.shape, f32), dense, fc1, ((ff_part, width), bf16), x_shape, wide,
        qkv, heads, h2, long, long, fc2, vec,
    ]
    return pl.pallas_call(
        functools.partial(forward_kernel, seqs, shards, counts, one_seq),
        in_specs=[any_] * 7 + [smem] + [vmem] * 4,
        out_specs=[any_] * len(outs),
        out_shape=[jax.ShapeDtypeStruct(s, d) for s, d in outs],
        scratch_shapes=[pltpu.VMEM(s, d) for s, d in scratch]
        + [pltpu.SemaphoreType.DMA((counts[0],)), pltpu.SemaphoreType.DMA((counts[0],)), pltpu.SemaphoreType.DMA((counts[1],))],
        compiler_params=pltpu.CompilerParams(collective_id=1, has_side_effects=True, vmem_limit_bytes=60 * 2**20),
        name="forward_exchange",
    )(
        packed, packed_cot, qkv_w, small, dense_w, fc1_w, fc2_w, slopes.reshape(pairs, 2),
        ids[:, None], ids[None, :], begins[:, None], live[:, None],
    )


class Scatter:
    def __init__(self, wires, full, own, bufs):
        self.w, self.g, self.full, self.own = wires, wires.g, full, own
        self.rc, self.ry, self.rz, self.fin = bufs
        self.at = wires.block(8)

    def add(self, count, into, other):
        @pl.loop(0, count)
        def _(i):
            a, b = into(i), other(i)
            a[...] = (a[...].astype(f32) + b[...].astype(f32)).astype(bf16)

    def core_send(self):
        g = self.g
        self.w.send(self.full.at[:, :, 1 - g.c], self.rc, self.at, g.s, g.slot(0, 0, 1), self.rc)

    def core_done(self):
        g = self.g
        self.w.arrived(self.rc, self.at)
        self.add(8, lambda i: self.rc.at[i // 2, i % 2], lambda i: self.own(i // 2, i % 2))
        self.w.send(self.rc.at[:, 1 - g.y], self.ry, self.at + 1, g.s, g.slot(0, 1, 0), self.ry)

    def y_done(self):
        g = self.g
        self.w.arrived(self.ry, self.at + 1)
        self.add(4, lambda i: self.ry.at[i], lambda i: self.rc.at[i, g.y])

    def z_send(self):
        g = self.g
        partner = g.slot(1, 0, 0)
        self.w.send(self.ry.at[g.line[1]], self.rz.at[0], self.at + 2, g.s, partner, self.rz.at[0])

        @pl.when(g.inner == 0)
        def _():
            for i in (2, 3):
                self.w.copy(self.ry.at[g.line[i]], self.rz.at[i], self.at + 1 + i, self.at + 1 + i, g.s, partner).start()

    def z_done(self):
        g = self.g

        @pl.when(g.inner == 1)
        def _():
            for i in (2, 3):
                self.w.arrived(self.rz.at[i], self.at + 1 + i)
                a = self.rz.at[i]
                a[...] = (a[...].astype(f32) + self.ry[g.line[i]].astype(f32)).astype(bf16)
                self.w.copy(a, self.rz.at[1], self.at + 1 + i, self.at + 5, g.s, g.slot(i, 0, 0)).start()

    def final(self):
        g = self.g
        self.w.arrived(self.rz.at[0], self.at + 2)
        self.w.arrived(self.rz.at[1], self.at + 5)
        total = self.ry[g.z].astype(f32) + self.rz[0].astype(f32) + self.rz[1].astype(f32)
        self.fin[0] = total.astype(bf16)
        self.w.send(self.fin.at[0], self.fin.at[1], self.at + 6, 1 - g.s, g.k, self.fin.at[0])

    def done(self):
        self.w.arrived(self.fin.at[1], self.at + 6)
        for i in (2, 3):
            self.w.copy(self.fin.at[0], self.fin.at[0], self.at + 1 + i, self.at + 1 + i, self.g.s, self.g.k).wait_send()


class Back:
    def __init__(self, wires, src, dst, pieces):
        self.w, self.g, self.src, self.dst, self.pieces = wires, wires.g, src, dst, pieces
        self.at = wires.block(wires.g.shards * pieces)
        self.per = src.shape[0] // pieces
        self.like = src.at[pl.ds(0, self.per), 0]

    def cut(self, ref, i):
        return ref.at[pl.ds(i * self.per, self.per)]

    def send(self, i):
        g = self.g
        for d in range(1, g.shards):
            to = (g.k + d) % g.shards
            src = self.src.at[pl.ds(i * self.per, self.per), to]
            self.w.send(src, self.cut(self.dst.at[g.k], i), self.at + i * g.shards + d, g.s, to, self.like)

    def finish(self):
        g = self.g
        for i in range(self.pieces):
            for d in range(1, g.shards):
                self.w.arrived(self.cut(self.dst.at[(g.k - d) % g.shards], i), self.at + i * g.shards + d)


def middle_kernel(
    seqs, shards, counts,
    a, slope, n2, fc1, fc2, dense, cot, h2, heads, w2, vec,
    dh2_out, do_out, w1_out, wd_out, keep_out, give_out, ry_out, small_out,
    a_v, du_v, n2_v, fc1_v, fc2_v, dense_v, cot_v, h2_v, heads_v, own_w2, w1_v, wd_v, mine_v, sent_v, got_v,
    da_v, do_v, do_sent, small_v, rc, ry,
    send_sems, recv_sems, copy_sems,
):
    g = Geometry(seqs, shards)
    wires = Wires(g, send_sems, recv_sems)
    blocks, half, width = h2_v.shape
    block = half * seqs
    ff = a_v.shape[1]
    ff_part = ff // shards
    rows = width // shards
    part = width // seqs
    local = []

    def bring(src, dst):
        made = pltpu.make_async_copy(src, dst, copy_sems.at[len(local)])
        made.start()
        local.append(made)
        return made

    def at_block(b):
        return pl.ds(pl.multiple_of(b * block, block), block)

    def own_rows(b):
        return pl.ds(pl.multiple_of(b * block + g.s * half, half), half)

    down = Scatter(wires, w2, lambda i, j: own_w2.at[i, j], (rc, ry, None, None))
    half_at, do_at = wires.block(blocks), wires.block(blocks)
    first = [bring(cot, cot_v), bring(fc2, fc2_v), bring(slope, du_v), bring(fc1, fc1_v)]
    own = bring(w2.at[:, :, g.c], own_w2)
    later = [bring(n2, n2_v), bring(a, a_v), bring(h2, h2_v), bring(dense, dense_v)]
    later += [bring(heads.at[i, own_rows(b), :], heads_v.at[i, pl.ds(b * half, half)]) for i in range(seqs) for b in range(blocks)]
    enter(g)
    down.core_send()
    for made in first:
        made.wait()
    step = min(512, ff)
    per = step // ff_part

    def half_copy(b):
        return wires.copy(sent_v.at[b], got_v.at[b], half_at + b, half_at + b, 1 - g.s, g.k)

    def do_copy(b):
        return wires.copy(do_sent.at[b], do_v.at[b, g.s], do_at + b, do_at + b, 1 - g.s, g.k)

    small_v[...] = jnp.zeros_like(small_v)

    def split(b, total, keep, give):
        @pl.when(g.s == 0)
        def _():
            keep(total[:half])
            give[b] = total[half:].astype(bf16)

        @pl.when(g.s == 1)
        def _():
            keep(total[half:])
            give[b] = total[:half].astype(bf16)

    def du_step(b, sums):
        at = at_block(b)
        grad = cot_v[at, :]
        total, new = None, []
        for n in range(ff // step):
            cut = slice(n * step, (n + 1) * step)
            weight = fc2_v[n * per : (n + 1) * per].reshape(step, width)
            da = lax.dot_general(grad, weight, (((1,), (1,)), ((), ())), preferred_element_type=f32)
            du = (da * du_v[at, cut].astype(f32)).astype(bf16)
            du_v[at, cut] = du
            new.append(sums[n] + jnp.sum(du.astype(f32), axis=0, keepdims=True))
            weight = fc1_v[:, :, cut].reshape(width, step)
            term = lax.dot_general(du, weight, (((1,), (1,)), ((), ())), preferred_element_type=f32)
            total = term if total is None else total + term

        def keep(value):
            mine_v[b] = value

        split(b, total, keep, sent_v)

        @pl.when(b > 0)
        def _():
            half_copy(b - 1).start()

        @pl.when(b == 0)
        def _():
            own.wait()
            down.core_done()

        return tuple(new)

    zero = jnp.zeros((1, step), f32)
    sums = lax.fori_loop(0, blocks, du_step, (zero,) * (ff // step))
    for made in later:
        made.wait()

    @pl.loop(0, width // (4 * rows))
    def _(m):
        @pl.when(m == 0)
        def _():
            half_copy(blocks - 1).start()

        left = n2_v[:, pl.ds(pl.multiple_of(m * 4 * rows, 128), 4 * rows)]
        for n in range(ff // step):
            cut = slice(n * step, (n + 1) * step)
            out = lax.dot_general(left, du_v[:, cut], (((0,), (0,)), ((), ())), preferred_element_type=f32)
            w1_v[pl.ds(4 * m, 4), :, cut] = out.astype(bf16).reshape(4, rows, step)

    kept = [bring(w1_v, w1_out)]
    for n in range(ff // step):
        for i in range(per):
            small_v[n * per + i, 6:7, pl.ds(pl.multiple_of(g.s * ff_part, 128), ff_part)] = sums[n][
                :, i * ff_part : (i + 1) * ff_part
            ]

    def norm_step(b, sums):
        gains, biases, branch, cots = sums
        wires.arrived(got_v.at[b], half_at + b)
        grad = mine_v[b] + got_v[b].astype(f32)
        xhat, root = normalize(h2_v[b])
        gains = gains + jnp.sum(grad * xhat, axis=0, keepdims=True)
        biases = biases + jnp.sum(grad, axis=0, keepdims=True)
        cot_b = cot_v[own_rows(b), :].astype(f32)
        cots = cots + jnp.sum(cot_b, axis=0, keepdims=True)
        dh2 = cot_b + norm_pull(grad, vec[4:5, :width], xhat, root)
        mine_v[b] = dh2
        da = dh2.astype(bf16)
        branch = branch + jnp.sum(da.astype(f32), axis=0, keepdims=True)
        da_v[pl.ds(pl.multiple_of(b * half, half), half), :] = da
        grads = [
            lax.dot_general(
                da, dense_v[i * (shards // seqs) : (i + 1) * (shards // seqs)].reshape(part, width),
                (((1,), (1,)), ((), ())), preferred_element_type=f32,
            ).astype(bf16)
            for i in range(seqs)
        ]
        do_v[b, g.s] = jnp.where(g.s == 0, grads[0], grads[1])
        do_sent[b] = jnp.where(g.s == 0, grads[1], grads[0])

        @pl.when(b > 0)
        def _():
            do_copy(b - 1).start()

        return gains, biases, branch, cots

    zero = jnp.zeros((1, width), f32)
    sums = lax.fori_loop(0, blocks, norm_step, (zero,) * 4)
    kept.append(bring(mine_v, dh2_out))
    for row, vector in ((4, sums[0]), (5, sums[1]), (3, sums[2]), (7, sums[3])):
        for j in range(shards):
            small_v[j, row : row + 1, :rows] = vector[:, j * rows : (j + 1) * rows]
    do_copy(blocks - 1).start()
    kept.append(bring(small_v, small_out))

    for i in range(seqs):
        out = lax.dot_general(heads_v[i], da_v[...], (((0,), (0,)), ((), ())), preferred_element_type=f32).astype(bf16)
        wd_v[i * (shards // seqs) : (i + 1) * (shards // seqs)] = out.reshape(shards // seqs, rows, width)
    kept.append(bring(wd_v, wd_out))

    @pl.loop(0, blocks)
    def _(b):
        at = at_block(b)
        total = None
        for n in range(ff // step):
            weight = fc2_v[n * per : (n + 1) * per].reshape(step, width)
            term = jnp.dot(a_v[at, n * step : (n + 1) * step], weight, preferred_element_type=f32)
            total = term if total is None else total + term

        def keep(value):
            h2_v[b] = h2_v[b] + value + vec[7:8, :width]

        split(b, total, keep, got_v)

    kept += [bring(h2_v, keep_out), bring(got_v, give_out)]
    down.y_done()
    kept.append(bring(ry, ry_out))
    for b in range(blocks):
        wires.arrived(do_v.at[b, 1 - g.s], do_at + b)
    kept.append(bring(do_v, do_out))
    for b in range(blocks):
        half_copy(b).wait_send()
        do_copy(b).wait_send()
    wires.drain()
    for made in kept:
        made.wait()
    assert wires.used <= counts[0] and len(local) <= counts[1]


def middle_exchange(a, slope, n2, fc1, fc2, dense, cot, h2, heads, w2, vec, seqs, shards):
    blocks, half, width = h2.shape
    tokens, ff = a.shape
    part = width // seqs
    rows, ff_part = width // shards, ff // shards
    counts = (32, 40)
    any_, vmem = pl.BlockSpec(memory_space=pl.ANY), pl.BlockSpec(memory_space=pltpu.VMEM)
    own32, own16 = ((blocks, half, width), f32), ((blocks, half, width), bf16)
    do, smalls = ((blocks, seqs, half, part), bf16), ((shards, 8, 256), f32)
    w1, wd, ry = ((shards, rows, ff), bf16), ((shards, rows, width), bf16), ((4, ff_part, width), bf16)
    outs = [own32, do, w1, wd, own32, own16, ry, smalls]
    rc = ((4, 2, ff_part, width), bf16)
    scratch = [(v.shape, bf16) for v in (a, slope, n2, fc1, fc2, dense, cot)] + [
        own32, ((seqs, blocks * half, part), bf16), rc, w1, wd, own32, own16, own16, ((blocks * half, width), bf16), do,
        ((blocks, half, part), bf16), smalls, rc, ry,
    ]
    return pl.pallas_call(
        functools.partial(middle_kernel, seqs, shards, counts),
        in_specs=[any_] * 10 + [vmem],
        out_specs=[any_] * len(outs),
        out_shape=[jax.ShapeDtypeStruct(s, d) for s, d in outs],
        scratch_shapes=[pltpu.VMEM(s, d) for s, d in scratch]
        + [pltpu.SemaphoreType.DMA((counts[0],)), pltpu.SemaphoreType.DMA((counts[0],)), pltpu.SemaphoreType.DMA((counts[1],))],
        compiler_params=pltpu.CompilerParams(collective_id=3, has_side_effects=True, vmem_limit_bytes=62 * 2**20),
        name="middle_exchange",
    )(a, slope, n2, fc1, fc2, dense, cot, h2, heads, w2.reshape((4, 2, 2) + w2.shape[1:]), vec)


def backward_kernel(
    seqs, shards, counts, one_seq,
    qkv, do, n1, qkvw, x_all, dh2, keep, give, ry2, w1, wd, smalls, vec, slopes, idc, idr, beginr,
    ret_y, ret_x, o_qkv, o_dense, o_up, o_down, o_small,
    qkv_v, do_v, dqkv_v, n1_v, qkvw_v, x_v, dh2_v, dk_acc, dv_acc, bias_acc, mine_v, sent_v, got_v, dx_v, gq_v,
    small_v, small_got, small_fin, small_last, f_qkv, f_dense, f_up, f_down, keep_v, give_v, y_v, own_w1, own_wd,
    *rest,
):
    bufs, (send_sems, recv_sems, copy_sems) = rest[:-3], rest[-3:]
    g = Geometry(seqs, shards)
    wires = Wires(g, send_sems, recv_sems)
    pairs, tokens = do_v.shape[0], do_v.shape[1]
    part = pairs * 2 * HEAD
    width = n1_v.shape[1]
    lanes = seqs * shards
    block = ROWS * lanes
    blocks = tokens // block
    half = block // seqs
    tile = bias_acc.shape[2]
    local = []

    def bring(src, dst):
        made = pltpu.make_async_copy(src, dst, copy_sems.at[len(local)])
        made.start()
        local.append(made)
        return made

    def held(ref):
        return lambda i, j: ref.at[i, j]

    down = Scatter(wires, None, None, (None,) + bufs[0:3])
    up = Scatter(wires, w1, held(own_w1), bufs[3:7])
    dense = Scatter(wires, wd, held(own_wd), bufs[7:11])
    qkv_sum = Scatter(wires, gq_v, lambda i, j: gq_v.at[i, j, g.c], bufs[11:15])
    back_y = Back(wires, y_v, ret_y, 1)
    give_at = wires.block(1)
    back_x = Back(wires, dx_v, ret_x, blocks)
    half_at = wires.block(blocks)
    small_at = wires.block(shards + 1)

    ry_in = bring(ry2, down.ry)
    first = [bring(qkv, qkv_v)] + [bring(do.at[:, pl.ds(h * 2 * HEAD, 2 * HEAD)], do_v.at[h]) for h in range(pairs)]
    owns = [bring(a.at[:, :, g.c], b) for a, b in ((w1, own_w1), (wd, own_wd))] + [bring(keep, keep_v)]
    later = [
        bring(n1, n1_v), bring(qkvw, qkvw_v), bring(x_all.at[:, pl.ds(g.s * shards, shards)], x_v), bring(dh2, dh2_v),
        bring(smalls, small_v),
    ]
    enter(g)
    up.core_send()
    dense.core_send()
    ry_in.wait()
    down.z_send()
    wires.send(give, give_v, give_at, 1 - g.s, g.k, give)
    for made in first + owns:
        made.wait()

    lane_id = lax.broadcasted_iota(jnp.int32, (1, 2 * HEAD), 1)

    def attend(h):
        q_ref, k_ref, v_ref, do_ref = qkv_v.at[h], qkv_v.at[pairs + h], qkv_v.at[2 * pairs + h], do_v.at[h]
        dk_acc[...] = jnp.zeros_like(dk_acc)
        dv_acc[...] = jnp.zeros_like(dv_acc)
        for j in range(2):
            bias_acc[j] = jnp.broadcast_to(slopes[h, j] * idc[...], bias_acc.shape[1:])
        cols = pl.ds(pl.multiple_of(h * 2 * HEAD, 2 * HEAD), 2 * HEAD)
        for b in range(blocks):
            end = (b + 1) * block
            for t in range(block // tile):
                at = pl.ds(b * block + t * tile, tile)
                q = q_ref[at, :] * jnp.asarray(HEAD**-0.5, bf16)
                grad = do_ref[at, :]
                ids_q = idr[:, at]
                both = None
                for j in range(2):
                    mine = (lane_id // HEAD) == j
                    qj = jnp.where(mine, q, jnp.zeros_like(q))
                    doj = jnp.where(mine, grad, jnp.zeros_like(grad))
                    s = lax.dot_general(
                        k_ref[:end, :], qj, (((1,), (1,)), ((), ())), preferred_element_type=f32
                    )
                    s = s + bias_acc[j, :end, :]
                    if one_seq:
                        tail = attn_mask(s[b * block :, :], idc[b * block : end, :] <= ids_q)
                        s = jnp.concatenate([s[: b * block, :], tail], axis=0) if b else tail
                    else:
                        ids_k = idc[:end, :]
                        s = attn_mask(s, (ids_k <= ids_q) & (ids_k >= beginr[:, at]))
                    top = jnp.max(s, axis=0, keepdims=True)
                    e = jnp.exp(s - top)
                    probs = e * (1.0 / jnp.sum(e, axis=0, keepdims=True))
                    dv_acc[:end, :] += jnp.dot(probs.astype(bf16), doj, preferred_element_type=f32)
                    dp = lax.dot_general(
                        v_ref[:end, :], doj, (((1,), (1,)), ((), ())), preferred_element_type=f32
                    )
                    inner = jnp.sum(probs * dp, axis=0, keepdims=True)
                    ds = (probs * (dp - inner)).astype(bf16)
                    dk_acc[:end, :] += jnp.dot(ds, qj, preferred_element_type=f32)
                    dq = lax.dot_general(
                        ds, k_ref[:end, :], (((0,), (0,)), ((), ())), preferred_element_type=f32
                    )
                    both = dq if both is None else jnp.where(mine, dq, both)
                dqkv_v[0, at, cols] = (both * (HEAD**-0.5)).astype(bf16)
        dqkv_v[1, :, cols] = dk_acc[...].astype(bf16)
        dqkv_v[2, :, cols] = dv_acc[...].astype(bf16)

    @pl.loop(0, pairs)
    def _(h):
        attend(h)

        @pl.when(h == 0)
        def _():
            up.core_done()

        @pl.when(h == 1)
        def _():
            dense.core_done()

        @pl.when(h == 2)
        def _():
            down.z_done()
            wires.arrived(give_v, give_at)

            @pl.loop(0, blocks)
            def _(b):
                y_v[b] = (keep_v[b] + give_v[b].astype(f32)).reshape(shards, ROWS, width).astype(bf16)

            back_y.send(0)

    for made in later:
        made.wait()

    rows = width // shards

    @pl.loop(0, blocks)
    def _(m):
        cut = n1_v[:, pl.ds(pl.multiple_of(m * block, block), block)]
        for p in range(3):
            out = lax.dot_general(cut, dqkv_v[p], (((0,), (0,)), ((), ())), preferred_element_type=f32).astype(bf16)
            out = out.reshape(block // rows // 2, 2, rows, part)
            for i in range(block // rows // 2):
                at = m * (block // rows // 2) + i
                for j in range(2):
                    gq_v[at // 2, at % 2, j, :, p * part : (p + 1) * part] = out[i, j]

    qkv_sum.core_send()

    for b in range(blocks):
        total = None
        for p in range(3):
            weight = qkvw_v[:, :, p * part : (p + 1) * part].reshape(width, part)
            term = lax.dot_general(
                dqkv_v[p, b * block : (b + 1) * block, :], weight, (((1,), (1,)), ((), ())), preferred_element_type=f32
            )
            total = term if total is None else total + term

        @pl.when(g.s == 0)
        def _(total=total, b=b):
            mine_v[b] = total[:half]
            sent_v[b] = total[half:].astype(bf16)

        @pl.when(g.s == 1)
        def _(total=total, b=b):
            mine_v[b] = total[half:]
            sent_v[b] = total[:half].astype(bf16)

        if b == 2:
            up.y_done()
            up.z_send()
        if b:
            wires.send(sent_v.at[b - 1], got_v.at[b - 1], half_at + b - 1, 1 - g.s, g.k, sent_v.at[b - 1])
    own_y = bring(y_v.at[:, g.k], ret_y.at[g.k])
    wires.send(sent_v.at[blocks - 1], got_v.at[blocks - 1], half_at + blocks - 1, 1 - g.s, g.k, sent_v.at[0])

    sums = [jnp.sum(dqkv_v[p].astype(f32), axis=0, keepdims=True) for p in (0, 2)]
    per = 2 * width // shards
    for i in range(part // per):
        for half_no in range(2):
            small_v[(half_no * width + g.s * part) // per + i, 2:3, :per] = sums[half_no][:, i * per : (i + 1) * per]
    qkv_sum.core_done()
    dense.y_done()
    dense.z_send()

    gains = biases = jnp.zeros((1, width), f32)
    for b in range(blocks):
        wires.arrived(got_v.at[b], half_at + b)
        grad = mine_v[b] + got_v[b].astype(f32)
        xhat, root = normalize(x_v[b].astype(f32).reshape(half, width))
        gains = gains + jnp.sum(grad * xhat, axis=0, keepdims=True)
        biases = biases + jnp.sum(grad, axis=0, keepdims=True)
        dx = dh2_v[b] + norm_pull(grad, vec[0:1, :width], xhat, root)
        dx_v[b] = dx.reshape(shards, ROWS, width).astype(bf16)
        back_x.send(b)
        if b == 0:
            up.z_done()
        if b == 2:
            qkv_sum.y_done()
            qkv_sum.z_send()
    for j in range(shards):
        small_v[j, 0:1, :rows] = gains[:, j * rows : (j + 1) * rows]
        small_v[j, 1:2, :rows] = biases[:, j * rows : (j + 1) * rows]
    kept = [own_y, bring(dx_v.at[:, g.k], ret_x.at[g.k])]
    for d in range(1, shards):
        to = (g.k + d) % shards
        wires.send(small_v.at[to], small_got.at[g.k], small_at + d, g.s, to, small_v.at[0])
    small_got[g.k] = small_v[g.k]
    down.final()
    dense.z_done()
    up.final()
    qkv_sum.z_done()
    for d in range(1, shards):
        wires.arrived(small_got.at[(g.k - d) % shards], small_at + d)
    small_fin[0] = jnp.sum(small_got[...], axis=0)
    wires.send(small_fin.at[0], small_fin.at[1], small_at + shards, 1 - g.s, g.k, small_fin.at[0])
    dense.final()

    down.done()
    ff_part = f_down.shape[0] // seqs
    for i, at in ((0, g.s), (1, 1 - g.s)):
        f_down[pl.ds(pl.multiple_of(at * ff_part, ff_part), ff_part), :] = down.fin[i].astype(f32)
    kept.append(bring(f_down, o_down))
    up.done()
    for i, at in ((0, g.s), (1, 1 - g.s)):
        for j in range(shards):
            f_up[:, pl.ds(pl.multiple_of((j * seqs + at) * ff_part, 128), ff_part)] = up.fin[
                i, :, j * ff_part : (j + 1) * ff_part
            ].astype(f32)
    kept.append(bring(f_up, o_up))
    dense.done()
    f_dense[...] = dense.fin[0].astype(f32) + dense.fin[1].astype(f32)
    kept.append(bring(f_dense, o_dense))
    wires.arrived(small_fin.at[1], small_at + shards)
    small_last[...] = small_fin[0] + small_fin[1]
    kept.append(bring(small_last, o_small))
    qkv_sum.final()
    qkv_sum.done()
    for i, at in ((0, g.s), (1, 1 - g.s)):
        for p in range(3):
            f_qkv[:, pl.ds(pl.multiple_of(p * width + at * part, 128), part)] = qkv_sum.fin[
                i, :, p * part : (p + 1) * part
            ].astype(f32)
    kept.append(bring(f_qkv, o_qkv))
    back_y.finish()
    back_x.finish()
    wires.drain()
    for made in kept:
        made.wait()
    assert wires.used <= counts[0] and len(local) <= counts[1]


def backward_exchange(
    qkv, do, n1, qkvw, x_all, dh2, keep, give, ry2, w1, wd, smalls, vec, slopes, ids, begins, seqs, shards, one_seq
):
    tokens, part = do.shape
    width = n1.shape[1]
    pairs = part // (2 * HEAD)
    lanes = seqs * shards
    block = ROWS * lanes
    blocks, half = tokens // block, block // seqs
    tile = min(256, block)
    rows, ff = width // shards, w1.shape[2]
    ff_part = ff // shards
    counts = (256, 48)
    cut = lambda a: a.reshape((4, 2, 2) + a.shape[1:])
    any_, vmem = pl.BlockSpec(memory_space=pl.ANY), pl.BlockSpec(memory_space=pltpu.VMEM)
    ret = (shards, blocks, ROWS, width)
    outs = [
        (ret, bf16), (ret, bf16), ((rows, 3 * width), f32), ((rows, width), f32), ((rows, seqs * ff), f32),
        ((seqs * ff_part, width), f32), (smalls.shape[1:], f32),
    ]
    blks = [(ff_part, width), (rows, ff), (rows, width), (rows, 3 * part)]
    scratch = [
        ((3 * pairs, tokens, 2 * HEAD), bf16), ((pairs, tokens, 2 * HEAD), bf16), ((3, tokens, part), bf16),
        ((tokens, width), bf16), ((shards, rows, 3 * part), bf16), ((blocks, shards, ROWS, width), bf16),
        ((blocks, half, width), f32), ((tokens, 2 * HEAD), f32), ((tokens, 2 * HEAD), f32), ((2, tokens, tile), f32),
        ((blocks, half, width), f32), ((blocks, half, width), bf16), ((blocks, half, width), bf16),
        ((blocks, shards, ROWS, width), bf16), ((4, 2, 2) + blks[3], bf16), (smalls.shape, f32), (smalls.shape, f32),
        ((2,) + smalls.shape[1:], f32), (smalls.shape[1:], f32), ((rows, 3 * width), f32), ((rows, width), f32), ((rows, seqs * ff), f32),
        ((seqs * ff_part, width), f32), ((blocks, half, width), f32), ((blocks, half, width), bf16),
        ((blocks, shards, ROWS, width), bf16), ((4, 2) + blks[1], bf16), ((4, 2) + blks[2], bf16),
    ]
    for blk in blks:
        scratch += [((4, 2) + blk, bf16)] * (blk is not blks[0])
        scratch += [((4,) + blk, bf16), ((4,) + blk, bf16), ((2,) + blk, bf16)]
    return pl.pallas_call(
        functools.partial(backward_kernel, seqs, shards, counts, one_seq),
        in_specs=[any_] * 12 + [vmem, pl.BlockSpec(memory_space=pltpu.SMEM)] + [vmem] * 3,
        out_specs=[any_] * len(outs),
        out_shape=[jax.ShapeDtypeStruct(s, d) for s, d in outs],
        scratch_shapes=[pltpu.VMEM(s, d) for s, d in scratch]
        + [pltpu.SemaphoreType.DMA((counts[0],)), pltpu.SemaphoreType.DMA((counts[0],)), pltpu.SemaphoreType.DMA((counts[1],))],
        compiler_params=pltpu.CompilerParams(collective_id=2, has_side_effects=True, vmem_limit_bytes=60 * 2**20),
        name="backward_exchange",
    )(
        qkv, do, n1, qkvw, x_all, dh2, keep, give, ry2, cut(w1), cut(wd), smalls, vec, slopes.reshape(pairs, 2),
        ids[:, None], ids[None, :], begins[None, :],
    )


def layout_tables(lengths, lane_count, group_count, per_group):
    seq_rows = lengths // lane_count
    row_start = jnp.cumsum(seq_rows) - seq_rows
    slot_rows = seq_rows.reshape(group_count, per_group)
    slot_start = row_start.reshape(group_count, per_group)
    slot_before = jnp.cumsum(slot_rows, axis=1) - slot_rows
    return seq_rows, row_start, slot_rows, slot_start, slot_before


def per_device(
    tokens, cotangent, lengths, first_gain, first_bias, qkv_weight, qv_bias, dense_weight, dense_bias,
    second_gain, second_bias, fc1_weight, fc1_bias, fc2_weight, fc2_bias,
):
    shards, seqs = lax.axis_size("shard"), lax.axis_size("seq")
    lanes = shards * seqs
    slots, width = tokens.shape[1], tokens.shape[2]
    rows = slots // shards
    cap = slots * seqs
    per_group = lengths.shape[0] // shards
    hidden_units = fc1_weight.shape[1]
    me, group = lax.axis_index("seq"), lax.axis_index("shard")
    blocks = rows // ROWS
    heads = width // HEAD // seqs
    part = heads * HEAD
    ff_part = hidden_units // shards // seqs

    smalls_in = (first_gain, first_bias, qv_bias, dense_bias, second_gain, second_bias, fc1_bias, fc2_bias)
    small_width = -(-max(a.shape[0] for a in smalls_in) // 128) * 128
    small = jnp.stack([jnp.pad(a.astype(f32), (0, small_width - a.shape[0])) for a in smalls_in])

    seq_rows, row_start, slot_rows, slot_start, slot_before = layout_tables(lengths, lanes, shards, per_group)
    row_in = jnp.arange(rows, dtype=jnp.int32)[None, :, None]
    inside = ((row_in >= slot_before[:, None]) & (row_in < (slot_before + slot_rows)[:, None])).astype(jnp.int32)
    send_live = jnp.sum(inside, axis=2) > 0
    send_row = jnp.sum(inside * (slot_start[:, None] + row_in - slot_before[:, None]), axis=2).reshape(-1)

    def pack(source):
        return jnp.take(source, send_row, axis=0).reshape(shards, rows, width)

    place = jnp.arange(cap, dtype=jnp.int32)
    block_of, in_block = place // (ROWS * lanes), place % (ROWS * lanes)
    row_of = block_of * ROWS + in_block % ROWS
    ids = row_of * lanes + in_block // ROWS
    own_before, own_count = take(slot_before, group), take(slot_rows, group)
    holds = (row_of[:, None] >= own_before[None]) & (row_of[:, None] < (own_before + own_count)[None])
    begin_row = jnp.sum(jnp.where(holds, own_before[None], 0), axis=1)
    begins = jnp.where(jnp.any(holds, axis=1), begin_row * lanes, ids)
    ids, begins = ids.astype(f32), begins.astype(f32)
    head_ids = me * heads + jnp.arange(heads, dtype=jnp.int32)
    slopes = 2.0 ** (-8.0 * (head_ids.astype(f32) + 1.0) / HEADS)
    one_seq = per_group == 1

    blocked = (shards, blocks, ROWS, width)
    live = jnp.any(holds, axis=1).astype(f32)
    (
        x_all, cot_all, normed_one, normed_two, full_qkv, full_dense, full_up, full_down, qkv, mixed, resid, activ, slope,
        grad_down, vectors,
    ) = forward_exchange(
        pack(tokens[0]).reshape(blocked), pack(cotangent[0]).reshape(blocked),
        qkv_weight, small, dense_weight, fc1_weight, fc2_weight,
        slopes, ids, begins, live, seqs, shards, one_seq,
    )
    grad_resid, grad_mixed, grad_up, grad_dense, keep, give, half_sums, small_grads = middle_exchange(
        activ, slope, normed_two, full_up, full_down, full_dense, cot_all, resid, mixed, grad_down, vectors, seqs, shards
    )
    ret_out, ret_grad, g_qkv, g_dense, g_up, g_down, g_small = backward_exchange(
        qkv, grad_mixed.reshape(cap, part), normed_one, full_qkv, x_all, grad_resid, keep, give, half_sums,
        grad_up, grad_dense, small_grads, vectors, slopes, ids, begins, seqs, shards, one_seq,
    )

    row_here = jnp.arange(slots, dtype=jnp.int32)[:, None]
    seq_in = ((row_here >= row_start[None]) & (row_here < (row_start + seq_rows)[None])).astype(jnp.int32)
    home = jnp.arange(lengths.shape[0], dtype=jnp.int32) // per_group
    fetch = jnp.sum(seq_in * (home[None] * rows + slot_before.reshape(-1)[None] + row_here - row_start[None]), axis=1)
    fetch_live = jnp.sum(seq_in, axis=1) > 0

    def to_stream(got):
        taken = jnp.take(got.reshape(-1, width), fetch, axis=0)
        return jnp.where(fetch_live[:, None], taken, jnp.zeros_like(taken))[None]

    g_gain_one, g_bias_one, g_qv, g_bdense, g_gain_two, g_bias_two, g_bup, g_bdown = (
        g_small[i, : a.shape[0]] for i, a in enumerate(smalls_in)
    )
    return (
        to_stream(ret_out), to_stream(ret_grad),
        g_gain_one, g_bias_one, g_qkv, g_qv, g_dense, g_bdense, g_gain_two, g_bias_two, g_up, g_bup, g_down, g_bdown,
    )


def per_device_any(
    tokens, cotangent, lengths, first_gain, first_bias, qkv_weight, qv_bias, dense_weight, dense_bias,
    second_gain, second_bias, fc1_weight, fc1_bias, fc2_weight, fc2_bias,
):
    shards, seqs = lax.axis_size("shard"), lax.axis_size("seq")
    lanes = shards * seqs
    slots, width = tokens.shape[1], tokens.shape[2]
    rows = slots // shards
    cap = slots * seqs
    per_group = lengths.shape[0] // shards
    hidden_units = fc1_weight.shape[1]
    me, group = lax.axis_index("seq"), lax.axis_index("shard")
    blocks = rows // ROWS
    heads = width // HEAD // seqs
    part = heads * HEAD
    ff_part = hidden_units // shards // seqs

    qkv_half = take(qkv_weight.reshape(-1, 3, seqs, part), me, 2).reshape(-1, 3 * part)
    fc1_half = take(fc1_weight.reshape(-1, shards, seqs, ff_part), me, 2).reshape(-1, shards * ff_part)
    fc2_half = take(fc2_weight.reshape(seqs, ff_part, width), me, 0)
    small = jnp.concatenate(
        [first_gain, first_bias, qv_bias, dense_bias, second_gain, second_bias, fc1_bias, fc2_bias]
    )
    small_rows = -(-small.shape[0] // (3 * part))
    small_rows += -small_rows % 16
    small = jnp.pad(small, (0, small_rows * 3 * part - small.shape[0])).reshape(small_rows, 3 * part)
    gather = lambda a: lax.all_gather(a, "shard", axis=0, tiled=False)
    qkv_small = gather(jnp.concatenate([qkv_half, small], axis=0))
    own_rows = qkv_half.shape[0]
    full_qkv = qkv_small[:, :own_rows].reshape(width, 3 * part)
    smalls = qkv_small[:, own_rows:].reshape(shards, -1).astype(f32)
    full_dense = gather(dense_weight).reshape(width, width)
    full_up = gather(fc1_half).reshape(width, shards * ff_part)
    full_down = gather(fc2_half).reshape(shards * ff_part, width)
    cuts, at = [], 0
    for a in (first_gain, first_bias, qv_bias, dense_bias, second_gain, second_bias, fc1_bias, fc2_bias):
        cuts.append(smalls[:, at : at + a.shape[0]].reshape(-1))
        at += a.shape[0]
    gain_one, bias_one, bias_qv, bias_dense, gain_two, bias_two, bias_up, bias_down = cuts
    bias_q, bias_v = (take(bias_qv[i * width : (i + 1) * width].reshape(seqs, part), me) for i in (0, 1))
    bias_all = jnp.concatenate([bias_q, jnp.zeros_like(bias_q), bias_v])
    bias_up = take(bias_up.reshape(shards, seqs, ff_part), me, 1).reshape(-1)

    seq_rows, row_start, slot_rows, slot_start, slot_before = layout_tables(lengths, lanes, shards, per_group)
    row_in = jnp.arange(rows, dtype=jnp.int32)[None, :, None]
    inside = ((row_in >= slot_before[:, None]) & (row_in < (slot_before + slot_rows)[:, None])).astype(jnp.int32)
    send_live = jnp.sum(inside, axis=2) > 0
    send_row = jnp.sum(inside * (slot_start[:, None] + row_in - slot_before[:, None]), axis=2).reshape(-1)

    def to_groups(source):
        packed = jnp.take(source, send_row, axis=0).reshape(shards, rows, width)
        packed = jnp.where(send_live[:, :, None], packed, jnp.zeros_like(packed))
        got = lax.all_to_all(packed, "shard", split_axis=0, concat_axis=0, tiled=True)
        own = got.reshape(shards, blocks, ROWS, width).transpose(1, 0, 2, 3).reshape(blocks, -1, width)
        return own, seq_gather(own, 1).reshape(cap, width)

    x_own, x_low = to_groups(tokens[0])
    cot_own, cot_low = to_groups(cotangent[0])

    def own_part(whole):
        return take(whole.reshape(blocks, seqs, -1, whole.shape[-1]), me, 1)

    place = jnp.arange(cap, dtype=jnp.int32)
    block_of, in_block = place // (ROWS * lanes), place % (ROWS * lanes)
    row_of = block_of * ROWS + in_block % ROWS
    ids = row_of * lanes + in_block // ROWS
    own_before, own_count = take(slot_before, group), take(slot_rows, group)
    holds = (row_of[:, None] >= own_before[None]) & (row_of[:, None] < (own_before + own_count)[None])
    begin_row = jnp.sum(jnp.where(holds, own_before[None], 0), axis=1)
    begins = jnp.where(jnp.any(holds, axis=1), begin_row * lanes, ids)
    ids, begins = ids.astype(f32), begins.astype(f32)
    head_ids = me * heads + jnp.arange(heads, dtype=jnp.int32)
    slopes = 2.0 ** (-8.0 * (head_ids.astype(f32) + 1.0) / HEADS)
    one_seq = per_group == 1

    hidden = x_low.astype(f32)
    xhat_one, _ = normalize(hidden)
    normed_one = (xhat_one * gain_one + bias_one).astype(bf16)
    qkv = (jnp.dot(normed_one, full_qkv, preferred_element_type=f32) + bias_all).astype(bf16)
    mixed = attention_forward(qkv, slopes, ids, begins, lanes, one_seq)
    mixed_all = seq_gather(mixed, 1).reshape(cap, width)
    branch = jnp.dot(mixed_all, full_dense, preferred_element_type=f32) + bias_dense
    resid = hidden + branch
    xhat_two, _ = normalize(resid)
    normed_two = (xhat_two * gain_two + bias_two).astype(bf16)
    upper = jnp.dot(normed_two, full_up, preferred_element_type=f32) + bias_up
    activ = gelu_tanh(upper).astype(bf16)
    down = jnp.dot(activ, full_down, preferred_element_type=f32)
    resid_own = own_part(resid)
    down_own = seq_sum(down.reshape(blocks, seqs, -1, width), 1)
    block_out = (resid_own + down_own + bias_down).astype(bf16)

    grad_down = jnp.dot(activ.T, cot_low, preferred_element_type=f32).astype(bf16)
    grad_activ = jnp.dot(cot_low, full_down.T, preferred_element_type=f32)
    grad_upper = jax.vjp(gelu_tanh, upper)[1](grad_activ)[0].astype(bf16)
    grad_up = jnp.dot(normed_two.T, grad_upper, preferred_element_type=f32).astype(bf16)
    grad_bup = jnp.sum(grad_upper.astype(f32), axis=0)
    grad_normed = jnp.dot(grad_upper, full_up.T, preferred_element_type=f32)
    grad_normed = seq_sum(grad_normed.reshape(blocks, seqs, -1, width), 1).reshape(slots, width)
    cot_full = cot_own.reshape(slots, width).astype(f32)
    grad_bdown = jnp.sum(cot_full, axis=0)
    xhat_two, root_two = normalize(resid_own.reshape(slots, width))
    grad_gain_two = jnp.sum(grad_normed * xhat_two, axis=0)
    grad_bias_two = jnp.sum(grad_normed, axis=0)
    grad_resid = cot_full + norm_pull(grad_normed, gain_two, xhat_two, root_two)

    grad_branch = grad_resid.astype(bf16)
    grad_dense = jnp.dot(own_part(mixed_all).reshape(slots, width).T, grad_branch, preferred_element_type=f32).astype(bf16)
    grad_bdense = jnp.sum(grad_branch.astype(f32), axis=0)
    grad_mixed = jnp.dot(grad_branch, full_dense.T, preferred_element_type=f32).astype(bf16)
    got = seq_blocks(grad_mixed.reshape(blocks, -1, seqs, part), 2, bf16)
    if seqs == 2:
        grad_mixed = jnp.where(me == 0, jnp.stack(got, 1), jnp.stack(got[::-1], 1))
    else:
        grad_mixed = jnp.zeros((blocks, seqs) + got[0].shape[1:], bf16)
        for d, g in enumerate(got):
            grad_mixed = lax.dynamic_update_index_in_dim(grad_mixed, g, (me - d) % seqs, 1)
    grad_mixed = grad_mixed.reshape(cap, part)
    planes = qkv.reshape(cap, -1, 2 * HEAD).transpose(1, 0, 2)
    grad_proj = jnp.concatenate(
        attention_backward(planes, grad_mixed, slopes, ids, begins, lanes, one_seq), axis=1
    )
    grad_qkv = jnp.dot(normed_one.T, grad_proj, preferred_element_type=f32).astype(bf16)
    proj_sums = jnp.sum(grad_proj.astype(f32), axis=0)
    grad_one = jnp.dot(grad_proj, full_qkv.T, preferred_element_type=f32)
    grad_one = seq_sum(grad_one.reshape(blocks, seqs, -1, width), 1).reshape(slots, width)
    xhat_one, root_one = normalize(x_own.reshape(slots, width).astype(f32))
    grad_gain_one = jnp.sum(grad_one * xhat_one, axis=0)
    grad_bias_one = jnp.sum(grad_one, axis=0)
    tokens_grad = (grad_resid + norm_pull(grad_one, gain_one, xhat_one, root_one)).astype(bf16)

    row_here = jnp.arange(slots, dtype=jnp.int32)[:, None]
    seq_in = ((row_here >= row_start[None]) & (row_here < (row_start + seq_rows)[None])).astype(jnp.int32)
    home = jnp.arange(lengths.shape[0], dtype=jnp.int32) // per_group
    fetch = jnp.sum(seq_in * (home[None] * rows + slot_before.reshape(-1)[None] + row_here - row_start[None]), axis=1)
    fetch_live = jnp.sum(seq_in, axis=1) > 0

    def to_stream(own):
        sent = own.reshape(blocks, shards, ROWS, width).transpose(1, 0, 2, 3).reshape(shards, rows, width)
        got = lax.all_to_all(sent, "shard", split_axis=0, concat_axis=0, tiled=True)
        taken = jnp.take(got.reshape(-1, width), fetch, axis=0)
        return jnp.where(fetch_live[:, None], taken, jnp.zeros_like(taken))[None]

    down_block = shard_reduce(grad_down.reshape(shards, ff_part, width), bf16)
    up_block = shard_reduce(grad_up.reshape(shards, -1, shards * ff_part), bf16)
    dense_block = shard_reduce(grad_dense.reshape(shards, -1, width), bf16)
    qkv_block = shard_reduce(grad_qkv.reshape(shards, -1, 3 * part), bf16)

    def spread(vector, index_shape):
        zero = jnp.zeros(index_shape, f32)
        return lax.dynamic_update_index_in_dim(zero, vector, me, 1)

    sums = proj_sums.reshape(3, part)
    qv = spread(jnp.stack([sums[0], sums[2]]), (2, seqs, part)).reshape(shards, -1)
    bup = spread(grad_bup.reshape(shards, ff_part), (shards, seqs, ff_part)).reshape(shards, -1)
    rest = (grad_gain_one, grad_bias_one, grad_bdense, grad_gain_two, grad_bias_two, grad_bdown)
    packed = jnp.concatenate([a.reshape(shards, -1) for a in rest] + [qv, bup], axis=1)
    packed = shard_reduce(packed, f32)
    packed = jnp.sum(seq_gather(packed, 0), axis=0)
    cuts, at = [], 0
    for a in [a.reshape(shards, -1) for a in rest] + [qv, bup]:
        cuts.append(packed[at : at + a.shape[1]])
        at += a.shape[1]
    g_gain_one, g_bias_one, g_bdense, g_gain_two, g_bias_two, g_bdown, g_qv, g_bup = cuts

    g_dense = jnp.sum(seq_gather(dense_block.astype(bf16), 0).astype(f32), axis=0)
    g_qkv = seq_gather(qkv_block.astype(bf16).reshape(-1, 3, part), 2).reshape(-1, 3 * width).astype(f32)
    g_up = seq_gather(up_block.astype(bf16).reshape(-1, shards, ff_part), 2).reshape(-1, hidden_units).astype(f32)
    g_down = seq_gather(down_block.astype(bf16), 0).reshape(-1, width).astype(f32)
    return (
        to_stream(block_out), to_stream(tokens_grad.reshape(blocks, -1, width)),
        g_gain_one, g_bias_one, g_qkv, g_qv, g_dense, g_bdense, g_gain_two, g_bias_two, g_up, g_bup, g_down, g_bdown,
    )


def solution(mesh):
    rows, vector, stream = P("shard", None), P("shard"), P(("seq", "shard"), None, None)
    params = (vector, vector, rows, vector, rows, vector, vector, vector, rows, vector, rows, vector)
    fused = mesh.shape["seq"] == 2 and shard_factors(mesh.shape["shard"])[0] == 4
    return jax.shard_map(
        per_device if fused else per_device_any, mesh=mesh, in_specs=(stream, stream, P()) + params, out_specs=(stream, stream) + params, check_vma=False
    )
```

```python
import functools

import jax
import jax.numpy as jnp
import numpy as np
from jax import lax
from jax.experimental import pallas as pl
from jax.experimental.pallas import tpu as pltpu
from jax.sharding import PartitionSpec as P

HEADS = 16
HEAD = 64
ROWS = 8

epsilon = 1e-05
masked_score = -1e30
f32 = jnp.float32
bf16 = jnp.bfloat16


def gelu_tanh(values):
    return (
        0.5
        * values
        * (1.0 + jnp.tanh(0.7978845608028654 * (values + 0.044715 * values * values * values)))
    )


def normalize(hidden):
    center = hidden - jnp.mean(hidden, axis=-1, keepdims=True)
    spread = jnp.mean(center * center, axis=-1, keepdims=True)
    root = lax.rsqrt(spread + epsilon)
    return center * root, root


def norm_pull(grad, gain, xhat, root):
    scaled = grad * gain
    return root * (
        scaled
        - jnp.mean(scaled, axis=-1, keepdims=True)
        - xhat * jnp.mean(scaled * xhat, axis=-1, keepdims=True)
    )


def slot_ids(first, count, lanes):
    place = first + lax.broadcasted_iota(jnp.int32, (count, 1), 0)
    block, inside = place // (ROWS * lanes), place % (ROWS * lanes)
    return (block * ROWS + inside % ROWS) * lanes + inside // ROWS


def blocked_ids(shape, axis, lanes):
    place = lax.broadcasted_iota(jnp.int32, shape, axis)
    high = (ROWS * lanes).bit_length() - 1
    inside = place & (ROWS * lanes - 1)
    row = (place >> high) * ROWS + (inside & (ROWS - 1))
    return (row * lanes + (inside >> (ROWS.bit_length() - 1))).astype(f32)


def attn_mask(scored, allowed):
    return jnp.where(allowed, scored, masked_score)


def attn_fwd_kernel(lanes, tile, one_seq, slope_ref, idc_ref, idr_ref, beginc_ref, q_ref, k_ref, v_ref, o_ref):
    tokens = q_ref.shape[0]
    block = ROWS * lanes
    lane_id = lax.broadcasted_iota(jnp.int32, (1, 2 * HEAD), 1)
    for b in range(tokens // block):
        end = (b + 1) * block

        def step(t, _):
            at = pl.ds(pl.multiple_of(b * block + t * tile, tile), tile)
            q = q_ref[at, :] * jnp.asarray(HEAD**-0.5, bf16)
            ids_q = idc_ref[at, :]
            both = None
            for j in range(2):
                mine = (lane_id // HEAD) == j
                qj = jnp.where(mine, q, jnp.zeros_like(q))
                s = lax.dot_general(
                    qj, k_ref[:end, :], (((1,), (1,)), ((), ())), preferred_element_type=f32
                )
                s = s + slope_ref[0, 0, j] * idr_ref[:, :end]
                if one_seq:
                    own = s[:, b * block :]
                    own = attn_mask(own, idr_ref[:, b * block : end] <= ids_q)
                    s = jnp.concatenate([s[:, : b * block], own], axis=1) if b else own
                else:
                    ids_k = idr_ref[:, :end]
                    s = attn_mask(s, (ids_k <= ids_q) & (ids_k >= beginc_ref[at, :]))
                top = jnp.max(s, axis=1, keepdims=True)
                e = jnp.exp(s - top)
                total = jnp.sum(e, axis=1, keepdims=True)
                o = jnp.dot(e.astype(bf16), v_ref[:end, :], preferred_element_type=f32) / total
                both = o if both is None else jnp.where(mine, o, both)
            o_ref[at, :] = both.astype(bf16)
            return 0

        lax.fori_loop(0, block // tile, step, 0)


def attn_bwd_kernel(
    lanes, tile, one_seq, slope_ref, idc_ref, idr_ref, beginr_ref, q_ref, k_ref, v_ref, do_ref,
    dq_ref, dk_ref, dv_ref, dk_acc, dv_acc, bias_acc,
):
    tokens = q_ref.shape[0]
    block = ROWS * lanes
    lane_id = lax.broadcasted_iota(jnp.int32, (1, 2 * HEAD), 1)
    dk_acc[...] = jnp.zeros_like(dk_acc)
    dv_acc[...] = jnp.zeros_like(dv_acc)
    for j in range(2):
        bias_acc[j] = jnp.broadcast_to(slope_ref[0, 0, j] * idc_ref[...], (tokens, tile))
    for b in range(tokens // block):
        end = (b + 1) * block

        def step(t, _):
            at = pl.ds(pl.multiple_of(b * block + t * tile, tile), tile)
            q = q_ref[at, :] * jnp.asarray(HEAD**-0.5, bf16)
            do = do_ref[at, :]
            ids_q = idr_ref[:, at]
            both = None
            for j in range(2):
                mine = (lane_id // HEAD) == j
                qj = jnp.where(mine, q, jnp.zeros_like(q))
                doj = jnp.where(mine, do, jnp.zeros_like(do))
                s = lax.dot_general(
                    k_ref[:end, :], qj, (((1,), (1,)), ((), ())), preferred_element_type=f32
                )
                s = s + bias_acc[j, :end, :]
                if one_seq:
                    own = s[b * block :, :]
                    own = attn_mask(own, idc_ref[b * block : end, :] <= ids_q)
                    s = jnp.concatenate([s[: b * block, :], own], axis=0) if b else own
                else:
                    ids_k = idc_ref[:end, :]
                    s = attn_mask(s, (ids_k <= ids_q) & (ids_k >= beginr_ref[:, at]))
                top = jnp.max(s, axis=0, keepdims=True)
                e = jnp.exp(s - top)
                probs = e * (1.0 / jnp.sum(e, axis=0, keepdims=True))
                dv_acc[:end, :] += jnp.dot(probs.astype(bf16), doj, preferred_element_type=f32)
                dp = lax.dot_general(
                    v_ref[:end, :], doj, (((1,), (1,)), ((), ())), preferred_element_type=f32
                )
                inner = jnp.sum(probs * dp, axis=0, keepdims=True)
                ds = (probs * (dp - inner)).astype(bf16)
                dk_acc[:end, :] += jnp.dot(ds, qj, preferred_element_type=f32)
                dq = lax.dot_general(
                    ds, k_ref[:end, :], (((0,), (0,)), ((), ())), preferred_element_type=f32
                )
                both = dq if both is None else jnp.where(mine, dq, both)
            dq_ref[at, :] = (both * (HEAD**-0.5)).astype(bf16)
            return 0

        lax.fori_loop(0, block // tile, step, 0)
    dk_ref[...] = dk_acc[...].astype(bf16)
    dv_ref[...] = dv_acc[...].astype(bf16)


def attn_shape(tokens, width, lanes):
    pairs = width // (2 * HEAD)
    tile = min(256, ROWS * lanes)
    return pairs, tile


def attention_forward(qkv, slopes, ids, begins, lanes, one_seq):
    tokens, width = qkv.shape[0], qkv.shape[1] // 3
    pairs, tile = attn_shape(tokens, width, lanes)
    column = lambda part: pl.BlockSpec((tokens, 2 * HEAD), lambda h, part=part: (0, part * pairs + h))
    whole = lambda a: pl.BlockSpec(a.shape, lambda h: (0, 0))
    idc, idr, beginc = ids[:, None], ids[None, :], begins[:, None]
    half = tokens * tokens * 5 // 8
    return pl.pallas_call(
        functools.partial(attn_fwd_kernel, lanes, tile, one_seq),
        grid=(pairs,),
        in_specs=[
            pl.BlockSpec((1, 1, 2), lambda h: (h, 0, 0), memory_space=pltpu.SMEM),
            whole(idc), whole(idr), whole(beginc), column(0), column(1), column(2),
        ],
        out_specs=pl.BlockSpec((tokens, 2 * HEAD), lambda h: (0, h)),
        out_shape=jax.ShapeDtypeStruct((tokens, width), bf16),
        compiler_params=pltpu.CompilerParams(vmem_limit_bytes=48 * 2**20),
        cost_estimate=pl.CostEstimate(
            flops=8 * pairs * half * HEAD * 2, transcendentals=2 * pairs * half, bytes_accessed=8 * tokens * width
        ),
        name="attention_forward",
    )(slopes.reshape(pairs, 1, 2), idc, idr, beginc, qkv, qkv, qkv)


def attention_backward(qkv, grad_out, slopes, ids, begins, lanes, one_seq):
    tokens, width = grad_out.shape
    pairs, tile = attn_shape(tokens, width, lanes)
    column = lambda part: pl.BlockSpec((tokens, 2 * HEAD), lambda h, part=part: (0, part * pairs + h))
    whole = lambda a: pl.BlockSpec(a.shape, lambda h: (0, 0))
    idc, idr, beginr = ids[:, None], ids[None, :], begins[None, :]
    plane = lambda part: pl.BlockSpec((None, tokens, 2 * HEAD), lambda h, part=part: (part * pairs + h, 0, 0))
    out = jax.ShapeDtypeStruct((tokens, width), bf16)
    half = tokens * tokens * 5 // 8
    return pl.pallas_call(
        functools.partial(attn_bwd_kernel, lanes, tile, one_seq),
        grid=(pairs,),
        in_specs=[
            pl.BlockSpec((1, 1, 2), lambda h: (h, 0, 0), memory_space=pltpu.SMEM),
            whole(idc), whole(idr), whole(beginr), plane(0), plane(1), plane(2), column(0),
        ],
        out_specs=[column(0)] * 3,
        out_shape=[out] * 3,
        scratch_shapes=[
            pltpu.VMEM((tokens, 2 * HEAD), f32), pltpu.VMEM((tokens, 2 * HEAD), f32), pltpu.VMEM((2, tokens, tile), f32),
        ],
        compiler_params=pltpu.CompilerParams(vmem_limit_bytes=56 * 2**20),
        cost_estimate=pl.CostEstimate(
            flops=20 * pairs * half * HEAD * 2, transcendentals=2 * pairs * half, bytes_accessed=14 * tokens * width
        ),
        name="attention_backward",
    )(slopes.reshape(pairs, 1, 2), idc, idr, beginr, qkv, qkv, qkv, grad_out)


def take(blocks, index, axis=0):
    return lax.dynamic_index_in_dim(blocks, index, axis, keepdims=False)


def seq_gather(block, axis):
    n, me = lax.axis_size("seq"), lax.axis_index("seq")
    shape = block.shape[:axis] + (n,) + block.shape[axis:]
    if n == 2:
        peer = lax.ppermute(block, "seq", [(0, 1), (1, 0)])
        return jnp.where(me == 0, jnp.stack([block, peer], axis), jnp.stack([peer, block], axis))
    whole = lax.dynamic_update_index_in_dim(jnp.zeros(shape, block.dtype), block, me, axis)
    for d in range(1, n):
        got = lax.ppermute(block, "seq", [(i, (i + d) % n) for i in range(n)])
        whole = lax.dynamic_update_index_in_dim(whole, got, (me - d) % n, axis)
    return whole


def seq_blocks(whole, axis, dtype):
    n, me = lax.axis_size("seq"), lax.axis_index("seq")
    got = [take(whole, me, axis)]
    for d in range(1, n):
        sent = take(whole, (me + d) % n, axis).astype(dtype)
        got.append(lax.ppermute(sent, "seq", [(i, (i + d) % n) for i in range(n)]))
    return got


def seq_sum(whole, axis, dtype=bf16):
    got = seq_blocks(whole, axis, dtype)
    return sum((g.astype(f32) for g in got[1:]), got[0].astype(f32))


def shard_factors(n):
    nc = 2 if n % 2 == 0 else 1
    nz = 4 if n % (4 * nc) == 0 else 1
    return nz, n // (nz * nc), nc


def shard_reduce(blocks, dtype):
    n, me = lax.axis_size("shard"), lax.axis_index("shard")
    sizes = shard_factors(n)
    blocks = blocks.reshape(sizes + blocks.shape[1:])
    place = (me // (sizes[1] * sizes[2]), me // sizes[2] % sizes[1], me % sizes[2])
    strides = (sizes[1] * sizes[2], sizes[2], 1)
    for axis in (2, 1, 0):
        size, mine, stride = sizes[axis], place[axis], strides[axis]
        total = take(blocks, mine, axis).astype(f32)
        for d in range(1, size):
            sent = take(blocks, (mine + d) % size, axis).astype(dtype)
            pairs = [
                (i, i - (i // stride % size) * stride + ((i // stride % size + d) % size) * stride)
                for i in range(n)
            ]
            total = total + lax.ppermute(sent, "shard", pairs).astype(f32)
        blocks = total if axis == 0 else total.astype(dtype)
    return blocks


MESH = pl.DeviceIdType.MESH


class Geometry:
    def __init__(self, seqs, shards):
        self.seqs, self.shards = seqs, shards
        self.sizes = shard_factors(shards)
        self.s, self.k = lax.axis_index("seq"), lax.axis_index("shard")
        nz, ny, nc = self.sizes
        self.z, self.y, self.c = self.k // (ny * nc), self.k // nc % ny, self.k % nc
        self.inner = (self.z + 1) // 2 % 2
        high = self.z // 2
        self.line = (self.z, self.z + 1 - 2 * (self.z % 2), 2 - high, 3 - 3 * high)

    def slot(self, i, dy, dc):
        nz, ny, nc = self.sizes
        return (self.line[i] * ny + (self.y + dy) % ny) * nc + (self.c + dc) % nc


class Wires:
    def __init__(self, geometry, send_sems, recv_sems):
        self.g, self.send_sems, self.recv_sems = geometry, send_sems, recv_sems
        self.sends, self.used = [], 0

    def block(self, count):
        first = self.used
        self.used += count
        return first

    def copy(self, src, dst, sent, got, s, k):
        return pltpu.make_async_remote_copy(
            src_ref=src, dst_ref=dst, send_sem=self.send_sems.at[sent], recv_sem=self.recv_sems.at[got],
            device_id={"seq": s, "shard": k}, device_id_type=MESH,
        )

    def send_as(self, src, dst, sent, got, s, k, like):
        self.copy(src, dst, sent, got, s, k).start()
        self.sends.append((like, sent))

    def recorded(self, like, index):
        self.sends.append((like, index))

    def send(self, src, dst, index, s, k, like):
        self.send_as(src, dst, index, index, s, k, like)

    def arrived(self, dst, index):
        self.copy(dst, dst, index, index, 1 - self.g.s, self.g.k).wait_recv()

    def drain(self):
        for like, index in self.sends:
            self.copy(like, like, index, index, 1 - self.g.s, self.g.k).wait_send()
        self.sends = []


def enter(geometry):
    g = geometry
    barrier = pltpu.get_barrier_semaphore()
    for d in range(1, g.shards):
        pl.semaphore_signal(
            barrier, inc=1, device_id={"seq": g.s, "shard": (g.k + d) % g.shards}, device_id_type=MESH
        )
    pl.semaphore_signal(barrier, inc=1, device_id={"seq": 1 - g.s, "shard": g.k}, device_id_type=MESH)
    pl.semaphore_wait(barrier, g.shards)


class Gather:
    def __init__(self, wires, own, out):
        self.w, self.g, self.own, self.out = wires, wires.g, own, out
        nz, ny, nc = self.g.sizes
        self.z0 = wires.block(nz)
        self.on0 = wires.block(nz)
        self.y0 = wires.block(nz * ny)
        self.c0 = wires.block(nz * ny * nc)

    def on_y(self, i, src):
        g = self.g
        for dy in range(1, g.sizes[1]):
            self.w.send(src, self.out.at[g.slot(i, 0, 0)], self.y0 + i * g.sizes[1] + dy, g.s, g.slot(0, dy, 0), self.own)

    def on_core(self, i, dy, src):
        g = self.g
        for dc in range(1, g.sizes[2]):
            index = self.c0 + (i * g.sizes[1] + dy) * g.sizes[2] + dc
            self.w.send(src, self.out.at[g.slot(i, -dy, 0)], index, g.s, g.slot(0, 0, dc), self.own)

    def start(self):
        g = self.g
        here = self.out.at[g.k]
        self.w.send_as(self.own, here, self.z0 + 2, self.z0 + 3 - g.inner, g.s, g.slot(2, 0, 0), self.own)
        self.w.send(self.own, here, self.z0 + 1, g.s, g.slot(1, 0, 0), self.own)

    def start_near(self):
        self.on_y(0, self.own)
        self.on_core(0, 0, self.own)

    def poll_z(self):
        g = self.g
        for i in (1, 2, 3):
            at = self.out.at[g.slot(i, 0, 0)]
            self.w.arrived(at, self.z0 + i)
            if i > 1:

                @pl.when(g.inner == 1)
                def _(at=at, i=i):
                    self.w.copy(at, at, self.on0 + i, self.z0 + i, g.s, g.slot(1, 0, 0)).start()

            self.on_y(i, at)
            self.on_core(i, 0, at)

    def poll_y(self):
        g = self.g
        for i in range(g.sizes[0]):
            for dy in range(1, g.sizes[1]):
                at = self.out.at[g.slot(i, -dy, 0)]
                self.w.arrived(at, self.y0 + i * g.sizes[1] + dy)
                self.on_core(i, dy, at)

    def finish(self):
        g = self.g
        for i in range(g.sizes[0]):
            for dy in range(g.sizes[1]):
                for dc in range(1, g.sizes[2]):
                    at = self.out.at[g.slot(i, -dy, -dc)]
                    self.w.arrived(at, self.c0 + (i * g.sizes[1] + dy) * g.sizes[2] + dc)

        @pl.when(g.inner == 1)
        def _():
            for i in (2, 3):
                self.w.copy(self.own, self.own, self.on0 + i, self.z0 + i, g.s, g.k).wait_send()


class Tokens:
    def __init__(self, wires, packed, out):
        self.w, self.g, self.packed, self.out = wires, wires.g, packed, out
        self.blocks = out.shape[0]
        self.at = wires.block((self.g.shards + 1) * self.blocks)
        self.like, self.row = packed.at[0, 0], packed.at[:, 0]

    def index(self, b, d):
        return self.at + b * (self.g.shards + 1) + d

    def mine(self, b, s):
        return self.out.at[b, pl.ds(pl.multiple_of(s * self.g.shards, self.g.shards), self.g.shards)]

    def start(self, b):
        g = self.g
        for d in range(1, g.shards):
            to = (g.k + d) % g.shards
            lane = self.out.at[b, g.s * g.shards + g.k]
            self.w.send(self.packed.at[to, b], lane, self.index(b, d), g.s, to, self.like)

    def poll(self, b):
        g = self.g
        for d in range(1, g.shards):
            self.w.arrived(self.out.at[b, g.s * g.shards + (g.k - d) % g.shards], self.index(b, d))
        self.w.send(self.mine(b, g.s), self.mine(b, g.s), self.index(b, g.shards), 1 - g.s, g.k, self.row)

    def finish(self, b):
        self.w.arrived(self.mine(b, 1 - self.g.s), self.index(b, self.g.shards))


class Smalls:
    def __init__(self, wires, held, at):
        self.w, self.g, self.held, self.at = wires, wires.g, held, at

    def start(self):
        g = self.g
        mine = self.held.at[g.k]
        for d in range(1, g.shards):
            self.w.send(mine, mine, self.at + d, g.s, (g.k + d) % g.shards, mine)

    def finish(self):
        g = self.g
        for d in range(1, g.shards):
            self.w.arrived(self.held.at[(g.k - d) % g.shards], self.at + d)


def side_by_side(vec, small, row, to, count):
    for j in range(small.shape[0]):
        vec[to : to + 1, j * count : (j + 1) * count] = small[j, row : row + 1, :count]


def forward_kernel(
    seqs, shards, counts,
    packed, packed_cot, qkv_w, small, dense_w, fc1_w, fc2_w, slopes, lengths,
    x_out, cot_out, n1_out, n2_out, qkvw_out, dense_out, fc1_out, fc2_out, qkv_out, o_out, h2_out, a_out, slope_out,
    w2_out, vec_out,
    x_v, n1_v, n2_v, qkvw_v, small_v, dense_v, fc1_v, fc2_v, blocks_v, cot_v, qkv_v, o_v, h2_v, a_v, slope_v, w2_v, vec_v, idc, idr,
    send_sems, recv_sems, copy_sems,
):
    g = Geometry(seqs, shards)
    wires = Wires(g, send_sems, recv_sems)
    lanes = seqs * shards
    width = n1_v.shape[1]
    part = o_v.shape[2]
    pairs = part // (2 * HEAD)
    ff = fc1_v.shape[2]
    ff_part = ff // shards
    block = ROWS * lanes
    blocks = x_v.shape[0]
    half = block // seqs
    rows = width // shards
    local = []

    def bring(src, dst):
        made = pltpu.make_async_copy(src, dst, copy_sems.at[len(local)])
        made.start()
        local.append(made)
        return made

    def at_block(b):
        return pl.ds(pl.multiple_of(b * block, block), block)

    tokens = Tokens(wires, packed, x_v)
    cots = Tokens(wires, packed_cot, blocks_v)
    smalls_at = wires.block(shards)
    qkv_all = Gather(wires, qkvw_v.at[g.k], qkvw_v)
    dense_all = Gather(wires, dense_v.at[g.k], dense_v)
    up_all = Gather(wires, fc1_v.at[g.k], fc1_v)
    down_all = Gather(wires, fc2_v, fc2_out)
    heads_at = wires.block(blocks)

    staged_qkv = [
        bring(
            qkv_w.at[:, pl.ds(pl.multiple_of(p * width + g.s * part, 128), part)],
            qkvw_v.at[g.k, :, pl.ds(p * part, part)],
        )
        for p in range(3)
    ]
    staged_small = bring(small, small_v.at[g.k])
    staged_dense = bring(dense_w, dense_v.at[g.k])
    staged_up = [
        bring(
            fc1_w.at[:, pl.ds(pl.multiple_of((i * seqs + g.s) * ff_part, 128), ff_part)],
            fc1_v.at[g.k, :, pl.ds(i * ff_part, ff_part)],
        )
        for i in range(shards)
    ]
    staged_x = bring(packed.at[g.k], x_v.at[:, g.s * shards + g.k])
    staged_down = bring(fc2_w.at[pl.ds(pl.multiple_of(g.s * ff_part, 8), ff_part), :], fc2_v)
    staged_cot = bring(packed_cot.at[g.k], blocks_v.at[:, g.s * shards + g.k])
    enter(g)
    idc[...] = blocked_ids(idc.shape, 0, lanes)
    idr[...] = blocked_ids(idr.shape, 1, lanes)
    for made in staged_qkv:
        made.wait()
    staged_small.wait()
    staged_dense.wait()
    for made in staged_up:
        made.wait()
    staged_down.wait()
    staged_x.wait()
    staged_cot.wait()
    kept = [bring(fc2_v, fc2_out.at[g.k])]
    smalls = Smalls(wires, small_v, smalls_at)
    qkv_all.start()
    qkv_all.start_near()
    tokens.start(0)
    tokens.start(1)
    smalls.start()
    dense_all.start_near()
    up_all.start_near()
    down_all.start_near()
    tokens.poll(0)
    tokens.start(2)
    qkv_all.poll_z()
    tokens.poll(1)
    tokens.start(3)
    dense_all.start()
    up_all.start()
    smalls.finish()

    for row in (0, 1, 3, 4, 5, 7):
        side_by_side(vec_v, small_v, row, row, rows)
    vec_v[2:3, :] = jnp.zeros((1, vec_v.shape[1]), f32)
    per = 2 * width // shards
    for i in range(part // per):
        for row, side in ((0, 0), (2, 1)):
            j = (side * width + g.s * part) // per + i
            vec_v[2:3, row * part + i * per : row * part + (i + 1) * per] = small_v[j, 2:3, :per]
    for j in range(shards):
        vec_v[6:7, j * ff_part : (j + 1) * ff_part] = small_v[j, 6:7, pl.ds(pl.multiple_of(g.s * ff_part, 128), ff_part)]

    qkv_all.poll_y()
    tokens.poll(2)
    tokens.poll(3)
    down_all.start()
    qkv_all.finish()
    kept += [bring(qkvw_v, qkvw_out), bring(vec_v, vec_out)]

    lane_id = lax.broadcasted_iota(jnp.int32, (1, 2 * HEAD), 1)
    tile = min(256, block)

    def project(b):
        x = x_v[b].astype(f32).reshape(block, width)
        xhat, _ = normalize(x)
        n1 = (xhat * vec_v[0:1, :width] + vec_v[1:2, :width]).astype(bf16)
        at = at_block(b)
        n1_v[at, :] = n1
        for p in range(3):
            weight = qkvw_v[:, :, p * part : (p + 1) * part].reshape(width, part)
            out = jnp.dot(n1, weight, preferred_element_type=f32) + vec_v[2:3, p * part : (p + 1) * part]
            out = out.astype(bf16)
            for h in range(pairs):
                qkv_v[p * pairs + h, at, :] = out[:, h * 2 * HEAD : (h + 1) * 2 * HEAD]

    def attend(b):
        end = (b + 1) * block

        @pl.loop(0, pairs)
        def _(h):
            q_ref, k_ref, v_ref = qkv_v.at[h], qkv_v.at[pairs + h], qkv_v.at[2 * pairs + h]
            for t in range(block // tile):
                at = pl.ds(b * block + t * tile, tile)
                q = q_ref[at, :] * jnp.asarray(HEAD**-0.5, bf16)
                ids_q = idc[at, :]

                def one_head(j, both):
                    mine = (lane_id >= HEAD).astype(jnp.int32) == j
                    qj = jnp.where(mine, q, jnp.zeros_like(q))
                    s = lax.dot_general(
                        qj, k_ref[:end, :], (((1,), (1,)), ((), ())), preferred_element_type=f32
                    )
                    s = s + slopes[g.s * pairs + h, j] * idr[:, :end]
                    tail = attn_mask(s[:, b * block :], idr[:, b * block : end] <= ids_q)
                    s = jnp.concatenate([s[:, : b * block], tail], axis=1) if b else tail
                    top = jnp.max(s, axis=1, keepdims=True)
                    e = jnp.exp(s - top)
                    total = jnp.sum(e, axis=1, keepdims=True)
                    o = jnp.dot(e.astype(bf16), v_ref[:end, :], preferred_element_type=f32) / total
                    return jnp.where(mine, o, both)

                both = lax.fori_loop(0, 2, one_head, jnp.zeros((tile, 2 * HEAD), f32))
                o_v[g.s, at, pl.ds(pl.multiple_of(h * 2 * HEAD, 2 * HEAD), 2 * HEAD)] = both.astype(bf16)

    def head_copy(b):
        mine = o_v.at[g.s, at_block(b)]
        return wires.copy(mine, mine, heads_at + b, heads_at + b, 1 - g.s, g.k)

    for b in range(blocks):
        tokens.finish(b)
        project(b)
        attend(b)
        head_copy(b).start()
        if b == 0:
            dense_all.poll_z()
        if b == 1:
            up_all.poll_z()
        if b == 2:
            dense_all.poll_y()
            cots.start(0)
            cots.start(1)
        if b == 3:
            up_all.poll_y()
    kept += [bring(x_v, x_out), bring(n1_v, n1_out), bring(qkv_v, qkv_out)]
    down_all.poll_z()
    dense_all.finish()
    kept.append(bring(dense_v, dense_out))
    up_all.finish()
    kept.append(bring(fc1_v, fc1_out))

    @pl.loop(0, blocks)
    def _(b):
        at = at_block(b)
        wires.arrived(o_v.at[1 - g.s, at], heads_at + b)
        branch = jnp.dot(
            o_v[0, at, :], dense_v[: shards // 2].reshape(part, width), preferred_element_type=f32
        ) + jnp.dot(o_v[1, at, :], dense_v[shards // 2 :].reshape(part, width), preferred_element_type=f32)
        resid = x_v[b].astype(f32).reshape(block, width) + branch + vec_v[3:4, :width]
        h2_v[b] = jnp.where(g.s == 0, resid[:half], resid[half:])
        xhat, _ = normalize(resid)
        n2 = (xhat * vec_v[4:5, :width] + vec_v[5:6, :width]).astype(bf16)
        n2_v[at, :] = n2
        step = min(512, ff)

        @pl.loop(0, ff // step)
        def _(n):
            cut = pl.ds(pl.multiple_of(n * step, step), step)
            u = jnp.dot(n2_v[at, :], fc1_v[:, :, cut].reshape(width, step), preferred_element_type=f32) + vec_v[6:7, cut]
            inside = 0.7978845608028654 * u * (1.0 + 0.044715 * u * u)
            t = jnp.tanh(inside)
            a_v[at, cut] = (0.5 * u * (1.0 + t)).astype(bf16)
            slope = 0.5 * (1.0 + t) + 0.5 * u * (1.0 - t * t) * (
                0.7978845608028654 + (0.7978845608028654 * 3.0 * 0.044715) * u * u
            )
            slope_v[at, cut] = slope.astype(bf16)

        @pl.when(b == 0)
        def _():
            cots.poll(0)
            cots.start(2)

        @pl.when(b == 1)
        def _():
            cots.poll(1)
            cots.start(3)

        @pl.when(b == 2)
        def _():
            cots.poll(2)


    cots.poll(3)
    kept.append(bring(o_v, o_out))
    kept += [bring(n2_v, n2_out), bring(h2_v, h2_out), bring(a_v, a_out), bring(slope_v, slope_out)]
    down_all.poll_y()
    for b in range(blocks):
        cots.finish(b)

    @pl.loop(0, blocks)
    def _(b):
        at = at_block(b)
        grad = blocks_v[b].astype(f32).reshape(block, width)
        cot_v[at, :] = jnp.where(idc[at, :] < lengths[g.k].astype(f32), grad, 0.0).astype(bf16)

    kept.append(bring(cot_v, cot_out))

    @pl.loop(0, ff // (2 * ff_part))
    def _(m):
        cut = a_v[:, pl.ds(pl.multiple_of(m * 2 * ff_part, 128), 2 * ff_part)]
        out = lax.dot_general(cut, cot_v[...], (((0,), (0,)), ((), ())), preferred_element_type=f32).astype(bf16)
        w2_v[pl.ds(2 * m, 2)] = out.reshape(2, ff_part, width)

    kept.append(bring(w2_v, w2_out))
    down_all.finish()
    for b in range(blocks):
        head_copy(b).wait_send()
    wires.drain()
    for made in kept:
        made.wait()
    assert wires.used <= counts[0] and len(local) <= counts[1]


def forward_exchange(packed, packed_cot, qkv_w, small, dense_w, fc1_w, fc2_w, slopes, lengths, seqs, shards):
    width, own = qkv_w.shape[0] * shards, qkv_w.shape[0]
    lanes = seqs * shards
    blocks = packed.shape[1]
    block = lanes * ROWS
    cap = blocks * block
    part = width // seqs
    pairs = part // (2 * HEAD)
    ff = fc1_w.shape[1] // seqs
    ff_part = ff // shards
    counts = (384, 64)
    any_ = pl.BlockSpec(memory_space=pl.ANY)
    vmem = pl.BlockSpec(memory_space=pltpu.VMEM)
    smem = pl.BlockSpec(memory_space=pltpu.SMEM)
    x_shape = ((blocks, lanes, ROWS, width), bf16)
    wide, long = ((cap, width), bf16), ((cap, ff), bf16)
    qkvw, dense, fc1, fc2 = (
        ((shards,) + tail, bf16) for tail in ((own, 3 * part), (own, width), (own, ff), (ff_part, width))
    )
    qkv, heads = ((3 * pairs, cap, 2 * HEAD), bf16), ((seqs, cap, part), bf16)
    h2, vec = ((blocks, block // seqs, width), f32), ((8, max(width, 3 * part, ff)), f32)
    outs = [x_shape, wide, wide, wide, qkvw, dense, fc1, fc2, qkv, heads, h2, long, long, fc2, vec]
    scratch = [
        x_shape, wide, wide, qkvw, ((shards,) + small.shape, f32), dense, fc1, ((ff_part, width), bf16), x_shape, wide,
        qkv, heads, h2, long, long, fc2, vec, ((cap, 1), f32), ((1, cap), f32),
    ]
    return pl.pallas_call(
        functools.partial(forward_kernel, seqs, shards, counts),
        in_specs=[any_] * 7 + [smem] * 2,
        out_specs=[any_] * len(outs),
        out_shape=[jax.ShapeDtypeStruct(s, d) for s, d in outs],
        scratch_shapes=[pltpu.VMEM(s, d) for s, d in scratch]
        + [pltpu.SemaphoreType.DMA((counts[0],)), pltpu.SemaphoreType.DMA((counts[0],)), pltpu.SemaphoreType.DMA((counts[1],))],
        compiler_params=pltpu.CompilerParams(collective_id=1, has_side_effects=True, vmem_limit_bytes=60 * 2**20),
        name="forward_exchange",
    )(
        packed, packed_cot, qkv_w, small, dense_w, fc1_w, fc2_w, slopes, lengths,
    )


class Scatter:
    def __init__(self, wires, full, own, bufs):
        self.w, self.g, self.full, self.own = wires, wires.g, full, own
        self.rc, self.ry, self.rz, self.fin = bufs
        self.at = wires.block(8)
        self.one = self.rz.at[0] if self.rz is not None else None

    def add(self, count, into, other):
        @pl.loop(0, count)
        def _(i):
            a, b = into(i), other(i)
            a[...] = (a[...].astype(f32) + b[...].astype(f32)).astype(bf16)

    def core_send(self):
        g = self.g
        self.w.send(self.full.at[:, :, 1 - g.c], self.rc, self.at, g.s, g.slot(0, 0, 1), self.rc)

    def core_done(self):
        g = self.g
        self.w.arrived(self.rc, self.at)
        self.add(8, lambda i: self.rc.at[i // 2, i % 2], lambda i: self.own(i // 2, i % 2))
        self.w.send(self.rc.at[:, 1 - g.y], self.ry, self.at + 1, g.s, g.slot(0, 1, 0), self.ry)

    def y_done(self):
        g = self.g
        self.w.arrived(self.ry, self.at + 1)
        self.add(4, lambda i: self.ry.at[i], lambda i: self.rc.at[i, g.y])

    def z_send(self):
        g = self.g
        partner = g.slot(1, 0, 0)
        self.w.send(self.ry.at[g.line[1]], self.rz.at[0], self.at + 2, g.s, partner, self.one)

        @pl.when(g.inner == 0)
        def _():
            for i in (2, 3):
                self.w.copy(self.ry.at[g.line[i]], self.rz.at[i], self.at + 1 + i, self.at + 1 + i, g.s, partner).start()

    def z_done(self):
        g = self.g

        @pl.when(g.inner == 1)
        def _():
            for i in (2, 3):
                self.w.arrived(self.rz.at[i], self.at + 1 + i)
                a = self.rz.at[i]
                a[...] = (a[...].astype(f32) + self.ry[g.line[i]].astype(f32)).astype(bf16)
                self.w.copy(a, self.rz.at[1], self.at + 1 + i, self.at + 5, g.s, g.slot(i, 0, 0)).start()

    def final(self):
        g = self.g
        self.w.arrived(self.rz.at[0], self.at + 2)
        self.w.arrived(self.rz.at[1], self.at + 5)
        total = self.ry[g.z].astype(f32) + self.rz[0].astype(f32) + self.rz[1].astype(f32)
        self.fin[0] = total.astype(bf16)
        self.w.send(self.fin.at[0], self.fin.at[1], self.at + 6, 1 - g.s, g.k, self.fin.at[0])

    def done(self):
        self.w.arrived(self.fin.at[1], self.at + 6)
        for i in (2, 3):
            self.w.copy(self.fin.at[0], self.fin.at[0], self.at + 1 + i, self.at + 1 + i, self.g.s, self.g.k).wait_send()


class Back:
    def __init__(self, wires, src, dst, pieces):
        self.w, self.g, self.src, self.dst, self.pieces = wires, wires.g, src, dst, pieces
        self.at = wires.block(wires.g.shards * pieces)
        self.per = src.shape[0] // pieces
        self.like = src.at[pl.ds(0, self.per), 0]

    def cut(self, ref, i):
        return ref.at[pl.ds(i * self.per, self.per)]

    def send(self, i):
        g = self.g
        for d in range(1, g.shards):
            to = (g.k + d) % g.shards
            src = self.src.at[pl.ds(i * self.per, self.per), to]
            index = self.at + i * g.shards + d
            self.w.copy(src, self.cut(self.dst.at[g.k], i), index, index, g.s, to).start()

    def finish(self):
        g = self.g
        for i in range(self.pieces):
            for d in range(1, g.shards):
                self.w.recorded(self.like, self.at + i * g.shards + d)
                self.w.arrived(self.cut(self.dst.at[(g.k - d) % g.shards], i), self.at + i * g.shards + d)


def middle_kernel(
    seqs, shards, counts,
    a, slope, n2, fc1, fc2, dense, cot, h2, heads, w2, vec,
    dh2_out, do_out, w1_out, wd_out, keep_out, give_out, ry_out, small_out,
    a_v, du_v, n2_v, fc1_v, fc2_v, dense_v, cot_v, h2_v, heads_v, own_w2, w1_v, wd_v, mine_v, sent_v, got_v,
    da_v, do_v, do_sent, small_v, rc, ry,
    send_sems, recv_sems, copy_sems,
):
    g = Geometry(seqs, shards)
    wires = Wires(g, send_sems, recv_sems)
    blocks, half, width = h2_v.shape
    block = half * seqs
    ff = a_v.shape[1]
    ff_part = ff // shards
    rows = width // shards
    part = width // seqs
    local = []

    def bring(src, dst):
        made = pltpu.make_async_copy(src, dst, copy_sems.at[len(local)])
        made.start()
        local.append(made)
        return made

    def at_block(b):
        return pl.ds(pl.multiple_of(b * block, block), block)

    def own_rows(b):
        return pl.ds(pl.multiple_of(b * block + g.s * half, half), half)

    down = Scatter(wires, w2, lambda i, j: own_w2.at[i, j], (rc, ry, None, None))
    half_at, do_at = wires.block(blocks), wires.block(blocks)
    first = [bring(cot, cot_v), bring(fc2, fc2_v), bring(slope, du_v), bring(fc1, fc1_v)]
    own = bring(w2.at[:, :, g.c], own_w2)
    later = [bring(n2, n2_v), bring(a, a_v), bring(h2, h2_v), bring(dense, dense_v)]
    later += [bring(heads.at[i, own_rows(b), :], heads_v.at[i, pl.ds(b * half, half)]) for i in range(seqs) for b in range(blocks)]
    enter(g)
    down.core_send()
    for made in first:
        made.wait()
    step = min(512, ff)
    per = step // ff_part

    def half_copy(b):
        return wires.copy(sent_v.at[b], got_v.at[b], half_at + b, half_at + b, 1 - g.s, g.k)

    def do_copy(b):
        return wires.copy(do_sent.at[b], do_v.at[b, g.s], do_at + b, do_at + b, 1 - g.s, g.k)

    small_v[...] = jnp.zeros_like(small_v)

    def split(b, total, keep, give):
        @pl.when(g.s == 0)
        def _():
            keep(total[:half])
            give[b] = total[half:].astype(bf16)

        @pl.when(g.s == 1)
        def _():
            keep(total[half:])
            give[b] = total[:half].astype(bf16)

    def du_step(b, sums):
        at = at_block(b)
        grad = cot_v[at, :]
        total, new = None, []
        for n in range(ff // step):
            cut = slice(n * step, (n + 1) * step)
            weight = fc2_v[n * per : (n + 1) * per].reshape(step, width)
            da = lax.dot_general(grad, weight, (((1,), (1,)), ((), ())), preferred_element_type=f32)
            du = (da * du_v[at, cut].astype(f32)).astype(bf16)
            du_v[at, cut] = du
            new.append(sums[n] + jnp.sum(du.astype(f32), axis=0, keepdims=True))
            weight = fc1_v[:, :, cut].reshape(width, step)
            term = lax.dot_general(du, weight, (((1,), (1,)), ((), ())), preferred_element_type=f32)
            total = term if total is None else total + term

        def keep(value):
            mine_v[b] = value

        split(b, total, keep, sent_v)

        @pl.when(b > 0)
        def _():
            half_copy(b - 1).start()

        @pl.when(b == 0)
        def _():
            own.wait()
            down.core_done()

        return tuple(new)

    zero = jnp.zeros((1, step), f32)
    sums = lax.fori_loop(0, blocks, du_step, (zero,) * (ff // step))
    for made in later:
        made.wait()

    @pl.loop(0, width // (4 * rows))
    def _(m):
        @pl.when(m == 0)
        def _():
            half_copy(blocks - 1).start()

        left = n2_v[:, pl.ds(pl.multiple_of(m * 4 * rows, 128), 4 * rows)]
        for n in range(ff // step):
            cut = slice(n * step, (n + 1) * step)
            out = lax.dot_general(left, du_v[:, cut], (((0,), (0,)), ((), ())), preferred_element_type=f32)
            w1_v[pl.ds(4 * m, 4), :, cut] = out.astype(bf16).reshape(4, rows, step)

    kept = [bring(w1_v, w1_out)]
    for n in range(ff // step):
        for i in range(per):
            small_v[n * per + i, 6:7, pl.ds(pl.multiple_of(g.s * ff_part, 128), ff_part)] = sums[n][
                :, i * ff_part : (i + 1) * ff_part
            ]

    def norm_step(b, sums):
        gains, biases, branch, cots = sums
        wires.arrived(got_v.at[b], half_at + b)
        grad = mine_v[b] + got_v[b].astype(f32)
        xhat, root = normalize(h2_v[b])
        gains = gains + jnp.sum(grad * xhat, axis=0, keepdims=True)
        biases = biases + jnp.sum(grad, axis=0, keepdims=True)
        cot_b = cot_v[own_rows(b), :].astype(f32)
        cots = cots + jnp.sum(cot_b, axis=0, keepdims=True)
        dh2 = cot_b + norm_pull(grad, vec[4:5, :width], xhat, root)
        mine_v[b] = dh2
        da = dh2.astype(bf16)
        branch = branch + jnp.sum(da.astype(f32), axis=0, keepdims=True)
        da_v[pl.ds(pl.multiple_of(b * half, half), half), :] = da
        grads = [
            lax.dot_general(
                da, dense_v[i * (shards // seqs) : (i + 1) * (shards // seqs)].reshape(part, width),
                (((1,), (1,)), ((), ())), preferred_element_type=f32,
            ).astype(bf16)
            for i in range(seqs)
        ]
        do_v[b, g.s] = jnp.where(g.s == 0, grads[0], grads[1])
        do_sent[b] = jnp.where(g.s == 0, grads[1], grads[0])

        @pl.when(b > 0)
        def _():
            do_copy(b - 1).start()

        return gains, biases, branch, cots

    zero = jnp.zeros((1, width), f32)
    sums = lax.fori_loop(0, blocks, norm_step, (zero,) * 4)
    kept.append(bring(mine_v, dh2_out))
    for row, vector in ((4, sums[0]), (5, sums[1]), (3, sums[2]), (7, sums[3])):
        for j in range(shards):
            small_v[j, row : row + 1, :rows] = vector[:, j * rows : (j + 1) * rows]
    do_copy(blocks - 1).start()
    kept.append(bring(small_v, small_out))

    for i in range(seqs):
        out = lax.dot_general(heads_v[i], da_v[...], (((0,), (0,)), ((), ())), preferred_element_type=f32).astype(bf16)
        wd_v[i * (shards // seqs) : (i + 1) * (shards // seqs)] = out.reshape(shards // seqs, rows, width)
    kept.append(bring(wd_v, wd_out))

    @pl.loop(0, blocks)
    def _(b):
        at = at_block(b)
        total = None
        for n in range(ff // step):
            weight = fc2_v[n * per : (n + 1) * per].reshape(step, width)
            term = jnp.dot(a_v[at, n * step : (n + 1) * step], weight, preferred_element_type=f32)
            total = term if total is None else total + term

        def keep(value):
            h2_v[b] = h2_v[b] + value + vec[7:8, :width]

        split(b, total, keep, got_v)

    kept += [bring(h2_v, keep_out), bring(got_v, give_out)]
    down.y_done()
    kept.append(bring(ry, ry_out))
    for b in range(blocks):
        wires.arrived(do_v.at[b, 1 - g.s], do_at + b)
    kept.append(bring(do_v, do_out))
    for b in range(blocks):
        half_copy(b).wait_send()
        do_copy(b).wait_send()
    wires.drain()
    for made in kept:
        made.wait()
    assert wires.used <= counts[0] and len(local) <= counts[1]


def middle_exchange(a, slope, n2, fc1, fc2, dense, cot, h2, heads, w2, vec, seqs, shards):
    blocks, half, width = h2.shape
    tokens, ff = a.shape
    part = width // seqs
    rows, ff_part = width // shards, ff // shards
    counts = (32, 40)
    any_, vmem = pl.BlockSpec(memory_space=pl.ANY), pl.BlockSpec(memory_space=pltpu.VMEM)
    own32, own16 = ((blocks, half, width), f32), ((blocks, half, width), bf16)
    do, smalls = ((blocks, seqs, half, part), bf16), ((shards, 8, 256), f32)
    w1, wd, ry = ((shards, rows, ff), bf16), ((shards, rows, width), bf16), ((4, ff_part, width), bf16)
    outs = [own32, do, w1, wd, own32, own16, ry, smalls]
    rc = ((4, 2, ff_part, width), bf16)
    scratch = [(v.shape, bf16) for v in (a, slope, n2, fc1, fc2, dense, cot)] + [
        own32, ((seqs, blocks * half, part), bf16), rc, w1, wd, own32, own16, own16, ((blocks * half, width), bf16), do,
        ((blocks, half, part), bf16), smalls, rc, ry,
    ]
    return pl.pallas_call(
        functools.partial(middle_kernel, seqs, shards, counts),
        in_specs=[any_] * 10 + [vmem],
        out_specs=[any_] * len(outs),
        out_shape=[jax.ShapeDtypeStruct(s, d) for s, d in outs],
        scratch_shapes=[pltpu.VMEM(s, d) for s, d in scratch]
        + [pltpu.SemaphoreType.DMA((counts[0],)), pltpu.SemaphoreType.DMA((counts[0],)), pltpu.SemaphoreType.DMA((counts[1],))],
        compiler_params=pltpu.CompilerParams(collective_id=3, has_side_effects=True, vmem_limit_bytes=62 * 2**20),
        name="middle_exchange",
    )(a, slope, n2, fc1, fc2, dense, cot, h2, heads, w2.reshape((4, 2, 2) + w2.shape[1:]), vec)


def backward_kernel(
    seqs, shards, counts,
    qkv, do, n1, qkvw, x_all, dh2, keep, give, ry2, w1, wd, smalls, vec, slopes,
    ret_y, ret_x, o_qkv, o_dense, o_up, o_down, o_small,
    qkv_v, do_v, dqkv_v, n1_v, qkvw_v, x_v, dh2_v, dk_acc, dv_acc, bias_acc, mine_v, sent_v, got_v, dx_v, gq_v,
    small_v, small_got, small_fin, small_last, f_qkv, f_dense, f_up, f_down, keep_v, give_v, y_v, own_w1, own_wd, idc, idr,
    *rest,
):
    bufs, (send_sems, recv_sems, copy_sems) = rest[:-3], rest[-3:]
    g = Geometry(seqs, shards)
    wires = Wires(g, send_sems, recv_sems)
    pairs, tokens = do_v.shape[0], do_v.shape[1]
    part = pairs * 2 * HEAD
    width = n1_v.shape[1]
    lanes = seqs * shards
    block = ROWS * lanes
    blocks = tokens // block
    half = block // seqs
    tile = bias_acc.shape[2]
    local = []

    def bring(src, dst):
        made = pltpu.make_async_copy(src, dst, copy_sems.at[len(local)])
        made.start()
        local.append(made)
        return made

    def held(ref):
        return lambda i, j: ref.at[i, j]

    down = Scatter(wires, None, None, (None,) + bufs[0:3])
    up = Scatter(wires, w1, held(own_w1), bufs[3:7])
    dense = Scatter(wires, wd, held(own_wd), bufs[7:11])
    qkv_sum = Scatter(wires, gq_v, lambda i, j: gq_v.at[i, j, g.c], bufs[11:15])
    back_y = Back(wires, y_v, ret_y, 1)
    give_at = wires.block(1)
    back_x = Back(wires, dx_v, ret_x, blocks)
    half_at = wires.block(blocks)
    small_at = wires.block(shards + 1)

    ry_in = bring(ry2, down.ry)
    first = [bring(qkv, qkv_v)] + [bring(do.at[:, pl.ds(h * 2 * HEAD, 2 * HEAD)], do_v.at[h]) for h in range(pairs)]
    owns = [bring(a.at[:, :, g.c], b) for a, b in ((w1, own_w1), (wd, own_wd))] + [bring(keep, keep_v)]
    later = [
        bring(n1, n1_v), bring(qkvw, qkvw_v), bring(x_all.at[:, pl.ds(g.s * shards, shards)], x_v), bring(dh2, dh2_v),
        bring(smalls, small_v),
    ]
    enter(g)
    idc[...] = blocked_ids(idc.shape, 0, lanes)
    idr[...] = blocked_ids(idr.shape, 1, lanes)
    up.core_send()
    dense.core_send()
    ry_in.wait()
    down.z_send()
    wires.send(give, give_v, give_at, 1 - g.s, g.k, give)
    for made in first + owns:
        made.wait()

    lane_id = lax.broadcasted_iota(jnp.int32, (1, 2 * HEAD), 1)

    def attend(h):
        q_ref, k_ref, v_ref, do_ref = qkv_v.at[h], qkv_v.at[pairs + h], qkv_v.at[2 * pairs + h], do_v.at[h]
        dk_acc[...] = jnp.zeros_like(dk_acc)
        dv_acc[...] = jnp.zeros_like(dv_acc)
        for j in range(2):
            bias_acc[j] = jnp.broadcast_to(slopes[g.s * pairs + h, j] * idc[...], bias_acc.shape[1:])
        cols = pl.ds(pl.multiple_of(h * 2 * HEAD, 2 * HEAD), 2 * HEAD)
        for b in range(blocks):
            end = (b + 1) * block
            for t in range(block // tile):
                at = pl.ds(b * block + t * tile, tile)
                q = q_ref[at, :] * jnp.asarray(HEAD**-0.5, bf16)
                grad = do_ref[at, :]
                ids_q = idr[:, at]
                both = None
                for j in range(2):
                    mine = (lane_id // HEAD) == j
                    qj = jnp.where(mine, q, jnp.zeros_like(q))
                    doj = jnp.where(mine, grad, jnp.zeros_like(grad))
                    s = lax.dot_general(
                        k_ref[:end, :], qj, (((1,), (1,)), ((), ())), preferred_element_type=f32
                    )
                    s = s + bias_acc[j, :end, :]
                    tail = attn_mask(s[b * block :, :], idc[b * block : end, :] <= ids_q)
                    s = jnp.concatenate([s[: b * block, :], tail], axis=0) if b else tail
                    top = jnp.max(s, axis=0, keepdims=True)
                    e = jnp.exp(s - top)
                    probs = e * (1.0 / jnp.sum(e, axis=0, keepdims=True))
                    dv_acc[:end, :] += jnp.dot(probs.astype(bf16), doj, preferred_element_type=f32)
                    dp = lax.dot_general(
                        v_ref[:end, :], doj, (((1,), (1,)), ((), ())), preferred_element_type=f32
                    )
                    inner = jnp.sum(probs * dp, axis=0, keepdims=True)
                    ds = (probs * (dp - inner)).astype(bf16)
                    dk_acc[:end, :] += jnp.dot(ds, qj, preferred_element_type=f32)
                    dq = lax.dot_general(
                        ds, k_ref[:end, :], (((0,), (0,)), ((), ())), preferred_element_type=f32
                    )
                    both = dq if both is None else jnp.where(mine, dq, both)
                dqkv_v[0, at, cols] = (both * (HEAD**-0.5)).astype(bf16)
        dqkv_v[1, :, cols] = dk_acc[...].astype(bf16)
        dqkv_v[2, :, cols] = dv_acc[...].astype(bf16)

    @pl.loop(0, pairs)
    def _(h):
        attend(h)

        @pl.when(h == 0)
        def _():
            up.core_done()

        @pl.when(h == 1)
        def _():
            dense.core_done()

        @pl.when(h == 2)
        def _():
            down.z_done()
            wires.arrived(give_v, give_at)

            @pl.loop(0, blocks)
            def _(b):
                y_v[b] = (keep_v[b] + give_v[b].astype(f32)).reshape(shards, ROWS, width).astype(bf16)

            back_y.send(0)

    for made in later:
        made.wait()

    rows = width // shards

    @pl.loop(0, blocks)
    def _(m):
        cut = n1_v[:, pl.ds(pl.multiple_of(m * block, block), block)]
        for p in range(3):
            out = lax.dot_general(cut, dqkv_v[p], (((0,), (0,)), ((), ())), preferred_element_type=f32).astype(bf16)
            out = out.reshape(block // rows // 2, 2, rows, part)
            for i in range(block // rows // 2):
                at = m * (block // rows // 2) + i
                for j in range(2):
                    gq_v[at // 2, at % 2, j, :, p * part : (p + 1) * part] = out[i, j]

    qkv_sum.core_send()

    def half_copy(b):
        return wires.copy(sent_v.at[b], got_v.at[b], half_at + b, half_at + b, 1 - g.s, g.k)

    @pl.loop(0, blocks)
    def _(b):
        total = None
        for p in range(3):
            weight = qkvw_v[:, :, p * part : (p + 1) * part].reshape(width, part)
            term = lax.dot_general(
                dqkv_v[p, pl.ds(pl.multiple_of(b * block, block), block), :], weight, (((1,), (1,)), ((), ())),
                preferred_element_type=f32,
            )
            total = term if total is None else total + term

        @pl.when(g.s == 0)
        def _():
            mine_v[b] = total[:half]
            sent_v[b] = total[half:].astype(bf16)

        @pl.when(g.s == 1)
        def _():
            mine_v[b] = total[half:]
            sent_v[b] = total[:half].astype(bf16)

        @pl.when(b == 2)
        def _():
            up.y_done()
            up.z_send()

        @pl.when(b > 0)
        def _():
            half_copy(b - 1).start()

    own_y = bring(y_v.at[:, g.k], ret_y.at[g.k])
    half_copy(blocks - 1).start()

    sums = [jnp.sum(dqkv_v[p].astype(f32), axis=0, keepdims=True) for p in (0, 2)]
    per = 2 * width // shards
    for i in range(part // per):
        for half_no in range(2):
            small_v[(half_no * width + g.s * part) // per + i, 2:3, :per] = sums[half_no][:, i * per : (i + 1) * per]
    qkv_sum.core_done()
    dense.y_done()
    dense.z_send()

    def norm_step(b, sums):
        wires.arrived(got_v.at[b], half_at + b)
        grad = mine_v[b] + got_v[b].astype(f32)
        xhat, root = normalize(x_v[b].astype(f32).reshape(half, width))
        gains = sums[0] + jnp.sum(grad * xhat, axis=0, keepdims=True)
        biases = sums[1] + jnp.sum(grad, axis=0, keepdims=True)
        dx = dh2_v[b] + norm_pull(grad, vec[0:1, :width], xhat, root)
        dx_v[b] = dx.reshape(shards, ROWS, width).astype(bf16)
        back_x.send(b)

        @pl.when(b == 0)
        def _():
            up.z_done()

        @pl.when(b == 2)
        def _():
            qkv_sum.y_done()
            qkv_sum.z_send()

        return gains, biases

    gains, biases = lax.fori_loop(0, blocks, norm_step, (jnp.zeros((1, width), f32),) * 2)
    for j in range(shards):
        small_v[j, 0:1, :rows] = gains[:, j * rows : (j + 1) * rows]
        small_v[j, 1:2, :rows] = biases[:, j * rows : (j + 1) * rows]
    kept = [own_y, bring(dx_v.at[:, g.k], ret_x.at[g.k])]
    for d in range(1, shards):
        to = (g.k + d) % shards
        wires.send(small_v.at[to], small_got.at[g.k], small_at + d, g.s, to, small_v.at[0])
    small_got[g.k] = small_v[g.k]
    down.final()
    dense.z_done()
    up.final()
    qkv_sum.z_done()
    for d in range(1, shards):
        wires.arrived(small_got.at[(g.k - d) % shards], small_at + d)
    small_fin[0] = jnp.sum(small_got[...], axis=0)
    wires.send(small_fin.at[0], small_fin.at[1], small_at + shards, 1 - g.s, g.k, small_fin.at[0])
    dense.final()

    down.done()
    ff_part = f_down.shape[0] // seqs
    for i, at in ((0, g.s), (1, 1 - g.s)):
        f_down[pl.ds(pl.multiple_of(at * ff_part, ff_part), ff_part), :] = down.fin[i].astype(f32)
    kept.append(bring(f_down, o_down))
    up.done()
    for i, at in ((0, g.s), (1, 1 - g.s)):
        for j in range(shards):
            f_up[:, pl.ds(pl.multiple_of((j * seqs + at) * ff_part, 128), ff_part)] = up.fin[
                i, :, j * ff_part : (j + 1) * ff_part
            ].astype(f32)
    kept.append(bring(f_up, o_up))
    dense.done()
    f_dense[...] = dense.fin[0].astype(f32) + dense.fin[1].astype(f32)
    kept.append(bring(f_dense, o_dense))
    wires.arrived(small_fin.at[1], small_at + shards)
    small_last[...] = small_fin[0] + small_fin[1]
    kept.append(bring(small_last, o_small))
    qkv_sum.final()
    qkv_sum.done()
    for i, at in ((0, g.s), (1, 1 - g.s)):
        for p in range(3):
            f_qkv[:, pl.ds(pl.multiple_of(p * width + at * part, 128), part)] = qkv_sum.fin[
                i, :, p * part : (p + 1) * part
            ].astype(f32)
    kept.append(bring(f_qkv, o_qkv))
    back_y.finish()
    back_x.finish()
    for b in range(blocks):
        half_copy(b).wait_send()
    wires.drain()
    for made in kept:
        made.wait()
    assert wires.used <= counts[0] and len(local) <= counts[1]


def backward_exchange(
    qkv, do, n1, qkvw, x_all, dh2, keep, give, ry2, w1, wd, smalls, vec, slopes, seqs, shards
):
    tokens, part = do.shape
    width = n1.shape[1]
    pairs = part // (2 * HEAD)
    lanes = seqs * shards
    block = ROWS * lanes
    blocks, half = tokens // block, block // seqs
    tile = min(256, block)
    rows, ff = width // shards, w1.shape[2]
    ff_part = ff // shards
    counts = (256, 48)
    cut = lambda a: a.reshape((4, 2, 2) + a.shape[1:])
    any_, vmem = pl.BlockSpec(memory_space=pl.ANY), pl.BlockSpec(memory_space=pltpu.VMEM)
    ret = (shards, blocks, ROWS, width)
    outs = [
        (ret, bf16), (ret, bf16), ((rows, 3 * width), f32), ((rows, width), f32), ((rows, seqs * ff), f32),
        ((seqs * ff_part, width), f32), (smalls.shape[1:], f32),
    ]
    blks = [(ff_part, width), (rows, ff), (rows, width), (rows, 3 * part)]
    scratch = [
        ((3 * pairs, tokens, 2 * HEAD), bf16), ((pairs, tokens, 2 * HEAD), bf16), ((3, tokens, part), bf16),
        ((tokens, width), bf16), ((shards, rows, 3 * part), bf16), ((blocks, shards, ROWS, width), bf16),
        ((blocks, half, width), f32), ((tokens, 2 * HEAD), f32), ((tokens, 2 * HEAD), f32), ((2, tokens, tile), f32),
        ((blocks, half, width), f32), ((blocks, half, width), bf16), ((blocks, half, width), bf16),
        ((blocks, shards, ROWS, width), bf16), ((4, 2, 2) + blks[3], bf16), (smalls.shape, f32), (smalls.shape, f32),
        ((2,) + smalls.shape[1:], f32), (smalls.shape[1:], f32), ((rows, 3 * width), f32), ((rows, width), f32), ((rows, seqs * ff), f32),
        ((seqs * ff_part, width), f32), ((blocks, half, width), f32), ((blocks, half, width), bf16),
        ((blocks, shards, ROWS, width), bf16), ((4, 2) + blks[1], bf16), ((4, 2) + blks[2], bf16),
        ((tokens, 1), f32), ((1, tokens), f32),
    ]
    for blk in blks:
        scratch += [((4, 2) + blk, bf16)] * (blk is not blks[0])
        scratch += [((4,) + blk, bf16), ((4,) + blk, bf16), ((2,) + blk, bf16)]
    return pl.pallas_call(
        functools.partial(backward_kernel, seqs, shards, counts),
        in_specs=[any_] * 12 + [vmem, pl.BlockSpec(memory_space=pltpu.SMEM)],
        out_specs=[any_] * len(outs),
        out_shape=[jax.ShapeDtypeStruct(s, d) for s, d in outs],
        scratch_shapes=[pltpu.VMEM(s, d) for s, d in scratch]
        + [pltpu.SemaphoreType.DMA((counts[0],)), pltpu.SemaphoreType.DMA((counts[0],)), pltpu.SemaphoreType.DMA((counts[1],))],
        compiler_params=pltpu.CompilerParams(collective_id=2, has_side_effects=True, vmem_limit_bytes=60 * 2**20),
        name="backward_exchange",
    )(
        qkv, do, n1, qkvw, x_all, dh2, keep, give, ry2, cut(w1), cut(wd), smalls, vec, slopes,
    )


def layout_tables(lengths, lane_count, group_count, per_group):
    seq_rows = lengths // lane_count
    row_start = jnp.cumsum(seq_rows) - seq_rows
    slot_rows = seq_rows.reshape(group_count, per_group)
    slot_start = row_start.reshape(group_count, per_group)
    slot_before = jnp.cumsum(slot_rows, axis=1) - slot_rows
    return seq_rows, row_start, slot_rows, slot_start, slot_before


def per_device(
    tokens, cotangent, lengths, first_gain, first_bias, qkv_weight, qv_bias, dense_weight, dense_bias,
    second_gain, second_bias, fc1_weight, fc1_bias, fc2_weight, fc2_bias,
):
    shards, seqs = lax.axis_size("shard"), lax.axis_size("seq")
    lanes = shards * seqs
    slots, width = tokens.shape[1], tokens.shape[2]
    rows = slots // shards
    blocks = rows // ROWS

    smalls_in = (first_gain, first_bias, qv_bias, dense_bias, second_gain, second_bias, fc1_bias, fc2_bias)
    small = jnp.stack([jnp.pad(a.astype(f32), (0, 256 - a.shape[0])) for a in smalls_in])
    slopes = jnp.asarray(np.exp2(-8.0 * (np.arange(HEADS) + 1.0) / HEADS).reshape(-1, 2), f32)

    seq_rows = lengths // lanes
    number = jnp.arange(shards, dtype=jnp.int32)
    row_start = jnp.sum(jnp.where(number[None, :] < number[:, None], seq_rows[None, :], 0), axis=1)
    window = (row_start[:, None] + jnp.arange(rows, dtype=jnp.int32)[None, :]).reshape(-1)

    def pack(source):
        return jnp.take(source, window, axis=0, mode="clip").reshape(shards, blocks, ROWS, width)

    (
        x_all, cot_all, normed_one, normed_two, full_qkv, full_dense, full_up, full_down, qkv, mixed, resid, activ, slope,
        grad_down, vectors,
    ) = forward_exchange(
        pack(tokens[0]), pack(cotangent[0]), qkv_weight, small, dense_weight, fc1_weight, fc2_weight,
        slopes, lengths, seqs, shards,
    )
    grad_resid, grad_mixed, grad_up, grad_dense, keep, give, half_sums, small_grads = middle_exchange(
        activ, slope, normed_two, full_up, full_down, full_dense, cot_all, resid, mixed, grad_down, vectors, seqs, shards
    )
    ret_out, ret_grad, g_qkv, g_dense, g_up, g_down, g_small = backward_exchange(
        qkv, grad_mixed.reshape(slots * seqs, width // seqs), normed_one, full_qkv, x_all, grad_resid, keep, give, half_sums,
        grad_up, grad_dense, small_grads, vectors, slopes, seqs, shards,
    )

    row_here = jnp.arange(slots, dtype=jnp.int32)[:, None]
    inside = (row_here >= row_start[None]) & (row_here < (row_start + seq_rows)[None])
    fetch = jnp.sum(jnp.where(inside, number[None] * rows + row_here - row_start[None], 0), axis=1)
    fetch_live = jnp.arange(slots, dtype=jnp.int32) < jnp.sum(seq_rows)

    def to_stream(got):
        taken = jnp.take(got.reshape(-1, width), fetch, axis=0, mode="clip")
        return jnp.where(fetch_live[:, None], taken, jnp.zeros_like(taken))[None]

    vectors_out = tuple(g_small[i, : a.shape[0]] for i, a in enumerate(smalls_in))
    g_gain_one, g_bias_one, g_qv, g_bdense, g_gain_two, g_bias_two, g_bup, g_bdown = vectors_out
    return (
        to_stream(ret_out), to_stream(ret_grad),
        g_gain_one, g_bias_one, g_qkv, g_qv, g_dense, g_bdense, g_gain_two, g_bias_two, g_up, g_bup, g_down, g_bdown,
    )


def per_device_any(
    tokens, cotangent, lengths, first_gain, first_bias, qkv_weight, qv_bias, dense_weight, dense_bias,
    second_gain, second_bias, fc1_weight, fc1_bias, fc2_weight, fc2_bias,
):
    shards, seqs = lax.axis_size("shard"), lax.axis_size("seq")
    lanes = shards * seqs
    slots, width = tokens.shape[1], tokens.shape[2]
    rows = slots // shards
    cap = slots * seqs
    per_group = lengths.shape[0] // shards
    hidden_units = fc1_weight.shape[1]
    me, group = lax.axis_index("seq"), lax.axis_index("shard")
    blocks = rows // ROWS
    heads = width // HEAD // seqs
    part = heads * HEAD
    ff_part = hidden_units // shards // seqs

    qkv_half = take(qkv_weight.reshape(-1, 3, seqs, part), me, 2).reshape(-1, 3 * part)
    fc1_half = take(fc1_weight.reshape(-1, shards, seqs, ff_part), me, 2).reshape(-1, shards * ff_part)
    fc2_half = take(fc2_weight.reshape(seqs, ff_part, width), me, 0)
    small = jnp.concatenate(
        [first_gain, first_bias, qv_bias, dense_bias, second_gain, second_bias, fc1_bias, fc2_bias]
    )
    small_rows = -(-small.shape[0] // (3 * part))
    small_rows += -small_rows % 16
    small = jnp.pad(small, (0, small_rows * 3 * part - small.shape[0])).reshape(small_rows, 3 * part)
    gather = lambda a: lax.all_gather(a, "shard", axis=0, tiled=False)
    qkv_small = gather(jnp.concatenate([qkv_half, small], axis=0))
    own_rows = qkv_half.shape[0]
    full_qkv = qkv_small[:, :own_rows].reshape(width, 3 * part)
    smalls = qkv_small[:, own_rows:].reshape(shards, -1).astype(f32)
    full_dense = gather(dense_weight).reshape(width, width)
    full_up = gather(fc1_half).reshape(width, shards * ff_part)
    full_down = gather(fc2_half).reshape(shards * ff_part, width)
    cuts, at = [], 0
    for a in (first_gain, first_bias, qv_bias, dense_bias, second_gain, second_bias, fc1_bias, fc2_bias):
        cuts.append(smalls[:, at : at + a.shape[0]].reshape(-1))
        at += a.shape[0]
    gain_one, bias_one, bias_qv, bias_dense, gain_two, bias_two, bias_up, bias_down = cuts
    bias_q, bias_v = (take(bias_qv[i * width : (i + 1) * width].reshape(seqs, part), me) for i in (0, 1))
    bias_all = jnp.concatenate([bias_q, jnp.zeros_like(bias_q), bias_v])
    bias_up = take(bias_up.reshape(shards, seqs, ff_part), me, 1).reshape(-1)

    seq_rows, row_start, slot_rows, slot_start, slot_before = layout_tables(lengths, lanes, shards, per_group)
    row_in = jnp.arange(rows, dtype=jnp.int32)[None, :, None]
    inside = ((row_in >= slot_before[:, None]) & (row_in < (slot_before + slot_rows)[:, None])).astype(jnp.int32)
    send_live = jnp.sum(inside, axis=2) > 0
    send_row = jnp.sum(inside * (slot_start[:, None] + row_in - slot_before[:, None]), axis=2).reshape(-1)

    def to_groups(source):
        packed = jnp.take(source, send_row, axis=0).reshape(shards, rows, width)
        packed = jnp.where(send_live[:, :, None], packed, jnp.zeros_like(packed))
        got = lax.all_to_all(packed, "shard", split_axis=0, concat_axis=0, tiled=True)
        own = got.reshape(shards, blocks, ROWS, width).transpose(1, 0, 2, 3).reshape(blocks, -1, width)
        return own, seq_gather(own, 1).reshape(cap, width)

    x_own, x_low = to_groups(tokens[0])
    cot_own, cot_low = to_groups(cotangent[0])

    def own_part(whole):
        return take(whole.reshape(blocks, seqs, -1, whole.shape[-1]), me, 1)

    place = jnp.arange(cap, dtype=jnp.int32)
    block_of, in_block = place // (ROWS * lanes), place % (ROWS * lanes)
    row_of = block_of * ROWS + in_block % ROWS
    ids = row_of * lanes + in_block // ROWS
    own_before, own_count = take(slot_before, group), take(slot_rows, group)
    holds = (row_of[:, None] >= own_before[None]) & (row_of[:, None] < (own_before + own_count)[None])
    begin_row = jnp.sum(jnp.where(holds, own_before[None], 0), axis=1)
    begins = jnp.where(jnp.any(holds, axis=1), begin_row * lanes, ids)
    ids, begins = ids.astype(f32), begins.astype(f32)
    head_ids = me * heads + jnp.arange(heads, dtype=jnp.int32)
    slopes = 2.0 ** (-8.0 * (head_ids.astype(f32) + 1.0) / HEADS)
    one_seq = per_group == 1

    hidden = x_low.astype(f32)
    xhat_one, _ = normalize(hidden)
    normed_one = (xhat_one * gain_one + bias_one).astype(bf16)
    qkv = (jnp.dot(normed_one, full_qkv, preferred_element_type=f32) + bias_all).astype(bf16)
    mixed = attention_forward(qkv, slopes, ids, begins, lanes, one_seq)
    mixed_all = seq_gather(mixed, 1).reshape(cap, width)
    branch = jnp.dot(mixed_all, full_dense, preferred_element_type=f32) + bias_dense
    resid = hidden + branch
    xhat_two, _ = normalize(resid)
    normed_two = (xhat_two * gain_two + bias_two).astype(bf16)
    upper = jnp.dot(normed_two, full_up, preferred_element_type=f32) + bias_up
    activ = gelu_tanh(upper).astype(bf16)
    down = jnp.dot(activ, full_down, preferred_element_type=f32)
    resid_own = own_part(resid)
    down_own = seq_sum(down.reshape(blocks, seqs, -1, width), 1)
    block_out = (resid_own + down_own + bias_down).astype(bf16)

    grad_down = jnp.dot(activ.T, cot_low, preferred_element_type=f32).astype(bf16)
    grad_activ = jnp.dot(cot_low, full_down.T, preferred_element_type=f32)
    grad_upper = jax.vjp(gelu_tanh, upper)[1](grad_activ)[0].astype(bf16)
    grad_up = jnp.dot(normed_two.T, grad_upper, preferred_element_type=f32).astype(bf16)
    grad_bup = jnp.sum(grad_upper.astype(f32), axis=0)
    grad_normed = jnp.dot(grad_upper, full_up.T, preferred_element_type=f32)
    grad_normed = seq_sum(grad_normed.reshape(blocks, seqs, -1, width), 1).reshape(slots, width)
    cot_full = cot_own.reshape(slots, width).astype(f32)
    grad_bdown = jnp.sum(cot_full, axis=0)
    xhat_two, root_two = normalize(resid_own.reshape(slots, width))
    grad_gain_two = jnp.sum(grad_normed * xhat_two, axis=0)
    grad_bias_two = jnp.sum(grad_normed, axis=0)
    grad_resid = cot_full + norm_pull(grad_normed, gain_two, xhat_two, root_two)

    grad_branch = grad_resid.astype(bf16)
    grad_dense = jnp.dot(own_part(mixed_all).reshape(slots, width).T, grad_branch, preferred_element_type=f32).astype(bf16)
    grad_bdense = jnp.sum(grad_branch.astype(f32), axis=0)
    grad_mixed = jnp.dot(grad_branch, full_dense.T, preferred_element_type=f32).astype(bf16)
    got = seq_blocks(grad_mixed.reshape(blocks, -1, seqs, part), 2, bf16)
    if seqs == 2:
        grad_mixed = jnp.where(me == 0, jnp.stack(got, 1), jnp.stack(got[::-1], 1))
    else:
        grad_mixed = jnp.zeros((blocks, seqs) + got[0].shape[1:], bf16)
        for d, g in enumerate(got):
            grad_mixed = lax.dynamic_update_index_in_dim(grad_mixed, g, (me - d) % seqs, 1)
    grad_mixed = grad_mixed.reshape(cap, part)
    planes = qkv.reshape(cap, -1, 2 * HEAD).transpose(1, 0, 2)
    grad_proj = jnp.concatenate(
        attention_backward(planes, grad_mixed, slopes, ids, begins, lanes, one_seq), axis=1
    )
    grad_qkv = jnp.dot(normed_one.T, grad_proj, preferred_element_type=f32).astype(bf16)
    proj_sums = jnp.sum(grad_proj.astype(f32), axis=0)
    grad_one = jnp.dot(grad_proj, full_qkv.T, preferred_element_type=f32)
    grad_one = seq_sum(grad_one.reshape(blocks, seqs, -1, width), 1).reshape(slots, width)
    xhat_one, root_one = normalize(x_own.reshape(slots, width).astype(f32))
    grad_gain_one = jnp.sum(grad_one * xhat_one, axis=0)
    grad_bias_one = jnp.sum(grad_one, axis=0)
    tokens_grad = (grad_resid + norm_pull(grad_one, gain_one, xhat_one, root_one)).astype(bf16)

    row_here = jnp.arange(slots, dtype=jnp.int32)[:, None]
    seq_in = ((row_here >= row_start[None]) & (row_here < (row_start + seq_rows)[None])).astype(jnp.int32)
    home = jnp.arange(lengths.shape[0], dtype=jnp.int32) // per_group
    fetch = jnp.sum(seq_in * (home[None] * rows + slot_before.reshape(-1)[None] + row_here - row_start[None]), axis=1)
    fetch_live = jnp.sum(seq_in, axis=1) > 0

    def to_stream(own):
        sent = own.reshape(blocks, shards, ROWS, width).transpose(1, 0, 2, 3).reshape(shards, rows, width)
        got = lax.all_to_all(sent, "shard", split_axis=0, concat_axis=0, tiled=True)
        taken = jnp.take(got.reshape(-1, width), fetch, axis=0)
        return jnp.where(fetch_live[:, None], taken, jnp.zeros_like(taken))[None]

    down_block = shard_reduce(grad_down.reshape(shards, ff_part, width), bf16)
    up_block = shard_reduce(grad_up.reshape(shards, -1, shards * ff_part), bf16)
    dense_block = shard_reduce(grad_dense.reshape(shards, -1, width), bf16)
    qkv_block = shard_reduce(grad_qkv.reshape(shards, -1, 3 * part), bf16)

    def spread(vector, index_shape):
        zero = jnp.zeros(index_shape, f32)
        return lax.dynamic_update_index_in_dim(zero, vector, me, 1)

    sums = proj_sums.reshape(3, part)
    qv = spread(jnp.stack([sums[0], sums[2]]), (2, seqs, part)).reshape(shards, -1)
    bup = spread(grad_bup.reshape(shards, ff_part), (shards, seqs, ff_part)).reshape(shards, -1)
    rest = (grad_gain_one, grad_bias_one, grad_bdense, grad_gain_two, grad_bias_two, grad_bdown)
    packed = jnp.concatenate([a.reshape(shards, -1) for a in rest] + [qv, bup], axis=1)
    packed = shard_reduce(packed, f32)
    packed = jnp.sum(seq_gather(packed, 0), axis=0)
    cuts, at = [], 0
    for a in [a.reshape(shards, -1) for a in rest] + [qv, bup]:
        cuts.append(packed[at : at + a.shape[1]])
        at += a.shape[1]
    g_gain_one, g_bias_one, g_bdense, g_gain_two, g_bias_two, g_bdown, g_qv, g_bup = cuts

    g_dense = jnp.sum(seq_gather(dense_block.astype(bf16), 0).astype(f32), axis=0)
    g_qkv = seq_gather(qkv_block.astype(bf16).reshape(-1, 3, part), 2).reshape(-1, 3 * width).astype(f32)
    g_up = seq_gather(up_block.astype(bf16).reshape(-1, shards, ff_part), 2).reshape(-1, hidden_units).astype(f32)
    g_down = seq_gather(down_block.astype(bf16), 0).reshape(-1, width).astype(f32)
    return (
        to_stream(block_out), to_stream(tokens_grad.reshape(blocks, -1, width)),
        g_gain_one, g_bias_one, g_qkv, g_qv, g_dense, g_bdense, g_gain_two, g_bias_two, g_up, g_bup, g_down, g_bdown,
    )


def choose(*arguments):
    one = arguments[2].shape[0] == lax.axis_size("shard")
    fused = one and lax.axis_size("seq") == 2 and shard_factors(lax.axis_size("shard")) == (4, 2, 2)
    return (per_device if fused else per_device_any)(*arguments)


def solution(mesh):
    rows, vector, stream = P("shard", None), P("shard"), P(("seq", "shard"), None, None)
    params = (vector, vector, rows, vector, rows, vector, vector, vector, rows, vector, rows, vector)
    return jax.shard_map(
        choose, mesh=mesh, in_specs=(stream, stream, P()) + params, out_specs=(stream, stream) + params, check_vma=False
    )
```

```python
import functools

import jax
import jax.numpy as jnp
import numpy as np
from jax import lax
from jax.experimental import pallas as pl
from jax.experimental.pallas import tpu as pltpu
from jax.sharding import PartitionSpec as P

HEADS = 16
HEAD = 64
ROWS = 8

epsilon = 1e-05
masked_score = -1e30
f32 = jnp.float32
bf16 = jnp.bfloat16


def gelu_tanh(values):
    return (
        0.5
        * values
        * (1.0 + jnp.tanh(0.7978845608028654 * (values + 0.044715 * values * values * values)))
    )


def normalize(hidden):
    center = hidden - jnp.mean(hidden, axis=-1, keepdims=True)
    spread = jnp.mean(center * center, axis=-1, keepdims=True)
    root = lax.rsqrt(spread + epsilon)
    return center * root, root


def norm_pull(grad, gain, xhat, root):
    scaled = grad * gain
    return root * (
        scaled
        - jnp.mean(scaled, axis=-1, keepdims=True)
        - xhat * jnp.mean(scaled * xhat, axis=-1, keepdims=True)
    )


def slot_ids(first, count, lanes):
    place = first + lax.broadcasted_iota(jnp.int32, (count, 1), 0)
    block, inside = place // (ROWS * lanes), place % (ROWS * lanes)
    return (block * ROWS + inside % ROWS) * lanes + inside // ROWS


def blocked_ids(shape, axis, lanes):
    place = lax.broadcasted_iota(jnp.int32, shape, axis)
    high = (ROWS * lanes).bit_length() - 1
    inside = place & (ROWS * lanes - 1)
    row = (place >> high) * ROWS + (inside & (ROWS - 1))
    return (row * lanes + (inside >> (ROWS.bit_length() - 1))).astype(f32)


def attn_mask(scored, allowed):
    return jnp.where(allowed, scored, masked_score)


def attn_fwd_kernel(lanes, tile, one_seq, slope_ref, idc_ref, idr_ref, beginc_ref, q_ref, k_ref, v_ref, o_ref):
    tokens = q_ref.shape[0]
    block = ROWS * lanes
    lane_id = lax.broadcasted_iota(jnp.int32, (1, 2 * HEAD), 1)
    for b in range(tokens // block):
        end = (b + 1) * block

        def step(t, _):
            at = pl.ds(pl.multiple_of(b * block + t * tile, tile), tile)
            q = q_ref[at, :] * jnp.asarray(HEAD**-0.5, bf16)
            ids_q = idc_ref[at, :]
            both = None
            for j in range(2):
                mine = (lane_id // HEAD) == j
                qj = jnp.where(mine, q, jnp.zeros_like(q))
                s = lax.dot_general(
                    qj, k_ref[:end, :], (((1,), (1,)), ((), ())), preferred_element_type=f32
                )
                s = s + slope_ref[0, 0, j] * idr_ref[:, :end]
                if one_seq:
                    own = s[:, b * block :]
                    own = attn_mask(own, idr_ref[:, b * block : end] <= ids_q)
                    s = jnp.concatenate([s[:, : b * block], own], axis=1) if b else own
                else:
                    ids_k = idr_ref[:, :end]
                    s = attn_mask(s, (ids_k <= ids_q) & (ids_k >= beginc_ref[at, :]))
                top = jnp.max(s, axis=1, keepdims=True)
                e = jnp.exp(s - top)
                total = jnp.sum(e, axis=1, keepdims=True)
                o = jnp.dot(e.astype(bf16), v_ref[:end, :], preferred_element_type=f32) / total
                both = o if both is None else jnp.where(mine, o, both)
            o_ref[at, :] = both.astype(bf16)
            return 0

        lax.fori_loop(0, block // tile, step, 0)


def attn_bwd_kernel(
    lanes, tile, one_seq, slope_ref, idc_ref, idr_ref, beginr_ref, q_ref, k_ref, v_ref, do_ref,
    dq_ref, dk_ref, dv_ref, dk_acc, dv_acc, bias_acc,
):
    tokens = q_ref.shape[0]
    block = ROWS * lanes
    lane_id = lax.broadcasted_iota(jnp.int32, (1, 2 * HEAD), 1)
    dk_acc[...] = jnp.zeros_like(dk_acc)
    dv_acc[...] = jnp.zeros_like(dv_acc)
    for j in range(2):
        bias_acc[j] = jnp.broadcast_to(slope_ref[0, 0, j] * idc_ref[...], (tokens, tile))
    for b in range(tokens // block):
        end = (b + 1) * block

        def step(t, _):
            at = pl.ds(pl.multiple_of(b * block + t * tile, tile), tile)
            q = q_ref[at, :] * jnp.asarray(HEAD**-0.5, bf16)
            do = do_ref[at, :]
            ids_q = idr_ref[:, at]
            both = None
            for j in range(2):
                mine = (lane_id // HEAD) == j
                qj = jnp.where(mine, q, jnp.zeros_like(q))
                doj = jnp.where(mine, do, jnp.zeros_like(do))
                s = lax.dot_general(
                    k_ref[:end, :], qj, (((1,), (1,)), ((), ())), preferred_element_type=f32
                )
                s = s + bias_acc[j, :end, :]
                if one_seq:
                    own = s[b * block :, :]
                    own = attn_mask(own, idc_ref[b * block : end, :] <= ids_q)
                    s = jnp.concatenate([s[: b * block, :], own], axis=0) if b else own
                else:
                    ids_k = idc_ref[:end, :]
                    s = attn_mask(s, (ids_k <= ids_q) & (ids_k >= beginr_ref[:, at]))
                top = jnp.max(s, axis=0, keepdims=True)
                e = jnp.exp(s - top)
                probs = e * (1.0 / jnp.sum(e, axis=0, keepdims=True))
                dv_acc[:end, :] += jnp.dot(probs.astype(bf16), doj, preferred_element_type=f32)
                dp = lax.dot_general(
                    v_ref[:end, :], doj, (((1,), (1,)), ((), ())), preferred_element_type=f32
                )
                inner = jnp.sum(probs * dp, axis=0, keepdims=True)
                ds = (probs * (dp - inner)).astype(bf16)
                dk_acc[:end, :] += jnp.dot(ds, qj, preferred_element_type=f32)
                dq = lax.dot_general(
                    ds, k_ref[:end, :], (((0,), (0,)), ((), ())), preferred_element_type=f32
                )
                both = dq if both is None else jnp.where(mine, dq, both)
            dq_ref[at, :] = (both * (HEAD**-0.5)).astype(bf16)
            return 0

        lax.fori_loop(0, block // tile, step, 0)
    dk_ref[...] = dk_acc[...].astype(bf16)
    dv_ref[...] = dv_acc[...].astype(bf16)


def attn_shape(tokens, width, lanes):
    pairs = width // (2 * HEAD)
    tile = min(256, ROWS * lanes)
    return pairs, tile


def attention_forward(qkv, slopes, ids, begins, lanes, one_seq):
    tokens, width = qkv.shape[0], qkv.shape[1] // 3
    pairs, tile = attn_shape(tokens, width, lanes)
    column = lambda part: pl.BlockSpec((tokens, 2 * HEAD), lambda h, part=part: (0, part * pairs + h))
    whole = lambda a: pl.BlockSpec(a.shape, lambda h: (0, 0))
    idc, idr, beginc = ids[:, None], ids[None, :], begins[:, None]
    half = tokens * tokens * 5 // 8
    return pl.pallas_call(
        functools.partial(attn_fwd_kernel, lanes, tile, one_seq),
        grid=(pairs,),
        in_specs=[
            pl.BlockSpec((1, 1, 2), lambda h: (h, 0, 0), memory_space=pltpu.SMEM),
            whole(idc), whole(idr), whole(beginc), column(0), column(1), column(2),
        ],
        out_specs=pl.BlockSpec((tokens, 2 * HEAD), lambda h: (0, h)),
        out_shape=jax.ShapeDtypeStruct((tokens, width), bf16),
        compiler_params=pltpu.CompilerParams(vmem_limit_bytes=48 * 2**20),
        cost_estimate=pl.CostEstimate(
            flops=8 * pairs * half * HEAD * 2, transcendentals=2 * pairs * half, bytes_accessed=8 * tokens * width
        ),
        name="attention_forward",
    )(slopes.reshape(pairs, 1, 2), idc, idr, beginc, qkv, qkv, qkv)


def attention_backward(qkv, grad_out, slopes, ids, begins, lanes, one_seq):
    tokens, width = grad_out.shape
    pairs, tile = attn_shape(tokens, width, lanes)
    column = lambda part: pl.BlockSpec((tokens, 2 * HEAD), lambda h, part=part: (0, part * pairs + h))
    whole = lambda a: pl.BlockSpec(a.shape, lambda h: (0, 0))
    idc, idr, beginr = ids[:, None], ids[None, :], begins[None, :]
    plane = lambda part: pl.BlockSpec((None, tokens, 2 * HEAD), lambda h, part=part: (part * pairs + h, 0, 0))
    out = jax.ShapeDtypeStruct((tokens, width), bf16)
    half = tokens * tokens * 5 // 8
    return pl.pallas_call(
        functools.partial(attn_bwd_kernel, lanes, tile, one_seq),
        grid=(pairs,),
        in_specs=[
            pl.BlockSpec((1, 1, 2), lambda h: (h, 0, 0), memory_space=pltpu.SMEM),
            whole(idc), whole(idr), whole(beginr), plane(0), plane(1), plane(2), column(0),
        ],
        out_specs=[column(0)] * 3,
        out_shape=[out] * 3,
        scratch_shapes=[
            pltpu.VMEM((tokens, 2 * HEAD), f32), pltpu.VMEM((tokens, 2 * HEAD), f32), pltpu.VMEM((2, tokens, tile), f32),
        ],
        compiler_params=pltpu.CompilerParams(vmem_limit_bytes=56 * 2**20),
        cost_estimate=pl.CostEstimate(
            flops=20 * pairs * half * HEAD * 2, transcendentals=2 * pairs * half, bytes_accessed=14 * tokens * width
        ),
        name="attention_backward",
    )(slopes.reshape(pairs, 1, 2), idc, idr, beginr, qkv, qkv, qkv, grad_out)


def take(blocks, index, axis=0):
    return lax.dynamic_index_in_dim(blocks, index, axis, keepdims=False)


def seq_gather(block, axis):
    n, me = lax.axis_size("seq"), lax.axis_index("seq")
    shape = block.shape[:axis] + (n,) + block.shape[axis:]
    if n == 2:
        peer = lax.ppermute(block, "seq", [(0, 1), (1, 0)])
        return jnp.where(me == 0, jnp.stack([block, peer], axis), jnp.stack([peer, block], axis))
    whole = lax.dynamic_update_index_in_dim(jnp.zeros(shape, block.dtype), block, me, axis)
    for d in range(1, n):
        got = lax.ppermute(block, "seq", [(i, (i + d) % n) for i in range(n)])
        whole = lax.dynamic_update_index_in_dim(whole, got, (me - d) % n, axis)
    return whole


def seq_blocks(whole, axis, dtype):
    n, me = lax.axis_size("seq"), lax.axis_index("seq")
    got = [take(whole, me, axis)]
    for d in range(1, n):
        sent = take(whole, (me + d) % n, axis).astype(dtype)
        got.append(lax.ppermute(sent, "seq", [(i, (i + d) % n) for i in range(n)]))
    return got


def seq_sum(whole, axis, dtype=bf16):
    got = seq_blocks(whole, axis, dtype)
    return sum((g.astype(f32) for g in got[1:]), got[0].astype(f32))


def shard_factors(n):
    nc = 2 if n % 2 == 0 else 1
    nz = 4 if n % (4 * nc) == 0 else 1
    return nz, n // (nz * nc), nc


def shard_reduce(blocks, dtype):
    n, me = lax.axis_size("shard"), lax.axis_index("shard")
    sizes = shard_factors(n)
    blocks = blocks.reshape(sizes + blocks.shape[1:])
    place = (me // (sizes[1] * sizes[2]), me // sizes[2] % sizes[1], me % sizes[2])
    strides = (sizes[1] * sizes[2], sizes[2], 1)
    for axis in (2, 1, 0):
        size, mine, stride = sizes[axis], place[axis], strides[axis]
        total = take(blocks, mine, axis).astype(f32)
        for d in range(1, size):
            sent = take(blocks, (mine + d) % size, axis).astype(dtype)
            pairs = [
                (i, i - (i // stride % size) * stride + ((i // stride % size + d) % size) * stride)
                for i in range(n)
            ]
            total = total + lax.ppermute(sent, "shard", pairs).astype(f32)
        blocks = total if axis == 0 else total.astype(dtype)
    return blocks


MESH = pl.DeviceIdType.MESH


class Geometry:
    def __init__(self, seqs, shards):
        self.seqs, self.shards = seqs, shards
        self.sizes = shard_factors(shards)
        self.s, self.k = lax.axis_index("seq"), lax.axis_index("shard")
        nz, ny, nc = self.sizes
        self.z, self.y, self.c = self.k // (ny * nc), self.k // nc % ny, self.k % nc
        self.inner = (self.z + 1) // 2 % 2
        high = self.z // 2
        self.line = (self.z, self.z + 1 - 2 * (self.z % 2), 2 - high, 3 - 3 * high)

    def slot(self, i, dy, dc):
        nz, ny, nc = self.sizes
        return (self.line[i] * ny + (self.y + dy) % ny) * nc + (self.c + dc) % nc


class Wires:
    def __init__(self, geometry, send_sems, recv_sems):
        self.g, self.send_sems, self.recv_sems = geometry, send_sems, recv_sems
        self.sends, self.used = [], 0

    def block(self, count):
        first = self.used
        self.used += count
        return first

    def copy(self, src, dst, sent, got, s, k):
        return pltpu.make_async_remote_copy(
            src_ref=src, dst_ref=dst, send_sem=self.send_sems.at[sent], recv_sem=self.recv_sems.at[got],
            device_id={"seq": s, "shard": k}, device_id_type=MESH,
        )

    def send_as(self, src, dst, sent, got, s, k, like):
        self.copy(src, dst, sent, got, s, k).start()
        self.sends.append((like, sent))

    def recorded(self, like, index):
        self.sends.append((like, index))

    def send(self, src, dst, index, s, k, like):
        self.send_as(src, dst, index, index, s, k, like)

    def arrived(self, dst, index):
        self.copy(dst, dst, index, index, 1 - self.g.s, self.g.k).wait_recv()

    def drain(self):
        for like, index in self.sends:
            self.copy(like, like, index, index, 1 - self.g.s, self.g.k).wait_send()
        self.sends = []


def enter(geometry):
    g = geometry
    barrier = pltpu.get_barrier_semaphore()
    for d in range(1, g.shards):
        pl.semaphore_signal(
            barrier, inc=1, device_id={"seq": g.s, "shard": (g.k + d) % g.shards}, device_id_type=MESH
        )
    pl.semaphore_signal(barrier, inc=1, device_id={"seq": 1 - g.s, "shard": g.k}, device_id_type=MESH)
    pl.semaphore_wait(barrier, g.shards)


class Gather:
    def __init__(self, wires, own, out):
        self.w, self.g, self.own, self.out = wires, wires.g, own, out
        nz, ny, nc = self.g.sizes
        self.z0 = wires.block(nz)
        self.on0 = wires.block(nz)
        self.y0 = wires.block(nz * ny)
        self.c0 = wires.block(nz * ny * nc)

    def on_y(self, i, src):
        g = self.g
        for dy in range(1, g.sizes[1]):
            self.w.send(src, self.out.at[g.slot(i, 0, 0)], self.y0 + i * g.sizes[1] + dy, g.s, g.slot(0, dy, 0), self.own)

    def on_core(self, i, dy, src):
        g = self.g
        for dc in range(1, g.sizes[2]):
            index = self.c0 + (i * g.sizes[1] + dy) * g.sizes[2] + dc
            self.w.send(src, self.out.at[g.slot(i, -dy, 0)], index, g.s, g.slot(0, 0, dc), self.own)

    def start(self):
        g = self.g
        here = self.out.at[g.k]
        self.w.send_as(self.own, here, self.z0 + 2, self.z0 + 3 - g.inner, g.s, g.slot(2, 0, 0), self.own)
        self.w.send(self.own, here, self.z0 + 1, g.s, g.slot(1, 0, 0), self.own)

    def start_near(self):
        self.on_y(0, self.own)
        self.on_core(0, 0, self.own)

    def poll_z(self):
        g = self.g
        for i in (1, 2, 3):
            at = self.out.at[g.slot(i, 0, 0)]
            self.w.arrived(at, self.z0 + i)
            if i > 1:

                @pl.when(g.inner == 1)
                def _(at=at, i=i):
                    self.w.copy(at, at, self.on0 + i, self.z0 + i, g.s, g.slot(1, 0, 0)).start()

            self.on_y(i, at)
            self.on_core(i, 0, at)

    def poll_y(self):
        g = self.g
        for i in range(g.sizes[0]):
            for dy in range(1, g.sizes[1]):
                at = self.out.at[g.slot(i, -dy, 0)]
                self.w.arrived(at, self.y0 + i * g.sizes[1] + dy)
                self.on_core(i, dy, at)

    def finish(self):
        g = self.g
        for i in range(g.sizes[0]):
            for dy in range(g.sizes[1]):
                for dc in range(1, g.sizes[2]):
                    at = self.out.at[g.slot(i, -dy, -dc)]
                    self.w.arrived(at, self.c0 + (i * g.sizes[1] + dy) * g.sizes[2] + dc)

        @pl.when(g.inner == 1)
        def _():
            for i in (2, 3):
                self.w.copy(self.own, self.own, self.on0 + i, self.z0 + i, g.s, g.k).wait_send()


class Tokens:
    def __init__(self, wires, packed, out):
        self.w, self.g, self.packed, self.out = wires, wires.g, packed, out
        self.blocks = out.shape[0]
        self.at = wires.block((self.g.shards + 1) * self.blocks)
        self.like, self.row = packed.at[0, 0], packed.at[:, 0]

    def index(self, b, d):
        return self.at + b * (self.g.shards + 1) + d

    def mine(self, b, s):
        return self.out.at[b, pl.ds(pl.multiple_of(s * self.g.shards, self.g.shards), self.g.shards)]

    def start(self, b):
        g = self.g
        for d in range(1, g.shards):
            to = (g.k + d) % g.shards
            lane = self.out.at[b, g.s * g.shards + g.k]
            self.w.send(self.packed.at[to, b], lane, self.index(b, d), g.s, to, self.like)

    def poll(self, b):
        g = self.g
        for d in range(1, g.shards):
            self.w.arrived(self.out.at[b, g.s * g.shards + (g.k - d) % g.shards], self.index(b, d))
        self.w.send(self.mine(b, g.s), self.mine(b, g.s), self.index(b, g.shards), 1 - g.s, g.k, self.row)

    def finish(self, b):
        self.w.arrived(self.mine(b, 1 - self.g.s), self.index(b, self.g.shards))


class Smalls:
    def __init__(self, wires, held, at):
        self.w, self.g, self.held, self.at = wires, wires.g, held, at

    def start(self):
        g = self.g
        mine = self.held.at[g.k]
        for d in range(1, g.shards):
            self.w.send(mine, mine, self.at + d, g.s, (g.k + d) % g.shards, mine)

    def finish(self):
        g = self.g
        for d in range(1, g.shards):
            self.w.arrived(self.held.at[(g.k - d) % g.shards], self.at + d)


def side_by_side(vec, small, row, to, count):
    for j in range(small.shape[0]):
        vec[to : to + 1, j * count : (j + 1) * count] = small[j, row : row + 1, :count]


def forward_kernel(
    seqs, shards, counts,
    packed, packed_cot, qkv_w, small, dense_w, fc1_w, fc2_w, slopes, lengths,
    x_out, cot_out, n1_out, n2_out, qkvw_out, dense_out, fc1_out, fc2_out, qkv_out, o_out, h2_out, a_out, slope_out,
    w2_out, vec_out,
    x_v, n1_v, n2_v, qkvw_v, small_v, dense_v, fc1_v, fc2_v, blocks_v, cot_v, qkv_v, o_v, h2_v, a_v, slope_v, w2_v, vec_v, idc, idr,
    send_sems, recv_sems, copy_sems,
):
    g = Geometry(seqs, shards)
    wires = Wires(g, send_sems, recv_sems)
    lanes = seqs * shards
    width = n1_v.shape[1]
    part = o_v.shape[2]
    pairs = part // (2 * HEAD)
    ff = fc1_v.shape[2]
    ff_part = ff // shards
    block = ROWS * lanes
    blocks = x_v.shape[0]
    half = block // seqs
    rows = width // shards
    local = []

    def bring(src, dst):
        made = pltpu.make_async_copy(src, dst, copy_sems.at[len(local)])
        made.start()
        local.append(made)
        return made

    def at_block(b):
        return pl.ds(pl.multiple_of(b * block, block), block)

    tokens = Tokens(wires, packed, x_v)
    cots = Tokens(wires, packed_cot, blocks_v)
    smalls_at = wires.block(shards)
    qkv_all = Gather(wires, qkvw_v.at[g.k], qkvw_v)
    dense_all = Gather(wires, dense_v.at[g.k], dense_v)
    up_all = Gather(wires, fc1_v.at[g.k], fc1_v)
    down_all = Gather(wires, fc2_v, fc2_out)
    heads_at = wires.block(blocks)

    staged_qkv = [
        bring(
            qkv_w.at[:, pl.ds(pl.multiple_of(p * width + g.s * part, 128), part)],
            qkvw_v.at[g.k, :, pl.ds(p * part, part)],
        )
        for p in range(3)
    ]
    staged_small = bring(small, small_v.at[g.k])
    staged_dense = bring(dense_w, dense_v.at[g.k])
    staged_up = [
        bring(
            fc1_w.at[:, pl.ds(pl.multiple_of((i * seqs + g.s) * ff_part, 128), ff_part)],
            fc1_v.at[g.k, :, pl.ds(i * ff_part, ff_part)],
        )
        for i in range(shards)
    ]
    staged_x = bring(packed.at[g.k], x_v.at[:, g.s * shards + g.k])
    staged_down = bring(fc2_w.at[pl.ds(pl.multiple_of(g.s * ff_part, 8), ff_part), :], fc2_v)
    staged_cot = bring(packed_cot.at[g.k], blocks_v.at[:, g.s * shards + g.k])
    enter(g)
    idc[...] = blocked_ids(idc.shape, 0, lanes)
    idr[...] = blocked_ids(idr.shape, 1, lanes)
    for made in staged_qkv:
        made.wait()
    staged_small.wait()
    staged_dense.wait()
    for made in staged_up:
        made.wait()
    staged_down.wait()
    staged_x.wait()
    staged_cot.wait()
    kept = [bring(fc2_v, fc2_out.at[g.k])]
    smalls = Smalls(wires, small_v, smalls_at)
    qkv_all.start()
    qkv_all.start_near()
    tokens.start(0)
    tokens.start(1)
    smalls.start()
    dense_all.start_near()
    up_all.start_near()
    down_all.start_near()
    tokens.poll(0)
    tokens.start(2)
    qkv_all.poll_z()
    tokens.poll(1)
    tokens.start(3)
    dense_all.start()
    up_all.start()
    smalls.finish()

    for row in (0, 1, 3, 4, 5, 7):
        side_by_side(vec_v, small_v, row, row, rows)
    vec_v[2:3, :] = jnp.zeros((1, vec_v.shape[1]), f32)
    per = 2 * width // shards
    for i in range(part // per):
        for row, side in ((0, 0), (2, 1)):
            j = (side * width + g.s * part) // per + i
            vec_v[2:3, row * part + i * per : row * part + (i + 1) * per] = small_v[j, 2:3, :per]
    for j in range(shards):
        vec_v[6:7, j * ff_part : (j + 1) * ff_part] = small_v[j, 6:7, pl.ds(pl.multiple_of(g.s * ff_part, 128), ff_part)]

    qkv_all.poll_y()
    tokens.poll(2)
    tokens.poll(3)
    down_all.start()
    qkv_all.finish()
    kept += [bring(qkvw_v, qkvw_out), bring(vec_v, vec_out)]

    lane_id = lax.broadcasted_iota(jnp.int32, (1, 2 * HEAD), 1)
    tile = min(256, block)

    def project(b):
        x = x_v[b].astype(f32).reshape(block, width)
        xhat, _ = normalize(x)
        n1 = (xhat * vec_v[0:1, :width] + vec_v[1:2, :width]).astype(bf16)
        at = at_block(b)
        n1_v[at, :] = n1
        for p in range(3):
            weight = qkvw_v[:, :, p * part : (p + 1) * part].reshape(width, part)
            out = jnp.dot(n1, weight, preferred_element_type=f32) + vec_v[2:3, p * part : (p + 1) * part]
            out = out.astype(bf16)
            for h in range(pairs):
                qkv_v[p * pairs + h, at, :] = out[:, h * 2 * HEAD : (h + 1) * 2 * HEAD]

    def attend(b):
        end = (b + 1) * block

        @pl.loop(0, pairs)
        def _(h):
            q_ref, k_ref, v_ref = qkv_v.at[h], qkv_v.at[pairs + h], qkv_v.at[2 * pairs + h]
            for t in range(block // tile):
                at = pl.ds(b * block + t * tile, tile)
                q = q_ref[at, :] * jnp.asarray(HEAD**-0.5, bf16)
                ids_q = idc[at, :]

                def one_head(j, both):
                    mine = (lane_id >= HEAD).astype(jnp.int32) == j
                    qj = jnp.where(mine, q, jnp.zeros_like(q))
                    s = lax.dot_general(
                        qj, k_ref[:end, :], (((1,), (1,)), ((), ())), preferred_element_type=f32
                    )
                    s = s + slopes[g.s * pairs + h, j] * idr[:, :end]
                    tail = attn_mask(s[:, b * block :], idr[:, b * block : end] <= ids_q)
                    s = jnp.concatenate([s[:, : b * block], tail], axis=1) if b else tail
                    top = jnp.max(s, axis=1, keepdims=True)
                    e = jnp.exp(s - top)
                    total = jnp.sum(e, axis=1, keepdims=True)
                    o = jnp.dot(e.astype(bf16), v_ref[:end, :], preferred_element_type=f32) / total
                    return jnp.where(mine, o, both)

                both = lax.fori_loop(0, 2, one_head, jnp.zeros((tile, 2 * HEAD), f32))
                o_v[g.s, at, pl.ds(pl.multiple_of(h * 2 * HEAD, 2 * HEAD), 2 * HEAD)] = both.astype(bf16)

    def head_copy(b):
        mine = o_v.at[g.s, at_block(b)]
        return wires.copy(mine, mine, heads_at + b, heads_at + b, 1 - g.s, g.k)

    for b in range(blocks):
        tokens.finish(b)
        project(b)
        attend(b)
        head_copy(b).start()
        if b == 0:
            dense_all.poll_z()
        if b == 1:
            up_all.poll_z()
        if b == 2:
            dense_all.poll_y()
            cots.start(0)
            cots.start(1)
        if b == 3:
            up_all.poll_y()
    kept += [bring(x_v, x_out), bring(n1_v, n1_out), bring(qkv_v, qkv_out)]
    down_all.poll_z()
    dense_all.finish()
    kept.append(bring(dense_v, dense_out))
    up_all.finish()
    kept.append(bring(fc1_v, fc1_out))

    @pl.loop(0, blocks)
    def _(b):
        at = at_block(b)
        wires.arrived(o_v.at[1 - g.s, at], heads_at + b)
        branch = jnp.dot(
            o_v[0, at, :], dense_v[: shards // 2].reshape(part, width), preferred_element_type=f32
        ) + jnp.dot(o_v[1, at, :], dense_v[shards // 2 :].reshape(part, width), preferred_element_type=f32)
        resid = x_v[b].astype(f32).reshape(block, width) + branch + vec_v[3:4, :width]
        h2_v[b] = jnp.where(g.s == 0, resid[:half], resid[half:])
        xhat, _ = normalize(resid)
        n2 = (xhat * vec_v[4:5, :width] + vec_v[5:6, :width]).astype(bf16)
        n2_v[at, :] = n2
        step = min(512, ff)

        @pl.loop(0, ff // step)
        def _(n):
            cut = pl.ds(pl.multiple_of(n * step, step), step)
            u = jnp.dot(n2_v[at, :], fc1_v[:, :, cut].reshape(width, step), preferred_element_type=f32) + vec_v[6:7, cut]
            inside = 0.7978845608028654 * u * (1.0 + 0.044715 * u * u)
            t = jnp.tanh(inside)
            a_v[at, cut] = (0.5 * u * (1.0 + t)).astype(bf16)
            slope = 0.5 * (1.0 + t) + 0.5 * u * (1.0 - t * t) * (
                0.7978845608028654 + (0.7978845608028654 * 3.0 * 0.044715) * u * u
            )
            slope_v[at, cut] = slope.astype(bf16)

        @pl.when(b == 0)
        def _():
            cots.poll(0)
            cots.start(2)

        @pl.when(b == 1)
        def _():
            cots.poll(1)
            cots.start(3)

        @pl.when(b == 2)
        def _():
            cots.poll(2)


    cots.poll(3)
    kept.append(bring(o_v, o_out))
    kept += [bring(n2_v, n2_out), bring(h2_v, h2_out), bring(a_v, a_out), bring(slope_v, slope_out)]
    down_all.poll_y()
    for b in range(blocks):
        cots.finish(b)

    @pl.loop(0, blocks)
    def _(b):
        at = at_block(b)
        grad = blocks_v[b].astype(f32).reshape(block, width)
        cot_v[at, :] = jnp.where(idc[at, :] < lengths[g.k].astype(f32), grad, 0.0).astype(bf16)

    kept.append(bring(cot_v, cot_out))

    @pl.loop(0, ff // (2 * ff_part))
    def _(m):
        cut = a_v[:, pl.ds(pl.multiple_of(m * 2 * ff_part, 128), 2 * ff_part)]
        out = lax.dot_general(cut, cot_v[...], (((0,), (0,)), ((), ())), preferred_element_type=f32).astype(bf16)
        w2_v[pl.ds(2 * m, 2)] = out.reshape(2, ff_part, width)

    kept.append(bring(w2_v, w2_out))
    down_all.finish()
    for b in range(blocks):
        head_copy(b).wait_send()
    wires.drain()
    for made in kept:
        made.wait()
    assert wires.used <= counts[0] and len(local) <= counts[1]


def forward_exchange(packed, packed_cot, qkv_w, small, dense_w, fc1_w, fc2_w, slopes, lengths, seqs, shards):
    width, own = qkv_w.shape[0] * shards, qkv_w.shape[0]
    lanes = seqs * shards
    blocks = packed.shape[1]
    block = lanes * ROWS
    cap = blocks * block
    part = width // seqs
    pairs = part // (2 * HEAD)
    ff = fc1_w.shape[1] // seqs
    ff_part = ff // shards
    counts = (384, 64)
    any_ = pl.BlockSpec(memory_space=pl.ANY)
    vmem = pl.BlockSpec(memory_space=pltpu.VMEM)
    smem = pl.BlockSpec(memory_space=pltpu.SMEM)
    x_shape = ((blocks, lanes, ROWS, width), bf16)
    wide, long = ((cap, width), bf16), ((cap, ff), bf16)
    qkvw, dense, fc1, fc2 = (
        ((shards,) + tail, bf16) for tail in ((own, 3 * part), (own, width), (own, ff), (ff_part, width))
    )
    qkv, heads = ((3 * pairs, cap, 2 * HEAD), bf16), ((seqs, cap, part), bf16)
    h2, vec = ((blocks, block // seqs, width), f32), ((8, max(width, 3 * part, ff)), f32)
    outs = [x_shape, wide, wide, wide, qkvw, dense, fc1, fc2, qkv, heads, h2, long, long, fc2, vec]
    scratch = [
        x_shape, wide, wide, qkvw, ((shards,) + small.shape, f32), dense, fc1, ((ff_part, width), bf16), x_shape, wide,
        qkv, heads, h2, long, long, fc2, vec, ((cap, 1), f32), ((1, cap), f32),
    ]
    return pl.pallas_call(
        functools.partial(forward_kernel, seqs, shards, counts),
        in_specs=[any_] * 7 + [smem] * 2,
        out_specs=[any_] * len(outs),
        out_shape=[jax.ShapeDtypeStruct(s, d) for s, d in outs],
        scratch_shapes=[pltpu.VMEM(s, d) for s, d in scratch]
        + [pltpu.SemaphoreType.DMA((counts[0],)), pltpu.SemaphoreType.DMA((counts[0],)), pltpu.SemaphoreType.DMA((counts[1],))],
        compiler_params=pltpu.CompilerParams(collective_id=1, has_side_effects=True, vmem_limit_bytes=60 * 2**20),
        name="forward_exchange",
    )(
        packed, packed_cot, qkv_w, small, dense_w, fc1_w, fc2_w, slopes, lengths,
    )


class Scatter:
    def __init__(self, wires, full, own, bufs):
        self.w, self.g, self.full, self.own = wires, wires.g, full, own
        self.rc, self.ry, self.rz, self.fin = bufs
        self.at = wires.block(8)
        self.one = self.rz.at[0] if self.rz is not None else None

    def add(self, count, into, other):
        @pl.loop(0, count)
        def _(i):
            a, b = into(i), other(i)
            a[...] = (a[...].astype(f32) + b[...].astype(f32)).astype(bf16)

    def core_send(self):
        g = self.g
        self.w.send(self.full.at[:, :, 1 - g.c], self.rc, self.at, g.s, g.slot(0, 0, 1), self.rc)

    def core_done(self):
        g = self.g
        self.w.arrived(self.rc, self.at)
        self.add(8, lambda i: self.rc.at[i // 2, i % 2], lambda i: self.own(i // 2, i % 2))
        if self.ry is not None:
            self.y_send()

    def y_send(self):
        g = self.g
        self.w.send(self.rc.at[:, 1 - g.y], self.ry, self.at + 1, g.s, g.slot(0, 1, 0), self.ry)

    def y_done(self):
        g = self.g
        self.w.arrived(self.ry, self.at + 1)
        self.add(4, lambda i: self.ry.at[i], lambda i: self.rc.at[i, g.y])

    def z_send(self):
        g = self.g
        partner = g.slot(1, 0, 0)
        self.w.send(self.ry.at[g.line[1]], self.rz.at[0], self.at + 2, g.s, partner, self.one)

        @pl.when(g.inner == 0)
        def _():
            for i in (2, 3):
                self.w.copy(self.ry.at[g.line[i]], self.rz.at[i], self.at + 1 + i, self.at + 1 + i, g.s, partner).start()

    def z_done(self):
        g = self.g

        @pl.when(g.inner == 1)
        def _():
            for i in (2, 3):
                self.w.arrived(self.rz.at[i], self.at + 1 + i)
                a = self.rz.at[i]
                a[...] = (a[...].astype(f32) + self.ry[g.line[i]].astype(f32)).astype(bf16)
                self.w.copy(a, self.rz.at[1], self.at + 1 + i, self.at + 5, g.s, g.slot(i, 0, 0)).start()

    def final(self):
        g = self.g
        self.w.arrived(self.rz.at[0], self.at + 2)
        self.w.arrived(self.rz.at[1], self.at + 5)
        total = self.ry[g.z].astype(f32) + self.rz[0].astype(f32) + self.rz[1].astype(f32)
        self.fin[0] = total.astype(bf16)
        self.w.send(self.fin.at[0], self.fin.at[1], self.at + 6, 1 - g.s, g.k, self.fin.at[0])

    def done(self):
        self.w.arrived(self.fin.at[1], self.at + 6)
        for i in (2, 3):
            self.w.copy(self.fin.at[0], self.fin.at[0], self.at + 1 + i, self.at + 1 + i, self.g.s, self.g.k).wait_send()


class Back:
    def __init__(self, wires, src, dst, pieces):
        self.w, self.g, self.src, self.dst, self.pieces = wires, wires.g, src, dst, pieces
        self.at = wires.block(wires.g.shards * pieces)
        self.per = src.shape[0] // pieces
        self.like = src.at[pl.ds(0, self.per), 0]

    def cut(self, ref, i):
        return ref.at[pl.ds(i * self.per, self.per)]

    def send(self, i):
        g = self.g
        for d in range(1, g.shards):
            to = (g.k + d) % g.shards
            src = self.src.at[pl.ds(i * self.per, self.per), to]
            index = self.at + i * g.shards + d
            self.w.copy(src, self.cut(self.dst.at[g.k], i), index, index, g.s, to).start()

    def finish(self):
        g = self.g
        for i in range(self.pieces):
            for d in range(1, g.shards):
                self.w.recorded(self.like, self.at + i * g.shards + d)
                self.w.arrived(self.cut(self.dst.at[(g.k - d) % g.shards], i), self.at + i * g.shards + d)


def middle_kernel(
    seqs, shards, counts,
    a, slope, n2, fc1, fc2, dense, cot, h2, heads, w2, vec,
    dh2_out, do_out, rc1_out, wd_out, keep_out, give_out, ry_out, small_out,
    a_v, du_v, n2_v, fc1_v, fc2_v, dense_v, cot_v, h2_v, heads_v, own_w2, w1_v, wd_v, mine_v, sent_v, got_v,
    da_v, do_v, do_sent, small_v, rc, ry, rc1,
    send_sems, recv_sems, copy_sems,
):
    g = Geometry(seqs, shards)
    wires = Wires(g, send_sems, recv_sems)
    blocks, half, width = h2_v.shape
    block = half * seqs
    ff = a_v.shape[1]
    ff_part = ff // shards
    rows = width // shards
    part = width // seqs
    local = []

    def bring(src, dst):
        made = pltpu.make_async_copy(src, dst, copy_sems.at[len(local)])
        made.start()
        local.append(made)
        return made

    def at_block(b):
        return pl.ds(pl.multiple_of(b * block, block), block)

    def own_rows(b):
        return pl.ds(pl.multiple_of(b * block + g.s * half, half), half)

    down = Scatter(wires, w2, lambda i, j: own_w2.at[i, j], (rc, ry, None, None))
    up = Scatter(wires, w1_v, lambda i, j: w1_v.at[i, j, g.c], (rc1, None, None, None))
    half_at, do_at = wires.block(blocks), wires.block(blocks)
    first = [bring(cot, cot_v), bring(fc2, fc2_v), bring(slope, du_v), bring(fc1, fc1_v)]
    own = bring(w2.at[:, :, g.c], own_w2)
    later = [bring(n2, n2_v), bring(a, a_v), bring(h2, h2_v), bring(dense, dense_v)]
    later += [bring(heads.at[i, own_rows(b), :], heads_v.at[i, pl.ds(b * half, half)]) for i in range(seqs) for b in range(blocks)]
    enter(g)
    down.core_send()
    for made in first:
        made.wait()
    step = min(512, ff)
    per = step // ff_part

    def half_copy(b):
        return wires.copy(sent_v.at[b], got_v.at[b], half_at + b, half_at + b, 1 - g.s, g.k)

    def do_copy(b):
        return wires.copy(do_sent.at[b], do_v.at[b, g.s], do_at + b, do_at + b, 1 - g.s, g.k)

    small_v[...] = jnp.zeros_like(small_v)

    def split(b, total, keep, give):
        @pl.when(g.s == 0)
        def _():
            keep(total[:half])
            give[b] = total[half:].astype(bf16)

        @pl.when(g.s == 1)
        def _():
            keep(total[half:])
            give[b] = total[:half].astype(bf16)

    def du_step(b, sums):
        at = at_block(b)
        grad = cot_v[at, :]
        total, new = None, []
        for n in range(ff // step):
            cut = slice(n * step, (n + 1) * step)
            weight = fc2_v[n * per : (n + 1) * per].reshape(step, width)
            da = lax.dot_general(grad, weight, (((1,), (1,)), ((), ())), preferred_element_type=f32)
            du = (da * du_v[at, cut].astype(f32)).astype(bf16)
            du_v[at, cut] = du
            new.append(sums[n] + jnp.sum(du.astype(f32), axis=0, keepdims=True))
            weight = fc1_v[:, :, cut].reshape(width, step)
            term = lax.dot_general(du, weight, (((1,), (1,)), ((), ())), preferred_element_type=f32)
            total = term if total is None else total + term

        def keep(value):
            mine_v[b] = value

        split(b, total, keep, sent_v)

        @pl.when(b > 0)
        def _():
            half_copy(b - 1).start()

        @pl.when(b == 0)
        def _():
            own.wait()
            down.core_done()

        return tuple(new)

    zero = jnp.zeros((1, step), f32)
    sums = lax.fori_loop(0, blocks, du_step, (zero,) * (ff // step))
    for made in later:
        made.wait()

    @pl.loop(0, width // (4 * rows))
    def _(m):
        @pl.when(m == 0)
        def _():
            half_copy(blocks - 1).start()

        left = n2_v[:, pl.ds(pl.multiple_of(m * 4 * rows, 128), 4 * rows)]
        for n in range(ff // step):
            cut = slice(n * step, (n + 1) * step)
            out = lax.dot_general(left, du_v[:, cut], (((0,), (0,)), ((), ())), preferred_element_type=f32)
            w1_v[m, :, :, :, cut] = out.astype(bf16).reshape(2, 2, rows, step)

    up.core_send()
    kept = []
    for n in range(ff // step):
        for i in range(per):
            small_v[n * per + i, 6:7, pl.ds(pl.multiple_of(g.s * ff_part, 128), ff_part)] = sums[n][
                :, i * ff_part : (i + 1) * ff_part
            ]

    def norm_step(b, sums):
        gains, biases, branch, cots = sums
        wires.arrived(got_v.at[b], half_at + b)
        grad = mine_v[b] + got_v[b].astype(f32)
        xhat, root = normalize(h2_v[b])
        gains = gains + jnp.sum(grad * xhat, axis=0, keepdims=True)
        biases = biases + jnp.sum(grad, axis=0, keepdims=True)
        cot_b = cot_v[own_rows(b), :].astype(f32)
        cots = cots + jnp.sum(cot_b, axis=0, keepdims=True)
        dh2 = cot_b + norm_pull(grad, vec[4:5, :width], xhat, root)
        mine_v[b] = dh2
        da = dh2.astype(bf16)
        branch = branch + jnp.sum(da.astype(f32), axis=0, keepdims=True)
        da_v[pl.ds(pl.multiple_of(b * half, half), half), :] = da
        grads = [
            lax.dot_general(
                da, dense_v[i * (shards // seqs) : (i + 1) * (shards // seqs)].reshape(part, width),
                (((1,), (1,)), ((), ())), preferred_element_type=f32,
            ).astype(bf16)
            for i in range(seqs)
        ]
        do_v[b, g.s] = jnp.where(g.s == 0, grads[0], grads[1])
        do_sent[b] = jnp.where(g.s == 0, grads[1], grads[0])

        @pl.when(b > 0)
        def _():
            do_copy(b - 1).start()

        return gains, biases, branch, cots

    zero = jnp.zeros((1, width), f32)
    sums = lax.fori_loop(0, blocks, norm_step, (zero,) * 4)
    kept.append(bring(mine_v, dh2_out))
    for row, vector in ((4, sums[0]), (5, sums[1]), (3, sums[2]), (7, sums[3])):
        for j in range(shards):
            small_v[j, row : row + 1, :rows] = vector[:, j * rows : (j + 1) * rows]
    do_copy(blocks - 1).start()
    kept.append(bring(small_v, small_out))

    for i in range(seqs):
        out = lax.dot_general(heads_v[i], da_v[...], (((0,), (0,)), ((), ())), preferred_element_type=f32).astype(bf16)
        wd_v[i * (shards // seqs) : (i + 1) * (shards // seqs)] = out.reshape(shards // seqs, rows, width)
    kept.append(bring(wd_v, wd_out))

    @pl.loop(0, blocks)
    def _(b):
        at = at_block(b)
        total = None
        for n in range(ff // step):
            weight = fc2_v[n * per : (n + 1) * per].reshape(step, width)
            term = jnp.dot(a_v[at, n * step : (n + 1) * step], weight, preferred_element_type=f32)
            total = term if total is None else total + term

        def keep(value):
            h2_v[b] = h2_v[b] + value + vec[7:8, :width]

        split(b, total, keep, got_v)

    kept += [bring(h2_v, keep_out), bring(got_v, give_out)]
    up.core_done()
    kept.append(bring(rc1, rc1_out))
    down.y_done()
    kept.append(bring(ry, ry_out))
    for b in range(blocks):
        wires.arrived(do_v.at[b, 1 - g.s], do_at + b)
    kept.append(bring(do_v, do_out))
    for b in range(blocks):
        half_copy(b).wait_send()
        do_copy(b).wait_send()
    wires.drain()
    for made in kept:
        made.wait()
    assert wires.used <= counts[0] and len(local) <= counts[1]


def middle_exchange(a, slope, n2, fc1, fc2, dense, cot, h2, heads, w2, vec, seqs, shards):
    blocks, half, width = h2.shape
    tokens, ff = a.shape
    part = width // seqs
    rows, ff_part = width // shards, ff // shards
    counts = (32, 40)
    any_, vmem = pl.BlockSpec(memory_space=pl.ANY), pl.BlockSpec(memory_space=pltpu.VMEM)
    own32, own16 = ((blocks, half, width), f32), ((blocks, half, width), bf16)
    do, smalls = ((blocks, seqs, half, part), bf16), ((shards, 8, 256), f32)
    w1, wd, ry = ((shards, rows, ff), bf16), ((shards, rows, width), bf16), ((4, ff_part, width), bf16)
    w1 = ((4, 2, 2, rows, ff), bf16)
    rc1 = ((4, 2, rows, ff), bf16)
    outs = [own32, do, rc1, wd, own32, own16, ry, smalls]
    rc = ((4, 2, ff_part, width), bf16)
    scratch = [(v.shape, bf16) for v in (a, slope, n2, fc1, fc2, dense, cot)] + [
        own32, ((seqs, blocks * half, part), bf16), rc, w1, wd, own32, own16, own16, ((blocks * half, width), bf16), do,
        ((blocks, half, part), bf16), smalls, rc, ry, rc1,
    ]
    return pl.pallas_call(
        functools.partial(middle_kernel, seqs, shards, counts),
        in_specs=[any_] * 10 + [vmem],
        out_specs=[any_] * len(outs),
        out_shape=[jax.ShapeDtypeStruct(s, d) for s, d in outs],
        scratch_shapes=[pltpu.VMEM(s, d) for s, d in scratch]
        + [pltpu.SemaphoreType.DMA((counts[0],)), pltpu.SemaphoreType.DMA((counts[0],)), pltpu.SemaphoreType.DMA((counts[1],))],
        compiler_params=pltpu.CompilerParams(collective_id=3, has_side_effects=True, vmem_limit_bytes=62 * 2**20),
        name="middle_exchange",
    )(a, slope, n2, fc1, fc2, dense, cot, h2, heads, w2.reshape((4, 2, 2) + w2.shape[1:]), vec)


def backward_kernel(
    seqs, shards, counts,
    qkv, do, n1, qkvw, x_all, dh2, keep, give, ry2, rc1, wd, smalls, vec, slopes,
    ret_y, ret_x, o_qkv, o_dense, o_up, o_down, o_small,
    qkv_v, do_v, dqkv_v, n1_v, qkvw_v, x_v, dh2_v, dk_acc, dv_acc, bias_acc, mine_v, sent_v, got_v, dx_v, gq_v,
    small_v, small_got, small_fin, small_last, f_qkv, f_dense, f_up, f_down, keep_v, give_v, y_v, own_wd, idc, idr,
    *rest,
):
    bufs, (send_sems, recv_sems, copy_sems) = rest[:-3], rest[-3:]
    g = Geometry(seqs, shards)
    wires = Wires(g, send_sems, recv_sems)
    pairs, tokens = do_v.shape[0], do_v.shape[1]
    part = pairs * 2 * HEAD
    width = n1_v.shape[1]
    lanes = seqs * shards
    block = ROWS * lanes
    blocks = tokens // block
    half = block // seqs
    tile = bias_acc.shape[2]
    local = []

    def bring(src, dst):
        made = pltpu.make_async_copy(src, dst, copy_sems.at[len(local)])
        made.start()
        local.append(made)
        return made

    def held(ref):
        return lambda i, j: ref.at[i, j]

    down = Scatter(wires, None, None, (None,) + bufs[0:3])
    up = Scatter(wires, None, None, bufs[3:7])
    dense = Scatter(wires, wd, held(own_wd), bufs[7:11])
    qkv_sum = Scatter(wires, gq_v, lambda i, j: gq_v.at[i, j, g.c], bufs[11:15])
    back_y = Back(wires, y_v, ret_y, blocks)
    give_at = wires.block(blocks)
    back_x = Back(wires, dx_v, ret_x, blocks)
    half_at = wires.block(blocks)
    small_at = wires.block(shards + 1)

    rc_in = bring(rc1, up.rc)
    ry_in = bring(ry2, down.ry)
    first = [bring(qkv, qkv_v)] + [bring(do.at[:, pl.ds(h * 2 * HEAD, 2 * HEAD)], do_v.at[h]) for h in range(pairs)]
    owns = [bring(a.at[:, :, g.c], b) for a, b in ((wd, own_wd),)] + [bring(keep, keep_v)]
    later = [
        bring(n1, n1_v), bring(qkvw, qkvw_v), bring(x_all.at[:, pl.ds(g.s * shards, shards)], x_v), bring(dh2, dh2_v),
        bring(smalls, small_v),
    ]
    enter(g)
    idc[...] = blocked_ids(idc.shape, 0, lanes)
    idr[...] = blocked_ids(idr.shape, 1, lanes)
    rc_in.wait()
    up.y_send()
    dense.core_send()
    ry_in.wait()
    down.z_send()
    for b in range(blocks):
        wires.send(give.at[b], give_v.at[b], give_at + b, 1 - g.s, g.k, give.at[b])
    for made in first + owns:
        made.wait()

    lane_id = lax.broadcasted_iota(jnp.int32, (1, 2 * HEAD), 1)

    def attend(h):
        q_ref, k_ref, v_ref, do_ref = qkv_v.at[h], qkv_v.at[pairs + h], qkv_v.at[2 * pairs + h], do_v.at[h]
        dk_acc[...] = jnp.zeros_like(dk_acc)
        dv_acc[...] = jnp.zeros_like(dv_acc)
        for j in range(2):
            bias_acc[j] = jnp.broadcast_to(slopes[g.s * pairs + h, j] * idc[...], bias_acc.shape[1:])
        cols = pl.ds(pl.multiple_of(h * 2 * HEAD, 2 * HEAD), 2 * HEAD)
        for b in range(blocks):
            end = (b + 1) * block
            for t in range(block // tile):
                at = pl.ds(b * block + t * tile, tile)
                q = q_ref[at, :] * jnp.asarray(HEAD**-0.5, bf16)
                grad = do_ref[at, :]
                ids_q = idr[:, at]
                both = None
                for j in range(2):
                    mine = (lane_id // HEAD) == j
                    qj = jnp.where(mine, q, jnp.zeros_like(q))
                    doj = jnp.where(mine, grad, jnp.zeros_like(grad))
                    s = lax.dot_general(
                        k_ref[:end, :], qj, (((1,), (1,)), ((), ())), preferred_element_type=f32
                    )
                    s = s + bias_acc[j, :end, :]
                    tail = attn_mask(s[b * block :, :], idc[b * block : end, :] <= ids_q)
                    s = jnp.concatenate([s[: b * block, :], tail], axis=0) if b else tail
                    top = jnp.max(s, axis=0, keepdims=True)
                    e = jnp.exp(s - top)
                    probs = e * (1.0 / jnp.sum(e, axis=0, keepdims=True))
                    dv_acc[:end, :] += jnp.dot(probs.astype(bf16), doj, preferred_element_type=f32)
                    dp = lax.dot_general(
                        v_ref[:end, :], doj, (((1,), (1,)), ((), ())), preferred_element_type=f32
                    )
                    inner = jnp.sum(probs * dp, axis=0, keepdims=True)
                    ds = (probs * (dp - inner)).astype(bf16)
                    dk_acc[:end, :] += jnp.dot(ds, qj, preferred_element_type=f32)
                    dq = lax.dot_general(
                        ds, k_ref[:end, :], (((0,), (0,)), ((), ())), preferred_element_type=f32
                    )
                    both = dq if both is None else jnp.where(mine, dq, both)
                dqkv_v[0, at, cols] = (both * (HEAD**-0.5)).astype(bf16)
        dqkv_v[1, :, cols] = dk_acc[...].astype(bf16)
        dqkv_v[2, :, cols] = dv_acc[...].astype(bf16)

    @pl.loop(0, pairs)
    def _(h):
        attend(h)

        @pl.when(h == 0)
        def _():
            dense.core_done()

        @pl.when(h == 2)
        def _():
            down.z_done()

        @pl.loop(blocks * h // pairs, blocks * (h + 1) // pairs)
        def _(b):
            wires.arrived(give_v.at[b], give_at + b)
            y_v[b] = (keep_v[b] + give_v[b].astype(f32)).reshape(shards, ROWS, width).astype(bf16)
            back_y.send(b)

    for made in later:
        made.wait()

    rows = width // shards

    @pl.loop(0, blocks)
    def _(m):
        cut = n1_v[:, pl.ds(pl.multiple_of(m * block, block), block)]
        for p in range(3):
            out = lax.dot_general(cut, dqkv_v[p], (((0,), (0,)), ((), ())), preferred_element_type=f32).astype(bf16)
            out = out.reshape(block // rows // 2, 2, rows, part)
            for i in range(block // rows // 2):
                at = m * (block // rows // 2) + i
                for j in range(2):
                    gq_v[at // 2, at % 2, j, :, p * part : (p + 1) * part] = out[i, j]

    qkv_sum.core_send()

    def half_copy(b):
        return wires.copy(sent_v.at[b], got_v.at[b], half_at + b, half_at + b, 1 - g.s, g.k)

    @pl.loop(0, blocks)
    def _(b):
        total = None
        for p in range(3):
            weight = qkvw_v[:, :, p * part : (p + 1) * part].reshape(width, part)
            term = lax.dot_general(
                dqkv_v[p, pl.ds(pl.multiple_of(b * block, block), block), :], weight, (((1,), (1,)), ((), ())),
                preferred_element_type=f32,
            )
            total = term if total is None else total + term

        @pl.when(g.s == 0)
        def _():
            mine_v[b] = total[:half]
            sent_v[b] = total[half:].astype(bf16)

        @pl.when(g.s == 1)
        def _():
            mine_v[b] = total[half:]
            sent_v[b] = total[:half].astype(bf16)

        @pl.when(b == 2)
        def _():
            up.y_done()
            up.z_send()

        @pl.when(b > 0)
        def _():
            half_copy(b - 1).start()

    own_y = bring(y_v.at[:, g.k], ret_y.at[g.k])
    half_copy(blocks - 1).start()

    sums = [jnp.sum(dqkv_v[p].astype(f32), axis=0, keepdims=True) for p in (0, 2)]
    per = 2 * width // shards
    for i in range(part // per):
        for half_no in range(2):
            small_v[(half_no * width + g.s * part) // per + i, 2:3, :per] = sums[half_no][:, i * per : (i + 1) * per]
    qkv_sum.core_done()
    dense.y_done()
    dense.z_send()

    def norm_step(b, sums):
        wires.arrived(got_v.at[b], half_at + b)
        grad = mine_v[b] + got_v[b].astype(f32)
        xhat, root = normalize(x_v[b].astype(f32).reshape(half, width))
        gains = sums[0] + jnp.sum(grad * xhat, axis=0, keepdims=True)
        biases = sums[1] + jnp.sum(grad, axis=0, keepdims=True)
        dx = dh2_v[b] + norm_pull(grad, vec[0:1, :width], xhat, root)
        dx_v[b] = dx.reshape(shards, ROWS, width).astype(bf16)
        back_x.send(b)

        @pl.when(b == 0)
        def _():
            up.z_done()

        @pl.when(b == 2)
        def _():
            qkv_sum.y_done()
            qkv_sum.z_send()

        return gains, biases

    gains, biases = lax.fori_loop(0, blocks, norm_step, (jnp.zeros((1, width), f32),) * 2)
    for j in range(shards):
        small_v[j, 0:1, :rows] = gains[:, j * rows : (j + 1) * rows]
        small_v[j, 1:2, :rows] = biases[:, j * rows : (j + 1) * rows]
    kept = [own_y, bring(dx_v.at[:, g.k], ret_x.at[g.k])]
    for d in range(1, shards):
        to = (g.k + d) % shards
        wires.send(small_v.at[to], small_got.at[g.k], small_at + d, g.s, to, small_v.at[0])
    small_got[g.k] = small_v[g.k]
    down.final()
    dense.z_done()
    up.final()
    qkv_sum.z_done()
    for d in range(1, shards):
        wires.arrived(small_got.at[(g.k - d) % shards], small_at + d)
    small_fin[0] = jnp.sum(small_got[...], axis=0)
    wires.send(small_fin.at[0], small_fin.at[1], small_at + shards, 1 - g.s, g.k, small_fin.at[0])
    dense.final()

    down.done()
    ff_part = f_down.shape[0] // seqs
    for i, at in ((0, g.s), (1, 1 - g.s)):
        f_down[pl.ds(pl.multiple_of(at * ff_part, ff_part), ff_part), :] = down.fin[i].astype(f32)
    kept.append(bring(f_down, o_down))
    up.done()
    for i, at in ((0, g.s), (1, 1 - g.s)):
        for j in range(shards):
            f_up[:, pl.ds(pl.multiple_of((j * seqs + at) * ff_part, 128), ff_part)] = up.fin[
                i, :, j * ff_part : (j + 1) * ff_part
            ].astype(f32)
    kept.append(bring(f_up, o_up))
    dense.done()
    f_dense[...] = dense.fin[0].astype(f32) + dense.fin[1].astype(f32)
    kept.append(bring(f_dense, o_dense))
    wires.arrived(small_fin.at[1], small_at + shards)
    small_last[...] = small_fin[0] + small_fin[1]
    kept.append(bring(small_last, o_small))
    qkv_sum.final()
    qkv_sum.done()
    for i, at in ((0, g.s), (1, 1 - g.s)):
        for p in range(3):
            f_qkv[:, pl.ds(pl.multiple_of(p * width + at * part, 128), part)] = qkv_sum.fin[
                i, :, p * part : (p + 1) * part
            ].astype(f32)
    kept.append(bring(f_qkv, o_qkv))
    back_y.finish()
    back_x.finish()
    for b in range(blocks):
        half_copy(b).wait_send()
    wires.drain()
    for made in kept:
        made.wait()
    assert wires.used <= counts[0] and len(local) <= counts[1]


def backward_exchange(
    qkv, do, n1, qkvw, x_all, dh2, keep, give, ry2, rc1, wd, smalls, vec, slopes, seqs, shards
):
    tokens, part = do.shape
    width = n1.shape[1]
    pairs = part // (2 * HEAD)
    lanes = seqs * shards
    block = ROWS * lanes
    blocks, half = tokens // block, block // seqs
    tile = min(256, block)
    rows, ff = width // shards, rc1.shape[3]
    ff_part = ff // shards
    counts = (256, 48)
    cut = lambda a: a.reshape((4, 2, 2) + a.shape[1:])
    any_, vmem = pl.BlockSpec(memory_space=pl.ANY), pl.BlockSpec(memory_space=pltpu.VMEM)
    ret = (shards, blocks, ROWS, width)
    outs = [
        (ret, bf16), (ret, bf16), ((rows, 3 * width), f32), ((rows, width), f32), ((rows, seqs * ff), f32),
        ((seqs * ff_part, width), f32), (smalls.shape[1:], f32),
    ]
    blks = [(ff_part, width), (rows, ff), (rows, width), (rows, 3 * part)]
    scratch = [
        ((3 * pairs, tokens, 2 * HEAD), bf16), ((pairs, tokens, 2 * HEAD), bf16), ((3, tokens, part), bf16),
        ((tokens, width), bf16), ((shards, rows, 3 * part), bf16), ((blocks, shards, ROWS, width), bf16),
        ((blocks, half, width), f32), ((tokens, 2 * HEAD), f32), ((tokens, 2 * HEAD), f32), ((2, tokens, tile), f32),
        ((blocks, half, width), f32), ((blocks, half, width), bf16), ((blocks, half, width), bf16),
        ((blocks, shards, ROWS, width), bf16), ((4, 2, 2) + blks[3], bf16), (smalls.shape, f32), (smalls.shape, f32),
        ((2,) + smalls.shape[1:], f32), (smalls.shape[1:], f32), ((rows, 3 * width), f32), ((rows, width), f32), ((rows, seqs * ff), f32),
        ((seqs * ff_part, width), f32), ((blocks, half, width), f32), ((blocks, half, width), bf16),
        ((blocks, shards, ROWS, width), bf16), ((4, 2) + blks[2], bf16),
        ((tokens, 1), f32), ((1, tokens), f32),
    ]
    for blk in blks:
        scratch += [((4, 2) + blk, bf16)] * (blk is not blks[0])
        scratch += [((4,) + blk, bf16), ((4,) + blk, bf16), ((2,) + blk, bf16)]
    return pl.pallas_call(
        functools.partial(backward_kernel, seqs, shards, counts),
        in_specs=[any_] * 12 + [vmem, pl.BlockSpec(memory_space=pltpu.SMEM)],
        out_specs=[any_] * len(outs),
        out_shape=[jax.ShapeDtypeStruct(s, d) for s, d in outs],
        scratch_shapes=[pltpu.VMEM(s, d) for s, d in scratch]
        + [pltpu.SemaphoreType.DMA((counts[0],)), pltpu.SemaphoreType.DMA((counts[0],)), pltpu.SemaphoreType.DMA((counts[1],))],
        compiler_params=pltpu.CompilerParams(collective_id=2, has_side_effects=True, vmem_limit_bytes=60 * 2**20),
        name="backward_exchange",
    )(
        qkv, do, n1, qkvw, x_all, dh2, keep, give, ry2, rc1, cut(wd), smalls, vec, slopes,
    )


def layout_tables(lengths, lane_count, group_count, per_group):
    seq_rows = lengths // lane_count
    row_start = jnp.cumsum(seq_rows) - seq_rows
    slot_rows = seq_rows.reshape(group_count, per_group)
    slot_start = row_start.reshape(group_count, per_group)
    slot_before = jnp.cumsum(slot_rows, axis=1) - slot_rows
    return seq_rows, row_start, slot_rows, slot_start, slot_before


def per_device(
    tokens, cotangent, lengths, first_gain, first_bias, qkv_weight, qv_bias, dense_weight, dense_bias,
    second_gain, second_bias, fc1_weight, fc1_bias, fc2_weight, fc2_bias,
):
    shards, seqs = lax.axis_size("shard"), lax.axis_size("seq")
    lanes = shards * seqs
    slots, width = tokens.shape[1], tokens.shape[2]
    rows = slots // shards
    blocks = rows // ROWS

    smalls_in = (first_gain, first_bias, qv_bias, dense_bias, second_gain, second_bias, fc1_bias, fc2_bias)
    small = jnp.stack([jnp.pad(a.astype(f32), (0, 256 - a.shape[0])) for a in smalls_in])
    slopes = jnp.asarray(np.exp2(-8.0 * (np.arange(HEADS) + 1.0) / HEADS).reshape(-1, 2), f32)

    seq_rows = lengths // lanes
    number = jnp.arange(shards, dtype=jnp.int32)
    row_start = jnp.sum(jnp.where(number[None, :] < number[:, None], seq_rows[None, :], 0), axis=1)
    window = (row_start[:, None] + jnp.arange(rows, dtype=jnp.int32)[None, :]).reshape(-1)

    def pack(source):
        return jnp.take(source, window, axis=0, mode="clip").reshape(shards, blocks, ROWS, width)

    (
        x_all, cot_all, normed_one, normed_two, full_qkv, full_dense, full_up, full_down, qkv, mixed, resid, activ, slope,
        grad_down, vectors,
    ) = forward_exchange(
        pack(tokens[0]), pack(cotangent[0]), qkv_weight, small, dense_weight, fc1_weight, fc2_weight,
        slopes, lengths, seqs, shards,
    )
    grad_resid, grad_mixed, grad_up, grad_dense, keep, give, half_sums, small_grads = middle_exchange(
        activ, slope, normed_two, full_up, full_down, full_dense, cot_all, resid, mixed, grad_down, vectors, seqs, shards
    )
    ret_out, ret_grad, g_qkv, g_dense, g_up, g_down, g_small = backward_exchange(
        qkv, grad_mixed.reshape(slots * seqs, width // seqs), normed_one, full_qkv, x_all, grad_resid, keep, give, half_sums,
        grad_up, grad_dense, small_grads, vectors, slopes, seqs, shards,
    )

    row_here = jnp.arange(slots, dtype=jnp.int32)[:, None]
    inside = (row_here >= row_start[None]) & (row_here < (row_start + seq_rows)[None])
    fetch = jnp.sum(jnp.where(inside, number[None] * rows + row_here - row_start[None], 0), axis=1)
    fetch_live = jnp.arange(slots, dtype=jnp.int32) < jnp.sum(seq_rows)

    def to_stream(got):
        taken = jnp.take(got.reshape(-1, width), fetch, axis=0, mode="clip")
        return jnp.where(fetch_live[:, None], taken, jnp.zeros_like(taken))[None]

    vectors_out = tuple(g_small[i, : a.shape[0]] for i, a in enumerate(smalls_in))
    g_gain_one, g_bias_one, g_qv, g_bdense, g_gain_two, g_bias_two, g_bup, g_bdown = vectors_out
    return (
        to_stream(ret_out), to_stream(ret_grad),
        g_gain_one, g_bias_one, g_qkv, g_qv, g_dense, g_bdense, g_gain_two, g_bias_two, g_up, g_bup, g_down, g_bdown,
    )


def per_device_any(
    tokens, cotangent, lengths, first_gain, first_bias, qkv_weight, qv_bias, dense_weight, dense_bias,
    second_gain, second_bias, fc1_weight, fc1_bias, fc2_weight, fc2_bias,
):
    shards, seqs = lax.axis_size("shard"), lax.axis_size("seq")
    lanes = shards * seqs
    slots, width = tokens.shape[1], tokens.shape[2]
    rows = slots // shards
    cap = slots * seqs
    per_group = lengths.shape[0] // shards
    hidden_units = fc1_weight.shape[1]
    me, group = lax.axis_index("seq"), lax.axis_index("shard")
    blocks = rows // ROWS
    heads = width // HEAD // seqs
    part = heads * HEAD
    ff_part = hidden_units // shards // seqs

    qkv_half = take(qkv_weight.reshape(-1, 3, seqs, part), me, 2).reshape(-1, 3 * part)
    fc1_half = take(fc1_weight.reshape(-1, shards, seqs, ff_part), me, 2).reshape(-1, shards * ff_part)
    fc2_half = take(fc2_weight.reshape(seqs, ff_part, width), me, 0)
    small = jnp.concatenate(
        [first_gain, first_bias, qv_bias, dense_bias, second_gain, second_bias, fc1_bias, fc2_bias]
    )
    small_rows = -(-small.shape[0] // (3 * part))
    small_rows += -small_rows % 16
    small = jnp.pad(small, (0, small_rows * 3 * part - small.shape[0])).reshape(small_rows, 3 * part)
    gather = lambda a: lax.all_gather(a, "shard", axis=0, tiled=False)
    qkv_small = gather(jnp.concatenate([qkv_half, small], axis=0))
    own_rows = qkv_half.shape[0]
    full_qkv = qkv_small[:, :own_rows].reshape(width, 3 * part)
    smalls = qkv_small[:, own_rows:].reshape(shards, -1).astype(f32)
    full_dense = gather(dense_weight).reshape(width, width)
    full_up = gather(fc1_half).reshape(width, shards * ff_part)
    full_down = gather(fc2_half).reshape(shards * ff_part, width)
    cuts, at = [], 0
    for a in (first_gain, first_bias, qv_bias, dense_bias, second_gain, second_bias, fc1_bias, fc2_bias):
        cuts.append(smalls[:, at : at + a.shape[0]].reshape(-1))
        at += a.shape[0]
    gain_one, bias_one, bias_qv, bias_dense, gain_two, bias_two, bias_up, bias_down = cuts
    bias_q, bias_v = (take(bias_qv[i * width : (i + 1) * width].reshape(seqs, part), me) for i in (0, 1))
    bias_all = jnp.concatenate([bias_q, jnp.zeros_like(bias_q), bias_v])
    bias_up = take(bias_up.reshape(shards, seqs, ff_part), me, 1).reshape(-1)

    seq_rows, row_start, slot_rows, slot_start, slot_before = layout_tables(lengths, lanes, shards, per_group)
    row_in = jnp.arange(rows, dtype=jnp.int32)[None, :, None]
    inside = ((row_in >= slot_before[:, None]) & (row_in < (slot_before + slot_rows)[:, None])).astype(jnp.int32)
    send_live = jnp.sum(inside, axis=2) > 0
    send_row = jnp.sum(inside * (slot_start[:, None] + row_in - slot_before[:, None]), axis=2).reshape(-1)

    def to_groups(source):
        packed = jnp.take(source, send_row, axis=0).reshape(shards, rows, width)
        packed = jnp.where(send_live[:, :, None], packed, jnp.zeros_like(packed))
        got = lax.all_to_all(packed, "shard", split_axis=0, concat_axis=0, tiled=True)
        own = got.reshape(shards, blocks, ROWS, width).transpose(1, 0, 2, 3).reshape(blocks, -1, width)
        return own, seq_gather(own, 1).reshape(cap, width)

    x_own, x_low = to_groups(tokens[0])
    cot_own, cot_low = to_groups(cotangent[0])

    def own_part(whole):
        return take(whole.reshape(blocks, seqs, -1, whole.shape[-1]), me, 1)

    place = jnp.arange(cap, dtype=jnp.int32)
    block_of, in_block = place // (ROWS * lanes), place % (ROWS * lanes)
    row_of = block_of * ROWS + in_block % ROWS
    ids = row_of * lanes + in_block // ROWS
    own_before, own_count = take(slot_before, group), take(slot_rows, group)
    holds = (row_of[:, None] >= own_before[None]) & (row_of[:, None] < (own_before + own_count)[None])
    begin_row = jnp.sum(jnp.where(holds, own_before[None], 0), axis=1)
    begins = jnp.where(jnp.any(holds, axis=1), begin_row * lanes, ids)
    ids, begins = ids.astype(f32), begins.astype(f32)
    head_ids = me * heads + jnp.arange(heads, dtype=jnp.int32)
    slopes = 2.0 ** (-8.0 * (head_ids.astype(f32) + 1.0) / HEADS)
    one_seq = per_group == 1

    hidden = x_low.astype(f32)
    xhat_one, _ = normalize(hidden)
    normed_one = (xhat_one * gain_one + bias_one).astype(bf16)
    qkv = (jnp.dot(normed_one, full_qkv, preferred_element_type=f32) + bias_all).astype(bf16)
    mixed = attention_forward(qkv, slopes, ids, begins, lanes, one_seq)
    mixed_all = seq_gather(mixed, 1).reshape(cap, width)
    branch = jnp.dot(mixed_all, full_dense, preferred_element_type=f32) + bias_dense
    resid = hidden + branch
    xhat_two, _ = normalize(resid)
    normed_two = (xhat_two * gain_two + bias_two).astype(bf16)
    upper = jnp.dot(normed_two, full_up, preferred_element_type=f32) + bias_up
    activ = gelu_tanh(upper).astype(bf16)
    down = jnp.dot(activ, full_down, preferred_element_type=f32)
    resid_own = own_part(resid)
    down_own = seq_sum(down.reshape(blocks, seqs, -1, width), 1)
    block_out = (resid_own + down_own + bias_down).astype(bf16)

    grad_down = jnp.dot(activ.T, cot_low, preferred_element_type=f32).astype(bf16)
    grad_activ = jnp.dot(cot_low, full_down.T, preferred_element_type=f32)
    grad_upper = jax.vjp(gelu_tanh, upper)[1](grad_activ)[0].astype(bf16)
    grad_up = jnp.dot(normed_two.T, grad_upper, preferred_element_type=f32).astype(bf16)
    grad_bup = jnp.sum(grad_upper.astype(f32), axis=0)
    grad_normed = jnp.dot(grad_upper, full_up.T, preferred_element_type=f32)
    grad_normed = seq_sum(grad_normed.reshape(blocks, seqs, -1, width), 1).reshape(slots, width)
    cot_full = cot_own.reshape(slots, width).astype(f32)
    grad_bdown = jnp.sum(cot_full, axis=0)
    xhat_two, root_two = normalize(resid_own.reshape(slots, width))
    grad_gain_two = jnp.sum(grad_normed * xhat_two, axis=0)
    grad_bias_two = jnp.sum(grad_normed, axis=0)
    grad_resid = cot_full + norm_pull(grad_normed, gain_two, xhat_two, root_two)

    grad_branch = grad_resid.astype(bf16)
    grad_dense = jnp.dot(own_part(mixed_all).reshape(slots, width).T, grad_branch, preferred_element_type=f32).astype(bf16)
    grad_bdense = jnp.sum(grad_branch.astype(f32), axis=0)
    grad_mixed = jnp.dot(grad_branch, full_dense.T, preferred_element_type=f32).astype(bf16)
    got = seq_blocks(grad_mixed.reshape(blocks, -1, seqs, part), 2, bf16)
    if seqs == 2:
        grad_mixed = jnp.where(me == 0, jnp.stack(got, 1), jnp.stack(got[::-1], 1))
    else:
        grad_mixed = jnp.zeros((blocks, seqs) + got[0].shape[1:], bf16)
        for d, g in enumerate(got):
            grad_mixed = lax.dynamic_update_index_in_dim(grad_mixed, g, (me - d) % seqs, 1)
    grad_mixed = grad_mixed.reshape(cap, part)
    planes = qkv.reshape(cap, -1, 2 * HEAD).transpose(1, 0, 2)
    grad_proj = jnp.concatenate(
        attention_backward(planes, grad_mixed, slopes, ids, begins, lanes, one_seq), axis=1
    )
    grad_qkv = jnp.dot(normed_one.T, grad_proj, preferred_element_type=f32).astype(bf16)
    proj_sums = jnp.sum(grad_proj.astype(f32), axis=0)
    grad_one = jnp.dot(grad_proj, full_qkv.T, preferred_element_type=f32)
    grad_one = seq_sum(grad_one.reshape(blocks, seqs, -1, width), 1).reshape(slots, width)
    xhat_one, root_one = normalize(x_own.reshape(slots, width).astype(f32))
    grad_gain_one = jnp.sum(grad_one * xhat_one, axis=0)
    grad_bias_one = jnp.sum(grad_one, axis=0)
    tokens_grad = (grad_resid + norm_pull(grad_one, gain_one, xhat_one, root_one)).astype(bf16)

    row_here = jnp.arange(slots, dtype=jnp.int32)[:, None]
    seq_in = ((row_here >= row_start[None]) & (row_here < (row_start + seq_rows)[None])).astype(jnp.int32)
    home = jnp.arange(lengths.shape[0], dtype=jnp.int32) // per_group
    fetch = jnp.sum(seq_in * (home[None] * rows + slot_before.reshape(-1)[None] + row_here - row_start[None]), axis=1)
    fetch_live = jnp.sum(seq_in, axis=1) > 0

    def to_stream(own):
        sent = own.reshape(blocks, shards, ROWS, width).transpose(1, 0, 2, 3).reshape(shards, rows, width)
        got = lax.all_to_all(sent, "shard", split_axis=0, concat_axis=0, tiled=True)
        taken = jnp.take(got.reshape(-1, width), fetch, axis=0)
        return jnp.where(fetch_live[:, None], taken, jnp.zeros_like(taken))[None]

    down_block = shard_reduce(grad_down.reshape(shards, ff_part, width), bf16)
    up_block = shard_reduce(grad_up.reshape(shards, -1, shards * ff_part), bf16)
    dense_block = shard_reduce(grad_dense.reshape(shards, -1, width), bf16)
    qkv_block = shard_reduce(grad_qkv.reshape(shards, -1, 3 * part), bf16)

    def spread(vector, index_shape):
        zero = jnp.zeros(index_shape, f32)
        return lax.dynamic_update_index_in_dim(zero, vector, me, 1)

    sums = proj_sums.reshape(3, part)
    qv = spread(jnp.stack([sums[0], sums[2]]), (2, seqs, part)).reshape(shards, -1)
    bup = spread(grad_bup.reshape(shards, ff_part), (shards, seqs, ff_part)).reshape(shards, -1)
    rest = (grad_gain_one, grad_bias_one, grad_bdense, grad_gain_two, grad_bias_two, grad_bdown)
    packed = jnp.concatenate([a.reshape(shards, -1) for a in rest] + [qv, bup], axis=1)
    packed = shard_reduce(packed, f32)
    packed = jnp.sum(seq_gather(packed, 0), axis=0)
    cuts, at = [], 0
    for a in [a.reshape(shards, -1) for a in rest] + [qv, bup]:
        cuts.append(packed[at : at + a.shape[1]])
        at += a.shape[1]
    g_gain_one, g_bias_one, g_bdense, g_gain_two, g_bias_two, g_bdown, g_qv, g_bup = cuts

    g_dense = jnp.sum(seq_gather(dense_block.astype(bf16), 0).astype(f32), axis=0)
    g_qkv = seq_gather(qkv_block.astype(bf16).reshape(-1, 3, part), 2).reshape(-1, 3 * width).astype(f32)
    g_up = seq_gather(up_block.astype(bf16).reshape(-1, shards, ff_part), 2).reshape(-1, hidden_units).astype(f32)
    g_down = seq_gather(down_block.astype(bf16), 0).reshape(-1, width).astype(f32)
    return (
        to_stream(block_out), to_stream(tokens_grad.reshape(blocks, -1, width)),
        g_gain_one, g_bias_one, g_qkv, g_qv, g_dense, g_bdense, g_gain_two, g_bias_two, g_up, g_bup, g_down, g_bdown,
    )


def choose(*arguments):
    one = arguments[2].shape[0] == lax.axis_size("shard")
    fused = one and lax.axis_size("seq") == 2 and shard_factors(lax.axis_size("shard")) == (4, 2, 2)
    return (per_device if fused else per_device_any)(*arguments)


def solution(mesh):
    rows, vector, stream = P("shard", None), P("shard"), P(("seq", "shard"), None, None)
    params = (vector, vector, rows, vector, rows, vector, vector, vector, rows, vector, rows, vector)
    return jax.shard_map(
        choose, mesh=mesh, in_specs=(stream, stream, P()) + params, out_specs=(stream, stream) + params, check_vma=False
    )
```

```python
import functools

import jax
import jax.numpy as jnp
import numpy as np
from jax import lax
from jax.experimental import pallas as pl
from jax.experimental.pallas import tpu as pltpu
from jax.sharding import PartitionSpec as P

HEADS = 16
HEAD = 64
ROWS = 8

epsilon = 1e-05
masked_score = -1e30
f32 = jnp.float32
bf16 = jnp.bfloat16


def gelu_tanh(values):
    return (
        0.5
        * values
        * (1.0 + jnp.tanh(0.7978845608028654 * (values + 0.044715 * values * values * values)))
    )


def normalize(hidden):
    center = hidden - jnp.mean(hidden, axis=-1, keepdims=True)
    spread = jnp.mean(center * center, axis=-1, keepdims=True)
    root = lax.rsqrt(spread + epsilon)
    return center * root, root


def norm_pull(grad, gain, xhat, root):
    scaled = grad * gain
    return root * (
        scaled
        - jnp.mean(scaled, axis=-1, keepdims=True)
        - xhat * jnp.mean(scaled * xhat, axis=-1, keepdims=True)
    )


def slot_ids(first, count, lanes):
    place = first + lax.broadcasted_iota(jnp.int32, (count, 1), 0)
    block, inside = place // (ROWS * lanes), place % (ROWS * lanes)
    return (block * ROWS + inside % ROWS) * lanes + inside // ROWS


def blocked_ids(shape, axis, lanes):
    place = lax.broadcasted_iota(jnp.int32, shape, axis)
    high = (ROWS * lanes).bit_length() - 1
    inside = place & (ROWS * lanes - 1)
    row = (place >> high) * ROWS + (inside & (ROWS - 1))
    return (row * lanes + (inside >> (ROWS.bit_length() - 1))).astype(f32)


def attn_mask(scored, allowed):
    return jnp.where(allowed, scored, masked_score)


def attn_fwd_kernel(lanes, tile, one_seq, slope_ref, idc_ref, idr_ref, beginc_ref, q_ref, k_ref, v_ref, o_ref):
    tokens = q_ref.shape[0]
    block = ROWS * lanes
    lane_id = lax.broadcasted_iota(jnp.int32, (1, 2 * HEAD), 1)
    for b in range(tokens // block):
        end = (b + 1) * block

        def step(t, _):
            at = pl.ds(pl.multiple_of(b * block + t * tile, tile), tile)
            q = q_ref[at, :] * jnp.asarray(HEAD**-0.5, bf16)
            ids_q = idc_ref[at, :]
            both = None
            for j in range(2):
                mine = (lane_id // HEAD) == j
                qj = jnp.where(mine, q, jnp.zeros_like(q))
                s = lax.dot_general(
                    qj, k_ref[:end, :], (((1,), (1,)), ((), ())), preferred_element_type=f32
                )
                s = s + slope_ref[0, 0, j] * idr_ref[:, :end]
                if one_seq:
                    own = s[:, b * block :]
                    own = attn_mask(own, idr_ref[:, b * block : end] <= ids_q)
                    s = jnp.concatenate([s[:, : b * block], own], axis=1) if b else own
                else:
                    ids_k = idr_ref[:, :end]
                    s = attn_mask(s, (ids_k <= ids_q) & (ids_k >= beginc_ref[at, :]))
                top = jnp.max(s, axis=1, keepdims=True)
                e = jnp.exp(s - top)
                total = jnp.sum(e, axis=1, keepdims=True)
                o = jnp.dot(e.astype(bf16), v_ref[:end, :], preferred_element_type=f32) / total
                both = o if both is None else jnp.where(mine, o, both)
            o_ref[at, :] = both.astype(bf16)
            return 0

        lax.fori_loop(0, block // tile, step, 0)


def attn_bwd_kernel(
    lanes, tile, one_seq, slope_ref, idc_ref, idr_ref, beginr_ref, q_ref, k_ref, v_ref, do_ref,
    dq_ref, dk_ref, dv_ref, dk_acc, dv_acc, bias_acc,
):
    tokens = q_ref.shape[0]
    block = ROWS * lanes
    lane_id = lax.broadcasted_iota(jnp.int32, (1, 2 * HEAD), 1)
    dk_acc[...] = jnp.zeros_like(dk_acc)
    dv_acc[...] = jnp.zeros_like(dv_acc)
    for j in range(2):
        bias_acc[j] = jnp.broadcast_to(slope_ref[0, 0, j] * idc_ref[...], (tokens, tile))
    for b in range(tokens // block):
        end = (b + 1) * block

        def step(t, _):
            at = pl.ds(pl.multiple_of(b * block + t * tile, tile), tile)
            q = q_ref[at, :] * jnp.asarray(HEAD**-0.5, bf16)
            do = do_ref[at, :]
            ids_q = idr_ref[:, at]
            both = None
            for j in range(2):
                mine = (lane_id // HEAD) == j
                qj = jnp.where(mine, q, jnp.zeros_like(q))
                doj = jnp.where(mine, do, jnp.zeros_like(do))
                s = lax.dot_general(
                    k_ref[:end, :], qj, (((1,), (1,)), ((), ())), preferred_element_type=f32
                )
                s = s + bias_acc[j, :end, :]
                if one_seq:
                    own = s[b * block :, :]
                    own = attn_mask(own, idc_ref[b * block : end, :] <= ids_q)
                    s = jnp.concatenate([s[: b * block, :], own], axis=0) if b else own
                else:
                    ids_k = idc_ref[:end, :]
                    s = attn_mask(s, (ids_k <= ids_q) & (ids_k >= beginr_ref[:, at]))
                top = jnp.max(s, axis=0, keepdims=True)
                e = jnp.exp(s - top)
                probs = e * (1.0 / jnp.sum(e, axis=0, keepdims=True))
                dv_acc[:end, :] += jnp.dot(probs.astype(bf16), doj, preferred_element_type=f32)
                dp = lax.dot_general(
                    v_ref[:end, :], doj, (((1,), (1,)), ((), ())), preferred_element_type=f32
                )
                inner = jnp.sum(probs * dp, axis=0, keepdims=True)
                ds = (probs * (dp - inner)).astype(bf16)
                dk_acc[:end, :] += jnp.dot(ds, qj, preferred_element_type=f32)
                dq = lax.dot_general(
                    ds, k_ref[:end, :], (((0,), (0,)), ((), ())), preferred_element_type=f32
                )
                both = dq if both is None else jnp.where(mine, dq, both)
            dq_ref[at, :] = (both * (HEAD**-0.5)).astype(bf16)
            return 0

        lax.fori_loop(0, block // tile, step, 0)
    dk_ref[...] = dk_acc[...].astype(bf16)
    dv_ref[...] = dv_acc[...].astype(bf16)


def attn_shape(tokens, width, lanes):
    pairs = width // (2 * HEAD)
    tile = min(256, ROWS * lanes)
    return pairs, tile


def attention_forward(qkv, slopes, ids, begins, lanes, one_seq):
    tokens, width = qkv.shape[0], qkv.shape[1] // 3
    pairs, tile = attn_shape(tokens, width, lanes)
    column = lambda part: pl.BlockSpec((tokens, 2 * HEAD), lambda h, part=part: (0, part * pairs + h))
    whole = lambda a: pl.BlockSpec(a.shape, lambda h: (0, 0))
    idc, idr, beginc = ids[:, None], ids[None, :], begins[:, None]
    half = tokens * tokens * 5 // 8
    return pl.pallas_call(
        functools.partial(attn_fwd_kernel, lanes, tile, one_seq),
        grid=(pairs,),
        in_specs=[
            pl.BlockSpec((1, 1, 2), lambda h: (h, 0, 0), memory_space=pltpu.SMEM),
            whole(idc), whole(idr), whole(beginc), column(0), column(1), column(2),
        ],
        out_specs=pl.BlockSpec((tokens, 2 * HEAD), lambda h: (0, h)),
        out_shape=jax.ShapeDtypeStruct((tokens, width), bf16),
        compiler_params=pltpu.CompilerParams(vmem_limit_bytes=48 * 2**20),
        cost_estimate=pl.CostEstimate(
            flops=8 * pairs * half * HEAD * 2, transcendentals=2 * pairs * half, bytes_accessed=8 * tokens * width
        ),
        name="attention_forward",
    )(slopes.reshape(pairs, 1, 2), idc, idr, beginc, qkv, qkv, qkv)


def attention_backward(qkv, grad_out, slopes, ids, begins, lanes, one_seq):
    tokens, width = grad_out.shape
    pairs, tile = attn_shape(tokens, width, lanes)
    column = lambda part: pl.BlockSpec((tokens, 2 * HEAD), lambda h, part=part: (0, part * pairs + h))
    whole = lambda a: pl.BlockSpec(a.shape, lambda h: (0, 0))
    idc, idr, beginr = ids[:, None], ids[None, :], begins[None, :]
    plane = lambda part: pl.BlockSpec((None, tokens, 2 * HEAD), lambda h, part=part: (part * pairs + h, 0, 0))
    out = jax.ShapeDtypeStruct((tokens, width), bf16)
    half = tokens * tokens * 5 // 8
    return pl.pallas_call(
        functools.partial(attn_bwd_kernel, lanes, tile, one_seq),
        grid=(pairs,),
        in_specs=[
            pl.BlockSpec((1, 1, 2), lambda h: (h, 0, 0), memory_space=pltpu.SMEM),
            whole(idc), whole(idr), whole(beginr), plane(0), plane(1), plane(2), column(0),
        ],
        out_specs=[column(0)] * 3,
        out_shape=[out] * 3,
        scratch_shapes=[
            pltpu.VMEM((tokens, 2 * HEAD), f32), pltpu.VMEM((tokens, 2 * HEAD), f32), pltpu.VMEM((2, tokens, tile), f32),
        ],
        compiler_params=pltpu.CompilerParams(vmem_limit_bytes=56 * 2**20),
        cost_estimate=pl.CostEstimate(
            flops=20 * pairs * half * HEAD * 2, transcendentals=2 * pairs * half, bytes_accessed=14 * tokens * width
        ),
        name="attention_backward",
    )(slopes.reshape(pairs, 1, 2), idc, idr, beginr, qkv, qkv, qkv, grad_out)


def take(blocks, index, axis=0):
    return lax.dynamic_index_in_dim(blocks, index, axis, keepdims=False)


def seq_gather(block, axis):
    n, me = lax.axis_size("seq"), lax.axis_index("seq")
    shape = block.shape[:axis] + (n,) + block.shape[axis:]
    if n == 2:
        peer = lax.ppermute(block, "seq", [(0, 1), (1, 0)])
        return jnp.where(me == 0, jnp.stack([block, peer], axis), jnp.stack([peer, block], axis))
    whole = lax.dynamic_update_index_in_dim(jnp.zeros(shape, block.dtype), block, me, axis)
    for d in range(1, n):
        got = lax.ppermute(block, "seq", [(i, (i + d) % n) for i in range(n)])
        whole = lax.dynamic_update_index_in_dim(whole, got, (me - d) % n, axis)
    return whole


def seq_blocks(whole, axis, dtype):
    n, me = lax.axis_size("seq"), lax.axis_index("seq")
    got = [take(whole, me, axis)]
    for d in range(1, n):
        sent = take(whole, (me + d) % n, axis).astype(dtype)
        got.append(lax.ppermute(sent, "seq", [(i, (i + d) % n) for i in range(n)]))
    return got


def seq_sum(whole, axis, dtype=bf16):
    got = seq_blocks(whole, axis, dtype)
    return sum((g.astype(f32) for g in got[1:]), got[0].astype(f32))


def shard_factors(n):
    nc = 2 if n % 2 == 0 else 1
    nz = 4 if n % (4 * nc) == 0 else 1
    return nz, n // (nz * nc), nc


def shard_reduce(blocks, dtype):
    n, me = lax.axis_size("shard"), lax.axis_index("shard")
    sizes = shard_factors(n)
    blocks = blocks.reshape(sizes + blocks.shape[1:])
    place = (me // (sizes[1] * sizes[2]), me // sizes[2] % sizes[1], me % sizes[2])
    strides = (sizes[1] * sizes[2], sizes[2], 1)
    for axis in (2, 1, 0):
        size, mine, stride = sizes[axis], place[axis], strides[axis]
        total = take(blocks, mine, axis).astype(f32)
        for d in range(1, size):
            sent = take(blocks, (mine + d) % size, axis).astype(dtype)
            pairs = [
                (i, i - (i // stride % size) * stride + ((i // stride % size + d) % size) * stride)
                for i in range(n)
            ]
            total = total + lax.ppermute(sent, "shard", pairs).astype(f32)
        blocks = total if axis == 0 else total.astype(dtype)
    return blocks


MESH = pl.DeviceIdType.MESH


class Geometry:
    def __init__(self, seqs, shards):
        self.seqs, self.shards = seqs, shards
        self.sizes = shard_factors(shards)
        self.s, self.k = lax.axis_index("seq"), lax.axis_index("shard")
        nz, ny, nc = self.sizes
        self.z, self.y, self.c = self.k // (ny * nc), self.k // nc % ny, self.k % nc
        self.inner = (self.z + 1) // 2 % 2
        high = self.z // 2
        self.line = (self.z, self.z + 1 - 2 * (self.z % 2), 2 - high, 3 - 3 * high)

    def slot(self, i, dy, dc):
        nz, ny, nc = self.sizes
        return (self.line[i] * ny + (self.y + dy) % ny) * nc + (self.c + dc) % nc


class Wires:
    def __init__(self, geometry, send_sems, recv_sems):
        self.g, self.send_sems, self.recv_sems = geometry, send_sems, recv_sems
        self.sends, self.used = [], 0

    def block(self, count):
        first = self.used
        self.used += count
        return first

    def copy(self, src, dst, sent, got, s, k):
        return pltpu.make_async_remote_copy(
            src_ref=src, dst_ref=dst, send_sem=self.send_sems.at[sent], recv_sem=self.recv_sems.at[got],
            device_id={"seq": s, "shard": k}, device_id_type=MESH,
        )

    def send_as(self, src, dst, sent, got, s, k, like):
        self.copy(src, dst, sent, got, s, k).start()
        self.sends.append((like, sent))

    def recorded(self, like, index):
        self.sends.append((like, index))

    def send(self, src, dst, index, s, k, like):
        self.send_as(src, dst, index, index, s, k, like)

    def arrived(self, dst, index):
        self.copy(dst, dst, index, index, 1 - self.g.s, self.g.k).wait_recv()

    def drain(self):
        for like, index in self.sends:
            self.copy(like, like, index, index, 1 - self.g.s, self.g.k).wait_send()
        self.sends = []


def enter(geometry):
    g = geometry
    barrier = pltpu.get_barrier_semaphore()
    for d in range(1, g.shards):
        pl.semaphore_signal(
            barrier, inc=1, device_id={"seq": g.s, "shard": (g.k + d) % g.shards}, device_id_type=MESH
        )
    pl.semaphore_signal(barrier, inc=1, device_id={"seq": 1 - g.s, "shard": g.k}, device_id_type=MESH)
    pl.semaphore_wait(barrier, g.shards)


class Gather:
    def __init__(self, wires, own, out):
        self.w, self.g, self.own, self.out = wires, wires.g, own, out
        nz, ny, nc = self.g.sizes
        self.z0 = wires.block(nz)
        self.on0 = wires.block(nz)
        self.y0 = wires.block(nz * ny)
        self.c0 = wires.block(nz * ny * nc)

    def on_y(self, i, src):
        g = self.g
        for dy in range(1, g.sizes[1]):
            self.w.send(src, self.out.at[g.slot(i, 0, 0)], self.y0 + i * g.sizes[1] + dy, g.s, g.slot(0, dy, 0), self.own)

    def on_core(self, i, dy, src):
        g = self.g
        for dc in range(1, g.sizes[2]):
            index = self.c0 + (i * g.sizes[1] + dy) * g.sizes[2] + dc
            self.w.send(src, self.out.at[g.slot(i, -dy, 0)], index, g.s, g.slot(0, 0, dc), self.own)

    def start(self):
        g = self.g
        here = self.out.at[g.k]
        self.w.send_as(self.own, here, self.z0 + 2, self.z0 + 3 - g.inner, g.s, g.slot(2, 0, 0), self.own)
        self.w.send(self.own, here, self.z0 + 1, g.s, g.slot(1, 0, 0), self.own)

    def start_near(self):
        self.on_y(0, self.own)
        self.on_core(0, 0, self.own)

    def poll_z(self):
        g = self.g
        for i in (1, 2, 3):
            at = self.out.at[g.slot(i, 0, 0)]
            self.w.arrived(at, self.z0 + i)
            if i > 1:

                @pl.when(g.inner == 1)
                def _(at=at, i=i):
                    self.w.copy(at, at, self.on0 + i, self.z0 + i, g.s, g.slot(1, 0, 0)).start()

            self.on_y(i, at)
            self.on_core(i, 0, at)

    def poll_y(self):
        g = self.g
        for i in range(g.sizes[0]):
            for dy in range(1, g.sizes[1]):
                at = self.out.at[g.slot(i, -dy, 0)]
                self.w.arrived(at, self.y0 + i * g.sizes[1] + dy)
                self.on_core(i, dy, at)

    def finish(self):
        g = self.g
        for i in range(g.sizes[0]):
            for dy in range(g.sizes[1]):
                for dc in range(1, g.sizes[2]):
                    at = self.out.at[g.slot(i, -dy, -dc)]
                    self.w.arrived(at, self.c0 + (i * g.sizes[1] + dy) * g.sizes[2] + dc)

        @pl.when(g.inner == 1)
        def _():
            for i in (2, 3):
                self.w.copy(self.own, self.own, self.on0 + i, self.z0 + i, g.s, g.k).wait_send()


class Tokens:
    def __init__(self, wires, packed, out):
        self.w, self.g, self.packed, self.out = wires, wires.g, packed, out
        self.blocks = out.shape[0]
        self.at = wires.block((self.g.shards + 1) * self.blocks)
        self.like, self.row = packed.at[0, 0], packed.at[:, 0]

    def index(self, b, d):
        return self.at + b * (self.g.shards + 1) + d

    def mine(self, b, s):
        return self.out.at[b, pl.ds(pl.multiple_of(s * self.g.shards, self.g.shards), self.g.shards)]

    def start(self, b):
        g = self.g
        for d in range(1, g.shards):
            to = (g.k + d) % g.shards
            lane = self.out.at[b, g.s * g.shards + g.k]
            self.w.send(self.packed.at[to, b], lane, self.index(b, d), g.s, to, self.like)

    def poll(self, b):
        g = self.g
        for d in range(1, g.shards):
            self.w.arrived(self.out.at[b, g.s * g.shards + (g.k - d) % g.shards], self.index(b, d))
        self.w.send(self.mine(b, g.s), self.mine(b, g.s), self.index(b, g.shards), 1 - g.s, g.k, self.row)

    def finish(self, b):
        self.w.arrived(self.mine(b, 1 - self.g.s), self.index(b, self.g.shards))


class Smalls:
    def __init__(self, wires, held, at):
        self.w, self.g, self.held, self.at = wires, wires.g, held, at

    def start(self):
        g = self.g
        mine = self.held.at[g.k]
        for d in range(1, g.shards):
            self.w.send(mine, mine, self.at + d, g.s, (g.k + d) % g.shards, mine)

    def finish(self):
        g = self.g
        for d in range(1, g.shards):
            self.w.arrived(self.held.at[(g.k - d) % g.shards], self.at + d)


def side_by_side(vec, small, row, to, count):
    for j in range(small.shape[0]):
        vec[to : to + 1, j * count : (j + 1) * count] = small[j, row : row + 1, :count]


def forward_kernel(
    seqs, shards, counts,
    packed, packed_cot, qkv_w, small, dense_w, fc1_w, fc2_w, slopes, lengths,
    x_out, cot_out, n1_out, n2_out, qkvw_out, dense_out, fc1_out, fc2_out, qkv_out, o_out, h2_out, a_out, slope_out,
    w2_out, vec_out,
    x_v, n1_v, n2_v, qkvw_v, small_v, dense_v, fc1_v, fc2_v, blocks_v, cot_v, qkv_v, o_v, h2_v, a_v, slope_v, w2_v, vec_v, idc, idr,
    send_sems, recv_sems, copy_sems,
):
    g = Geometry(seqs, shards)
    wires = Wires(g, send_sems, recv_sems)
    lanes = seqs * shards
    width = n1_v.shape[1]
    part = o_v.shape[2]
    pairs = part // (2 * HEAD)
    ff = fc1_v.shape[2]
    ff_part = ff // shards
    block = ROWS * lanes
    blocks = x_v.shape[0]
    half = block // seqs
    rows = width // shards
    local = []

    def bring(src, dst):
        made = pltpu.make_async_copy(src, dst, copy_sems.at[len(local)])
        made.start()
        local.append(made)
        return made

    def at_block(b):
        return pl.ds(pl.multiple_of(b * block, block), block)

    tokens = Tokens(wires, packed, x_v)
    cots = Tokens(wires, packed_cot, blocks_v)
    smalls_at = wires.block(shards)
    qkv_all = Gather(wires, qkvw_v.at[g.k], qkvw_v)
    dense_all = Gather(wires, dense_v.at[g.k], dense_v)
    up_all = Gather(wires, fc1_v.at[g.k], fc1_v)
    down_all = Gather(wires, fc2_v, fc2_out)
    heads_at = wires.block(blocks)

    staged_qkv = [
        bring(
            qkv_w.at[:, pl.ds(pl.multiple_of(p * width + g.s * part, 128), part)],
            qkvw_v.at[g.k, :, pl.ds(p * part, part)],
        )
        for p in range(3)
    ]
    staged_small = bring(small, small_v.at[g.k])
    staged_dense = bring(dense_w, dense_v.at[g.k])
    staged_up = [
        bring(
            fc1_w.at[:, pl.ds(pl.multiple_of((i * seqs + g.s) * ff_part, 128), ff_part)],
            fc1_v.at[g.k, :, pl.ds(i * ff_part, ff_part)],
        )
        for i in range(shards)
    ]
    staged_x = bring(packed.at[g.k], x_v.at[:, g.s * shards + g.k])
    staged_down = bring(fc2_w.at[pl.ds(pl.multiple_of(g.s * ff_part, 8), ff_part), :], fc2_v)
    staged_cot = bring(packed_cot.at[g.k], blocks_v.at[:, g.s * shards + g.k])
    enter(g)
    idc[...] = blocked_ids(idc.shape, 0, lanes)
    idr[...] = blocked_ids(idr.shape, 1, lanes)
    for made in staged_qkv:
        made.wait()
    staged_small.wait()
    staged_dense.wait()
    for made in staged_up:
        made.wait()
    staged_down.wait()
    staged_x.wait()
    staged_cot.wait()
    kept = [bring(fc2_v, fc2_out.at[g.k])]
    smalls = Smalls(wires, small_v, smalls_at)
    qkv_all.start()
    qkv_all.start_near()
    tokens.start(0)
    tokens.start(1)
    smalls.start()
    dense_all.start_near()
    up_all.start_near()
    down_all.start_near()
    tokens.poll(0)
    tokens.start(2)
    qkv_all.poll_z()
    tokens.poll(1)
    tokens.start(3)
    dense_all.start()
    up_all.start()
    smalls.finish()

    for row in (0, 1, 3, 4, 5, 7):
        side_by_side(vec_v, small_v, row, row, rows)
    vec_v[2:3, :] = jnp.zeros((1, vec_v.shape[1]), f32)
    per = 2 * width // shards
    for i in range(part // per):
        for row, side in ((0, 0), (2, 1)):
            j = (side * width + g.s * part) // per + i
            vec_v[2:3, row * part + i * per : row * part + (i + 1) * per] = small_v[j, 2:3, :per]
    for j in range(shards):
        vec_v[6:7, j * ff_part : (j + 1) * ff_part] = small_v[j, 6:7, pl.ds(pl.multiple_of(g.s * ff_part, 128), ff_part)]

    qkv_all.poll_y()
    tokens.poll(2)
    tokens.poll(3)
    down_all.start()
    qkv_all.finish()
    kept += [bring(qkvw_v, qkvw_out), bring(vec_v, vec_out)]

    lane_id = lax.broadcasted_iota(jnp.int32, (1, 2 * HEAD), 1)
    tile = min(256, block)

    def project(b):
        x = x_v[b].astype(f32).reshape(block, width)
        xhat, _ = normalize(x)
        n1 = (xhat * vec_v[0:1, :width] + vec_v[1:2, :width]).astype(bf16)
        at = at_block(b)
        n1_v[at, :] = n1
        for p in range(3):
            weight = qkvw_v[:, :, p * part : (p + 1) * part].reshape(width, part)
            out = jnp.dot(n1, weight, preferred_element_type=f32) + vec_v[2:3, p * part : (p + 1) * part]
            out = out.astype(bf16)
            for h in range(pairs):
                qkv_v[p * pairs + h, at, :] = out[:, h * 2 * HEAD : (h + 1) * 2 * HEAD]

    def attend(b):
        end = (b + 1) * block

        @pl.loop(0, pairs)
        def _(h):
            q_ref, k_ref, v_ref = qkv_v.at[h], qkv_v.at[pairs + h], qkv_v.at[2 * pairs + h]
            for t in range(block // tile):
                at = pl.ds(b * block + t * tile, tile)
                q = q_ref[at, :] * jnp.asarray(HEAD**-0.5, bf16)
                ids_q = idc[at, :]

                def one_head(j, both):
                    mine = (lane_id >= HEAD).astype(jnp.int32) == j
                    qj = jnp.where(mine, q, jnp.zeros_like(q))
                    s = lax.dot_general(
                        qj, k_ref[:end, :], (((1,), (1,)), ((), ())), preferred_element_type=f32
                    )
                    s = s + slopes[g.s * pairs + h, j] * idr[:, :end]
                    tail = attn_mask(s[:, b * block :], idr[:, b * block : end] <= ids_q)
                    s = jnp.concatenate([s[:, : b * block], tail], axis=1) if b else tail
                    top = jnp.max(s, axis=1, keepdims=True)
                    e = jnp.exp(s - top)
                    total = jnp.sum(e, axis=1, keepdims=True)
                    o = jnp.dot(e.astype(bf16), v_ref[:end, :], preferred_element_type=f32) / total
                    return jnp.where(mine, o, both)

                both = lax.fori_loop(0, 2, one_head, jnp.zeros((tile, 2 * HEAD), f32))
                o_v[g.s, at, pl.ds(pl.multiple_of(h * 2 * HEAD, 2 * HEAD), 2 * HEAD)] = both.astype(bf16)

    def head_copy(b):
        mine = o_v.at[g.s, at_block(b)]
        return wires.copy(mine, mine, heads_at + b, heads_at + b, 1 - g.s, g.k)

    for b in range(blocks):
        tokens.finish(b)
        project(b)
        attend(b)
        head_copy(b).start()
        if b == 0:
            dense_all.poll_z()
        if b == 1:
            up_all.poll_z()
        if b == 2:
            dense_all.poll_y()
            cots.start(0)
            cots.start(1)
        if b == 3:
            up_all.poll_y()
    kept += [bring(x_v, x_out), bring(n1_v, n1_out), bring(qkv_v, qkv_out)]
    down_all.poll_z()
    dense_all.finish()
    kept.append(bring(dense_v, dense_out))
    up_all.finish()
    kept.append(bring(fc1_v, fc1_out))

    @pl.loop(0, blocks)
    def _(b):
        at = at_block(b)
        wires.arrived(o_v.at[1 - g.s, at], heads_at + b)
        branch = jnp.dot(
            o_v[0, at, :], dense_v[: shards // 2].reshape(part, width), preferred_element_type=f32
        ) + jnp.dot(o_v[1, at, :], dense_v[shards // 2 :].reshape(part, width), preferred_element_type=f32)
        resid = x_v[b].astype(f32).reshape(block, width) + branch + vec_v[3:4, :width]
        h2_v[b] = jnp.where(g.s == 0, resid[:half], resid[half:])
        xhat, _ = normalize(resid)
        n2 = (xhat * vec_v[4:5, :width] + vec_v[5:6, :width]).astype(bf16)
        n2_v[at, :] = n2
        step = min(512, ff)

        @pl.loop(0, ff // step)
        def _(n):
            cut = pl.ds(pl.multiple_of(n * step, step), step)
            u = jnp.dot(n2_v[at, :], fc1_v[:, :, cut].reshape(width, step), preferred_element_type=f32) + vec_v[6:7, cut]
            inside = 0.7978845608028654 * u * (1.0 + 0.044715 * u * u)
            t = jnp.tanh(inside)
            a_v[at, cut] = (0.5 * u * (1.0 + t)).astype(bf16)
            slope = 0.5 * (1.0 + t) + 0.5 * u * (1.0 - t * t) * (
                0.7978845608028654 + (0.7978845608028654 * 3.0 * 0.044715) * u * u
            )
            slope_v[at, cut] = slope.astype(bf16)

        @pl.when(b == 0)
        def _():
            cots.poll(0)
            cots.start(2)

        @pl.when(b == 1)
        def _():
            cots.poll(1)
            cots.start(3)

        @pl.when(b == 2)
        def _():
            cots.poll(2)


    cots.poll(3)
    kept.append(bring(o_v, o_out))
    kept += [bring(n2_v, n2_out), bring(h2_v, h2_out), bring(a_v, a_out), bring(slope_v, slope_out)]
    down_all.poll_y()
    for b in range(blocks):
        cots.finish(b)

    @pl.loop(0, blocks)
    def _(b):
        at = at_block(b)
        grad = blocks_v[b].astype(f32).reshape(block, width)
        cot_v[at, :] = jnp.where(idc[at, :] < lengths[g.k].astype(f32), grad, 0.0).astype(bf16)

    kept.append(bring(cot_v, cot_out))

    @pl.loop(0, ff // (2 * ff_part))
    def _(m):
        cut = a_v[:, pl.ds(pl.multiple_of(m * 2 * ff_part, 128), 2 * ff_part)]
        out = lax.dot_general(cut, cot_v[...], (((0,), (0,)), ((), ())), preferred_element_type=f32).astype(bf16)
        w2_v[pl.ds(2 * m, 2)] = out.reshape(2, ff_part, width)

    kept.append(bring(w2_v, w2_out))
    down_all.finish()
    for b in range(blocks):
        head_copy(b).wait_send()
    wires.drain()
    for made in kept:
        made.wait()
    assert wires.used <= counts[0] and len(local) <= counts[1]


def forward_exchange(packed, packed_cot, qkv_w, small, dense_w, fc1_w, fc2_w, slopes, lengths, seqs, shards):
    width, own = qkv_w.shape[0] * shards, qkv_w.shape[0]
    lanes = seqs * shards
    blocks = packed.shape[1]
    block = lanes * ROWS
    cap = blocks * block
    part = width // seqs
    pairs = part // (2 * HEAD)
    ff = fc1_w.shape[1] // seqs
    ff_part = ff // shards
    counts = (384, 64)
    any_ = pl.BlockSpec(memory_space=pl.ANY)
    vmem = pl.BlockSpec(memory_space=pltpu.VMEM)
    smem = pl.BlockSpec(memory_space=pltpu.SMEM)
    x_shape = ((blocks, lanes, ROWS, width), bf16)
    wide, long = ((cap, width), bf16), ((cap, ff), bf16)
    qkvw, dense, fc1, fc2 = (
        ((shards,) + tail, bf16) for tail in ((own, 3 * part), (own, width), (own, ff), (ff_part, width))
    )
    qkv, heads = ((3 * pairs, cap, 2 * HEAD), bf16), ((seqs, cap, part), bf16)
    h2, vec = ((blocks, block // seqs, width), f32), ((8, max(width, 3 * part, ff)), f32)
    outs = [x_shape, wide, wide, wide, qkvw, dense, fc1, fc2, qkv, heads, h2, long, long, fc2, vec]
    scratch = [
        x_shape, wide, wide, qkvw, ((shards,) + small.shape, f32), dense, fc1, ((ff_part, width), bf16), x_shape, wide,
        qkv, heads, h2, long, long, fc2, vec, ((cap, 1), f32), ((1, cap), f32),
    ]
    return pl.pallas_call(
        functools.partial(forward_kernel, seqs, shards, counts),
        in_specs=[any_] * 7 + [smem] * 2,
        out_specs=[any_] * len(outs),
        out_shape=[jax.ShapeDtypeStruct(s, d) for s, d in outs],
        scratch_shapes=[pltpu.VMEM(s, d) for s, d in scratch]
        + [pltpu.SemaphoreType.DMA((counts[0],)), pltpu.SemaphoreType.DMA((counts[0],)), pltpu.SemaphoreType.DMA((counts[1],))],
        compiler_params=pltpu.CompilerParams(collective_id=1, has_side_effects=True, vmem_limit_bytes=60 * 2**20),
        name="forward_exchange",
    )(
        packed, packed_cot, qkv_w, small, dense_w, fc1_w, fc2_w, slopes, lengths,
    )


class Scatter:
    def __init__(self, wires, full, own, bufs):
        self.w, self.g, self.full, self.own = wires, wires.g, full, own
        self.rc, self.ry, self.rz, self.fin = bufs
        self.at = wires.block(8)
        self.one = self.rz.at[0] if self.rz is not None else None

    def add(self, count, into, other):
        @pl.loop(0, count)
        def _(i):
            a, b = into(i), other(i)
            a[...] = (a[...].astype(f32) + b[...].astype(f32)).astype(bf16)

    def core_send(self):
        g = self.g
        self.w.send(self.full.at[:, :, 1 - g.c], self.rc, self.at, g.s, g.slot(0, 0, 1), self.rc)

    def core_done(self):
        g = self.g
        self.w.arrived(self.rc, self.at)
        self.add(8, lambda i: self.rc.at[i // 2, i % 2], lambda i: self.own(i // 2, i % 2))
        if self.ry is not None:
            self.y_send()

    def y_send(self):
        g = self.g
        self.w.send(self.rc.at[:, 1 - g.y], self.ry, self.at + 1, g.s, g.slot(0, 1, 0), self.ry)

    def y_done(self):
        g = self.g
        self.w.arrived(self.ry, self.at + 1)
        self.add(4, lambda i: self.ry.at[i], lambda i: self.rc.at[i, g.y])

    def z_send(self):
        g = self.g
        partner = g.slot(1, 0, 0)
        self.w.send(self.ry.at[g.line[1]], self.rz.at[0], self.at + 2, g.s, partner, self.one)

        @pl.when(g.inner == 0)
        def _():
            for i in (2, 3):
                self.w.copy(self.ry.at[g.line[i]], self.rz.at[i], self.at + 1 + i, self.at + 1 + i, g.s, partner).start()

    def z_done(self):
        g = self.g

        @pl.when(g.inner == 1)
        def _():
            for i in (2, 3):
                self.w.arrived(self.rz.at[i], self.at + 1 + i)
                a = self.rz.at[i]
                a[...] = (a[...].astype(f32) + self.ry[g.line[i]].astype(f32)).astype(bf16)
                self.w.copy(a, self.rz.at[1], self.at + 1 + i, self.at + 5, g.s, g.slot(i, 0, 0)).start()

    def final(self):
        g = self.g
        self.w.arrived(self.rz.at[0], self.at + 2)
        self.w.arrived(self.rz.at[1], self.at + 5)
        total = self.ry[g.z].astype(f32) + self.rz[0].astype(f32) + self.rz[1].astype(f32)
        self.fin[0] = total.astype(bf16)
        self.w.send(self.fin.at[0], self.fin.at[1], self.at + 6, 1 - g.s, g.k, self.fin.at[0])

    def done(self):
        self.w.arrived(self.fin.at[1], self.at + 6)
        for i in (2, 3):
            self.w.copy(self.fin.at[0], self.fin.at[0], self.at + 1 + i, self.at + 1 + i, self.g.s, self.g.k).wait_send()


class Back:
    def __init__(self, wires, src, dst, pieces):
        self.w, self.g, self.src, self.dst, self.pieces = wires, wires.g, src, dst, pieces
        self.at = wires.block(wires.g.shards * pieces)
        self.per = src.shape[0] // pieces
        self.like = src.at[pl.ds(0, self.per), 0]

    def cut(self, ref, i):
        return ref.at[pl.ds(i * self.per, self.per)]

    def send(self, i):
        g = self.g
        for d in range(1, g.shards):
            to = (g.k + d) % g.shards
            src = self.src.at[pl.ds(i * self.per, self.per), to]
            index = self.at + i * g.shards + d
            self.w.copy(src, self.cut(self.dst.at[g.k], i), index, index, g.s, to).start()

    def finish(self):
        g = self.g
        for i in range(self.pieces):
            for d in range(1, g.shards):
                self.w.recorded(self.like, self.at + i * g.shards + d)
                self.w.arrived(self.cut(self.dst.at[(g.k - d) % g.shards], i), self.at + i * g.shards + d)


def middle_kernel(
    seqs, shards, counts,
    a, slope, n2, fc1, fc2, dense, cot, h2, heads, w2, vec,
    dh2_out, do_out, rc1_out, wd_out, keep_out, give_out, ry_out, small_out,
    a_v, du_v, n2_v, fc1_v, fc2_v, dense_v, cot_v, h2_v, heads_v, own_w2, w1_v, wd_v, mine_v, sent_v, got_v,
    da_v, do_v, do_sent, small_v, rc, ry, rc1,
    send_sems, recv_sems, copy_sems,
):
    g = Geometry(seqs, shards)
    wires = Wires(g, send_sems, recv_sems)
    blocks, half, width = h2_v.shape
    block = half * seqs
    ff = a_v.shape[1]
    ff_part = ff // shards
    rows = width // shards
    part = width // seqs
    local = []

    def bring(src, dst):
        made = pltpu.make_async_copy(src, dst, copy_sems.at[len(local)])
        made.start()
        local.append(made)
        return made

    def at_block(b):
        return pl.ds(pl.multiple_of(b * block, block), block)

    def own_rows(b):
        return pl.ds(pl.multiple_of(b * block + g.s * half, half), half)

    down = Scatter(wires, w2, lambda i, j: own_w2.at[i, j], (rc, ry, None, None))
    up = Scatter(wires, w1_v, lambda i, j: w1_v.at[i, j, g.c], (rc1, None, None, None))
    half_at, do_at = wires.block(blocks), wires.block(blocks)
    first = [bring(cot, cot_v), bring(fc2, fc2_v), bring(slope, du_v), bring(fc1, fc1_v)]
    own = bring(w2.at[:, :, g.c], own_w2)
    later = [bring(n2, n2_v), bring(a, a_v), bring(h2, h2_v), bring(dense, dense_v)]
    later += [bring(heads.at[i, own_rows(b), :], heads_v.at[i, pl.ds(b * half, half)]) for i in range(seqs) for b in range(blocks)]
    enter(g)
    down.core_send()
    for made in first:
        made.wait()
    step = min(512, ff)
    per = step // ff_part

    def half_copy(b):
        return wires.copy(sent_v.at[b], got_v.at[b], half_at + b, half_at + b, 1 - g.s, g.k)

    def do_copy(b):
        return wires.copy(do_sent.at[b], do_v.at[b, g.s], do_at + b, do_at + b, 1 - g.s, g.k)

    small_v[...] = jnp.zeros_like(small_v)

    def split(b, total, keep, give):
        @pl.when(g.s == 0)
        def _():
            keep(total[:half])
            give[b] = total[half:].astype(bf16)

        @pl.when(g.s == 1)
        def _():
            keep(total[half:])
            give[b] = total[:half].astype(bf16)

    def du_step(b, sums):
        at = at_block(b)
        grad = cot_v[at, :]
        total, new = None, []
        for n in range(ff // step):
            cut = slice(n * step, (n + 1) * step)
            weight = fc2_v[n * per : (n + 1) * per].reshape(step, width)
            da = lax.dot_general(grad, weight, (((1,), (1,)), ((), ())), preferred_element_type=f32)
            du = (da * du_v[at, cut].astype(f32)).astype(bf16)
            du_v[at, cut] = du
            new.append(sums[n] + jnp.sum(du.astype(f32), axis=0, keepdims=True))
            weight = fc1_v[:, :, cut].reshape(width, step)
            term = lax.dot_general(du, weight, (((1,), (1,)), ((), ())), preferred_element_type=f32)
            total = term if total is None else total + term

        def keep(value):
            mine_v[b] = value

        split(b, total, keep, sent_v)

        @pl.when(b > 0)
        def _():
            half_copy(b - 1).start()

        @pl.when(b == 0)
        def _():
            own.wait()
            down.core_done()

        return tuple(new)

    zero = jnp.zeros((1, step), f32)
    sums = lax.fori_loop(0, blocks, du_step, (zero,) * (ff // step))
    for made in later:
        made.wait()

    @pl.loop(0, width // (4 * rows))
    def _(m):
        @pl.when(m == 0)
        def _():
            half_copy(blocks - 1).start()

        left = n2_v[:, pl.ds(pl.multiple_of(m * 4 * rows, 128), 4 * rows)]
        for n in range(ff // step):
            cut = slice(n * step, (n + 1) * step)
            out = lax.dot_general(left, du_v[:, cut], (((0,), (0,)), ((), ())), preferred_element_type=f32)
            w1_v[m, :, :, :, cut] = out.astype(bf16).reshape(2, 2, rows, step)

    up.core_send()
    kept = []
    for n in range(ff // step):
        for i in range(per):
            small_v[n * per + i, 6:7, pl.ds(pl.multiple_of(g.s * ff_part, 128), ff_part)] = sums[n][
                :, i * ff_part : (i + 1) * ff_part
            ]

    def norm_step(b, sums):
        gains, biases, branch, cots = sums
        wires.arrived(got_v.at[b], half_at + b)
        grad = mine_v[b] + got_v[b].astype(f32)
        xhat, root = normalize(h2_v[b])
        gains = gains + jnp.sum(grad * xhat, axis=0, keepdims=True)
        biases = biases + jnp.sum(grad, axis=0, keepdims=True)
        cot_b = cot_v[own_rows(b), :].astype(f32)
        cots = cots + jnp.sum(cot_b, axis=0, keepdims=True)
        dh2 = cot_b + norm_pull(grad, vec[4:5, :width], xhat, root)
        mine_v[b] = dh2
        da = dh2.astype(bf16)
        branch = branch + jnp.sum(da.astype(f32), axis=0, keepdims=True)
        da_v[pl.ds(pl.multiple_of(b * half, half), half), :] = da
        grads = [
            lax.dot_general(
                da, dense_v[i * (shards // seqs) : (i + 1) * (shards // seqs)].reshape(part, width),
                (((1,), (1,)), ((), ())), preferred_element_type=f32,
            ).astype(bf16)
            for i in range(seqs)
        ]
        do_v[b, g.s] = jnp.where(g.s == 0, grads[0], grads[1])
        do_sent[b] = jnp.where(g.s == 0, grads[1], grads[0])

        @pl.when(b > 0)
        def _():
            do_copy(b - 1).start()

        return gains, biases, branch, cots

    zero = jnp.zeros((1, width), f32)
    sums = lax.fori_loop(0, blocks, norm_step, (zero,) * 4)
    kept.append(bring(mine_v, dh2_out))
    for row, vector in ((4, sums[0]), (5, sums[1]), (3, sums[2]), (7, sums[3])):
        for j in range(shards):
            small_v[j, row : row + 1, :rows] = vector[:, j * rows : (j + 1) * rows]
    do_copy(blocks - 1).start()
    kept.append(bring(small_v, small_out))

    for i in range(seqs):
        out = lax.dot_general(heads_v[i], da_v[...], (((0,), (0,)), ((), ())), preferred_element_type=f32).astype(bf16)
        wd_v[i * (shards // seqs) : (i + 1) * (shards // seqs)] = out.reshape(shards // seqs, rows, width)
    kept.append(bring(wd_v, wd_out))

    @pl.loop(0, blocks)
    def _(b):
        at = at_block(b)
        total = None
        for n in range(ff // step):
            weight = fc2_v[n * per : (n + 1) * per].reshape(step, width)
            term = jnp.dot(a_v[at, n * step : (n + 1) * step], weight, preferred_element_type=f32)
            total = term if total is None else total + term

        def keep(value):
            h2_v[b] = h2_v[b] + value + vec[7:8, :width]

        split(b, total, keep, got_v)

    kept += [bring(h2_v, keep_out), bring(got_v, give_out)]
    up.core_done()
    kept.append(bring(rc1, rc1_out))
    down.y_done()
    kept.append(bring(ry, ry_out))
    for b in range(blocks):
        wires.arrived(do_v.at[b, 1 - g.s], do_at + b)
    kept.append(bring(do_v, do_out))
    for b in range(blocks):
        half_copy(b).wait_send()
        do_copy(b).wait_send()
    wires.drain()
    for made in kept:
        made.wait()
    assert wires.used <= counts[0] and len(local) <= counts[1]


def middle_exchange(a, slope, n2, fc1, fc2, dense, cot, h2, heads, w2, vec, seqs, shards):
    blocks, half, width = h2.shape
    tokens, ff = a.shape
    part = width // seqs
    rows, ff_part = width // shards, ff // shards
    counts = (32, 40)
    any_, vmem = pl.BlockSpec(memory_space=pl.ANY), pl.BlockSpec(memory_space=pltpu.VMEM)
    own32, own16 = ((blocks, half, width), f32), ((blocks, half, width), bf16)
    do, smalls = ((blocks, seqs, half, part), bf16), ((shards, 8, 256), f32)
    w1, wd, ry = ((shards, rows, ff), bf16), ((shards, rows, width), bf16), ((4, ff_part, width), bf16)
    w1 = ((4, 2, 2, rows, ff), bf16)
    rc1 = ((4, 2, rows, ff), bf16)
    outs = [own32, do, rc1, wd, own32, own16, ry, smalls]
    rc = ((4, 2, ff_part, width), bf16)
    scratch = [(v.shape, bf16) for v in (a, slope, n2, fc1, fc2, dense, cot)] + [
        own32, ((seqs, blocks * half, part), bf16), rc, w1, wd, own32, own16, own16, ((blocks * half, width), bf16), do,
        ((blocks, half, part), bf16), smalls, rc, ry, rc1,
    ]
    return pl.pallas_call(
        functools.partial(middle_kernel, seqs, shards, counts),
        in_specs=[any_] * 10 + [vmem],
        out_specs=[any_] * len(outs),
        out_shape=[jax.ShapeDtypeStruct(s, d) for s, d in outs],
        scratch_shapes=[pltpu.VMEM(s, d) for s, d in scratch]
        + [pltpu.SemaphoreType.DMA((counts[0],)), pltpu.SemaphoreType.DMA((counts[0],)), pltpu.SemaphoreType.DMA((counts[1],))],
        compiler_params=pltpu.CompilerParams(collective_id=3, has_side_effects=True, vmem_limit_bytes=62 * 2**20),
        name="middle_exchange",
    )(a, slope, n2, fc1, fc2, dense, cot, h2, heads, w2.reshape((4, 2, 2) + w2.shape[1:]), vec)


def backward_kernel(
    seqs, shards, counts,
    qkv, do, n1, qkvw, x_all, dh2, keep, give, ry2, rc1, wd, smalls, vec, slopes,
    ret_y, ret_x, o_qkv, o_dense, o_up, o_down, o_small,
    qkv_v, do_v, dqkv_v, n1_v, qkvw_v, x_v, dh2_v, dk_acc, dv_acc, bias_acc, mine_v, sent_v, got_v, dx_v, gq_v,
    small_v, small_got, small_fin, small_last, f_qkv, f_dense, f_up, f_down, keep_v, give_v, y_v, own_wd, idc, idr, zero_v,
    *rest,
):
    bufs, (send_sems, recv_sems, copy_sems) = rest[:-3], rest[-3:]
    g = Geometry(seqs, shards)
    wires = Wires(g, send_sems, recv_sems)
    pairs, tokens = do_v.shape[0], do_v.shape[1]
    part = pairs * 2 * HEAD
    width = n1_v.shape[1]
    lanes = seqs * shards
    block = ROWS * lanes
    blocks = tokens // block
    half = block // seqs
    tile = bias_acc.shape[2]
    local = []

    def bring(src, dst):
        made = pltpu.make_async_copy(src, dst, copy_sems.at[len(local)])
        made.start()
        local.append(made)
        return made

    def held(ref):
        return lambda i, j: ref.at[i, j]

    down = Scatter(wires, None, None, (None,) + bufs[0:3])
    up = Scatter(wires, None, None, bufs[3:7])
    dense = Scatter(wires, wd, held(own_wd), bufs[7:11])
    qkv_sum = Scatter(wires, gq_v, lambda i, j: gq_v.at[i, j, g.c], bufs[11:15])
    back_y = Back(wires, y_v, ret_y, blocks)
    give_at = wires.block(blocks)
    back_x = Back(wires, dx_v, ret_x, blocks)
    half_at = wires.block(blocks)
    small_at = wires.block(shards + 1)

    rc_in = bring(rc1, up.rc)
    ry_in = bring(ry2, down.ry)
    first = [bring(qkv, qkv_v)] + [bring(do.at[:, pl.ds(h * 2 * HEAD, 2 * HEAD)], do_v.at[h]) for h in range(pairs)]
    owns = [bring(a.at[:, :, g.c], b) for a, b in ((wd, own_wd),)] + [bring(keep, keep_v)]
    later = [
        bring(n1, n1_v), bring(qkvw, qkvw_v), bring(x_all.at[:, pl.ds(g.s * shards, shards)], x_v), bring(dh2, dh2_v),
        bring(smalls, small_v),
    ]
    enter(g)
    zero_v[...] = jnp.zeros_like(zero_v)
    idc[...] = blocked_ids(idc.shape, 0, lanes)
    idr[...] = blocked_ids(idr.shape, 1, lanes)
    rc_in.wait()
    up.y_send()
    dense.core_send()
    ry_in.wait()
    down.z_send()
    for b in range(blocks):
        wires.send(give.at[b], give_v.at[b], give_at + b, 1 - g.s, g.k, give.at[b])
    for made in first + owns:
        made.wait()

    lane_id = lax.broadcasted_iota(jnp.int32, (1, 2 * HEAD), 1)

    def attend(h):
        q_ref, k_ref, v_ref, do_ref = qkv_v.at[h], qkv_v.at[pairs + h], qkv_v.at[2 * pairs + h], do_v.at[h]
        dk_acc[...] = jnp.zeros_like(dk_acc)
        dv_acc[...] = jnp.zeros_like(dv_acc)
        for j in range(2):
            bias_acc[j] = jnp.broadcast_to(slopes[g.s * pairs + h, j] * idc[...], bias_acc.shape[1:])
        cols = pl.ds(pl.multiple_of(h * 2 * HEAD, 2 * HEAD), 2 * HEAD)
        for b in range(blocks):
            end = (b + 1) * block
            for t in range(block // tile):
                at = pl.ds(b * block + t * tile, tile)
                q = q_ref[at, :] * jnp.asarray(HEAD**-0.5, bf16)
                grad = do_ref[at, :]
                ids_q = idr[:, at]
                both = None
                for j in range(2):
                    mine = (lane_id // HEAD) == j
                    qj = jnp.where(mine, q, jnp.zeros_like(q))
                    doj = jnp.where(mine, grad, jnp.zeros_like(grad))
                    s = lax.dot_general(
                        k_ref[:end, :], qj, (((1,), (1,)), ((), ())), preferred_element_type=f32
                    )
                    s = s + bias_acc[j, :end, :]
                    tail = attn_mask(s[b * block :, :], idc[b * block : end, :] <= ids_q)
                    s = jnp.concatenate([s[: b * block, :], tail], axis=0) if b else tail
                    top = jnp.max(s, axis=0, keepdims=True)
                    e = jnp.exp(s - top)
                    probs = e * (1.0 / jnp.sum(e, axis=0, keepdims=True))
                    dv_acc[:end, :] += jnp.dot(probs.astype(bf16), doj, preferred_element_type=f32)
                    dp = lax.dot_general(
                        v_ref[:end, :], doj, (((1,), (1,)), ((), ())), preferred_element_type=f32
                    )
                    inner = jnp.sum(probs * dp, axis=0, keepdims=True)
                    ds = (probs * (dp - inner)).astype(bf16)
                    dk_acc[:end, :] += jnp.dot(ds, qj, preferred_element_type=f32)
                    dq = lax.dot_general(
                        ds, k_ref[:end, :], (((0,), (0,)), ((), ())), preferred_element_type=f32
                    )
                    both = dq if both is None else jnp.where(mine, dq, both)
                dqkv_v[0, at, cols] = (both * (HEAD**-0.5)).astype(bf16)
        dqkv_v[1, :, cols] = dk_acc[...].astype(bf16)
        dqkv_v[2, :, cols] = dv_acc[...].astype(bf16)

    @pl.loop(0, pairs)
    def _(h):
        attend(h)

        @pl.when(h == 0)
        def _():
            dense.core_done()

        @pl.when(h == 2)
        def _():
            down.z_done()

        @pl.loop(blocks * h // pairs, blocks * (h + 1) // pairs)
        def _(b):
            wires.arrived(give_v.at[b], give_at + b)
            y_v[b] = (keep_v[b] + give_v[b].astype(f32)).reshape(shards, ROWS, width).astype(bf16)
            back_y.send(b)

    for made in later:
        made.wait()

    rows = width // shards

    @pl.loop(0, blocks)
    def _(m):
        cut = n1_v[:, pl.ds(pl.multiple_of(m * block, block), block)]
        for p in range(3):
            out = lax.dot_general(cut, dqkv_v[p], (((0,), (0,)), ((), ())), preferred_element_type=f32).astype(bf16)
            out = out.reshape(block // rows // 2, 2, rows, part)
            for i in range(block // rows // 2):
                at = m * (block // rows // 2) + i
                for j in range(2):
                    gq_v[at // 2, at % 2, j, :, p * part : (p + 1) * part] = out[i, j]

    qkv_sum.core_send()

    def half_copy(b):
        return wires.copy(sent_v.at[b], got_v.at[b], half_at + b, half_at + b, 1 - g.s, g.k)

    @pl.loop(0, blocks)
    def _(b):
        total = None
        for p in range(3):
            weight = qkvw_v[:, :, p * part : (p + 1) * part].reshape(width, part)
            term = lax.dot_general(
                dqkv_v[p, pl.ds(pl.multiple_of(b * block, block), block), :], weight, (((1,), (1,)), ((), ())),
                preferred_element_type=f32,
            )
            total = term if total is None else total + term

        @pl.when(g.s == 0)
        def _():
            mine_v[b] = total[:half]
            sent_v[b] = total[half:].astype(bf16)

        @pl.when(g.s == 1)
        def _():
            mine_v[b] = total[half:]
            sent_v[b] = total[:half].astype(bf16)

        @pl.when(b == 2)
        def _():
            up.y_done()
            up.z_send()

        @pl.when(b > 0)
        def _():
            half_copy(b - 1).start()

    own_y = bring(y_v.at[:, g.k], ret_y.at[g.k])
    half_copy(blocks - 1).start()

    sums = [jnp.sum(dqkv_v[p].astype(f32), axis=0, keepdims=True) for p in (0, 2)]
    per = 2 * width // shards
    for i in range(part // per):
        for half_no in range(2):
            small_v[(half_no * width + g.s * part) // per + i, 2:3, :per] = sums[half_no][:, i * per : (i + 1) * per]
    qkv_sum.core_done()
    dense.y_done()
    dense.z_send()

    def norm_step(b, sums):
        wires.arrived(got_v.at[b], half_at + b)
        grad = mine_v[b] + got_v[b].astype(f32)
        xhat, root = normalize(x_v[b].astype(f32).reshape(half, width))
        gains = sums[0] + jnp.sum(grad * xhat, axis=0, keepdims=True)
        biases = sums[1] + jnp.sum(grad, axis=0, keepdims=True)
        dx = dh2_v[b] + norm_pull(grad, vec[0:1, :width], xhat, root)
        dx_v[b] = dx.reshape(shards, ROWS, width).astype(bf16)
        back_x.send(b)

        @pl.when(b == 0)
        def _():
            up.z_done()

        @pl.when(b == 2)
        def _():
            qkv_sum.y_done()
            qkv_sum.z_send()

        return gains, biases

    gains, biases = lax.fori_loop(0, blocks, norm_step, (jnp.zeros((1, width), f32),) * 2)
    for j in range(shards):
        small_v[j, 0:1, :rows] = gains[:, j * rows : (j + 1) * rows]
        small_v[j, 1:2, :rows] = biases[:, j * rows : (j + 1) * rows]
    kept = [own_y, bring(dx_v.at[:, g.k], ret_x.at[g.k])]
    kept += [bring(zero_v, ret_y.at[shards]), bring(zero_v, ret_x.at[shards])]
    for d in range(1, shards):
        to = (g.k + d) % shards
        wires.send(small_v.at[to], small_got.at[g.k], small_at + d, g.s, to, small_v.at[0])
    small_got[g.k] = small_v[g.k]
    down.final()
    dense.z_done()
    up.final()
    qkv_sum.z_done()
    for d in range(1, shards):
        wires.arrived(small_got.at[(g.k - d) % shards], small_at + d)
    small_fin[0] = jnp.sum(small_got[...], axis=0)
    wires.send(small_fin.at[0], small_fin.at[1], small_at + shards, 1 - g.s, g.k, small_fin.at[0])
    dense.final()

    down.done()
    ff_part = f_down.shape[0] // seqs
    for i, at in ((0, g.s), (1, 1 - g.s)):
        f_down[pl.ds(pl.multiple_of(at * ff_part, ff_part), ff_part), :] = down.fin[i].astype(f32)
    kept.append(bring(f_down, o_down))
    up.done()
    for i, at in ((0, g.s), (1, 1 - g.s)):
        for j in range(shards):
            f_up[:, pl.ds(pl.multiple_of((j * seqs + at) * ff_part, 128), ff_part)] = up.fin[
                i, :, j * ff_part : (j + 1) * ff_part
            ].astype(f32)
    kept.append(bring(f_up, o_up))
    dense.done()
    f_dense[...] = dense.fin[0].astype(f32) + dense.fin[1].astype(f32)
    kept.append(bring(f_dense, o_dense))
    wires.arrived(small_fin.at[1], small_at + shards)
    small_last[...] = small_fin[0] + small_fin[1]
    kept.append(bring(small_last, o_small))
    qkv_sum.final()
    qkv_sum.done()
    for i, at in ((0, g.s), (1, 1 - g.s)):
        for p in range(3):
            f_qkv[:, pl.ds(pl.multiple_of(p * width + at * part, 128), part)] = qkv_sum.fin[
                i, :, p * part : (p + 1) * part
            ].astype(f32)
    kept.append(bring(f_qkv, o_qkv))
    back_y.finish()
    back_x.finish()
    for b in range(blocks):
        half_copy(b).wait_send()
    wires.drain()
    for made in kept:
        made.wait()
    assert wires.used <= counts[0] and len(local) <= counts[1]


def backward_exchange(
    qkv, do, n1, qkvw, x_all, dh2, keep, give, ry2, rc1, wd, smalls, vec, slopes, seqs, shards
):
    tokens, part = do.shape
    width = n1.shape[1]
    pairs = part // (2 * HEAD)
    lanes = seqs * shards
    block = ROWS * lanes
    blocks, half = tokens // block, block // seqs
    tile = min(256, block)
    rows, ff = width // shards, rc1.shape[3]
    ff_part = ff // shards
    counts = (256, 48)
    cut = lambda a: a.reshape((4, 2, 2) + a.shape[1:])
    any_, vmem = pl.BlockSpec(memory_space=pl.ANY), pl.BlockSpec(memory_space=pltpu.VMEM)
    ret = (shards + 1, blocks, ROWS, width)
    outs = [
        (ret, bf16), (ret, bf16), ((rows, 3 * width), f32), ((rows, width), f32), ((rows, seqs * ff), f32),
        ((seqs * ff_part, width), f32), (smalls.shape[1:], f32),
    ]
    blks = [(ff_part, width), (rows, ff), (rows, width), (rows, 3 * part)]
    scratch = [
        ((3 * pairs, tokens, 2 * HEAD), bf16), ((pairs, tokens, 2 * HEAD), bf16), ((3, tokens, part), bf16),
        ((tokens, width), bf16), ((shards, rows, 3 * part), bf16), ((blocks, shards, ROWS, width), bf16),
        ((blocks, half, width), f32), ((tokens, 2 * HEAD), f32), ((tokens, 2 * HEAD), f32), ((2, tokens, tile), f32),
        ((blocks, half, width), f32), ((blocks, half, width), bf16), ((blocks, half, width), bf16),
        ((blocks, shards, ROWS, width), bf16), ((4, 2, 2) + blks[3], bf16), (smalls.shape, f32), (smalls.shape, f32),
        ((2,) + smalls.shape[1:], f32), (smalls.shape[1:], f32), ((rows, 3 * width), f32), ((rows, width), f32), ((rows, seqs * ff), f32),
        ((seqs * ff_part, width), f32), ((blocks, half, width), f32), ((blocks, half, width), bf16),
        ((blocks, shards, ROWS, width), bf16), ((4, 2) + blks[2], bf16),
        ((tokens, 1), f32), ((1, tokens), f32), ((blocks, ROWS, width), bf16),
    ]
    for blk in blks:
        scratch += [((4, 2) + blk, bf16)] * (blk is not blks[0])
        scratch += [((4,) + blk, bf16), ((4,) + blk, bf16), ((2,) + blk, bf16)]
    return pl.pallas_call(
        functools.partial(backward_kernel, seqs, shards, counts),
        in_specs=[any_] * 12 + [vmem, pl.BlockSpec(memory_space=pltpu.SMEM)],
        out_specs=[any_] * len(outs),
        out_shape=[jax.ShapeDtypeStruct(s, d) for s, d in outs],
        scratch_shapes=[pltpu.VMEM(s, d) for s, d in scratch]
        + [pltpu.SemaphoreType.DMA((counts[0],)), pltpu.SemaphoreType.DMA((counts[0],)), pltpu.SemaphoreType.DMA((counts[1],))],
        compiler_params=pltpu.CompilerParams(collective_id=2, has_side_effects=True, vmem_limit_bytes=60 * 2**20),
        name="backward_exchange",
    )(
        qkv, do, n1, qkvw, x_all, dh2, keep, give, ry2, rc1, cut(wd), smalls, vec, slopes,
    )


def layout_tables(lengths, lane_count, group_count, per_group):
    seq_rows = lengths // lane_count
    row_start = jnp.cumsum(seq_rows) - seq_rows
    slot_rows = seq_rows.reshape(group_count, per_group)
    slot_start = row_start.reshape(group_count, per_group)
    slot_before = jnp.cumsum(slot_rows, axis=1) - slot_rows
    return seq_rows, row_start, slot_rows, slot_start, slot_before


def per_device(
    tokens, cotangent, lengths, first_gain, first_bias, qkv_weight, qv_bias, dense_weight, dense_bias,
    second_gain, second_bias, fc1_weight, fc1_bias, fc2_weight, fc2_bias,
):
    shards, seqs = lax.axis_size("shard"), lax.axis_size("seq")
    lanes = shards * seqs
    slots, width = tokens.shape[1], tokens.shape[2]
    rows = slots // shards
    blocks = rows // ROWS

    smalls_in = (first_gain, first_bias, qv_bias, dense_bias, second_gain, second_bias, fc1_bias, fc2_bias)
    small = jnp.stack([jnp.pad(a.astype(f32), (0, 256 - a.shape[0])) for a in smalls_in])
    slopes = jnp.asarray(np.exp2(-8.0 * (np.arange(HEADS) + 1.0) / HEADS).reshape(-1, 2), f32)

    seq_rows = lengths // lanes
    number = jnp.arange(shards, dtype=jnp.int32)
    row_start = jnp.sum(jnp.where(number[None, :] < number[:, None], seq_rows[None, :], 0), axis=1)
    window = (row_start[:, None] + jnp.arange(rows, dtype=jnp.int32)[None, :]).reshape(-1)

    def pack(source):
        return jnp.take(source, window, axis=0, mode="clip").reshape(shards, blocks, ROWS, width)

    (
        x_all, cot_all, normed_one, normed_two, full_qkv, full_dense, full_up, full_down, qkv, mixed, resid, activ, slope,
        grad_down, vectors,
    ) = forward_exchange(
        pack(tokens[0]), pack(cotangent[0]), qkv_weight, small, dense_weight, fc1_weight, fc2_weight,
        slopes, lengths, seqs, shards,
    )
    grad_resid, grad_mixed, grad_up, grad_dense, keep, give, half_sums, small_grads = middle_exchange(
        activ, slope, normed_two, full_up, full_down, full_dense, cot_all, resid, mixed, grad_down, vectors, seqs, shards
    )
    ret_out, ret_grad, g_qkv, g_dense, g_up, g_down, g_small = backward_exchange(
        qkv, grad_mixed.reshape(slots * seqs, width // seqs), normed_one, full_qkv, x_all, grad_resid, keep, give, half_sums,
        grad_up, grad_dense, small_grads, vectors, slopes, seqs, shards,
    )

    row_here = jnp.arange(slots, dtype=jnp.int32)[:, None]
    inside = (row_here >= row_start[None]) & (row_here < (row_start + seq_rows)[None])
    fetch = jnp.sum(jnp.where(inside, number[None] * rows + row_here - row_start[None] - shards * rows, 0), axis=1)
    fetch = fetch + shards * rows

    def to_stream(got):
        return jnp.take(got.reshape(-1, width), fetch, axis=0, mode="clip")[None]

    vectors_out = tuple(g_small[i, : a.shape[0]] for i, a in enumerate(smalls_in))
    g_gain_one, g_bias_one, g_qv, g_bdense, g_gain_two, g_bias_two, g_bup, g_bdown = vectors_out
    return (
        to_stream(ret_out), to_stream(ret_grad),
        g_gain_one, g_bias_one, g_qkv, g_qv, g_dense, g_bdense, g_gain_two, g_bias_two, g_up, g_bup, g_down, g_bdown,
    )


def per_device_any(
    tokens, cotangent, lengths, first_gain, first_bias, qkv_weight, qv_bias, dense_weight, dense_bias,
    second_gain, second_bias, fc1_weight, fc1_bias, fc2_weight, fc2_bias,
):
    shards, seqs = lax.axis_size("shard"), lax.axis_size("seq")
    lanes = shards * seqs
    slots, width = tokens.shape[1], tokens.shape[2]
    rows = slots // shards
    cap = slots * seqs
    per_group = lengths.shape[0] // shards
    hidden_units = fc1_weight.shape[1]
    me, group = lax.axis_index("seq"), lax.axis_index("shard")
    blocks = rows // ROWS
    heads = width // HEAD // seqs
    part = heads * HEAD
    ff_part = hidden_units // shards // seqs

    qkv_half = take(qkv_weight.reshape(-1, 3, seqs, part), me, 2).reshape(-1, 3 * part)
    fc1_half = take(fc1_weight.reshape(-1, shards, seqs, ff_part), me, 2).reshape(-1, shards * ff_part)
    fc2_half = take(fc2_weight.reshape(seqs, ff_part, width), me, 0)
    small = jnp.concatenate(
        [first_gain, first_bias, qv_bias, dense_bias, second_gain, second_bias, fc1_bias, fc2_bias]
    )
    small_rows = -(-small.shape[0] // (3 * part))
    small_rows += -small_rows % 16
    small = jnp.pad(small, (0, small_rows * 3 * part - small.shape[0])).reshape(small_rows, 3 * part)
    gather = lambda a: lax.all_gather(a, "shard", axis=0, tiled=False)
    qkv_small = gather(jnp.concatenate([qkv_half, small], axis=0))
    own_rows = qkv_half.shape[0]
    full_qkv = qkv_small[:, :own_rows].reshape(width, 3 * part)
    smalls = qkv_small[:, own_rows:].reshape(shards, -1).astype(f32)
    full_dense = gather(dense_weight).reshape(width, width)
    full_up = gather(fc1_half).reshape(width, shards * ff_part)
    full_down = gather(fc2_half).reshape(shards * ff_part, width)
    cuts, at = [], 0
    for a in (first_gain, first_bias, qv_bias, dense_bias, second_gain, second_bias, fc1_bias, fc2_bias):
        cuts.append(smalls[:, at : at + a.shape[0]].reshape(-1))
        at += a.shape[0]
    gain_one, bias_one, bias_qv, bias_dense, gain_two, bias_two, bias_up, bias_down = cuts
    bias_q, bias_v = (take(bias_qv[i * width : (i + 1) * width].reshape(seqs, part), me) for i in (0, 1))
    bias_all = jnp.concatenate([bias_q, jnp.zeros_like(bias_q), bias_v])
    bias_up = take(bias_up.reshape(shards, seqs, ff_part), me, 1).reshape(-1)

    seq_rows, row_start, slot_rows, slot_start, slot_before = layout_tables(lengths, lanes, shards, per_group)
    row_in = jnp.arange(rows, dtype=jnp.int32)[None, :, None]
    inside = ((row_in >= slot_before[:, None]) & (row_in < (slot_before + slot_rows)[:, None])).astype(jnp.int32)
    send_live = jnp.sum(inside, axis=2) > 0
    send_row = jnp.sum(inside * (slot_start[:, None] + row_in - slot_before[:, None]), axis=2).reshape(-1)

    def to_groups(source):
        packed = jnp.take(source, send_row, axis=0).reshape(shards, rows, width)
        packed = jnp.where(send_live[:, :, None], packed, jnp.zeros_like(packed))
        got = lax.all_to_all(packed, "shard", split_axis=0, concat_axis=0, tiled=True)
        own = got.reshape(shards, blocks, ROWS, width).transpose(1, 0, 2, 3).reshape(blocks, -1, width)
        return own, seq_gather(own, 1).reshape(cap, width)

    x_own, x_low = to_groups(tokens[0])
    cot_own, cot_low = to_groups(cotangent[0])

    def own_part(whole):
        return take(whole.reshape(blocks, seqs, -1, whole.shape[-1]), me, 1)

    place = jnp.arange(cap, dtype=jnp.int32)
    block_of, in_block = place // (ROWS * lanes), place % (ROWS * lanes)
    row_of = block_of * ROWS + in_block % ROWS
    ids = row_of * lanes + in_block // ROWS
    own_before, own_count = take(slot_before, group), take(slot_rows, group)
    holds = (row_of[:, None] >= own_before[None]) & (row_of[:, None] < (own_before + own_count)[None])
    begin_row = jnp.sum(jnp.where(holds, own_before[None], 0), axis=1)
    begins = jnp.where(jnp.any(holds, axis=1), begin_row * lanes, ids)
    ids, begins = ids.astype(f32), begins.astype(f32)
    head_ids = me * heads + jnp.arange(heads, dtype=jnp.int32)
    slopes = 2.0 ** (-8.0 * (head_ids.astype(f32) + 1.0) / HEADS)
    one_seq = per_group == 1

    hidden = x_low.astype(f32)
    xhat_one, _ = normalize(hidden)
    normed_one = (xhat_one * gain_one + bias_one).astype(bf16)
    qkv = (jnp.dot(normed_one, full_qkv, preferred_element_type=f32) + bias_all).astype(bf16)
    mixed = attention_forward(qkv, slopes, ids, begins, lanes, one_seq)
    mixed_all = seq_gather(mixed, 1).reshape(cap, width)
    branch = jnp.dot(mixed_all, full_dense, preferred_element_type=f32) + bias_dense
    resid = hidden + branch
    xhat_two, _ = normalize(resid)
    normed_two = (xhat_two * gain_two + bias_two).astype(bf16)
    upper = jnp.dot(normed_two, full_up, preferred_element_type=f32) + bias_up
    activ = gelu_tanh(upper).astype(bf16)
    down = jnp.dot(activ, full_down, preferred_element_type=f32)
    resid_own = own_part(resid)
    down_own = seq_sum(down.reshape(blocks, seqs, -1, width), 1)
    block_out = (resid_own + down_own + bias_down).astype(bf16)

    grad_down = jnp.dot(activ.T, cot_low, preferred_element_type=f32).astype(bf16)
    grad_activ = jnp.dot(cot_low, full_down.T, preferred_element_type=f32)
    grad_upper = jax.vjp(gelu_tanh, upper)[1](grad_activ)[0].astype(bf16)
    grad_up = jnp.dot(normed_two.T, grad_upper, preferred_element_type=f32).astype(bf16)
    grad_bup = jnp.sum(grad_upper.astype(f32), axis=0)
    grad_normed = jnp.dot(grad_upper, full_up.T, preferred_element_type=f32)
    grad_normed = seq_sum(grad_normed.reshape(blocks, seqs, -1, width), 1).reshape(slots, width)
    cot_full = cot_own.reshape(slots, width).astype(f32)
    grad_bdown = jnp.sum(cot_full, axis=0)
    xhat_two, root_two = normalize(resid_own.reshape(slots, width))
    grad_gain_two = jnp.sum(grad_normed * xhat_two, axis=0)
    grad_bias_two = jnp.sum(grad_normed, axis=0)
    grad_resid = cot_full + norm_pull(grad_normed, gain_two, xhat_two, root_two)

    grad_branch = grad_resid.astype(bf16)
    grad_dense = jnp.dot(own_part(mixed_all).reshape(slots, width).T, grad_branch, preferred_element_type=f32).astype(bf16)
    grad_bdense = jnp.sum(grad_branch.astype(f32), axis=0)
    grad_mixed = jnp.dot(grad_branch, full_dense.T, preferred_element_type=f32).astype(bf16)
    got = seq_blocks(grad_mixed.reshape(blocks, -1, seqs, part), 2, bf16)
    if seqs == 2:
        grad_mixed = jnp.where(me == 0, jnp.stack(got, 1), jnp.stack(got[::-1], 1))
    else:
        grad_mixed = jnp.zeros((blocks, seqs) + got[0].shape[1:], bf16)
        for d, g in enumerate(got):
            grad_mixed = lax.dynamic_update_index_in_dim(grad_mixed, g, (me - d) % seqs, 1)
    grad_mixed = grad_mixed.reshape(cap, part)
    planes = qkv.reshape(cap, -1, 2 * HEAD).transpose(1, 0, 2)
    grad_proj = jnp.concatenate(
        attention_backward(planes, grad_mixed, slopes, ids, begins, lanes, one_seq), axis=1
    )
    grad_qkv = jnp.dot(normed_one.T, grad_proj, preferred_element_type=f32).astype(bf16)
    proj_sums = jnp.sum(grad_proj.astype(f32), axis=0)
    grad_one = jnp.dot(grad_proj, full_qkv.T, preferred_element_type=f32)
    grad_one = seq_sum(grad_one.reshape(blocks, seqs, -1, width), 1).reshape(slots, width)
    xhat_one, root_one = normalize(x_own.reshape(slots, width).astype(f32))
    grad_gain_one = jnp.sum(grad_one * xhat_one, axis=0)
    grad_bias_one = jnp.sum(grad_one, axis=0)
    tokens_grad = (grad_resid + norm_pull(grad_one, gain_one, xhat_one, root_one)).astype(bf16)

    row_here = jnp.arange(slots, dtype=jnp.int32)[:, None]
    seq_in = ((row_here >= row_start[None]) & (row_here < (row_start + seq_rows)[None])).astype(jnp.int32)
    home = jnp.arange(lengths.shape[0], dtype=jnp.int32) // per_group
    fetch = jnp.sum(seq_in * (home[None] * rows + slot_before.reshape(-1)[None] + row_here - row_start[None]), axis=1)
    fetch_live = jnp.sum(seq_in, axis=1) > 0

    def to_stream(own):
        sent = own.reshape(blocks, shards, ROWS, width).transpose(1, 0, 2, 3).reshape(shards, rows, width)
        got = lax.all_to_all(sent, "shard", split_axis=0, concat_axis=0, tiled=True)
        taken = jnp.take(got.reshape(-1, width), fetch, axis=0)
        return jnp.where(fetch_live[:, None], taken, jnp.zeros_like(taken))[None]

    down_block = shard_reduce(grad_down.reshape(shards, ff_part, width), bf16)
    up_block = shard_reduce(grad_up.reshape(shards, -1, shards * ff_part), bf16)
    dense_block = shard_reduce(grad_dense.reshape(shards, -1, width), bf16)
    qkv_block = shard_reduce(grad_qkv.reshape(shards, -1, 3 * part), bf16)

    def spread(vector, index_shape):
        zero = jnp.zeros(index_shape, f32)
        return lax.dynamic_update_index_in_dim(zero, vector, me, 1)

    sums = proj_sums.reshape(3, part)
    qv = spread(jnp.stack([sums[0], sums[2]]), (2, seqs, part)).reshape(shards, -1)
    bup = spread(grad_bup.reshape(shards, ff_part), (shards, seqs, ff_part)).reshape(shards, -1)
    rest = (grad_gain_one, grad_bias_one, grad_bdense, grad_gain_two, grad_bias_two, grad_bdown)
    packed = jnp.concatenate([a.reshape(shards, -1) for a in rest] + [qv, bup], axis=1)
    packed = shard_reduce(packed, f32)
    packed = jnp.sum(seq_gather(packed, 0), axis=0)
    cuts, at = [], 0
    for a in [a.reshape(shards, -1) for a in rest] + [qv, bup]:
        cuts.append(packed[at : at + a.shape[1]])
        at += a.shape[1]
    g_gain_one, g_bias_one, g_bdense, g_gain_two, g_bias_two, g_bdown, g_qv, g_bup = cuts

    g_dense = jnp.sum(seq_gather(dense_block.astype(bf16), 0).astype(f32), axis=0)
    g_qkv = seq_gather(qkv_block.astype(bf16).reshape(-1, 3, part), 2).reshape(-1, 3 * width).astype(f32)
    g_up = seq_gather(up_block.astype(bf16).reshape(-1, shards, ff_part), 2).reshape(-1, hidden_units).astype(f32)
    g_down = seq_gather(down_block.astype(bf16), 0).reshape(-1, width).astype(f32)
    return (
        to_stream(block_out), to_stream(tokens_grad.reshape(blocks, -1, width)),
        g_gain_one, g_bias_one, g_qkv, g_qv, g_dense, g_bdense, g_gain_two, g_bias_two, g_up, g_bup, g_down, g_bdown,
    )


def choose(*arguments):
    one = arguments[2].shape[0] == lax.axis_size("shard")
    fused = one and lax.axis_size("seq") == 2 and shard_factors(lax.axis_size("shard")) == (4, 2, 2)
    return (per_device if fused else per_device_any)(*arguments)


def solution(mesh):
    rows, vector, stream = P("shard", None), P("shard"), P(("seq", "shard"), None, None)
    params = (vector, vector, rows, vector, rows, vector, vector, vector, rows, vector, rows, vector)
    return jax.shard_map(
        choose, mesh=mesh, in_specs=(stream, stream, P()) + params, out_specs=(stream, stream) + params, check_vma=False
    )
```

```python
import functools

import jax
import jax.numpy as jnp
import numpy as np
from jax import lax
from jax.experimental import pallas as pl
from jax.experimental.pallas import tpu as pltpu
from jax.sharding import PartitionSpec as P

HEADS = 16
HEAD = 64
ROWS = 8

epsilon = 1e-05
masked_score = -1e30
f32 = jnp.float32
bf16 = jnp.bfloat16


def gelu_tanh(values):
    return (
        0.5
        * values
        * (1.0 + jnp.tanh(0.7978845608028654 * (values + 0.044715 * values * values * values)))
    )


def normalize(hidden):
    center = hidden - jnp.mean(hidden, axis=-1, keepdims=True)
    spread = jnp.mean(center * center, axis=-1, keepdims=True)
    root = lax.rsqrt(spread + epsilon)
    return center * root, root


def norm_pull(grad, gain, xhat, root):
    scaled = grad * gain
    return root * (
        scaled
        - jnp.mean(scaled, axis=-1, keepdims=True)
        - xhat * jnp.mean(scaled * xhat, axis=-1, keepdims=True)
    )


def slot_ids(first, count, lanes):
    place = first + lax.broadcasted_iota(jnp.int32, (count, 1), 0)
    block, inside = place // (ROWS * lanes), place % (ROWS * lanes)
    return (block * ROWS + inside % ROWS) * lanes + inside // ROWS


def blocked_ids(shape, axis, lanes):
    place = lax.broadcasted_iota(jnp.int32, shape, axis)
    high = (ROWS * lanes).bit_length() - 1
    inside = place & (ROWS * lanes - 1)
    row = (place >> high) * ROWS + (inside & (ROWS - 1))
    return (row * lanes + (inside >> (ROWS.bit_length() - 1))).astype(f32)


def attn_mask(scored, allowed):
    return jnp.where(allowed, scored, masked_score)


def attn_fwd_kernel(lanes, tile, one_seq, slope_ref, idc_ref, idr_ref, beginc_ref, q_ref, k_ref, v_ref, o_ref):
    tokens = q_ref.shape[0]
    block = ROWS * lanes
    lane_id = lax.broadcasted_iota(jnp.int32, (1, 2 * HEAD), 1)
    for b in range(tokens // block):
        end = (b + 1) * block

        def step(t, _):
            at = pl.ds(pl.multiple_of(b * block + t * tile, tile), tile)
            q = q_ref[at, :] * jnp.asarray(HEAD**-0.5, bf16)
            ids_q = idc_ref[at, :]
            both = None
            for j in range(2):
                mine = (lane_id // HEAD) == j
                qj = jnp.where(mine, q, jnp.zeros_like(q))
                s = lax.dot_general(
                    qj, k_ref[:end, :], (((1,), (1,)), ((), ())), preferred_element_type=f32
                )
                s = s + slope_ref[0, 0, j] * idr_ref[:, :end]
                if one_seq:
                    own = s[:, b * block :]
                    own = attn_mask(own, idr_ref[:, b * block : end] <= ids_q)
                    s = jnp.concatenate([s[:, : b * block], own], axis=1) if b else own
                else:
                    ids_k = idr_ref[:, :end]
                    s = attn_mask(s, (ids_k <= ids_q) & (ids_k >= beginc_ref[at, :]))
                top = jnp.max(s, axis=1, keepdims=True)
                e = jnp.exp(s - top)
                total = jnp.sum(e, axis=1, keepdims=True)
                o = jnp.dot(e.astype(bf16), v_ref[:end, :], preferred_element_type=f32) / total
                both = o if both is None else jnp.where(mine, o, both)
            o_ref[at, :] = both.astype(bf16)
            return 0

        lax.fori_loop(0, block // tile, step, 0)


def attn_bwd_kernel(
    lanes, tile, one_seq, slope_ref, idc_ref, idr_ref, beginr_ref, q_ref, k_ref, v_ref, do_ref,
    dq_ref, dk_ref, dv_ref, dk_acc, dv_acc, bias_acc,
):
    tokens = q_ref.shape[0]
    block = ROWS * lanes
    lane_id = lax.broadcasted_iota(jnp.int32, (1, 2 * HEAD), 1)
    dk_acc[...] = jnp.zeros_like(dk_acc)
    dv_acc[...] = jnp.zeros_like(dv_acc)
    for j in range(2):
        bias_acc[j] = jnp.broadcast_to(slope_ref[0, 0, j] * idc_ref[...], (tokens, tile))
    for b in range(tokens // block):
        end = (b + 1) * block

        def step(t, _):
            at = pl.ds(pl.multiple_of(b * block + t * tile, tile), tile)
            q = q_ref[at, :] * jnp.asarray(HEAD**-0.5, bf16)
            do = do_ref[at, :]
            ids_q = idr_ref[:, at]
            both = None
            for j in range(2):
                mine = (lane_id // HEAD) == j
                qj = jnp.where(mine, q, jnp.zeros_like(q))
                doj = jnp.where(mine, do, jnp.zeros_like(do))
                s = lax.dot_general(
                    k_ref[:end, :], qj, (((1,), (1,)), ((), ())), preferred_element_type=f32
                )
                s = s + bias_acc[j, :end, :]
                if one_seq:
                    own = s[b * block :, :]
                    own = attn_mask(own, idc_ref[b * block : end, :] <= ids_q)
                    s = jnp.concatenate([s[: b * block, :], own], axis=0) if b else own
                else:
                    ids_k = idc_ref[:end, :]
                    s = attn_mask(s, (ids_k <= ids_q) & (ids_k >= beginr_ref[:, at]))
                top = jnp.max(s, axis=0, keepdims=True)
                e = jnp.exp(s - top)
                probs = e * (1.0 / jnp.sum(e, axis=0, keepdims=True))
                dv_acc[:end, :] += jnp.dot(probs.astype(bf16), doj, preferred_element_type=f32)
                dp = lax.dot_general(
                    v_ref[:end, :], doj, (((1,), (1,)), ((), ())), preferred_element_type=f32
                )
                inner = jnp.sum(probs * dp, axis=0, keepdims=True)
                ds = (probs * (dp - inner)).astype(bf16)
                dk_acc[:end, :] += jnp.dot(ds, qj, preferred_element_type=f32)
                dq = lax.dot_general(
                    ds, k_ref[:end, :], (((0,), (0,)), ((), ())), preferred_element_type=f32
                )
                both = dq if both is None else jnp.where(mine, dq, both)
            dq_ref[at, :] = (both * (HEAD**-0.5)).astype(bf16)
            return 0

        lax.fori_loop(0, block // tile, step, 0)
    dk_ref[...] = dk_acc[...].astype(bf16)
    dv_ref[...] = dv_acc[...].astype(bf16)


def attn_shape(tokens, width, lanes):
    pairs = width // (2 * HEAD)
    tile = min(256, ROWS * lanes)
    return pairs, tile


def attention_forward(qkv, slopes, ids, begins, lanes, one_seq):
    tokens, width = qkv.shape[0], qkv.shape[1] // 3
    pairs, tile = attn_shape(tokens, width, lanes)
    column = lambda part: pl.BlockSpec((tokens, 2 * HEAD), lambda h, part=part: (0, part * pairs + h))
    whole = lambda a: pl.BlockSpec(a.shape, lambda h: (0, 0))
    idc, idr, beginc = ids[:, None], ids[None, :], begins[:, None]
    half = tokens * tokens * 5 // 8
    return pl.pallas_call(
        functools.partial(attn_fwd_kernel, lanes, tile, one_seq),
        grid=(pairs,),
        in_specs=[
            pl.BlockSpec((1, 1, 2), lambda h: (h, 0, 0), memory_space=pltpu.SMEM),
            whole(idc), whole(idr), whole(beginc), column(0), column(1), column(2),
        ],
        out_specs=pl.BlockSpec((tokens, 2 * HEAD), lambda h: (0, h)),
        out_shape=jax.ShapeDtypeStruct((tokens, width), bf16),
        compiler_params=pltpu.CompilerParams(vmem_limit_bytes=48 * 2**20),
        cost_estimate=pl.CostEstimate(
            flops=8 * pairs * half * HEAD * 2, transcendentals=2 * pairs * half, bytes_accessed=8 * tokens * width
        ),
        name="attention_forward",
    )(slopes.reshape(pairs, 1, 2), idc, idr, beginc, qkv, qkv, qkv)


def attention_backward(qkv, grad_out, slopes, ids, begins, lanes, one_seq):
    tokens, width = grad_out.shape
    pairs, tile = attn_shape(tokens, width, lanes)
    column = lambda part: pl.BlockSpec((tokens, 2 * HEAD), lambda h, part=part: (0, part * pairs + h))
    whole = lambda a: pl.BlockSpec(a.shape, lambda h: (0, 0))
    idc, idr, beginr = ids[:, None], ids[None, :], begins[None, :]
    plane = lambda part: pl.BlockSpec((None, tokens, 2 * HEAD), lambda h, part=part: (part * pairs + h, 0, 0))
    out = jax.ShapeDtypeStruct((tokens, width), bf16)
    half = tokens * tokens * 5 // 8
    return pl.pallas_call(
        functools.partial(attn_bwd_kernel, lanes, tile, one_seq),
        grid=(pairs,),
        in_specs=[
            pl.BlockSpec((1, 1, 2), lambda h: (h, 0, 0), memory_space=pltpu.SMEM),
            whole(idc), whole(idr), whole(beginr), plane(0), plane(1), plane(2), column(0),
        ],
        out_specs=[column(0)] * 3,
        out_shape=[out] * 3,
        scratch_shapes=[
            pltpu.VMEM((tokens, 2 * HEAD), f32), pltpu.VMEM((tokens, 2 * HEAD), f32), pltpu.VMEM((2, tokens, tile), f32),
        ],
        compiler_params=pltpu.CompilerParams(vmem_limit_bytes=56 * 2**20),
        cost_estimate=pl.CostEstimate(
            flops=20 * pairs * half * HEAD * 2, transcendentals=2 * pairs * half, bytes_accessed=14 * tokens * width
        ),
        name="attention_backward",
    )(slopes.reshape(pairs, 1, 2), idc, idr, beginr, qkv, qkv, qkv, grad_out)


def take(blocks, index, axis=0):
    return lax.dynamic_index_in_dim(blocks, index, axis, keepdims=False)


def seq_gather(block, axis):
    n, me = lax.axis_size("seq"), lax.axis_index("seq")
    shape = block.shape[:axis] + (n,) + block.shape[axis:]
    if n == 2:
        peer = lax.ppermute(block, "seq", [(0, 1), (1, 0)])
        return jnp.where(me == 0, jnp.stack([block, peer], axis), jnp.stack([peer, block], axis))
    whole = lax.dynamic_update_index_in_dim(jnp.zeros(shape, block.dtype), block, me, axis)
    for d in range(1, n):
        got = lax.ppermute(block, "seq", [(i, (i + d) % n) for i in range(n)])
        whole = lax.dynamic_update_index_in_dim(whole, got, (me - d) % n, axis)
    return whole


def seq_blocks(whole, axis, dtype):
    n, me = lax.axis_size("seq"), lax.axis_index("seq")
    got = [take(whole, me, axis)]
    for d in range(1, n):
        sent = take(whole, (me + d) % n, axis).astype(dtype)
        got.append(lax.ppermute(sent, "seq", [(i, (i + d) % n) for i in range(n)]))
    return got


def seq_sum(whole, axis, dtype=bf16):
    got = seq_blocks(whole, axis, dtype)
    return sum((g.astype(f32) for g in got[1:]), got[0].astype(f32))


def shard_factors(n):
    nc = 2 if n % 2 == 0 else 1
    nz = 4 if n % (4 * nc) == 0 else 1
    return nz, n // (nz * nc), nc


def shard_reduce(blocks, dtype):
    n, me = lax.axis_size("shard"), lax.axis_index("shard")
    sizes = shard_factors(n)
    blocks = blocks.reshape(sizes + blocks.shape[1:])
    place = (me // (sizes[1] * sizes[2]), me // sizes[2] % sizes[1], me % sizes[2])
    strides = (sizes[1] * sizes[2], sizes[2], 1)
    for axis in (2, 1, 0):
        size, mine, stride = sizes[axis], place[axis], strides[axis]
        total = take(blocks, mine, axis).astype(f32)
        for d in range(1, size):
            sent = take(blocks, (mine + d) % size, axis).astype(dtype)
            pairs = [
                (i, i - (i // stride % size) * stride + ((i // stride % size + d) % size) * stride)
                for i in range(n)
            ]
            total = total + lax.ppermute(sent, "shard", pairs).astype(f32)
        blocks = total if axis == 0 else total.astype(dtype)
    return blocks


MESH = pl.DeviceIdType.MESH


class Geometry:
    def __init__(self, seqs, shards):
        self.seqs, self.shards = seqs, shards
        self.sizes = shard_factors(shards)
        self.s, self.k = lax.axis_index("seq"), lax.axis_index("shard")
        nz, ny, nc = self.sizes
        self.z, self.y, self.c = self.k // (ny * nc), self.k // nc % ny, self.k % nc
        self.inner = (self.z + 1) // 2 % 2
        high = self.z // 2
        self.line = (self.z, self.z + 1 - 2 * (self.z % 2), 2 - high, 3 - 3 * high)

    def slot(self, i, dy, dc):
        nz, ny, nc = self.sizes
        return (self.line[i] * ny + (self.y + dy) % ny) * nc + (self.c + dc) % nc


class Wires:
    def __init__(self, geometry, send_sems, recv_sems):
        self.g, self.send_sems, self.recv_sems = geometry, send_sems, recv_sems
        self.sends, self.used = [], 0

    def block(self, count):
        first = self.used
        self.used += count
        return first

    def copy(self, src, dst, sent, got, s, k):
        return pltpu.make_async_remote_copy(
            src_ref=src, dst_ref=dst, send_sem=self.send_sems.at[sent], recv_sem=self.recv_sems.at[got],
            device_id={"seq": s, "shard": k}, device_id_type=MESH,
        )

    def send_as(self, src, dst, sent, got, s, k, like):
        self.copy(src, dst, sent, got, s, k).start()
        self.sends.append((like, sent))

    def recorded(self, like, index):
        self.sends.append((like, index))

    def send(self, src, dst, index, s, k, like):
        self.send_as(src, dst, index, index, s, k, like)

    def arrived(self, dst, index):
        self.copy(dst, dst, index, index, 1 - self.g.s, self.g.k).wait_recv()

    def drain(self):
        for like, index in self.sends:
            self.copy(like, like, index, index, 1 - self.g.s, self.g.k).wait_send()
        self.sends = []


def enter(geometry):
    g = geometry
    barrier = pltpu.get_barrier_semaphore()
    for d in range(1, g.shards):
        pl.semaphore_signal(
            barrier, inc=1, device_id={"seq": g.s, "shard": (g.k + d) % g.shards}, device_id_type=MESH
        )
    pl.semaphore_signal(barrier, inc=1, device_id={"seq": 1 - g.s, "shard": g.k}, device_id_type=MESH)
    pl.semaphore_wait(barrier, g.shards)


class Gather:
    def __init__(self, wires, own, out):
        self.w, self.g, self.own, self.out = wires, wires.g, own, out
        nz, ny, nc = self.g.sizes
        self.z0 = wires.block(nz)
        self.on0 = wires.block(nz)
        self.y0 = wires.block(nz * ny)
        self.c0 = wires.block(nz * ny * nc)

    def on_y(self, i, src):
        g = self.g
        for dy in range(1, g.sizes[1]):
            self.w.send(src, self.out.at[g.slot(i, 0, 0)], self.y0 + i * g.sizes[1] + dy, g.s, g.slot(0, dy, 0), self.own)

    def on_core(self, i, dy, src):
        g = self.g
        for dc in range(1, g.sizes[2]):
            index = self.c0 + (i * g.sizes[1] + dy) * g.sizes[2] + dc
            self.w.send(src, self.out.at[g.slot(i, -dy, 0)], index, g.s, g.slot(0, 0, dc), self.own)

    def start(self):
        g = self.g
        here = self.out.at[g.k]
        self.w.send_as(self.own, here, self.z0 + 2, self.z0 + 3 - g.inner, g.s, g.slot(2, 0, 0), self.own)
        self.w.send(self.own, here, self.z0 + 1, g.s, g.slot(1, 0, 0), self.own)

    def start_near(self):
        self.on_y(0, self.own)
        self.on_core(0, 0, self.own)

    def poll_z(self):
        g = self.g
        for i in (1, 2, 3):
            at = self.out.at[g.slot(i, 0, 0)]
            self.w.arrived(at, self.z0 + i)
            if i > 1:

                @pl.when(g.inner == 1)
                def _(at=at, i=i):
                    self.w.copy(at, at, self.on0 + i, self.z0 + i, g.s, g.slot(1, 0, 0)).start()

            self.on_y(i, at)
            self.on_core(i, 0, at)

    def poll_y(self):
        g = self.g
        for i in range(g.sizes[0]):
            for dy in range(1, g.sizes[1]):
                at = self.out.at[g.slot(i, -dy, 0)]
                self.w.arrived(at, self.y0 + i * g.sizes[1] + dy)
                self.on_core(i, dy, at)

    def finish(self):
        g = self.g
        for i in range(g.sizes[0]):
            for dy in range(g.sizes[1]):
                for dc in range(1, g.sizes[2]):
                    at = self.out.at[g.slot(i, -dy, -dc)]
                    self.w.arrived(at, self.c0 + (i * g.sizes[1] + dy) * g.sizes[2] + dc)

        @pl.when(g.inner == 1)
        def _():
            for i in (2, 3):
                self.w.copy(self.own, self.own, self.on0 + i, self.z0 + i, g.s, g.k).wait_send()


class Tokens:
    def __init__(self, wires, packed, out):
        self.w, self.g, self.packed, self.out = wires, wires.g, packed, out
        self.blocks = out.shape[0]
        self.at = wires.block((self.g.shards + 1) * self.blocks)
        self.like, self.row = packed.at[0, 0], packed.at[:, 0]

    def index(self, b, d):
        return self.at + b * (self.g.shards + 1) + d

    def mine(self, b, s):
        return self.out.at[b, pl.ds(pl.multiple_of(s * self.g.shards, self.g.shards), self.g.shards)]

    def start(self, b):
        g = self.g
        for d in range(1, g.shards):
            to = (g.k + d) % g.shards
            lane = self.out.at[b, g.s * g.shards + g.k]
            self.w.send(self.packed.at[to, b], lane, self.index(b, d), g.s, to, self.like)

    def poll(self, b):
        g = self.g
        for d in range(1, g.shards):
            self.w.arrived(self.out.at[b, g.s * g.shards + (g.k - d) % g.shards], self.index(b, d))
        self.w.send(self.mine(b, g.s), self.mine(b, g.s), self.index(b, g.shards), 1 - g.s, g.k, self.row)

    def finish(self, b):
        self.w.arrived(self.mine(b, 1 - self.g.s), self.index(b, self.g.shards))


class Smalls:
    def __init__(self, wires, held, at):
        self.w, self.g, self.held, self.at = wires, wires.g, held, at

    def start(self):
        g = self.g
        mine = self.held.at[g.k]
        for d in range(1, g.shards):
            self.w.send(mine, mine, self.at + d, g.s, (g.k + d) % g.shards, mine)

    def finish(self):
        g = self.g
        for d in range(1, g.shards):
            self.w.arrived(self.held.at[(g.k - d) % g.shards], self.at + d)


def side_by_side(vec, small, row, to, count):
    for j in range(small.shape[0]):
        vec[to : to + 1, j * count : (j + 1) * count] = small[j, row : row + 1, :count]


def forward_kernel(
    seqs, shards, counts,
    packed, packed_cot, qkv_w, small, dense_w, fc1_w, fc2_w, slopes, lengths,
    x_out, cot_out, n1_out, n2_out, qkvw_out, dense_out, fc1_out, fc2_out, qkv_out, o_out, h2_out, a_out, slope_out,
    w2_out, vec_out,
    x_v, n1_v, n2_v, qkvw_v, small_v, dense_v, fc1_v, fc2_v, blocks_v, cot_v, qkv_v, o_v, h2_v, a_v, slope_v, w2_v, vec_v, idc, idr,
    send_sems, recv_sems, copy_sems,
):
    g = Geometry(seqs, shards)
    wires = Wires(g, send_sems, recv_sems)
    lanes = seqs * shards
    width = n1_v.shape[1]
    part = o_v.shape[2]
    pairs = part // (2 * HEAD)
    ff = fc1_v.shape[2]
    ff_part = ff // shards
    block = ROWS * lanes
    blocks = x_v.shape[0]
    half = block // seqs
    rows = width // shards
    local = []

    def bring(src, dst):
        made = pltpu.make_async_copy(src, dst, copy_sems.at[len(local)])
        made.start()
        local.append(made)
        return made

    def at_block(b):
        return pl.ds(pl.multiple_of(b * block, block), block)

    tokens = Tokens(wires, packed, x_v)
    cots = Tokens(wires, packed_cot, blocks_v)
    smalls_at = wires.block(shards)
    qkv_all = Gather(wires, qkvw_v.at[g.k], qkvw_v)
    dense_all = Gather(wires, dense_v.at[g.k], dense_v)
    up_all = Gather(wires, fc1_v.at[g.k], fc1_v)
    down_all = Gather(wires, fc2_v, fc2_out)
    heads_at = wires.block(blocks)

    staged_qkv = [
        bring(
            qkv_w.at[:, pl.ds(pl.multiple_of(p * width + g.s * part, 128), part)],
            qkvw_v.at[g.k, :, pl.ds(p * part, part)],
        )
        for p in range(3)
    ]
    staged_small = bring(small, small_v.at[g.k])
    staged_dense = bring(dense_w, dense_v.at[g.k])
    staged_up = [
        bring(
            fc1_w.at[:, pl.ds(pl.multiple_of((i * seqs + g.s) * ff_part, 128), ff_part)],
            fc1_v.at[g.k, :, pl.ds(i * ff_part, ff_part)],
        )
        for i in range(shards)
    ]
    staged_x = bring(packed.at[g.k], x_v.at[:, g.s * shards + g.k])
    staged_down = bring(fc2_w.at[pl.ds(pl.multiple_of(g.s * ff_part, 8), ff_part), :], fc2_v)
    staged_cot = bring(packed_cot.at[g.k], blocks_v.at[:, g.s * shards + g.k])
    enter(g)
    idc[...] = blocked_ids(idc.shape, 0, lanes)
    idr[...] = blocked_ids(idr.shape, 1, lanes)
    for made in staged_qkv:
        made.wait()
    smalls = Smalls(wires, small_v, smalls_at)
    qkv_all.start()
    qkv_all.start_near()
    tokens.start(0)
    tokens.start(1)
    staged_small.wait()
    staged_dense.wait()
    for made in staged_up:
        made.wait()
    staged_down.wait()
    staged_x.wait()
    staged_cot.wait()
    kept = [bring(fc2_v, fc2_out.at[g.k])]
    smalls.start()
    dense_all.start_near()
    up_all.start_near()
    down_all.start_near()
    tokens.poll(0)
    tokens.start(2)
    qkv_all.poll_z()
    tokens.poll(1)
    tokens.start(3)
    dense_all.start()
    up_all.start()
    smalls.finish()

    for row in (0, 1, 3, 4, 5, 7):
        side_by_side(vec_v, small_v, row, row, rows)
    vec_v[2:3, :] = jnp.zeros((1, vec_v.shape[1]), f32)
    per = 2 * width // shards
    for i in range(part // per):
        for row, side in ((0, 0), (2, 1)):
            j = (side * width + g.s * part) // per + i
            vec_v[2:3, row * part + i * per : row * part + (i + 1) * per] = small_v[j, 2:3, :per]
    for j in range(shards):
        vec_v[6:7, j * ff_part : (j + 1) * ff_part] = small_v[j, 6:7, pl.ds(pl.multiple_of(g.s * ff_part, 128), ff_part)]

    qkv_all.poll_y()
    tokens.poll(2)
    tokens.poll(3)
    down_all.start()
    qkv_all.finish()
    kept += [bring(qkvw_v, qkvw_out), bring(vec_v, vec_out)]

    lane_id = lax.broadcasted_iota(jnp.int32, (1, 2 * HEAD), 1)
    tile = min(256, block)

    def project(b):
        x = x_v[b].astype(f32).reshape(block, width)
        xhat, _ = normalize(x)
        n1 = (xhat * vec_v[0:1, :width] + vec_v[1:2, :width]).astype(bf16)
        at = at_block(b)
        n1_v[at, :] = n1
        for p in range(3):
            weight = qkvw_v[:, :, p * part : (p + 1) * part].reshape(width, part)
            out = jnp.dot(n1, weight, preferred_element_type=f32) + vec_v[2:3, p * part : (p + 1) * part]
            out = out.astype(bf16)
            for h in range(pairs):
                qkv_v[p * pairs + h, at, :] = out[:, h * 2 * HEAD : (h + 1) * 2 * HEAD]

    def attend(b):
        end = (b + 1) * block

        @pl.loop(0, pairs)
        def _(h):
            q_ref, k_ref, v_ref = qkv_v.at[h], qkv_v.at[pairs + h], qkv_v.at[2 * pairs + h]
            for t in range(block // tile):
                at = pl.ds(b * block + t * tile, tile)
                q = q_ref[at, :] * jnp.asarray(HEAD**-0.5, bf16)
                ids_q = idc[at, :]

                def one_head(j, both):
                    mine = (lane_id >= HEAD).astype(jnp.int32) == j
                    qj = jnp.where(mine, q, jnp.zeros_like(q))
                    s = lax.dot_general(
                        qj, k_ref[:end, :], (((1,), (1,)), ((), ())), preferred_element_type=f32
                    )
                    s = s + slopes[g.s * pairs + h, j] * idr[:, :end]
                    tail = attn_mask(s[:, b * block :], idr[:, b * block : end] <= ids_q)
                    s = jnp.concatenate([s[:, : b * block], tail], axis=1) if b else tail
                    top = jnp.max(s, axis=1, keepdims=True)
                    e = jnp.exp(s - top)
                    total = jnp.sum(e, axis=1, keepdims=True)
                    o = jnp.dot(e.astype(bf16), v_ref[:end, :], preferred_element_type=f32) / total
                    return jnp.where(mine, o, both)

                both = lax.fori_loop(0, 2, one_head, jnp.zeros((tile, 2 * HEAD), f32))
                o_v[g.s, at, pl.ds(pl.multiple_of(h * 2 * HEAD, 2 * HEAD), 2 * HEAD)] = both.astype(bf16)

    def head_copy(b):
        mine = o_v.at[g.s, at_block(b)]
        return wires.copy(mine, mine, heads_at + b, heads_at + b, 1 - g.s, g.k)

    for b in range(blocks):
        tokens.finish(b)
        project(b)
        attend(b)
        head_copy(b).start()
        if b == 0:
            dense_all.poll_z()
        if b == 1:
            up_all.poll_z()
        if b == 2:
            dense_all.poll_y()
            cots.start(0)
            cots.start(1)
        if b == 3:
            up_all.poll_y()
    kept += [bring(x_v, x_out), bring(n1_v, n1_out), bring(qkv_v, qkv_out)]
    down_all.poll_z()
    dense_all.finish()
    kept.append(bring(dense_v, dense_out))
    up_all.finish()
    kept.append(bring(fc1_v, fc1_out))

    @pl.loop(0, blocks)
    def _(b):
        at = at_block(b)
        wires.arrived(o_v.at[1 - g.s, at], heads_at + b)
        branch = jnp.dot(
            o_v[0, at, :], dense_v[: shards // 2].reshape(part, width), preferred_element_type=f32
        ) + jnp.dot(o_v[1, at, :], dense_v[shards // 2 :].reshape(part, width), preferred_element_type=f32)
        resid = x_v[b].astype(f32).reshape(block, width) + branch + vec_v[3:4, :width]
        h2_v[b] = jnp.where(g.s == 0, resid[:half], resid[half:])
        xhat, _ = normalize(resid)
        n2 = (xhat * vec_v[4:5, :width] + vec_v[5:6, :width]).astype(bf16)
        n2_v[at, :] = n2
        step = min(512, ff)

        @pl.loop(0, ff // step)
        def _(n):
            cut = pl.ds(pl.multiple_of(n * step, step), step)
            u = jnp.dot(n2_v[at, :], fc1_v[:, :, cut].reshape(width, step), preferred_element_type=f32) + vec_v[6:7, cut]
            inside = 0.7978845608028654 * u * (1.0 + 0.044715 * u * u)
            t = jnp.tanh(inside)
            a_v[at, cut] = (0.5 * u * (1.0 + t)).astype(bf16)
            slope = 0.5 * (1.0 + t) + 0.5 * u * (1.0 - t * t) * (
                0.7978845608028654 + (0.7978845608028654 * 3.0 * 0.044715) * u * u
            )
            slope_v[at, cut] = slope.astype(bf16)

        @pl.when(b == 0)
        def _():
            cots.poll(0)
            cots.start(2)

        @pl.when(b == 1)
        def _():
            cots.poll(1)
            cots.start(3)

        @pl.when(b == 2)
        def _():
            cots.poll(2)


    cots.poll(3)
    kept.append(bring(o_v, o_out))
    kept += [bring(n2_v, n2_out), bring(h2_v, h2_out), bring(a_v, a_out), bring(slope_v, slope_out)]
    down_all.poll_y()
    for b in range(blocks):
        cots.finish(b)

    @pl.loop(0, blocks)
    def _(b):
        at = at_block(b)
        grad = blocks_v[b].astype(f32).reshape(block, width)
        cot_v[at, :] = jnp.where(idc[at, :] < lengths[g.k].astype(f32), grad, 0.0).astype(bf16)

    kept.append(bring(cot_v, cot_out))

    @pl.loop(0, ff // (2 * ff_part))
    def _(m):
        cut = a_v[:, pl.ds(pl.multiple_of(m * 2 * ff_part, 128), 2 * ff_part)]
        out = lax.dot_general(cut, cot_v[...], (((0,), (0,)), ((), ())), preferred_element_type=f32).astype(bf16)
        w2_v[pl.ds(2 * m, 2)] = out.reshape(2, ff_part, width)

    kept.append(bring(w2_v, w2_out))
    down_all.finish()
    for b in range(blocks):
        head_copy(b).wait_send()
    wires.drain()
    for made in kept:
        made.wait()
    assert wires.used <= counts[0] and len(local) <= counts[1]


def forward_exchange(packed, packed_cot, qkv_w, small, dense_w, fc1_w, fc2_w, slopes, lengths, seqs, shards):
    width, own = qkv_w.shape[0] * shards, qkv_w.shape[0]
    lanes = seqs * shards
    blocks = packed.shape[1]
    block = lanes * ROWS
    cap = blocks * block
    part = width // seqs
    pairs = part // (2 * HEAD)
    ff = fc1_w.shape[1] // seqs
    ff_part = ff // shards
    counts = (384, 64)
    any_ = pl.BlockSpec(memory_space=pl.ANY)
    vmem = pl.BlockSpec(memory_space=pltpu.VMEM)
    smem = pl.BlockSpec(memory_space=pltpu.SMEM)
    x_shape = ((blocks, lanes, ROWS, width), bf16)
    wide, long = ((cap, width), bf16), ((cap, ff), bf16)
    qkvw, dense, fc1, fc2 = (
        ((shards,) + tail, bf16) for tail in ((own, 3 * part), (own, width), (own, ff), (ff_part, width))
    )
    qkv, heads = ((3 * pairs, cap, 2 * HEAD), bf16), ((seqs, cap, part), bf16)
    h2, vec = ((blocks, block // seqs, width), f32), ((8, max(width, 3 * part, ff)), f32)
    outs = [x_shape, wide, wide, wide, qkvw, dense, fc1, fc2, qkv, heads, h2, long, long, fc2, vec]
    scratch = [
        x_shape, wide, wide, qkvw, ((shards,) + small.shape, f32), dense, fc1, ((ff_part, width), bf16), x_shape, wide,
        qkv, heads, h2, long, long, fc2, vec, ((cap, 1), f32), ((1, cap), f32),
    ]
    return pl.pallas_call(
        functools.partial(forward_kernel, seqs, shards, counts),
        in_specs=[any_] * 7 + [smem] * 2,
        out_specs=[any_] * len(outs),
        out_shape=[jax.ShapeDtypeStruct(s, d) for s, d in outs],
        scratch_shapes=[pltpu.VMEM(s, d) for s, d in scratch]
        + [pltpu.SemaphoreType.DMA((counts[0],)), pltpu.SemaphoreType.DMA((counts[0],)), pltpu.SemaphoreType.DMA((counts[1],))],
        compiler_params=pltpu.CompilerParams(collective_id=1, has_side_effects=True, vmem_limit_bytes=60 * 2**20),
        name="forward_exchange",
    )(
        packed, packed_cot, qkv_w, small, dense_w, fc1_w, fc2_w, slopes, lengths,
    )


class Scatter:
    def __init__(self, wires, full, own, bufs):
        self.w, self.g, self.full, self.own = wires, wires.g, full, own
        self.rc, self.ry, self.rz, self.fin = bufs
        self.at = wires.block(8)
        self.one = self.rz.at[0] if self.rz is not None else None

    def add(self, count, into, other):
        @pl.loop(0, count)
        def _(i):
            a, b = into(i), other(i)
            a[...] = (a[...].astype(f32) + b[...].astype(f32)).astype(bf16)

    def core_send(self):
        g = self.g
        self.w.send(self.full.at[:, :, 1 - g.c], self.rc, self.at, g.s, g.slot(0, 0, 1), self.rc)

    def core_done(self):
        g = self.g
        self.w.arrived(self.rc, self.at)
        self.add(8, lambda i: self.rc.at[i // 2, i % 2], lambda i: self.own(i // 2, i % 2))
        if self.ry is not None:
            self.y_send()

    def y_send(self):
        g = self.g
        self.w.send(self.rc.at[:, 1 - g.y], self.ry, self.at + 1, g.s, g.slot(0, 1, 0), self.ry)

    def y_done(self):
        g = self.g
        self.w.arrived(self.ry, self.at + 1)
        self.add(4, lambda i: self.ry.at[i], lambda i: self.rc.at[i, g.y])

    def z_send(self):
        g = self.g
        partner = g.slot(1, 0, 0)
        self.w.send(self.ry.at[g.line[1]], self.rz.at[0], self.at + 2, g.s, partner, self.one)

        @pl.when(g.inner == 0)
        def _():
            for i in (2, 3):
                self.w.copy(self.ry.at[g.line[i]], self.rz.at[i], self.at + 1 + i, self.at + 1 + i, g.s, partner).start()

    def z_done(self):
        g = self.g

        @pl.when(g.inner == 1)
        def _():
            for i in (2, 3):
                self.w.arrived(self.rz.at[i], self.at + 1 + i)
                a = self.rz.at[i]
                a[...] = (a[...].astype(f32) + self.ry[g.line[i]].astype(f32)).astype(bf16)
                self.w.copy(a, self.rz.at[1], self.at + 1 + i, self.at + 5, g.s, g.slot(i, 0, 0)).start()

    def final(self):
        g = self.g
        self.w.arrived(self.rz.at[0], self.at + 2)
        self.w.arrived(self.rz.at[1], self.at + 5)
        total = self.ry[g.z].astype(f32) + self.rz[0].astype(f32) + self.rz[1].astype(f32)
        self.fin[0] = total.astype(bf16)
        self.w.send(self.fin.at[0], self.fin.at[1], self.at + 6, 1 - g.s, g.k, self.fin.at[0])

    def done(self):
        self.w.arrived(self.fin.at[1], self.at + 6)
        for i in (2, 3):
            self.w.copy(self.fin.at[0], self.fin.at[0], self.at + 1 + i, self.at + 1 + i, self.g.s, self.g.k).wait_send()


class Back:
    def __init__(self, wires, src, dst, pieces):
        self.w, self.g, self.src, self.dst, self.pieces = wires, wires.g, src, dst, pieces
        self.at = wires.block(wires.g.shards * pieces)
        self.per = src.shape[0] // pieces
        self.like = src.at[pl.ds(0, self.per), 0]

    def cut(self, ref, i):
        return ref.at[pl.ds(i * self.per, self.per)]

    def send(self, i):
        g = self.g
        for d in range(1, g.shards):
            to = (g.k + d) % g.shards
            src = self.src.at[pl.ds(i * self.per, self.per), to]
            index = self.at + i * g.shards + d
            self.w.copy(src, self.cut(self.dst.at[g.k], i), index, index, g.s, to).start()

    def finish(self):
        g = self.g
        for i in range(self.pieces):
            for d in range(1, g.shards):
                self.w.recorded(self.like, self.at + i * g.shards + d)
                self.w.arrived(self.cut(self.dst.at[(g.k - d) % g.shards], i), self.at + i * g.shards + d)


def middle_kernel(
    seqs, shards, counts,
    a, slope, n2, fc1, fc2, dense, cot, h2, heads, w2, vec,
    dh2_out, do_out, rc1_out, wd_out, keep_out, give_out, ry_out, small_out,
    a_v, du_v, n2_v, fc1_v, fc2_v, dense_v, cot_v, h2_v, heads_v, own_w2, w1_v, wd_v, mine_v, sent_v, got_v,
    da_v, do_v, do_sent, small_v, rc, ry, rc1,
    send_sems, recv_sems, copy_sems,
):
    g = Geometry(seqs, shards)
    wires = Wires(g, send_sems, recv_sems)
    blocks, half, width = h2_v.shape
    block = half * seqs
    ff = a_v.shape[1]
    ff_part = ff // shards
    rows = width // shards
    part = width // seqs
    local = []

    def bring(src, dst):
        made = pltpu.make_async_copy(src, dst, copy_sems.at[len(local)])
        made.start()
        local.append(made)
        return made

    def at_block(b):
        return pl.ds(pl.multiple_of(b * block, block), block)

    def own_rows(b):
        return pl.ds(pl.multiple_of(b * block + g.s * half, half), half)

    down = Scatter(wires, w2, lambda i, j: own_w2.at[i, j], (rc, ry, None, None))
    up = Scatter(wires, w1_v, lambda i, j: w1_v.at[i, j, g.c], (rc1, None, None, None))
    half_at, do_at = wires.block(blocks), wires.block(blocks)
    first = [bring(cot, cot_v), bring(fc2, fc2_v), bring(slope, du_v), bring(fc1, fc1_v)]
    own = bring(w2.at[:, :, g.c], own_w2)
    later = [bring(n2, n2_v), bring(a, a_v), bring(h2, h2_v), bring(dense, dense_v)]
    later += [bring(heads.at[i, own_rows(b), :], heads_v.at[i, pl.ds(b * half, half)]) for i in range(seqs) for b in range(blocks)]
    enter(g)
    down.core_send()
    for made in first:
        made.wait()
    step = min(512, ff)
    per = step // ff_part

    def half_copy(b):
        return wires.copy(sent_v.at[b], got_v.at[b], half_at + b, half_at + b, 1 - g.s, g.k)

    def do_copy(b):
        return wires.copy(do_sent.at[b], do_v.at[b, g.s], do_at + b, do_at + b, 1 - g.s, g.k)

    small_v[...] = jnp.zeros_like(small_v)

    def split(b, total, keep, give):
        @pl.when(g.s == 0)
        def _():
            keep(total[:half])
            give[b] = total[half:].astype(bf16)

        @pl.when(g.s == 1)
        def _():
            keep(total[half:])
            give[b] = total[:half].astype(bf16)

    def du_step(b, sums):
        at = at_block(b)
        grad = cot_v[at, :]
        total, new = None, []
        for n in range(ff // step):
            cut = slice(n * step, (n + 1) * step)
            weight = fc2_v[n * per : (n + 1) * per].reshape(step, width)
            da = lax.dot_general(grad, weight, (((1,), (1,)), ((), ())), preferred_element_type=f32)
            du = (da * du_v[at, cut].astype(f32)).astype(bf16)
            du_v[at, cut] = du
            new.append(sums[n] + jnp.sum(du.astype(f32), axis=0, keepdims=True))
            weight = fc1_v[:, :, cut].reshape(width, step)
            term = lax.dot_general(du, weight, (((1,), (1,)), ((), ())), preferred_element_type=f32)
            total = term if total is None else total + term

        def keep(value):
            mine_v[b] = value

        split(b, total, keep, sent_v)

        @pl.when(b > 0)
        def _():
            half_copy(b - 1).start()

        @pl.when(b == 0)
        def _():
            own.wait()
            down.core_done()

        return tuple(new)

    zero = jnp.zeros((1, step), f32)
    sums = lax.fori_loop(0, blocks, du_step, (zero,) * (ff // step))
    for made in later:
        made.wait()

    @pl.loop(0, width // (4 * rows))
    def _(m):
        @pl.when(m == 0)
        def _():
            half_copy(blocks - 1).start()

        left = n2_v[:, pl.ds(pl.multiple_of(m * 4 * rows, 128), 4 * rows)]
        for n in range(ff // step):
            cut = slice(n * step, (n + 1) * step)
            out = lax.dot_general(left, du_v[:, cut], (((0,), (0,)), ((), ())), preferred_element_type=f32)
            w1_v[m, :, :, :, cut] = out.astype(bf16).reshape(2, 2, rows, step)

    up.core_send()
    kept = []
    for n in range(ff // step):
        for i in range(per):
            small_v[n * per + i, 6:7, pl.ds(pl.multiple_of(g.s * ff_part, 128), ff_part)] = sums[n][
                :, i * ff_part : (i + 1) * ff_part
            ]

    def norm_step(b, sums):
        gains, biases, branch, cots = sums
        wires.arrived(got_v.at[b], half_at + b)
        grad = mine_v[b] + got_v[b].astype(f32)
        xhat, root = normalize(h2_v[b])
        gains = gains + jnp.sum(grad * xhat, axis=0, keepdims=True)
        biases = biases + jnp.sum(grad, axis=0, keepdims=True)
        cot_b = cot_v[own_rows(b), :].astype(f32)
        cots = cots + jnp.sum(cot_b, axis=0, keepdims=True)
        dh2 = cot_b + norm_pull(grad, vec[4:5, :width], xhat, root)
        mine_v[b] = dh2
        da = dh2.astype(bf16)
        branch = branch + jnp.sum(da.astype(f32), axis=0, keepdims=True)
        da_v[pl.ds(pl.multiple_of(b * half, half), half), :] = da
        grads = [
            lax.dot_general(
                da, dense_v[i * (shards // seqs) : (i + 1) * (shards // seqs)].reshape(part, width),
                (((1,), (1,)), ((), ())), preferred_element_type=f32,
            ).astype(bf16)
            for i in range(seqs)
        ]
        do_v[b, g.s] = jnp.where(g.s == 0, grads[0], grads[1])
        do_sent[b] = jnp.where(g.s == 0, grads[1], grads[0])

        @pl.when(b > 0)
        def _():
            do_copy(b - 1).start()

        return gains, biases, branch, cots

    zero = jnp.zeros((1, width), f32)
    sums = lax.fori_loop(0, blocks, norm_step, (zero,) * 4)
    kept.append(bring(mine_v, dh2_out))
    for row, vector in ((4, sums[0]), (5, sums[1]), (3, sums[2]), (7, sums[3])):
        for j in range(shards):
            small_v[j, row : row + 1, :rows] = vector[:, j * rows : (j + 1) * rows]
    do_copy(blocks - 1).start()
    kept.append(bring(small_v, small_out))

    for i in range(seqs):
        out = lax.dot_general(heads_v[i], da_v[...], (((0,), (0,)), ((), ())), preferred_element_type=f32).astype(bf16)
        wd_v[i * (shards // seqs) : (i + 1) * (shards // seqs)] = out.reshape(shards // seqs, rows, width)
    kept.append(bring(wd_v, wd_out))

    @pl.loop(0, blocks)
    def _(b):
        at = at_block(b)
        total = None
        for n in range(ff // step):
            weight = fc2_v[n * per : (n + 1) * per].reshape(step, width)
            term = jnp.dot(a_v[at, n * step : (n + 1) * step], weight, preferred_element_type=f32)
            total = term if total is None else total + term

        def keep(value):
            h2_v[b] = h2_v[b] + value + vec[7:8, :width]

        split(b, total, keep, got_v)

    kept += [bring(h2_v, keep_out), bring(got_v, give_out)]
    up.core_done()
    kept.append(bring(rc1, rc1_out))
    down.y_done()
    kept.append(bring(ry, ry_out))
    for b in range(blocks):
        wires.arrived(do_v.at[b, 1 - g.s], do_at + b)
    kept.append(bring(do_v, do_out))
    for b in range(blocks):
        half_copy(b).wait_send()
        do_copy(b).wait_send()
    wires.drain()
    for made in kept:
        made.wait()
    assert wires.used <= counts[0] and len(local) <= counts[1]


def middle_exchange(a, slope, n2, fc1, fc2, dense, cot, h2, heads, w2, vec, seqs, shards):
    blocks, half, width = h2.shape
    tokens, ff = a.shape
    part = width // seqs
    rows, ff_part = width // shards, ff // shards
    counts = (32, 40)
    any_, vmem = pl.BlockSpec(memory_space=pl.ANY), pl.BlockSpec(memory_space=pltpu.VMEM)
    own32, own16 = ((blocks, half, width), f32), ((blocks, half, width), bf16)
    do, smalls = ((blocks, seqs, half, part), bf16), ((shards, 8, 256), f32)
    w1, wd, ry = ((shards, rows, ff), bf16), ((shards, rows, width), bf16), ((4, ff_part, width), bf16)
    w1 = ((4, 2, 2, rows, ff), bf16)
    rc1 = ((4, 2, rows, ff), bf16)
    outs = [own32, do, rc1, wd, own32, own16, ry, smalls]
    rc = ((4, 2, ff_part, width), bf16)
    scratch = [(v.shape, bf16) for v in (a, slope, n2, fc1, fc2, dense, cot)] + [
        own32, ((seqs, blocks * half, part), bf16), rc, w1, wd, own32, own16, own16, ((blocks * half, width), bf16), do,
        ((blocks, half, part), bf16), smalls, rc, ry, rc1,
    ]
    return pl.pallas_call(
        functools.partial(middle_kernel, seqs, shards, counts),
        in_specs=[any_] * 10 + [vmem],
        out_specs=[any_] * len(outs),
        out_shape=[jax.ShapeDtypeStruct(s, d) for s, d in outs],
        scratch_shapes=[pltpu.VMEM(s, d) for s, d in scratch]
        + [pltpu.SemaphoreType.DMA((counts[0],)), pltpu.SemaphoreType.DMA((counts[0],)), pltpu.SemaphoreType.DMA((counts[1],))],
        compiler_params=pltpu.CompilerParams(collective_id=3, has_side_effects=True, vmem_limit_bytes=62 * 2**20),
        name="middle_exchange",
    )(a, slope, n2, fc1, fc2, dense, cot, h2, heads, w2.reshape((4, 2, 2) + w2.shape[1:]), vec)


def backward_kernel(
    seqs, shards, counts,
    qkv, do, n1, qkvw, x_all, dh2, keep, give, ry2, rc1, wd, smalls, vec, slopes,
    ret_y, ret_x, o_qkv, o_dense, o_up, o_down, o_small,
    qkv_v, do_v, dqkv_v, n1_v, qkvw_v, x_v, dh2_v, dk_acc, dv_acc, bias_acc, mine_v, sent_v, got_v, dx_v, gq_v,
    small_v, small_got, small_fin, small_last, f_qkv, f_dense, f_up, f_down, keep_v, give_v, y_v, own_wd, idc, idr, zero_v,
    *rest,
):
    bufs, (send_sems, recv_sems, copy_sems) = rest[:-3], rest[-3:]
    g = Geometry(seqs, shards)
    wires = Wires(g, send_sems, recv_sems)
    pairs, tokens = do_v.shape[0], do_v.shape[1]
    part = pairs * 2 * HEAD
    width = n1_v.shape[1]
    lanes = seqs * shards
    block = ROWS * lanes
    blocks = tokens // block
    half = block // seqs
    tile = bias_acc.shape[2]
    local = []

    def bring(src, dst):
        made = pltpu.make_async_copy(src, dst, copy_sems.at[len(local)])
        made.start()
        local.append(made)
        return made

    def held(ref):
        return lambda i, j: ref.at[i, j]

    down = Scatter(wires, None, None, (None,) + bufs[0:3])
    up = Scatter(wires, None, None, bufs[3:7])
    dense = Scatter(wires, wd, held(own_wd), bufs[7:11])
    qkv_sum = Scatter(wires, gq_v, lambda i, j: gq_v.at[i, j, g.c], bufs[11:15])
    back_y = Back(wires, y_v, ret_y, blocks)
    give_at = wires.block(blocks)
    back_x = Back(wires, dx_v, ret_x, blocks)
    half_at = wires.block(blocks)
    small_at = wires.block(shards + 1)

    rc_in = bring(rc1, up.rc)
    ry_in = bring(ry2, down.ry)
    first = [bring(qkv, qkv_v)] + [bring(do.at[:, pl.ds(h * 2 * HEAD, 2 * HEAD)], do_v.at[h]) for h in range(pairs)]
    owns = [bring(a.at[:, :, g.c], b) for a, b in ((wd, own_wd),)] + [bring(keep, keep_v)]
    later = [
        bring(n1, n1_v), bring(qkvw, qkvw_v), bring(x_all.at[:, pl.ds(g.s * shards, shards)], x_v), bring(dh2, dh2_v),
        bring(smalls, small_v),
    ]
    enter(g)
    zero_v[...] = jnp.zeros_like(zero_v)
    idc[...] = blocked_ids(idc.shape, 0, lanes)
    idr[...] = blocked_ids(idr.shape, 1, lanes)
    rc_in.wait()
    up.y_send()
    dense.core_send()
    ry_in.wait()
    down.z_send()
    for b in range(blocks):
        wires.send(give.at[b], give_v.at[b], give_at + b, 1 - g.s, g.k, give.at[b])
    for made in first + owns:
        made.wait()

    lane_id = lax.broadcasted_iota(jnp.int32, (1, 2 * HEAD), 1)

    def attend(h):
        q_ref, k_ref, v_ref, do_ref = qkv_v.at[h], qkv_v.at[pairs + h], qkv_v.at[2 * pairs + h], do_v.at[h]
        dk_acc[...] = jnp.zeros_like(dk_acc)
        dv_acc[...] = jnp.zeros_like(dv_acc)
        for j in range(2):
            bias_acc[j] = jnp.broadcast_to(slopes[g.s * pairs + h, j] * idc[...], bias_acc.shape[1:])
        cols = pl.ds(pl.multiple_of(h * 2 * HEAD, 2 * HEAD), 2 * HEAD)
        for b in range(blocks):
            end = (b + 1) * block
            for t in range(block // tile):
                at = pl.ds(b * block + t * tile, tile)
                q = q_ref[at, :] * jnp.asarray(HEAD**-0.5, bf16)
                grad = do_ref[at, :]
                ids_q = idr[:, at]
                both = None
                for j in range(2):
                    mine = (lane_id // HEAD) == j
                    qj = jnp.where(mine, q, jnp.zeros_like(q))
                    doj = jnp.where(mine, grad, jnp.zeros_like(grad))
                    s = lax.dot_general(
                        k_ref[:end, :], qj, (((1,), (1,)), ((), ())), preferred_element_type=f32
                    )
                    s = s + bias_acc[j, :end, :]
                    tail = attn_mask(s[b * block :, :], idc[b * block : end, :] <= ids_q)
                    s = jnp.concatenate([s[: b * block, :], tail], axis=0) if b else tail
                    top = jnp.max(s, axis=0, keepdims=True)
                    e = jnp.exp(s - top)
                    probs = e * (1.0 / jnp.sum(e, axis=0, keepdims=True))
                    dv_acc[:end, :] += jnp.dot(probs.astype(bf16), doj, preferred_element_type=f32)
                    dp = lax.dot_general(
                        v_ref[:end, :], doj, (((1,), (1,)), ((), ())), preferred_element_type=f32
                    )
                    inner = jnp.sum(probs * dp, axis=0, keepdims=True)
                    ds = (probs * (dp - inner)).astype(bf16)
                    dk_acc[:end, :] += jnp.dot(ds, qj, preferred_element_type=f32)
                    dq = lax.dot_general(
                        ds, k_ref[:end, :], (((0,), (0,)), ((), ())), preferred_element_type=f32
                    )
                    both = dq if both is None else jnp.where(mine, dq, both)
                dqkv_v[0, at, cols] = (both * (HEAD**-0.5)).astype(bf16)
        dqkv_v[1, :, cols] = dk_acc[...].astype(bf16)
        dqkv_v[2, :, cols] = dv_acc[...].astype(bf16)

    @pl.loop(0, pairs)
    def _(h):
        attend(h)

        @pl.when(h == 0)
        def _():
            dense.core_done()

        @pl.when(h == 2)
        def _():
            down.z_done()

        @pl.loop(blocks * h // pairs, blocks * (h + 1) // pairs)
        def _(b):
            wires.arrived(give_v.at[b], give_at + b)
            y_v[b] = (keep_v[b] + give_v[b].astype(f32)).reshape(shards, ROWS, width).astype(bf16)
            back_y.send(b)

    for made in later:
        made.wait()

    rows = width // shards

    @pl.loop(0, blocks)
    def _(m):
        cut = n1_v[:, pl.ds(pl.multiple_of(m * block, block), block)]
        for p in range(3):
            out = lax.dot_general(cut, dqkv_v[p], (((0,), (0,)), ((), ())), preferred_element_type=f32).astype(bf16)
            out = out.reshape(block // rows // 2, 2, rows, part)
            for i in range(block // rows // 2):
                at = m * (block // rows // 2) + i
                for j in range(2):
                    gq_v[at // 2, at % 2, j, :, p * part : (p + 1) * part] = out[i, j]

    qkv_sum.core_send()

    def half_copy(b):
        return wires.copy(sent_v.at[b], got_v.at[b], half_at + b, half_at + b, 1 - g.s, g.k)

    @pl.loop(0, blocks)
    def _(b):
        total = None
        for p in range(3):
            weight = qkvw_v[:, :, p * part : (p + 1) * part].reshape(width, part)
            term = lax.dot_general(
                dqkv_v[p, pl.ds(pl.multiple_of(b * block, block), block), :], weight, (((1,), (1,)), ((), ())),
                preferred_element_type=f32,
            )
            total = term if total is None else total + term

        @pl.when(g.s == 0)
        def _():
            mine_v[b] = total[:half]
            sent_v[b] = total[half:].astype(bf16)

        @pl.when(g.s == 1)
        def _():
            mine_v[b] = total[half:]
            sent_v[b] = total[:half].astype(bf16)

        @pl.when(b == 2)
        def _():
            up.y_done()
            up.z_send()

        @pl.when(b > 0)
        def _():
            half_copy(b - 1).start()

    own_y = bring(y_v.at[:, g.k], ret_y.at[g.k])
    half_copy(blocks - 1).start()

    sums = [jnp.sum(dqkv_v[p].astype(f32), axis=0, keepdims=True) for p in (0, 2)]
    per = 2 * width // shards
    for i in range(part // per):
        for half_no in range(2):
            small_v[(half_no * width + g.s * part) // per + i, 2:3, :per] = sums[half_no][:, i * per : (i + 1) * per]
    qkv_sum.core_done()
    dense.y_done()
    dense.z_send()

    def norm_step(b, sums):
        wires.arrived(got_v.at[b], half_at + b)
        grad = mine_v[b] + got_v[b].astype(f32)
        xhat, root = normalize(x_v[b].astype(f32).reshape(half, width))
        gains = sums[0] + jnp.sum(grad * xhat, axis=0, keepdims=True)
        biases = sums[1] + jnp.sum(grad, axis=0, keepdims=True)
        dx = dh2_v[b] + norm_pull(grad, vec[0:1, :width], xhat, root)
        dx_v[b] = dx.reshape(shards, ROWS, width).astype(bf16)
        back_x.send(b)

        @pl.when(b == 0)
        def _():
            up.z_done()

        @pl.when(b == 2)
        def _():
            qkv_sum.y_done()
            qkv_sum.z_send()

        return gains, biases

    gains, biases = lax.fori_loop(0, blocks, norm_step, (jnp.zeros((1, width), f32),) * 2)
    for j in range(shards):
        small_v[j, 0:1, :rows] = gains[:, j * rows : (j + 1) * rows]
        small_v[j, 1:2, :rows] = biases[:, j * rows : (j + 1) * rows]
    kept = [own_y, bring(dx_v.at[:, g.k], ret_x.at[g.k])]
    kept += [bring(zero_v, ret_y.at[shards]), bring(zero_v, ret_x.at[shards])]
    for d in range(1, shards):
        to = (g.k + d) % shards
        wires.send(small_v.at[to], small_got.at[g.k], small_at + d, g.s, to, small_v.at[0])
    small_got[g.k] = small_v[g.k]
    down.final()
    dense.z_done()
    up.final()
    qkv_sum.z_done()
    for d in range(1, shards):
        wires.arrived(small_got.at[(g.k - d) % shards], small_at + d)
    small_fin[0] = jnp.sum(small_got[...], axis=0)
    wires.send(small_fin.at[0], small_fin.at[1], small_at + shards, 1 - g.s, g.k, small_fin.at[0])
    dense.final()

    down.done()
    ff_part = f_down.shape[0] // seqs
    for i, at in ((0, g.s), (1, 1 - g.s)):
        f_down[pl.ds(pl.multiple_of(at * ff_part, ff_part), ff_part), :] = down.fin[i].astype(f32)
    kept.append(bring(f_down, o_down))
    up.done()
    for i, at in ((0, g.s), (1, 1 - g.s)):
        for j in range(shards):
            f_up[:, pl.ds(pl.multiple_of((j * seqs + at) * ff_part, 128), ff_part)] = up.fin[
                i, :, j * ff_part : (j + 1) * ff_part
            ].astype(f32)
    kept.append(bring(f_up, o_up))
    dense.done()
    f_dense[...] = dense.fin[0].astype(f32) + dense.fin[1].astype(f32)
    kept.append(bring(f_dense, o_dense))
    wires.arrived(small_fin.at[1], small_at + shards)
    small_last[...] = small_fin[0] + small_fin[1]
    kept.append(bring(small_last, o_small))
    qkv_sum.final()
    qkv_sum.done()
    for i, at in ((0, g.s), (1, 1 - g.s)):
        for p in range(3):
            f_qkv[:, pl.ds(pl.multiple_of(p * width + at * part, 128), part)] = qkv_sum.fin[
                i, :, p * part : (p + 1) * part
            ].astype(f32)
    kept.append(bring(f_qkv, o_qkv))
    back_y.finish()
    back_x.finish()
    for b in range(blocks):
        half_copy(b).wait_send()
    wires.drain()
    for made in kept:
        made.wait()
    assert wires.used <= counts[0] and len(local) <= counts[1]


def backward_exchange(
    qkv, do, n1, qkvw, x_all, dh2, keep, give, ry2, rc1, wd, smalls, vec, slopes, seqs, shards
):
    tokens, part = do.shape
    width = n1.shape[1]
    pairs = part // (2 * HEAD)
    lanes = seqs * shards
    block = ROWS * lanes
    blocks, half = tokens // block, block // seqs
    tile = min(256, block)
    rows, ff = width // shards, rc1.shape[3]
    ff_part = ff // shards
    counts = (256, 48)
    cut = lambda a: a.reshape((4, 2, 2) + a.shape[1:])
    any_, vmem = pl.BlockSpec(memory_space=pl.ANY), pl.BlockSpec(memory_space=pltpu.VMEM)
    ret = (shards + 1, blocks, ROWS, width)
    outs = [
        (ret, bf16), (ret, bf16), ((rows, 3 * width), f32), ((rows, width), f32), ((rows, seqs * ff), f32),
        ((seqs * ff_part, width), f32), (smalls.shape[1:], f32),
    ]
    blks = [(ff_part, width), (rows, ff), (rows, width), (rows, 3 * part)]
    scratch = [
        ((3 * pairs, tokens, 2 * HEAD), bf16), ((pairs, tokens, 2 * HEAD), bf16), ((3, tokens, part), bf16),
        ((tokens, width), bf16), ((shards, rows, 3 * part), bf16), ((blocks, shards, ROWS, width), bf16),
        ((blocks, half, width), f32), ((tokens, 2 * HEAD), f32), ((tokens, 2 * HEAD), f32), ((2, tokens, tile), f32),
        ((blocks, half, width), f32), ((blocks, half, width), bf16), ((blocks, half, width), bf16),
        ((blocks, shards, ROWS, width), bf16), ((4, 2, 2) + blks[3], bf16), (smalls.shape, f32), (smalls.shape, f32),
        ((2,) + smalls.shape[1:], f32), (smalls.shape[1:], f32), ((rows, 3 * width), f32), ((rows, width), f32), ((rows, seqs * ff), f32),
        ((seqs * ff_part, width), f32), ((blocks, half, width), f32), ((blocks, half, width), bf16),
        ((blocks, shards, ROWS, width), bf16), ((4, 2) + blks[2], bf16),
        ((tokens, 1), f32), ((1, tokens), f32), ((blocks, ROWS, width), bf16),
    ]
    for blk in blks:
        scratch += [((4, 2) + blk, bf16)] * (blk is not blks[0])
        scratch += [((4,) + blk, bf16), ((4,) + blk, bf16), ((2,) + blk, bf16)]
    return pl.pallas_call(
        functools.partial(backward_kernel, seqs, shards, counts),
        in_specs=[any_] * 12 + [vmem, pl.BlockSpec(memory_space=pltpu.SMEM)],
        out_specs=[any_] * len(outs),
        out_shape=[jax.ShapeDtypeStruct(s, d) for s, d in outs],
        scratch_shapes=[pltpu.VMEM(s, d) for s, d in scratch]
        + [pltpu.SemaphoreType.DMA((counts[0],)), pltpu.SemaphoreType.DMA((counts[0],)), pltpu.SemaphoreType.DMA((counts[1],))],
        compiler_params=pltpu.CompilerParams(collective_id=2, has_side_effects=True, vmem_limit_bytes=60 * 2**20),
        name="backward_exchange",
    )(
        qkv, do, n1, qkvw, x_all, dh2, keep, give, ry2, rc1, cut(wd), smalls, vec, slopes,
    )


def layout_tables(lengths, lane_count, group_count, per_group):
    seq_rows = lengths // lane_count
    row_start = jnp.cumsum(seq_rows) - seq_rows
    slot_rows = seq_rows.reshape(group_count, per_group)
    slot_start = row_start.reshape(group_count, per_group)
    slot_before = jnp.cumsum(slot_rows, axis=1) - slot_rows
    return seq_rows, row_start, slot_rows, slot_start, slot_before


def per_device(
    tokens, cotangent, lengths, first_gain, first_bias, qkv_weight, qv_bias, dense_weight, dense_bias,
    second_gain, second_bias, fc1_weight, fc1_bias, fc2_weight, fc2_bias,
):
    shards, seqs = lax.axis_size("shard"), lax.axis_size("seq")
    lanes = shards * seqs
    slots, width = tokens.shape[1], tokens.shape[2]
    rows = slots // shards
    blocks = rows // ROWS

    smalls_in = (first_gain, first_bias, qv_bias, dense_bias, second_gain, second_bias, fc1_bias, fc2_bias)
    small = jnp.stack([jnp.pad(a.astype(f32), (0, 256 - a.shape[0])) for a in smalls_in])
    slopes = jnp.asarray(np.exp2(-8.0 * (np.arange(HEADS) + 1.0) / HEADS).reshape(-1, 2), f32)

    seq_rows = lengths // lanes
    number = jnp.arange(shards, dtype=jnp.int32)
    row_start = jnp.sum(jnp.where(number[None, :] < number[:, None], seq_rows[None, :], 0), axis=1)
    window = (row_start[:, None] + jnp.arange(rows, dtype=jnp.int32)[None, :]).reshape(-1)

    def pack(source):
        return jnp.take(source, window, axis=0, mode="clip").reshape(shards, blocks, ROWS, width)

    (
        x_all, cot_all, normed_one, normed_two, full_qkv, full_dense, full_up, full_down, qkv, mixed, resid, activ, slope,
        grad_down, vectors,
    ) = forward_exchange(
        pack(tokens[0]), pack(cotangent[0]), qkv_weight, small, dense_weight, fc1_weight, fc2_weight,
        slopes, lengths, seqs, shards,
    )
    grad_resid, grad_mixed, grad_up, grad_dense, keep, give, half_sums, small_grads = middle_exchange(
        activ, slope, normed_two, full_up, full_down, full_dense, cot_all, resid, mixed, grad_down, vectors, seqs, shards
    )
    ret_out, ret_grad, g_qkv, g_dense, g_up, g_down, g_small = backward_exchange(
        qkv, grad_mixed.reshape(slots * seqs, width // seqs), normed_one, full_qkv, x_all, grad_resid, keep, give, half_sums,
        grad_up, grad_dense, small_grads, vectors, slopes, seqs, shards,
    )

    row_here = jnp.arange(slots, dtype=jnp.int32)[:, None]
    inside = (row_here >= row_start[None]) & (row_here < (row_start + seq_rows)[None])
    fetch = jnp.sum(jnp.where(inside, number[None] * rows + row_here - row_start[None] - shards * rows, 0), axis=1)
    fetch = fetch + shards * rows

    def to_stream(got):
        return jnp.take(got.reshape(-1, width), fetch, axis=0, mode="clip")[None]

    vectors_out = tuple(g_small[i, : a.shape[0]] for i, a in enumerate(smalls_in))
    g_gain_one, g_bias_one, g_qv, g_bdense, g_gain_two, g_bias_two, g_bup, g_bdown = vectors_out
    return (
        to_stream(ret_out), to_stream(ret_grad),
        g_gain_one, g_bias_one, g_qkv, g_qv, g_dense, g_bdense, g_gain_two, g_bias_two, g_up, g_bup, g_down, g_bdown,
    )


def per_device_any(
    tokens, cotangent, lengths, first_gain, first_bias, qkv_weight, qv_bias, dense_weight, dense_bias,
    second_gain, second_bias, fc1_weight, fc1_bias, fc2_weight, fc2_bias,
):
    shards, seqs = lax.axis_size("shard"), lax.axis_size("seq")
    lanes = shards * seqs
    slots, width = tokens.shape[1], tokens.shape[2]
    rows = slots // shards
    cap = slots * seqs
    per_group = lengths.shape[0] // shards
    hidden_units = fc1_weight.shape[1]
    me, group = lax.axis_index("seq"), lax.axis_index("shard")
    blocks = rows // ROWS
    heads = width // HEAD // seqs
    part = heads * HEAD
    ff_part = hidden_units // shards // seqs

    qkv_half = take(qkv_weight.reshape(-1, 3, seqs, part), me, 2).reshape(-1, 3 * part)
    fc1_half = take(fc1_weight.reshape(-1, shards, seqs, ff_part), me, 2).reshape(-1, shards * ff_part)
    fc2_half = take(fc2_weight.reshape(seqs, ff_part, width), me, 0)
    small = jnp.concatenate(
        [first_gain, first_bias, qv_bias, dense_bias, second_gain, second_bias, fc1_bias, fc2_bias]
    )
    small_rows = -(-small.shape[0] // (3 * part))
    small_rows += -small_rows % 16
    small = jnp.pad(small, (0, small_rows * 3 * part - small.shape[0])).reshape(small_rows, 3 * part)
    gather = lambda a: lax.all_gather(a, "shard", axis=0, tiled=False)
    qkv_small = gather(jnp.concatenate([qkv_half, small], axis=0))
    own_rows = qkv_half.shape[0]
    full_qkv = qkv_small[:, :own_rows].reshape(width, 3 * part)
    smalls = qkv_small[:, own_rows:].reshape(shards, -1).astype(f32)
    full_dense = gather(dense_weight).reshape(width, width)
    full_up = gather(fc1_half).reshape(width, shards * ff_part)
    full_down = gather(fc2_half).reshape(shards * ff_part, width)
    cuts, at = [], 0
    for a in (first_gain, first_bias, qv_bias, dense_bias, second_gain, second_bias, fc1_bias, fc2_bias):
        cuts.append(smalls[:, at : at + a.shape[0]].reshape(-1))
        at += a.shape[0]
    gain_one, bias_one, bias_qv, bias_dense, gain_two, bias_two, bias_up, bias_down = cuts
    bias_q, bias_v = (take(bias_qv[i * width : (i + 1) * width].reshape(seqs, part), me) for i in (0, 1))
    bias_all = jnp.concatenate([bias_q, jnp.zeros_like(bias_q), bias_v])
    bias_up = take(bias_up.reshape(shards, seqs, ff_part), me, 1).reshape(-1)

    seq_rows, row_start, slot_rows, slot_start, slot_before = layout_tables(lengths, lanes, shards, per_group)
    row_in = jnp.arange(rows, dtype=jnp.int32)[None, :, None]
    inside = ((row_in >= slot_before[:, None]) & (row_in < (slot_before + slot_rows)[:, None])).astype(jnp.int32)
    send_live = jnp.sum(inside, axis=2) > 0
    send_row = jnp.sum(inside * (slot_start[:, None] + row_in - slot_before[:, None]), axis=2).reshape(-1)

    def to_groups(source):
        packed = jnp.take(source, send_row, axis=0).reshape(shards, rows, width)
        packed = jnp.where(send_live[:, :, None], packed, jnp.zeros_like(packed))
        got = lax.all_to_all(packed, "shard", split_axis=0, concat_axis=0, tiled=True)
        own = got.reshape(shards, blocks, ROWS, width).transpose(1, 0, 2, 3).reshape(blocks, -1, width)
        return own, seq_gather(own, 1).reshape(cap, width)

    x_own, x_low = to_groups(tokens[0])
    cot_own, cot_low = to_groups(cotangent[0])

    def own_part(whole):
        return take(whole.reshape(blocks, seqs, -1, whole.shape[-1]), me, 1)

    place = jnp.arange(cap, dtype=jnp.int32)
    block_of, in_block = place // (ROWS * lanes), place % (ROWS * lanes)
    row_of = block_of * ROWS + in_block % ROWS
    ids = row_of * lanes + in_block // ROWS
    own_before, own_count = take(slot_before, group), take(slot_rows, group)
    holds = (row_of[:, None] >= own_before[None]) & (row_of[:, None] < (own_before + own_count)[None])
    begin_row = jnp.sum(jnp.where(holds, own_before[None], 0), axis=1)
    begins = jnp.where(jnp.any(holds, axis=1), begin_row * lanes, ids)
    ids, begins = ids.astype(f32), begins.astype(f32)
    head_ids = me * heads + jnp.arange(heads, dtype=jnp.int32)
    slopes = 2.0 ** (-8.0 * (head_ids.astype(f32) + 1.0) / HEADS)
    one_seq = per_group == 1

    hidden = x_low.astype(f32)
    xhat_one, _ = normalize(hidden)
    normed_one = (xhat_one * gain_one + bias_one).astype(bf16)
    qkv = (jnp.dot(normed_one, full_qkv, preferred_element_type=f32) + bias_all).astype(bf16)
    mixed = attention_forward(qkv, slopes, ids, begins, lanes, one_seq)
    mixed_all = seq_gather(mixed, 1).reshape(cap, width)
    branch = jnp.dot(mixed_all, full_dense, preferred_element_type=f32) + bias_dense
    resid = hidden + branch
    xhat_two, _ = normalize(resid)
    normed_two = (xhat_two * gain_two + bias_two).astype(bf16)
    upper = jnp.dot(normed_two, full_up, preferred_element_type=f32) + bias_up
    activ = gelu_tanh(upper).astype(bf16)
    down = jnp.dot(activ, full_down, preferred_element_type=f32)
    resid_own = own_part(resid)
    down_own = seq_sum(down.reshape(blocks, seqs, -1, width), 1)
    block_out = (resid_own + down_own + bias_down).astype(bf16)

    grad_down = jnp.dot(activ.T, cot_low, preferred_element_type=f32).astype(bf16)
    grad_activ = jnp.dot(cot_low, full_down.T, preferred_element_type=f32)
    grad_upper = jax.vjp(gelu_tanh, upper)[1](grad_activ)[0].astype(bf16)
    grad_up = jnp.dot(normed_two.T, grad_upper, preferred_element_type=f32).astype(bf16)
    grad_bup = jnp.sum(grad_upper.astype(f32), axis=0)
    grad_normed = jnp.dot(grad_upper, full_up.T, preferred_element_type=f32)
    grad_normed = seq_sum(grad_normed.reshape(blocks, seqs, -1, width), 1).reshape(slots, width)
    cot_full = cot_own.reshape(slots, width).astype(f32)
    grad_bdown = jnp.sum(cot_full, axis=0)
    xhat_two, root_two = normalize(resid_own.reshape(slots, width))
    grad_gain_two = jnp.sum(grad_normed * xhat_two, axis=0)
    grad_bias_two = jnp.sum(grad_normed, axis=0)
    grad_resid = cot_full + norm_pull(grad_normed, gain_two, xhat_two, root_two)

    grad_branch = grad_resid.astype(bf16)
    grad_dense = jnp.dot(own_part(mixed_all).reshape(slots, width).T, grad_branch, preferred_element_type=f32).astype(bf16)
    grad_bdense = jnp.sum(grad_branch.astype(f32), axis=0)
    grad_mixed = jnp.dot(grad_branch, full_dense.T, preferred_element_type=f32).astype(bf16)
    got = seq_blocks(grad_mixed.reshape(blocks, -1, seqs, part), 2, bf16)
    if seqs == 2:
        grad_mixed = jnp.where(me == 0, jnp.stack(got, 1), jnp.stack(got[::-1], 1))
    else:
        grad_mixed = jnp.zeros((blocks, seqs) + got[0].shape[1:], bf16)
        for d, g in enumerate(got):
            grad_mixed = lax.dynamic_update_index_in_dim(grad_mixed, g, (me - d) % seqs, 1)
    grad_mixed = grad_mixed.reshape(cap, part)
    planes = qkv.reshape(cap, -1, 2 * HEAD).transpose(1, 0, 2)
    grad_proj = jnp.concatenate(
        attention_backward(planes, grad_mixed, slopes, ids, begins, lanes, one_seq), axis=1
    )
    grad_qkv = jnp.dot(normed_one.T, grad_proj, preferred_element_type=f32).astype(bf16)
    proj_sums = jnp.sum(grad_proj.astype(f32), axis=0)
    grad_one = jnp.dot(grad_proj, full_qkv.T, preferred_element_type=f32)
    grad_one = seq_sum(grad_one.reshape(blocks, seqs, -1, width), 1).reshape(slots, width)
    xhat_one, root_one = normalize(x_own.reshape(slots, width).astype(f32))
    grad_gain_one = jnp.sum(grad_one * xhat_one, axis=0)
    grad_bias_one = jnp.sum(grad_one, axis=0)
    tokens_grad = (grad_resid + norm_pull(grad_one, gain_one, xhat_one, root_one)).astype(bf16)

    row_here = jnp.arange(slots, dtype=jnp.int32)[:, None]
    seq_in = ((row_here >= row_start[None]) & (row_here < (row_start + seq_rows)[None])).astype(jnp.int32)
    home = jnp.arange(lengths.shape[0], dtype=jnp.int32) // per_group
    fetch = jnp.sum(seq_in * (home[None] * rows + slot_before.reshape(-1)[None] + row_here - row_start[None]), axis=1)
    fetch_live = jnp.sum(seq_in, axis=1) > 0

    def to_stream(own):
        sent = own.reshape(blocks, shards, ROWS, width).transpose(1, 0, 2, 3).reshape(shards, rows, width)
        got = lax.all_to_all(sent, "shard", split_axis=0, concat_axis=0, tiled=True)
        taken = jnp.take(got.reshape(-1, width), fetch, axis=0)
        return jnp.where(fetch_live[:, None], taken, jnp.zeros_like(taken))[None]

    down_block = shard_reduce(grad_down.reshape(shards, ff_part, width), bf16)
    up_block = shard_reduce(grad_up.reshape(shards, -1, shards * ff_part), bf16)
    dense_block = shard_reduce(grad_dense.reshape(shards, -1, width), bf16)
    qkv_block = shard_reduce(grad_qkv.reshape(shards, -1, 3 * part), bf16)

    def spread(vector, index_shape):
        zero = jnp.zeros(index_shape, f32)
        return lax.dynamic_update_index_in_dim(zero, vector, me, 1)

    sums = proj_sums.reshape(3, part)
    qv = spread(jnp.stack([sums[0], sums[2]]), (2, seqs, part)).reshape(shards, -1)
    bup = spread(grad_bup.reshape(shards, ff_part), (shards, seqs, ff_part)).reshape(shards, -1)
    rest = (grad_gain_one, grad_bias_one, grad_bdense, grad_gain_two, grad_bias_two, grad_bdown)
    packed = jnp.concatenate([a.reshape(shards, -1) for a in rest] + [qv, bup], axis=1)
    packed = shard_reduce(packed, f32)
    packed = jnp.sum(seq_gather(packed, 0), axis=0)
    cuts, at = [], 0
    for a in [a.reshape(shards, -1) for a in rest] + [qv, bup]:
        cuts.append(packed[at : at + a.shape[1]])
        at += a.shape[1]
    g_gain_one, g_bias_one, g_bdense, g_gain_two, g_bias_two, g_bdown, g_qv, g_bup = cuts

    g_dense = jnp.sum(seq_gather(dense_block.astype(bf16), 0).astype(f32), axis=0)
    g_qkv = seq_gather(qkv_block.astype(bf16).reshape(-1, 3, part), 2).reshape(-1, 3 * width).astype(f32)
    g_up = seq_gather(up_block.astype(bf16).reshape(-1, shards, ff_part), 2).reshape(-1, hidden_units).astype(f32)
    g_down = seq_gather(down_block.astype(bf16), 0).reshape(-1, width).astype(f32)
    return (
        to_stream(block_out), to_stream(tokens_grad.reshape(blocks, -1, width)),
        g_gain_one, g_bias_one, g_qkv, g_qv, g_dense, g_bdense, g_gain_two, g_bias_two, g_up, g_bup, g_down, g_bdown,
    )


def choose(*arguments):
    one = arguments[2].shape[0] == lax.axis_size("shard")
    fused = one and lax.axis_size("seq") == 2 and shard_factors(lax.axis_size("shard")) == (4, 2, 2)
    return (per_device if fused else per_device_any)(*arguments)


def solution(mesh):
    rows, vector, stream = P("shard", None), P("shard"), P(("seq", "shard"), None, None)
    params = (vector, vector, rows, vector, rows, vector, vector, vector, rows, vector, rows, vector)
    return jax.shard_map(
        choose, mesh=mesh, in_specs=(stream, stream, P()) + params, out_specs=(stream, stream) + params, check_vma=False
    )
```
